32 devices in a mesh: dp: 16 (over z, y, core), tensor: 2 (over x).
Axes of the slice: x: 2, y: 2, z: 4, core: 2. Of those that a mesh axis runs over, the one named last changes fastest.
Arguments:
- source_embed: bfloat16 [16, 1024, 768], P('dp', 'tensor'), may hold values from -6 to 6
- target_embed: bfloat16 [16, 512, 768], P('dp', 'tensor'), may hold values from -6 to 6
- out_cotangent: bfloat16 [16, 512, 768], P('dp', 'tensor'), may hold values from -6 to 6
- row_flags: int32 [16, 1024], P('dp', 'tensor'), may hold values from 0 to 2, as said below
- source_mask: int32 [16, 1024], P('dp'), may hold values from 0 to 1, as said below
- target_mask: int32 [16, 512], P('dp'), may hold values from 0 to 1, as said below
- attention_weights: float32 [12, 768, 768], P(None, 'dp', 'tensor'), may hold values from -6 to 6
- feed_weights: float32 [4, 768, 3072], P(None, 'dp', 'tensor'), may hold values from -6 to 6
- rows_attention: float32 [12, 768], P(None, 'dp'), may hold values from 2457.6 to 2457600
- columns_attention: float32 [12, 768], P(None, 'tensor'), may hold values from 2457.6 to 2457600
- rows_feed: float32 [4, 768], P(None, 'dp'), may hold values from 7.3728 to 7372.8
- columns_feed: float32 [4, 3072], P(None, 'tensor'), may hold values from 7.3728 to 7372.8
- vector_params: float32 [14, 768], replicated, may hold values from -6 to 6
- vector_moments: float32 [14, 768], P(None, 'dp'), may hold values from 4915.2 to 4915200
Outputs:
- decoder_out: bfloat16 [16, 512, 768], P('dp', 'tensor')
- source_gradient: float32 [16, 1024, 768], P('dp', 'tensor')
- target_gradient: float32 [16, 512, 768], P('dp', 'tensor')
- attention_gradients: float32 [12, 768, 768], P(None, 'dp', 'tensor')
- feed_gradients: float32 [4, 768, 3072], P(None, 'dp', 'tensor')
- vector_gradients: float32 [14, 768], P(None, 'dp')
- attention_updated: float32 [12, 768, 768], P(None, 'dp', 'tensor')
- feed_updated: float32 [4, 768, 3072], P(None, 'dp', 'tensor')
- vector_updated: float32 [14, 768], P(None, 'dp')
- rows_attention_next: float32 [12, 768], P(None, 'dp')
- columns_attention_next: float32 [12, 768], P(None, 'tensor')
- rows_feed_next: float32 [4, 768], P(None, 'dp')
- columns_feed_next: float32 [4, 3072], P(None, 'tensor')
- vector_moments_next: float32 [14, 768], P(None, 'dp')
- final_norm_gradients: float32 [2, 768], P(None, 'dp')
The draws below stay inside these ranges and needn't reach their ends.
Inputs may be any that keep to these rules, and one draw needn't show every extreme that they name: `row_flags`: 0 keeps a source row, 1 marks a gap-sentence row and 2 a masked-token row. `source_mask`: each row is ones followed by zeros with 512 or more ones; the first row is all ones. `target_mask`: each row is ones followed by zeros with 256 or more ones; the first row is all ones.
All inputs are finite; a program needn't handle non-finite values.
Results may differ from the reference program's by a relative error of at most 0.019.
Values may be sent and summed in bfloat16 or wider, within the bound.
A program may use at most 256 MiB of HBM per device.

```python
import math
import jax
import jax.numpy as jnp
from jax import lax

D = 768
HEADS = 12
HEAD_DIM = 64
FF = 3072
SRC = 1024
TGT = 512
PAIRS_ALL = 16


def length_mask(key, pair_count, span_length):
    lengths = jax.random.randint(key, (pair_count,), span_length // 2, span_length + 1)
    lengths = lengths.at[0].set(span_length)
    positions = jnp.arange(span_length)[None, :]
    return (positions < lengths[:, None]).astype(jnp.int32)


def draw_row_flags(key, part):
    picks = jax.random.randint(jax.random.fold_in(key, 3), (PAIRS_ALL, SRC), 0, 10)
    return jnp.where(picks < 7, 0, jnp.where(picks < 9, 1, 2)).astype(jnp.int32)


def draw_source_mask(key, part):
    return length_mask(jax.random.fold_in(key, 1), PAIRS_ALL, SRC)


def draw_target_mask(key, part):
    return length_mask(jax.random.fold_in(key, 2), PAIRS_ALL, TGT)


def draw_attention_weights(key, part):
    normal = jnp.clip(jax.random.normal(key, (12, D, D), jnp.float32), -6.0, 6.0)
    output_slices = jnp.arange(12) % 4 == 3
    scales = jnp.where(output_slices, (SRC / (4.0 * D)) ** 0.5, D ** (-0.5))
    return normal * scales[:, None, None]


def draw_feed_weights(key, part):
    normal = jnp.clip(jax.random.normal(key, (4, D, FF), jnp.float32), -6.0, 6.0)
    second_slices = jnp.arange(4) % 2 == 1
    scales = jnp.where(second_slices, FF ** (-0.5), D ** (-0.5))
    return normal * scales[:, None, None]


def draw_vector_params(key, part):
    first_key, second_key, third_key = jax.random.split(key, 3)
    gains = jax.random.uniform(first_key, (14, D), jnp.float32, 0.5, 1.5)
    shifts = 0.3 * jnp.clip(jax.random.normal(second_key, (14, D), jnp.float32), -6.0, 6.0)
    embeds = jnp.clip(jax.random.normal(third_key, (14, D), jnp.float32), -6.0, 6.0)
    row_index = jnp.arange(14)[:, None]
    return jnp.where(row_index >= 12, embeds, jnp.where(row_index % 2 == 0, gains, shifts))


def block_levels(stream_key, dims, cuts, smallest, top_value):
    def one(position, shards_of):
        draws = jax.random.uniform(jax.random.fold_in(jax.random.fold_in(stream_key, 6), position), (shards_of,), jnp.float32, smallest / len(cuts), top_value / len(cuts))
        return jnp.repeat(jnp.exp(draws), dims[position] // shards_of).reshape((-1,) + (1,) * (len(dims) - position - 1))

    gain = one(*cuts[0])
    for cut in cuts[1:]:
        gain = gain * one(*cut)
    return gain


def noise(stream_key, dims, deviation, most, shards=(), held_as=jnp.bfloat16):
    factor_of = block_levels(stream_key, dims, shards, -0.22, 0.18) if shards else 1.0
    values = jax.random.normal(stream_key, dims, jnp.float32) * deviation * factor_of
    return jnp.minimum(jnp.maximum(values, -most), most).astype(held_as)


def setup_inputs(seed: int = 0) -> dict:
    arg_keys = jax.random.split(jax.random.key(seed), 15)
    source_embed = noise(arg_keys[0], (PAIRS_ALL, SRC, D), 1.0, 6.0, ((0, 16), (1, 2)))
    target_embed = noise(arg_keys[1], (PAIRS_ALL, TGT, D), 1.0, 6.0, ((0, 16), (1, 2)))
    out_cotangent = noise(arg_keys[2], (PAIRS_ALL, TGT, D), 1.0, 6.0, ((0, 16), (1, 2)))
    row_flags = draw_row_flags(jax.random.fold_in(arg_keys[14], 71), 0)
    source_mask = draw_source_mask(jax.random.fold_in(arg_keys[14], 71), 0)
    target_mask = draw_target_mask(jax.random.fold_in(arg_keys[14], 71), 0)
    attention_weights = draw_attention_weights(jax.random.fold_in(arg_keys[14], 71), 0)
    feed_weights = draw_feed_weights(jax.random.fold_in(arg_keys[14], 71), 0)
    rows_attention = jnp.clip(jnp.exp(math.log(2457600) - 6.9077552 * jax.random.uniform(arg_keys[8], (12, D), jnp.float32) ** block_levels(arg_keys[8], (12, D), ((1, 16),), -0.2, 0.2)), 2457.6, 2457600)
    columns_attention = jnp.clip(jnp.exp(math.log(2457600) - 6.9077552 * jax.random.uniform(arg_keys[9], (12, D), jnp.float32) ** block_levels(arg_keys[9], (12, D), ((1, 2),), -0.2, 0.2)), 2457.6, 2457600)
    rows_feed = jnp.clip(jnp.exp(math.log(7372.8) - 6.9077553 * jax.random.uniform(arg_keys[10], (4, D), jnp.float32) ** block_levels(arg_keys[10], (4, D), ((1, 16),), -0.2, 0.2)), 7.3728, 7372.8)
    columns_feed = jnp.clip(jnp.exp(math.log(7372.8) - 6.9077553 * jax.random.uniform(arg_keys[11], (4, FF), jnp.float32) ** block_levels(arg_keys[11], (4, FF), ((1, 2),), -0.2, 0.2)), 7.3728, 7372.8)
    vector_params = draw_vector_params(jax.random.fold_in(arg_keys[14], 71), 0)
    vector_moments = jnp.clip(jnp.exp(math.log(4915200) - 6.9077552 * jax.random.uniform(arg_keys[13], (14, D), jnp.float32) ** block_levels(arg_keys[13], (14, D), ((1, 16),), -0.2, 0.2)), 4915.2, 4915200)
    return {"source_embed": source_embed, "target_embed": target_embed, "out_cotangent": out_cotangent, "row_flags": row_flags, "source_mask": source_mask, "target_mask": target_mask, "attention_weights": attention_weights, "feed_weights": feed_weights, "rows_attention": rows_attention, "columns_attention": columns_attention, "rows_feed": rows_feed, "columns_feed": columns_feed, "vector_params": vector_params, "vector_moments": vector_moments}


@jax.custom_vjp
def low(v):
    return lax.optimization_barrier(v.astype(jnp.bfloat16)).astype(jnp.float32)

@jax.custom_vjp
def low_back(v):
    return v

def low_keep(v):
    return (low(v), None)

def low_pass(kept, grad):
    return (grad,)

def back_keep(v):
    return (v, None)

def back_low(kept, grad):
    return (low(grad),)
low.defvjp(low_keep, low_pass)
low_back.defvjp(back_keep, back_low)
norm_epsilon = 1e-05
decay_rate = 1.0 - 2.0 ** (-0.8)
step_rate = 0.2
masked_score = -1e+30
highest = lax.Precision.HIGHEST

def gelu_exact(values):
    return jax.nn.gelu(values, approximate=False)

def rounded_both(values):
    return low_back(low(values))

def matmul(left_side, right_side):
    return jnp.dot(left_side, right_side, precision=highest)

def matmul_back(left_side, right_side):
    return jnp.einsum('tx,dx->td', left_side, right_side, precision=highest)

def layer_norm(values, norm_gain, norm_shift):
    centre = lax.optimization_barrier(jnp.mean(values, axis=-1, keepdims=True))
    centred = values - centre
    spread = lax.optimization_barrier(jnp.mean(centred * centred, axis=-1, keepdims=True))
    return centred * lax.rsqrt(spread + norm_epsilon) * norm_gain + norm_shift

def attend(queries, key_rows, value_rows, allowed):
    query_heads = queries.reshape(queries.shape[0], HEADS, HEAD_DIM)
    key_heads = key_rows.reshape(key_rows.shape[0], HEADS, HEAD_DIM)
    value_heads = value_rows.reshape(value_rows.shape[0], HEADS, HEAD_DIM)
    scores = low_back(jnp.einsum('qhd,khd->hqk', query_heads, key_heads, precision=highest) * HEAD_DIM ** (-0.5))
    scores = jnp.where(allowed[None], scores, masked_score)
    weights = low(jax.nn.softmax(scores, axis=-1))
    attended = jnp.einsum('hqk,khd->qhd', weights, value_heads, precision=highest)
    return rounded_both(attended.reshape(queries.shape[0], HEADS * HEAD_DIM))

def attention_layer(residual, memory, matrices, vectors, norm_row, allowed):
    normed = low(layer_norm(residual, vectors[norm_row], vectors[norm_row + 1]))
    sources = normed if memory is None else memory
    queries = rounded_both(matmul(normed, matrices[0]))
    key_rows = rounded_both(matmul(sources, matrices[1]))
    value_rows = rounded_both(matmul(sources, matrices[2]))
    attended = attend(queries, key_rows, value_rows, allowed)
    return residual + low_back(matmul_back(attended, matrices[3]))

def feed_layer(residual, matrices, vectors, norm_row):
    normed = low(layer_norm(residual, vectors[norm_row], vectors[norm_row + 1]))
    hidden = low(gelu_exact(low_back(matmul(normed, matrices[0]))))
    return residual + low_back(matmul_back(hidden, matrices[1]))

def pair_forward(attention_low, feed_low, vectors, items):
    source, target, row_kinds, source_keep, target_keep = items
    start_rows = jnp.where((row_kinds == 1)[:, None], vectors[12][None, :], jnp.where((row_kinds == 2)[:, None], vectors[13][None, :], source))
    source_valid = source_keep > 0
    target_valid = target_keep > 0
    source_allowed = jnp.broadcast_to(source_valid[None, :], (source.shape[0], source.shape[0]))
    cross_allowed = jnp.broadcast_to(source_valid[None, :], (target.shape[0], source.shape[0]))
    query_place = jnp.arange(target.shape[0])[:, None]
    key_place = jnp.arange(target.shape[0])[None, :]
    target_allowed = (key_place <= query_place) & target_valid[None, :]
    encoder_mid = attention_layer(start_rows, None, attention_low[0:4], vectors, 0, source_allowed)
    encoder_final = feed_layer(encoder_mid, feed_low[0:2], vectors, 2)
    memory = low(layer_norm(encoder_final, vectors[4], vectors[5]))
    decoder_one = attention_layer(target, None, attention_low[4:8], vectors, 6, target_allowed)
    decoder_two = attention_layer(decoder_one, memory, attention_low[8:12], vectors, 8, cross_allowed)
    return feed_layer(decoder_two, feed_low[2:4], vectors, 10)

def factored_update(weights, grads, rows, columns):
    squares = grads * grads
    rows_next = decay_rate * rows + (1.0 - decay_rate) * lax.optimization_barrier(jnp.mean(squares, axis=2))
    columns_next = decay_rate * columns + (1.0 - decay_rate) * lax.optimization_barrier(jnp.mean(squares, axis=1))
    row_level = lax.optimization_barrier(jnp.mean(rows_next, axis=1))
    estimate = rows_next[:, :, None] * columns_next[:, None, :] / row_level[:, None, None]
    weight_scale = jnp.sqrt(lax.optimization_barrier(jnp.mean(weights * weights, axis=(1, 2))))
    updated = weights - step_rate * weight_scale[:, None, None] * grads * lax.rsqrt(estimate)
    return (updated, rows_next, columns_next)

def reference(source_embed, target_embed, out_cotangent, row_flags, source_mask, target_mask, attention_weights, feed_weights, rows_attention, columns_attention, rows_feed, columns_feed, vector_params, vector_moments):
    source = source_embed.astype(jnp.float32)
    target = target_embed.astype(jnp.float32)

    def whole(attention_full, feed_full, vectors, source_all, target_all):
        attention_low = low(attention_full)
        feed_low = low(feed_full)

        def one_pair(items):
            return pair_forward(attention_low, feed_low, vectors, items)
        return lax.map(jax.checkpoint(one_pair), (source_all, target_all, row_flags, source_mask, target_mask))
    outputs, backward = jax.vjp(whole, attention_weights, feed_weights, vector_params, source, target)
    cotangent = jnp.where(target_mask[:, :, None] > 0, out_cotangent.astype(jnp.float32), 0.0)
    grad_attention, grad_feed, grad_vectors, grad_source, grad_target = backward(cotangent)
    attention_updated, rows_attention_next, columns_attention_next = factored_update(attention_weights, grad_attention, rows_attention, columns_attention)
    feed_updated, rows_feed_next, columns_feed_next = factored_update(feed_weights, grad_feed, rows_feed, columns_feed)
    vector_moments_next = decay_rate * vector_moments + (1.0 - decay_rate) * grad_vectors * grad_vectors
    vector_scale = jnp.sqrt(lax.optimization_barrier(jnp.mean(vector_params * vector_params, axis=1)))
    vector_updated = vector_params - step_rate * vector_scale[:, None] * grad_vectors * lax.rsqrt(vector_moments_next)
    return (outputs.astype(jnp.bfloat16), grad_source, grad_target, grad_attention, grad_feed, grad_vectors, attention_updated, feed_updated, vector_updated, rows_attention_next, columns_attention_next, rows_feed_next, columns_feed_next, vector_moments_next, grad_vectors[10:12])
```

```python
import jax
import jax.numpy as jnp
from jax import lax
from jax.sharding import Mesh
from jax.sharding import PartitionSpec as P

HEAD_DIM = 64
norm_epsilon = 1e-05
decay_rate = 1.0 - 2.0 ** (-0.8)
step_rate = 0.2
masked_score = -1e30
low = jnp.bfloat16
wide = jnp.float32


def gelu_exact(values):
    return jax.nn.gelu(values, approximate=False)


def layer_norm(values, norm_gain, norm_shift):
    centre = jnp.mean(values, axis=-1, keepdims=True)
    centred = values - centre
    spread = jnp.mean(centred * centred, axis=-1, keepdims=True)
    return centred * lax.rsqrt(spread + norm_epsilon) * norm_gain + norm_shift


def swap_chips(array):
    return lax.ppermute(array, ("c", "x"), [(0, 0), (1, 2), (2, 1), (3, 3)])


def other_core(array):
    return lax.ppermute(array, "c", [(0, 1), (1, 0)])


def both_halves(own_half):
    received = other_core(own_half)
    first = lax.axis_index("c") == 0
    return jnp.concatenate(
        [jnp.where(first, own_half, received), jnp.where(first, received, own_half)], axis=0
    )


def core_sum(partial_rows):
    sent = partial_rows.astype(low)
    return sent.astype(wide) + other_core(sent).astype(wide)


def ring_next(array):
    size = lax.axis_size("z")
    return lax.ppermute(array, "z", [(i, (i + 1) % size) for i in range(size)])


def holds():
    return lax.axis_index("c") == lax.axis_index("x")


def spread_blocks(blocks, order):
    held = blocks[None, None]
    for axis in order:
        if axis == "x":
            received = lax.ppermute(held, ("c", "x"), [(0, 1), (3, 2)])
            held = jnp.where(holds(), held, received)
        elif axis == "y":
            received = lax.ppermute(held, "y", [(0, 1), (1, 0)])
            first = lax.axis_index("y") == 0
            held = jnp.concatenate(
                [jnp.where(first, held, received), jnp.where(first, received, held)], axis=1
            )
        else:
            size = lax.axis_size("z")
            if size != 4:
                held = lax.all_gather(held, "z", axis=0, tiled=True)
                continue
            place = lax.axis_index("z")
            whole = jnp.zeros((size,) + held.shape[1:], held.dtype)
            moving = held
            for step in range(size):
                where_from = lax.rem(place + size - step, size)
                whole = lax.dynamic_update_slice_in_dim(whole, moving, where_from, 0)
                if step < size - 1:
                    moving = ring_next(moving)
            held = whole
    return held


def reduce_blocks(parts, order):
    held = parts
    for position, axis in enumerate(order):
        final = position == len(order) - 1
        kind = wide if final else low
        if axis == "x":
            received = lax.ppermute(held, ("c", "x"), [(1, 0), (2, 3)])
            held = (held.astype(wide) + received.astype(wide)).astype(kind)
        elif axis == "y":
            mine = lax.axis_index("y")
            sent = lax.dynamic_slice_in_dim(held, 1 - mine, 1, 1)
            kept = lax.dynamic_slice_in_dim(held, mine, 1, 1)
            received = lax.ppermute(sent, "y", [(0, 1), (1, 0)])
            held = (kept.astype(wide) + received.astype(wide)).astype(kind)
        else:
            size = lax.axis_size("z")
            if size != 4:
                held = lax.psum_scatter(held, "z", scatter_dimension=0, tiled=True).astype(kind)
                continue
            place = lax.axis_index("z")
            moving = lax.dynamic_slice_in_dim(held, lax.rem(place + size - 1, size), 1, 0)
            for step in range(1, size):
                received = ring_next(moving)
                kept = lax.dynamic_slice_in_dim(held, lax.rem(place + size - 1 - step, size), 1, 0)
                last = step == size - 1
                moving = (kept.astype(wide) + received.astype(wide)).astype(kind if last else low)
            held = moving
    return held[0, 0]


def gather_weights(blocks, order):
    received = lax.ppermute(blocks, ("c", "x"), [(2, 0), (1, 3)])
    first = lax.axis_index("c") == 0
    both = jnp.concatenate(
        [jnp.where(first, blocks, received), jnp.where(first, received, blocks)], axis=0
    )
    spread = spread_blocks(both, order)
    return spread.reshape(-1, spread.shape[-1])


def scatter_gradient(gradient, order):
    depth, columns = gradient.shape
    z_size, y_size = lax.axis_size("z"), lax.axis_size("y")
    rows = depth // (z_size * y_size)
    total = reduce_blocks(gradient.astype(low).reshape(z_size, y_size, rows, columns), order)
    core = lax.axis_index("c")
    half = rows // 2
    kept = lax.dynamic_slice_in_dim(total, core * half, half, 0)
    sent = lax.dynamic_slice_in_dim(total, (1 - core) * half, half, 0)
    received = lax.ppermute(sent, ("c", "x"), [(0, 2), (3, 1)])
    return jnp.where(holds(), kept, received)


def data_sum(values):
    values = values + other_core(values)
    if lax.axis_size("z") != 4:
        return lax.psum(values, ("z", "y"))
    values = values + lax.ppermute(values, "y", [(0, 1), (1, 0)])
    values = values + lax.ppermute(values, "z", [(0, 1), (1, 0), (2, 3), (3, 2)])
    return values + lax.ppermute(values, "z", [(0, 2), (2, 0), (1, 3), (3, 1)])


def tensor_sum(values):
    return values + lax.ppermute(values, "x", [(0, 1), (1, 0)])


def project(left_side, right_side):
    return jnp.dot(left_side, right_side, preferred_element_type=wide)


def project_back(left_side, right_side):
    return jnp.einsum("tx,dx->td", left_side, right_side, preferred_element_type=wide)


def weight_product(left_side, right_side):
    return jnp.einsum("td,tx->dx", left_side, right_side, preferred_element_type=wide)


def split_heads(matrix):
    return matrix.reshape(matrix.shape[0], matrix.shape[1] // HEAD_DIM, HEAD_DIM)


def block_scores(query_block, key_heads, first_row, key_valid, causal):
    scores = jnp.einsum(
        "qhd,khd->hqk", query_block, key_heads, preferred_element_type=wide
    ) * HEAD_DIM ** (-0.5)
    allowed = jnp.broadcast_to(key_valid[None, :], (query_block.shape[0], key_valid.shape[0]))
    if causal:
        query_place = first_row + lax.broadcasted_iota(jnp.int32, allowed.shape, 0)
        key_place = lax.broadcasted_iota(jnp.int32, allowed.shape, 1)
        allowed = allowed & (key_place <= query_place)
    return jnp.where(allowed[None], scores, masked_score)


def attend_forward(query_rows, key_rows, value_rows, key_valid, causal):
    query_heads = split_heads(query_rows)
    key_heads = split_heads(key_rows)
    value_heads = split_heads(value_rows)
    scores = block_scores(query_heads, key_heads, 0, key_valid, causal)
    row_peak = jnp.max(scores, axis=-1, keepdims=True)
    weights = jnp.exp(scores - row_peak)
    row_total = jnp.sum(weights, axis=-1, keepdims=True)
    weights_low = (weights / row_total).astype(low)
    attended = jnp.einsum("hqk,khd->qhd", weights_low, value_heads, preferred_element_type=wide)
    totals = row_peak[:, :, 0] + jnp.log(row_total[:, :, 0])
    return attended.astype(low).reshape(query_rows.shape), totals


def attend_backward(grad_attended, query_rows, key_rows, value_rows, log_totals, key_valid, causal):
    query_heads = split_heads(query_rows)
    key_heads = split_heads(key_rows)
    value_heads = split_heads(value_rows)
    grad_heads = split_heads(grad_attended)
    scale = HEAD_DIM ** (-0.5)
    scores = block_scores(query_heads, key_heads, 0, key_valid, causal)
    weights = jnp.exp(scores - log_totals[:, :, None])
    grad_weights = jnp.einsum("qhd,khd->hqk", grad_heads, value_heads, preferred_element_type=wide)
    row_dot = jnp.sum(weights * grad_weights, axis=-1, keepdims=True)
    grad_scores = (weights * (grad_weights - row_dot)).astype(low)
    grad_query = jnp.einsum("hqk,khd->qhd", grad_scores, key_heads, preferred_element_type=wide)
    grad_key = jnp.einsum("hqk,qhd->khd", grad_scores, query_heads, preferred_element_type=wide)
    grad_value = jnp.einsum(
        "hqk,qhd->khd", weights.astype(low), grad_heads, preferred_element_type=wide
    )
    return (
        (grad_query * scale).reshape(query_rows.shape).astype(low),
        (grad_key * scale).reshape(key_rows.shape).astype(low),
        grad_value.reshape(value_rows.shape).astype(low),
    )


def attention_forward(residual, vectors, norm_row, memory_rows, weights, key_valid, causal):
    width = weights.shape[1] // 4
    normed = layer_norm(residual, vectors[norm_row], vectors[norm_row + 1]).astype(low)
    source_rows = normed if memory_rows is None else memory_rows
    query_rows = project(normed, weights[:, :width]).astype(low)
    key_rows = project(source_rows, weights[:, width : 2 * width]).astype(low)
    value_rows = project(source_rows, weights[:, 2 * width : 3 * width]).astype(low)
    attended, log_totals = attend_forward(query_rows, key_rows, value_rows, key_valid, causal)
    branch = core_sum(project_back(attended, weights[:, 3 * width :]))
    stored = {
        "normed": normed,
        "source": source_rows,
        "query": query_rows,
        "key": key_rows,
        "value": value_rows,
        "attended": attended,
        "totals": log_totals,
    }
    return residual + branch, stored


def feed_forward(residual, vectors, norm_row, weights):
    width = weights.shape[1] // 2
    normed = layer_norm(residual, vectors[norm_row], vectors[norm_row + 1]).astype(low)
    before = project(normed, weights[:, :width])
    hidden = gelu_exact(before).astype(low)
    branch = core_sum(project_back(hidden, weights[:, width:]))
    return residual + branch, {"normed": normed, "hidden": hidden, "before": before}


def norm_backward(residual, vectors, norm_row, grad_normed):
    unused_out, norm_back = jax.vjp(layer_norm, residual, vectors[norm_row], vectors[norm_row + 1])
    return norm_back(grad_normed)


def attention_backward(grad_residual, stored, weights, key_valid, causal):
    width = weights.shape[1] // 4
    grad_branch = grad_residual.astype(low)
    grad_output = weight_product(grad_branch, stored["attended"])
    grad_attended = project(grad_branch, weights[:, 3 * width :]).astype(low)
    grad_query, grad_key, grad_value = attend_backward(
        grad_attended,
        stored["query"],
        stored["key"],
        stored["value"],
        stored["totals"],
        key_valid,
        causal,
    )
    weight_terms = jnp.concatenate(
        [
            weight_product(stored["normed"], grad_query).astype(low),
            weight_product(stored["source"], grad_key).astype(low),
            weight_product(stored["source"], grad_value).astype(low),
            grad_output.astype(low),
        ],
        axis=1,
    )
    from_query = project_back(grad_query, weights[:, :width])
    from_source = project_back(grad_key, weights[:, width : 2 * width]) + project_back(
        grad_value, weights[:, 2 * width : 3 * width]
    )
    return weight_terms, from_query, from_source


def feed_backward(grad_residual, residual, vectors, norm_row, stored, weights):
    width = weights.shape[1] // 2
    grad_branch = grad_residual.astype(low)
    grad_second = weight_product(grad_branch, stored["hidden"])
    grad_hidden = project(grad_branch, weights[:, width:])
    unused_value, gelu_back = jax.vjp(gelu_exact, stored["before"])
    grad_hidden = gelu_back(grad_hidden)[0].astype(low)
    grad_first = weight_product(stored["normed"], grad_hidden)
    weight_terms = jnp.concatenate([grad_first.astype(low), grad_second.astype(low)], axis=1)
    grad_input, grad_gain, grad_shift = norm_backward(
        residual, vectors, norm_row, core_sum(project_back(grad_hidden, weights[:, :width]))
    )
    return grad_residual + grad_input, weight_terms, [grad_gain, grad_shift]


def factored_step(weights, grads, rows_next, columns_next, row_level, mean_square):
    estimate = rows_next[:, :, None] * columns_next[:, None, :] / row_level[:, None, None]
    return weights - step_rate * jnp.sqrt(mean_square)[:, None, None] * grads * lax.rsqrt(estimate)


ORDERS = ("zyx", "zxy", "xyz")


def on_device(
    source_embed,
    target_embed,
    out_cotangent,
    row_flags,
    source_mask,
    target_mask,
    attention_weights,
    feed_weights,
    rows_attention,
    columns_attention,
    rows_feed,
    columns_feed,
    vector_params,
    vector_moments,
):
    core = lax.axis_index("c")
    local_rows, half_width = attention_weights.shape[1:]
    half_units = feed_weights.shape[2]
    depth = vector_params.shape[1]
    units_all = 2 * half_units

    def attention_group(block):
        part = attention_weights[4 * block : 4 * block + 4].astype(low)
        return part.transpose(1, 0, 2).reshape(local_rows, 4 * half_width)

    def feed_group(index):
        part = feed_weights[2 * index : 2 * index + 2].astype(low)
        return part.transpose(1, 0, 2).reshape(local_rows, 2 * half_units)

    source_half = swap_chips(source_embed[0])
    flags_half = swap_chips(row_flags[0])
    source_all = both_halves(source_half)
    flags_all = both_halves(flags_half)
    masks = swap_chips(jnp.concatenate([source_mask[0], target_mask[0]]))
    source_valid = masks[: source_mask.shape[1]] > 0
    target_valid = masks[source_mask.shape[1] :] > 0
    target_all = both_halves(swap_chips(target_embed[0]))
    cotangent_all = both_halves(swap_chips(out_cotangent[0]))

    encoder_attention = gather_weights(attention_group(0), "zyx")
    decoder_attention = gather_weights(attention_group(1), "xyz")
    encoder_feed = gather_weights(feed_group(0), "zxy")
    cross_attention = gather_weights(attention_group(2), "zyx")
    decoder_feed_first = gather_weights(feed_group(1)[:, :half_units], "zyx")
    decoder_feed_second = gather_weights(feed_group(1)[:, half_units:], "xyz")
    decoder_feed = jnp.concatenate([decoder_feed_first, decoder_feed_second], axis=1)

    start_rows = jnp.where(
        (flags_all == 1)[:, None],
        vector_params[12][None, :],
        jnp.where((flags_all == 2)[:, None], vector_params[13][None, :], source_all.astype(wide)),
    )
    target_rows = target_all.astype(wide)

    encoder_mid, kept_first = attention_forward(
        start_rows, vector_params, 0, None, encoder_attention, source_valid, False
    )
    decoder_one, kept_third = attention_forward(
        target_rows, vector_params, 6, None, decoder_attention, target_valid, True
    )
    encoder_final, kept_second = feed_forward(encoder_mid, vector_params, 2, encoder_feed)
    memory_rows = layer_norm(encoder_final, vector_params[4], vector_params[5]).astype(low)
    decoder_two, kept_fourth = attention_forward(
        decoder_one, vector_params, 8, memory_rows, cross_attention, source_valid, False
    )
    decoder_three, kept_fifth = feed_forward(decoder_two, vector_params, 10, decoder_feed)

    def own_half(rows):
        half = rows.shape[0] // 2
        return lax.dynamic_slice_in_dim(rows, core * half, half, 0)

    decoder_out = swap_chips(own_half(decoder_three.astype(low)))

    grad_three = jnp.where(target_valid[:, None], cotangent_all.astype(wide), 0.0)
    vector_parts = [None] * 14
    grad_two, decoder_feed_terms, vector_parts[10:12] = feed_backward(
        grad_three, decoder_two, vector_params, 10, kept_fifth, decoder_feed
    )
    decoder_feed_grad = scatter_gradient(decoder_feed_terms, "xyz")
    cross_terms, from_query, from_source = attention_backward(
        grad_two, kept_fourth, cross_attention, source_valid, False
    )
    cross_grad = scatter_gradient(cross_terms, "zyx")
    grad_memory, vector_parts[4], vector_parts[5] = norm_backward(
        encoder_final, vector_params, 4, core_sum(from_source)
    )
    grad_input, vector_parts[8], vector_parts[9] = norm_backward(
        decoder_one, vector_params, 8, core_sum(from_query)
    )
    grad_one = grad_two + grad_input
    grad_mid, encoder_feed_terms, vector_parts[2:4] = feed_backward(
        grad_memory, encoder_mid, vector_params, 2, kept_second, encoder_feed
    )
    encoder_feed_grad = scatter_gradient(encoder_feed_terms, "yxz")
    decoder_terms, from_query, from_source = attention_backward(
        grad_one, kept_third, decoder_attention, target_valid, True
    )
    decoder_grad = scatter_gradient(decoder_terms, "zyx")
    grad_input, vector_parts[6], vector_parts[7] = norm_backward(
        target_rows, vector_params, 6, core_sum(from_query + from_source)
    )
    target_grad = swap_chips(own_half((grad_one + grad_input).astype(low))).astype(wide)
    encoder_terms, from_query, from_source = attention_backward(
        grad_mid, kept_first, encoder_attention, source_valid, False
    )
    grad_input, vector_parts[0], vector_parts[1] = norm_backward(
        start_rows, vector_params, 0, core_sum(from_query + from_source)
    )
    grad_start = grad_mid + grad_input
    vector_parts[12] = jnp.sum(jnp.where((flags_all == 1)[:, None], grad_start, 0.0), axis=0)
    vector_parts[13] = jnp.sum(jnp.where((flags_all == 2)[:, None], grad_start, 0.0), axis=0)
    source_grad = swap_chips(own_half(grad_start.astype(low))).astype(wide)
    source_grad = jnp.where((row_flags[0] == 0)[:, None], source_grad, 0.0)

    vector_terms = jnp.stack(vector_parts, axis=1).astype(low)
    vector_terms = jnp.pad(vector_terms, ((0, 0), (0, 128 - vector_terms.shape[1])))
    tail_first = scatter_gradient(
        jnp.concatenate([encoder_terms[:, : 2 * half_width], vector_terms], axis=1), "xyz"
    )
    tail_second = scatter_gradient(encoder_terms[:, 2 * half_width :], "zyx")
    vector_grad = tail_first[:, 2 * half_width : 2 * half_width + 14].T
    encoder_grad = jnp.concatenate([tail_first[:, : 2 * half_width], tail_second], axis=1)

    def as_matrices(rows, count):
        return rows.reshape(local_rows, count, -1).transpose(1, 0, 2)

    attention_grad = jnp.concatenate(
        [as_matrices(part, 4) for part in (encoder_grad, decoder_grad, cross_grad)], axis=0
    )
    feed_grad = jnp.concatenate(
        [as_matrices(part, 2) for part in (encoder_feed_grad, decoder_feed_grad)], axis=0
    )

    weight_squares = jnp.concatenate(
        [
            jnp.sum(attention_weights * attention_weights, axis=(1, 2)),
            jnp.sum(feed_weights * feed_weights, axis=(1, 2)),
            jnp.sum(rows_attention, axis=1) * 0.5,
            jnp.sum(rows_feed, axis=1) * 0.5,
        ]
    )
    early_sums = data_sum(tensor_sum(weight_squares))
    scale_attention, scale_feed = early_sums[:12], early_sums[12:16]
    rows_total_attention, rows_total_feed = early_sums[16:28], early_sums[28:32]
    attention_square = attention_grad * attention_grad
    feed_square = feed_grad * feed_grad
    row_sums = tensor_sum(
        jnp.concatenate([jnp.sum(attention_square, axis=2), jnp.sum(feed_square, axis=2)], axis=0)
    )
    column_attention = jnp.sum(attention_square, axis=1)
    column_feed = jnp.sum(feed_square, axis=1)
    square_totals = jnp.sum(row_sums, axis=1)
    column_sums = data_sum(
        jnp.concatenate([column_attention.reshape(-1), column_feed.reshape(-1), square_totals])
    )
    column_attention = column_sums[: column_attention.size].reshape(column_attention.shape)
    column_feed = column_sums[column_attention.size : -16].reshape(column_feed.shape)
    square_totals = column_sums[-16:]
    keep, take = decay_rate, 1.0 - decay_rate
    rows_attention_next = keep * rows_attention + take * row_sums[:12] / depth
    rows_feed_next = keep * rows_feed + take * row_sums[12:] / units_all
    total_attention = keep * rows_total_attention + take * square_totals[:12] / depth
    total_feed = keep * rows_total_feed + take * square_totals[12:] / units_all
    columns_attention_next = keep * columns_attention + take * column_attention / depth
    columns_feed_next = keep * columns_feed + take * column_feed / depth
    attention_updated = factored_step(
        attention_weights,
        attention_grad,
        rows_attention_next,
        columns_attention_next,
        total_attention / depth,
        scale_attention / (depth * depth),
    )
    feed_updated = factored_step(
        feed_weights,
        feed_grad,
        rows_feed_next,
        columns_feed_next,
        total_feed / depth,
        scale_feed / (depth * units_all),
    )
    local_width = vector_moments.shape[1]
    place = (lax.axis_index("z") * lax.axis_size("y") + lax.axis_index("y")) * 2 + core
    vector_local = lax.dynamic_slice_in_dim(vector_params, place * local_width, local_width, 1)
    vector_moments_next = keep * vector_moments + take * vector_grad * vector_grad
    vector_scale = jnp.sqrt(jnp.mean(vector_params * vector_params, axis=1))
    vector_updated = vector_local - step_rate * vector_scale[:, None] * vector_grad * lax.rsqrt(
        vector_moments_next
    )
    return (
        decoder_out[None],
        source_grad[None],
        target_grad[None],
        attention_grad,
        feed_grad,
        vector_grad,
        attention_updated,
        feed_updated,
        vector_updated,
        rows_attention_next,
        columns_attention_next,
        rows_feed_next,
        columns_feed_next,
        vector_moments_next,
        vector_grad[10:12],
    )


def solution(mesh):
    groups = mesh.shape["dp"] // 4
    inner = Mesh(mesh.devices.reshape(groups, 2, 2, 2), ("z", "y", "c", "x"))
    data = ("z", "y", "c")
    rows3, rows2 = P(data, "x", None), P(data, "x")
    matrix, row_spec, column_spec = P(None, data, "x"), P(None, data), P(None, "x")
    return jax.shard_map(
        on_device,
        mesh=inner,
        in_specs=(
            rows3,
            rows3,
            rows3,
            rows2,
            P(data, None),
            P(data, None),
            matrix,
            matrix,
            row_spec,
            column_spec,
            row_spec,
            column_spec,
            P(),
            row_spec,
        ),
        out_specs=(
            rows3,
            rows3,
            rows3,
            matrix,
            matrix,
            row_spec,
            matrix,
            matrix,
            row_spec,
            row_spec,
            column_spec,
            row_spec,
            column_spec,
            row_spec,
            row_spec,
        ),
        check_vma=False,
    )
```

```python
import functools

import jax
import jax.numpy as jnp
from jax import lax
from jax.experimental import pallas as pl
from jax.experimental.pallas import tpu as pltpu
from jax.sharding import Mesh
from jax.sharding import PartitionSpec as P

HEAD_DIM = 64
norm_epsilon = 1e-05
decay_rate = 1.0 - 2.0 ** (-0.8)
step_rate = 0.2
masked_score = -1e30
low = jnp.bfloat16
wide = jnp.float32
MESH = pl.DeviceIdType.MESH


def gelu_exact(values):
    return jax.nn.gelu(values, approximate=False)


def layer_norm(values, norm_gain, norm_shift):
    centre = jnp.mean(values, axis=-1, keepdims=True)
    centred = values - centre
    spread = jnp.mean(centred * centred, axis=-1, keepdims=True)
    return centred * lax.rsqrt(spread + norm_epsilon) * norm_gain + norm_shift


def swap_chips(array):
    return lax.ppermute(array, ("c", "x"), [(0, 0), (1, 2), (2, 1), (3, 3)])


def other_core(array):
    return lax.ppermute(array, "c", [(0, 1), (1, 0)])


def both_halves(own_half):
    received = other_core(own_half)
    first = lax.axis_index("c") == 0
    return jnp.concatenate(
        [jnp.where(first, own_half, received), jnp.where(first, received, own_half)], axis=0
    )


def core_sum(partial_rows):
    sent = partial_rows.astype(low)
    return sent.astype(wide) + other_core(sent).astype(wide)


def ring_next(array):
    size = lax.axis_size("z")
    return lax.ppermute(array, "z", [(i, (i + 1) % size) for i in range(size)])


def holds():
    return lax.axis_index("c") == lax.axis_index("x")


def spread_blocks(blocks, order):
    held = blocks[None, None]
    for axis in order:
        if axis == "x":
            received = lax.ppermute(held, ("c", "x"), [(0, 1), (3, 2)])
            held = jnp.where(holds(), held, received)
        elif axis == "y":
            received = lax.ppermute(held, "y", [(0, 1), (1, 0)])
            first = lax.axis_index("y") == 0
            held = jnp.concatenate(
                [jnp.where(first, held, received), jnp.where(first, received, held)], axis=1
            )
        else:
            size = lax.axis_size("z")
            if size != 4:
                held = lax.all_gather(held, "z", axis=0, tiled=True)
                continue
            place = lax.axis_index("z")
            whole = jnp.zeros((size,) + held.shape[1:], held.dtype)
            moving = held
            for step in range(size):
                where_from = lax.rem(place + size - step, size)
                whole = lax.dynamic_update_slice_in_dim(whole, moving, where_from, 0)
                if step < size - 1:
                    moving = ring_next(moving)
            held = whole
    return held


def reduce_blocks(parts, order):
    held = parts
    for position, axis in enumerate(order):
        final = position == len(order) - 1
        kind = wide if final else low
        if axis == "x":
            received = lax.ppermute(held, ("c", "x"), [(1, 0), (2, 3)])
            held = (held.astype(wide) + received.astype(wide)).astype(kind)
        elif axis == "y":
            mine = lax.axis_index("y")
            sent = lax.dynamic_slice_in_dim(held, 1 - mine, 1, 1)
            kept = lax.dynamic_slice_in_dim(held, mine, 1, 1)
            received = lax.ppermute(sent, "y", [(0, 1), (1, 0)])
            held = (kept.astype(wide) + received.astype(wide)).astype(kind)
        else:
            size = lax.axis_size("z")
            if size != 4:
                held = lax.psum_scatter(held, "z", scatter_dimension=0, tiled=True).astype(kind)
                continue
            place = lax.axis_index("z")
            moving = lax.dynamic_slice_in_dim(held, lax.rem(place + size - 1, size), 1, 0)
            for step in range(1, size):
                received = ring_next(moving)
                kept = lax.dynamic_slice_in_dim(held, lax.rem(place + size - 1 - step, size), 1, 0)
                last = step == size - 1
                moving = (kept.astype(wide) + received.astype(wide)).astype(kind if last else low)
            held = moving
    return held[0, 0]


def gather_weights(blocks, order):
    received = lax.ppermute(blocks, ("c", "x"), [(2, 0), (1, 3)])
    first = lax.axis_index("c") == 0
    both = jnp.concatenate(
        [jnp.where(first, blocks, received), jnp.where(first, received, blocks)], axis=0
    )
    spread = spread_blocks(both, order)
    return spread.reshape(-1, spread.shape[-1])


def scatter_gradient(gradient, order):
    depth, columns = gradient.shape
    z_size, y_size = lax.axis_size("z"), lax.axis_size("y")
    rows = depth // (z_size * y_size)
    total = reduce_blocks(gradient.astype(low).reshape(z_size, y_size, rows, columns), order)
    core = lax.axis_index("c")
    half = rows // 2
    kept = lax.dynamic_slice_in_dim(total, core * half, half, 0)
    sent = lax.dynamic_slice_in_dim(total, (1 - core) * half, half, 0)
    received = lax.ppermute(sent, ("c", "x"), [(0, 2), (3, 1)])
    return jnp.where(holds(), kept, received)


def data_sum(values):
    values = values + other_core(values)
    if lax.axis_size("z") != 4:
        return lax.psum(values, ("z", "y"))
    values = values + lax.ppermute(values, "y", [(0, 1), (1, 0)])
    values = values + lax.ppermute(values, "z", [(0, 1), (1, 0), (2, 3), (3, 2)])
    return values + lax.ppermute(values, "z", [(0, 2), (2, 0), (1, 3), (3, 1)])


def tensor_sum(values):
    return values + lax.ppermute(values, "x", [(0, 1), (1, 0)])


def column_cuts(columns):
    tiles = columns // 128
    first = (tiles * 42 + 50) // 100
    second = (tiles * 36 + 50) // 100
    edges = [0, first * 128, (first + second) * 128, columns]
    return list(zip(edges[:-1], edges[1:]))


class Place:
    def __init__(self):
        self.z, self.y, self.c, self.x = (lax.axis_index(name) for name in "zycx")
        self.holds = self.c == self.x

    def block(self, which):
        back, same_y = which
        z = lax.rem(self.z + 4 - back, 4)
        return z * 2 + (self.y if same_y else 1 - self.y)

    def target(self, axis):
        if axis == "z":
            return {"z": lax.rem(self.z + 1, 4)}
        if axis == "z_back":
            return {"z": lax.rem(self.z + 3, 4)}
        return {axis: 1 - getattr(self, axis)}


def greet(place):
    barrier = pltpu.get_barrier_semaphore()
    for axis in ("c", "x", "y", "z", "z_back"):
        pl.semaphore_signal(
            barrier, inc=1, device_id=place.target(axis), device_id_type=MESH
        )
    pl.semaphore_wait(barrier, 5)


def gather_kernel(own_ref, out_ref, local_sem, send_sems, recv_sems):
    place = Place()
    rows = own_ref.shape[0]
    cuts = column_cuts(own_ref.shape[1])
    holds = place.holds
    greet(place)
    own_block = place.block((0, True))
    own_rows = out_ref.at[own_block, pl.ds(place.c * rows, rows), :]
    to_other = pltpu.make_async_remote_copy(
        src_ref=own_ref,
        dst_ref=own_rows,
        send_sem=send_sems.at[72],
        recv_sem=recv_sems.at[24],
        device_id=place.target("c"),
        device_id_type=MESH,
    )
    to_self = pltpu.make_async_copy(own_ref, own_rows, local_sem)
    pl.when(jnp.logical_not(holds))(lambda: to_other.start())

    @pl.when(holds)
    def _():
        to_self.start()
        to_self.wait()
        to_other.wait_recv()

    pending = []

    def copy(group, which, axis):
        begin, end = cuts[group]
        block = place.block(which)
        piece = out_ref.at[block, :, pl.ds(begin, end - begin)]
        number = {"z": 0, "y": 1, "x": 2}[axis]
        return pltpu.make_async_remote_copy(
            src_ref=piece,
            dst_ref=piece,
            send_sem=send_sems.at[(group * 8 + block) * 3 + number],
            recv_sem=recv_sems.at[group * 8 + block],
            device_id=place.target(axis),
            device_id_type=MESH,
        )

    def send(group, which, axis, who):
        copy(group, which, axis).start()
        pending.append((functools.partial(copy, group, which, axis), who))

    def arrive(group, block):
        copy(group, block, "x").wait_recv()

    here, there = (lambda back: (back, True)), (lambda back: (back, False))
    first, second, third = 0, 1, 2

    @pl.when(holds)
    def _():
        send(first, here(0), "x", True)
        send(second, here(0), "y", True)
        send(third, here(0), "z", True)
        send(third, here(0), "y", True)
        send(third, here(0), "x", True)
        send(first, here(0), "z", True)
        send(first, here(0), "y", True)
        send(second, here(0), "z", True)
        send(second, here(0), "x", True)

    @pl.when(jnp.logical_not(holds))
    def _():
        arrive(third, here(0))
        send(third, here(0), "z", False)
        send(third, here(0), "y", False)

    for back in range(1, 5):

        @pl.when(holds)
        def _():
            if back < 4:
                arrive(first, here(back))
                if back < 3:
                    send(first, here(back), "z", True)
                send(first, here(back), "y", True)
                send(first, here(back), "x", True)
                arrive(second, here(back))
                if back < 3:
                    send(second, here(back), "z", True)
                send(second, here(back), "x", True)
                send(second, here(back), "y", True)
            arrive(first, there(back - 1))
            send(first, there(back - 1), "x", True)

        @pl.when(jnp.logical_not(holds))
        def _():
            arrive(second, here(back - 1))
            send(second, here(back - 1), "y", False)

        if back < 4:
            if back == 1:
                arrive(third, there(0))
                send(third, there(0), "z", None)
            arrive(third, here(back))
            if back < 3:
                send(third, here(back), "z", None)
            arrive(third, there(back))
            if back < 3:
                send(third, there(back), "z", None)
    for back in range(4):
        arrive(second, there(back))

    @pl.when(jnp.logical_not(holds))
    def _():
        for back in range(4):
            arrive(first, here(back))
            arrive(first, there(back))
        to_other.wait_send()
        for one, who in pending:
            if who is False:
                one().wait_send()

    @pl.when(holds)
    def _():
        for one, who in pending:
            if who is True:
                one().wait_send()

    for one, who in pending:
        if who is None:
            one().wait_send()


def gather_all(own):
    rows, columns = own.shape
    return pl.pallas_call(
        gather_kernel,
        out_shape=jax.ShapeDtypeStruct((8, 2 * rows, columns), own.dtype),
        in_specs=[pl.BlockSpec(memory_space=pl.ANY)],
        out_specs=pl.BlockSpec(memory_space=pl.ANY),
        scratch_shapes=[
            pltpu.SemaphoreType.DMA,
            pltpu.SemaphoreType.DMA((73,)),
            pltpu.SemaphoreType.DMA((25,)),
        ],
        compiler_params=pltpu.CompilerParams(collective_id=0, has_side_effects=True),
        name="gather_weights",
    )(own)


def scatter_kernel(widths, *refs):
    count = len(widths)
    grads = refs[:count]
    out_ref, total, final = refs[count : count + 3]
    buffers = refs[count + 3 : count + 6]
    load_sems, send_sems, recv_sems, end_sem = refs[count + 6 :]
    place = Place()
    holds = place.holds
    rows = total.shape[1]
    columns = total.shape[2]
    cuts = column_cuts(columns)
    loads = []
    begin = 0
    for number, width in enumerate(widths):
        one = pltpu.make_async_copy(
            grads[number], total.at[:, :, pl.ds(begin, width)], load_sems.at[number]
        )
        one.start()
        loads.append(one)
        begin += width
    greet(place)
    for one in loads:
        one.wait()
    here, there = (lambda back: (back, True)), (lambda back: (back, False))
    pending = []
    slots = {}

    def copy(group, which, slot, axis):
        begin, end = cuts[group]
        block = place.block(which)
        return pltpu.make_async_remote_copy(
            src_ref=total.at[block, :, pl.ds(begin, end - begin)],
            dst_ref=buffers[group].at[slot],
            send_sem=send_sems.at[group * 16 + slot],
            recv_sem=recv_sems.at[group * 16 + slot],
            device_id=place.target(axis),
            device_id_type=MESH,
        )

    def send(group, which, slot, axis, who):
        copy(group, which, slot, axis).start()
        pending.append((functools.partial(copy, group, which, slot, axis), who))

    def add(group, which, slot, last=False):
        copy(group, which, slot, "x").wait_recv()
        block = place.block(which)
        begin, end = cuts[group]
        part = pl.ds(begin, end - begin)

        @pl.loop(0, rows // 16)
        def _(step):
            at = pl.ds(pl.multiple_of(step * 16, 16), 16)
            held = total[block, at, part]
            came = buffers[group][slot, at, :]
            if last:
                final[at, part] = held.astype(wide) + came.astype(wide)
            else:
                total[block, at, part] = held + came

    first, second, third = 0, 1, 2
    for which, offset in ((there, 3), (here, 0)):
        send(third, which(3), offset + 2, "z_back", None)
    for back in (3, 2, 1, 0):
        send(second, there(back), back, "y", None)

    @pl.when(jnp.logical_not(holds))
    def _():
        for back in (3, 2, 1, 0):
            send(first, there(back), 4 + back, "x", False)
            send(first, here(back), back, "x", False)

    for back in (3, 2, 1, 0):
        if back < 3:
            for which, offset in ((there, 3), (here, 0)):
                add(third, which(back), offset + back)
                if back > 0:
                    send(third, which(back), offset + back - 1, "z_back", None)
                elif offset == 3:
                    send(third, which(0), 6, "y", None)
        add(second, here(back), back)

        @pl.when(jnp.logical_not(holds))
        def _():
            send(second, here(back), 4 + back, "x", False)

        @pl.when(holds)
        def _():
            add(first, there(back), 4 + back)
            send(first, there(back), 8 + back, "y", True)
            add(first, here(back), back)
            add(first, here(back), 8 + back, last=False)
            if back < 3:
                add(first, here(back), 12 + back, last=back == 0)
            if back > 0:
                send(first, here(back), 12 + back - 1, "z_back", True)

    add(third, here(0), 6)

    @pl.when(jnp.logical_not(holds))
    def _():
        send(third, here(0), 7, "x", False)

    end_copy = pltpu.make_async_remote_copy(
        src_ref=final.at[pl.ds((1 - place.c) * (rows // 2), rows // 2), :],
        dst_ref=out_ref,
        send_sem=end_sem.at[0],
        recv_sem=end_sem.at[1],
        device_id=place.target("c"),
        device_id_type=MESH,
    )
    keep_copy = pltpu.make_async_copy(
        final.at[pl.ds(place.c * (rows // 2), rows // 2), :], out_ref, end_sem.at[2]
    )

    @pl.when(holds)
    def _():
        for back in (3, 2, 1, 0):
            add(second, here(back), 4 + back)
            if back < 3:
                add(second, here(back), 8 + back, last=back == 0)
            if back > 0:
                send(second, here(back), 8 + back - 1, "z_back", True)
        add(third, here(0), 7, last=True)
        end_copy.start()
        keep_copy.start()
        keep_copy.wait()
        end_copy.wait_send()
        for one, who in pending:
            if who is True:
                one().wait_send()

    @pl.when(jnp.logical_not(holds))
    def _():
        end_copy.wait_recv()
        for one, who in pending:
            if who is False:
                one().wait_send()

    for one, who in pending:
        if who is None:
            one().wait_send()


def scatter_all(parts):
    depth = parts[0].shape[0]
    widths = [part.shape[1] for part in parts]
    columns = sum(widths)
    rows = depth // 8
    cuts = column_cuts(columns)
    return pl.pallas_call(
        functools.partial(scatter_kernel, widths),
        out_shape=jax.ShapeDtypeStruct((rows // 2, columns), wide),
        in_specs=[pl.BlockSpec(memory_space=pl.ANY)] * len(parts),
        out_specs=pl.BlockSpec(memory_space=pl.ANY),
        scratch_shapes=[
            pltpu.VMEM((8, rows, columns), low),
            pltpu.VMEM((rows, columns), wide),
            pltpu.VMEM((15, rows, cuts[0][1] - cuts[0][0]), low),
            pltpu.VMEM((11, rows, cuts[1][1] - cuts[1][0]), low),
            pltpu.VMEM((8, rows, cuts[2][1] - cuts[2][0]), low),
            pltpu.SemaphoreType.DMA((len(parts),)),
            pltpu.SemaphoreType.DMA((48,)),
            pltpu.SemaphoreType.DMA((48,)),
            pltpu.SemaphoreType.DMA((3,)),
        ],
        compiler_params=pltpu.CompilerParams(
            collective_id=1, has_side_effects=True, vmem_limit_bytes=56 << 20
        ),
        name="scatter_gradients",
    )(*[part.reshape(8, rows, part.shape[1]) for part in parts])


def fits_kernels():
    return lax.axis_size("z") == 4


def gather_groups(groups):
    if fits_kernels():
        whole = gather_all(jnp.concatenate(groups, axis=1))
        whole = whole.reshape(-1, whole.shape[2])
        pieces = []
        begin = 0
        for group in groups:
            pieces.append(whole[:, begin : begin + group.shape[1]])
            begin += group.shape[1]
        return pieces
    return [gather_weights(group, "zyx") for group in groups]


def scatter_groups(groups):
    if fits_kernels():
        whole = scatter_all(groups)
        pieces = []
        begin = 0
        for group in groups:
            pieces.append(whole[:, begin : begin + group.shape[1]])
            begin += group.shape[1]
        return pieces
    return [scatter_gradient(group, "xyz") for group in groups]


def project(left_side, right_side):
    return jnp.dot(left_side, right_side, preferred_element_type=wide)


def project_back(left_side, right_side):
    return jnp.einsum("tx,dx->td", left_side, right_side, preferred_element_type=wide)


def weight_product(left_side, right_side):
    return jnp.einsum("td,tx->dx", left_side, right_side, preferred_element_type=wide)


def split_heads(matrix):
    return matrix.reshape(matrix.shape[0], matrix.shape[1] // HEAD_DIM, HEAD_DIM)


def block_scores(query_block, key_heads, first_row, key_valid, causal):
    scores = jnp.einsum(
        "qhd,khd->hqk", query_block, key_heads, preferred_element_type=wide
    ) * HEAD_DIM ** (-0.5)
    allowed = jnp.broadcast_to(key_valid[None, :], (query_block.shape[0], key_valid.shape[0]))
    if causal:
        query_place = first_row + lax.broadcasted_iota(jnp.int32, allowed.shape, 0)
        key_place = lax.broadcasted_iota(jnp.int32, allowed.shape, 1)
        allowed = allowed & (key_place <= query_place)
    return jnp.where(allowed[None], scores, masked_score)


def attend_forward(query_rows, key_rows, value_rows, key_valid, causal):
    query_heads = split_heads(query_rows)
    key_heads = split_heads(key_rows)
    value_heads = split_heads(value_rows)
    scores = block_scores(query_heads, key_heads, 0, key_valid, causal)
    row_peak = jnp.max(scores, axis=-1, keepdims=True)
    weights = jnp.exp(scores - row_peak)
    row_total = jnp.sum(weights, axis=-1, keepdims=True)
    weights_low = (weights / row_total).astype(low)
    attended = jnp.einsum("hqk,khd->qhd", weights_low, value_heads, preferred_element_type=wide)
    totals = row_peak[:, :, 0] + jnp.log(row_total[:, :, 0])
    return attended.astype(low).reshape(query_rows.shape), totals


def attend_backward(grad_attended, query_rows, key_rows, value_rows, log_totals, key_valid, causal):
    query_heads = split_heads(query_rows)
    key_heads = split_heads(key_rows)
    value_heads = split_heads(value_rows)
    grad_heads = split_heads(grad_attended)
    scale = HEAD_DIM ** (-0.5)
    scores = block_scores(query_heads, key_heads, 0, key_valid, causal)
    weights = jnp.exp(scores - log_totals[:, :, None])
    grad_weights = jnp.einsum("qhd,khd->hqk", grad_heads, value_heads, preferred_element_type=wide)
    row_dot = jnp.sum(weights * grad_weights, axis=-1, keepdims=True)
    grad_scores = (weights * (grad_weights - row_dot)).astype(low)
    grad_query = jnp.einsum("hqk,khd->qhd", grad_scores, key_heads, preferred_element_type=wide)
    grad_key = jnp.einsum("hqk,qhd->khd", grad_scores, query_heads, preferred_element_type=wide)
    grad_value = jnp.einsum(
        "hqk,qhd->khd", weights.astype(low), grad_heads, preferred_element_type=wide
    )
    return (
        (grad_query * scale).reshape(query_rows.shape).astype(low),
        (grad_key * scale).reshape(key_rows.shape).astype(low),
        grad_value.reshape(value_rows.shape).astype(low),
    )


def attention_forward(residual, vectors, norm_row, memory_rows, weights, key_valid, causal):
    width = weights.shape[1] // 4
    normed = layer_norm(residual, vectors[norm_row], vectors[norm_row + 1]).astype(low)
    source_rows = normed if memory_rows is None else memory_rows
    query_rows = project(normed, weights[:, :width]).astype(low)
    key_rows = project(source_rows, weights[:, width : 2 * width]).astype(low)
    value_rows = project(source_rows, weights[:, 2 * width : 3 * width]).astype(low)
    attended, log_totals = attend_forward(query_rows, key_rows, value_rows, key_valid, causal)
    branch = core_sum(project_back(attended, weights[:, 3 * width :]))
    stored = {
        "normed": normed,
        "source": source_rows,
        "query": query_rows,
        "key": key_rows,
        "value": value_rows,
        "attended": attended,
        "totals": log_totals,
    }
    return residual + branch, stored


def feed_forward(residual, vectors, norm_row, weights):
    width = weights.shape[1] // 2
    normed = layer_norm(residual, vectors[norm_row], vectors[norm_row + 1]).astype(low)
    before = project(normed, weights[:, :width])
    hidden = gelu_exact(before).astype(low)
    branch = core_sum(project_back(hidden, weights[:, width:]))
    return residual + branch, {"normed": normed, "hidden": hidden, "before": before}


def norm_backward(residual, vectors, norm_row, grad_normed):
    unused_out, norm_back = jax.vjp(layer_norm, residual, vectors[norm_row], vectors[norm_row + 1])
    return norm_back(grad_normed)


def attention_backward(grad_residual, stored, weights, key_valid, causal):
    width = weights.shape[1] // 4
    grad_branch = grad_residual.astype(low)
    grad_output = weight_product(grad_branch, stored["attended"])
    grad_attended = project(grad_branch, weights[:, 3 * width :]).astype(low)
    grad_query, grad_key, grad_value = attend_backward(
        grad_attended,
        stored["query"],
        stored["key"],
        stored["value"],
        stored["totals"],
        key_valid,
        causal,
    )
    weight_terms = jnp.concatenate(
        [
            weight_product(stored["normed"], grad_query).astype(low),
            weight_product(stored["source"], grad_key).astype(low),
            weight_product(stored["source"], grad_value).astype(low),
            grad_output.astype(low),
        ],
        axis=1,
    )
    from_query = project_back(grad_query, weights[:, :width])
    from_source = project_back(grad_key, weights[:, width : 2 * width]) + project_back(
        grad_value, weights[:, 2 * width : 3 * width]
    )
    return weight_terms, from_query, from_source


def feed_backward(grad_residual, residual, vectors, norm_row, stored, weights):
    width = weights.shape[1] // 2
    grad_branch = grad_residual.astype(low)
    grad_second = weight_product(grad_branch, stored["hidden"])
    grad_hidden = project(grad_branch, weights[:, width:])
    unused_value, gelu_back = jax.vjp(gelu_exact, stored["before"])
    grad_hidden = gelu_back(grad_hidden)[0].astype(low)
    grad_first = weight_product(stored["normed"], grad_hidden)
    weight_terms = jnp.concatenate([grad_first.astype(low), grad_second.astype(low)], axis=1)
    grad_input, grad_gain, grad_shift = norm_backward(
        residual, vectors, norm_row, core_sum(project_back(grad_hidden, weights[:, :width]))
    )
    return grad_residual + grad_input, weight_terms, [grad_gain, grad_shift]


def factored_step(weights, grads, rows_next, columns_next, row_level, mean_square):
    estimate = rows_next[:, :, None] * columns_next[:, None, :] / row_level[:, None, None]
    return weights - step_rate * jnp.sqrt(mean_square)[:, None, None] * grads * lax.rsqrt(estimate)


ORDERS = ("zyx", "zxy", "xyz")


def on_device(
    source_embed,
    target_embed,
    out_cotangent,
    row_flags,
    source_mask,
    target_mask,
    attention_weights,
    feed_weights,
    rows_attention,
    columns_attention,
    rows_feed,
    columns_feed,
    vector_params,
    vector_moments,
):
    core = lax.axis_index("c")
    local_rows, half_width = attention_weights.shape[1:]
    half_units = feed_weights.shape[2]
    depth = vector_params.shape[1]
    units_all = 2 * half_units

    def attention_group(block):
        part = attention_weights[4 * block : 4 * block + 4].astype(low)
        return part.transpose(1, 0, 2).reshape(local_rows, 4 * half_width)

    def feed_group(index):
        part = feed_weights[2 * index : 2 * index + 2].astype(low)
        return part.transpose(1, 0, 2).reshape(local_rows, 2 * half_units)

    source_half = swap_chips(source_embed[0])
    flags_half = swap_chips(row_flags[0])
    source_all = both_halves(source_half)
    flags_all = both_halves(flags_half)
    masks = swap_chips(jnp.concatenate([source_mask[0], target_mask[0]]))
    source_valid = masks[: source_mask.shape[1]] > 0
    target_valid = masks[source_mask.shape[1] :] > 0
    target_all = both_halves(swap_chips(target_embed[0]))
    cotangent_all = both_halves(swap_chips(out_cotangent[0]))

    encoder_attention, decoder_attention, cross_attention, encoder_feed, decoder_feed = gather_groups(
        [attention_group(0), attention_group(1), attention_group(2), feed_group(0), feed_group(1)]
    )

    start_rows = jnp.where(
        (flags_all == 1)[:, None],
        vector_params[12][None, :],
        jnp.where((flags_all == 2)[:, None], vector_params[13][None, :], source_all.astype(wide)),
    )
    target_rows = target_all.astype(wide)

    encoder_mid, kept_first = attention_forward(
        start_rows, vector_params, 0, None, encoder_attention, source_valid, False
    )
    decoder_one, kept_third = attention_forward(
        target_rows, vector_params, 6, None, decoder_attention, target_valid, True
    )
    encoder_final, kept_second = feed_forward(encoder_mid, vector_params, 2, encoder_feed)
    memory_rows = layer_norm(encoder_final, vector_params[4], vector_params[5]).astype(low)
    decoder_two, kept_fourth = attention_forward(
        decoder_one, vector_params, 8, memory_rows, cross_attention, source_valid, False
    )
    decoder_three, kept_fifth = feed_forward(decoder_two, vector_params, 10, decoder_feed)

    def own_half(rows):
        half = rows.shape[0] // 2
        return lax.dynamic_slice_in_dim(rows, core * half, half, 0)

    decoder_out = swap_chips(own_half(decoder_three.astype(low)))

    grad_three = jnp.where(target_valid[:, None], cotangent_all.astype(wide), 0.0)
    vector_parts = [None] * 14
    grad_two, decoder_feed_terms, vector_parts[10:12] = feed_backward(
        grad_three, decoder_two, vector_params, 10, kept_fifth, decoder_feed
    )
    cross_terms, from_query, from_source = attention_backward(
        grad_two, kept_fourth, cross_attention, source_valid, False
    )
    grad_memory, vector_parts[4], vector_parts[5] = norm_backward(
        encoder_final, vector_params, 4, core_sum(from_source)
    )
    grad_input, vector_parts[8], vector_parts[9] = norm_backward(
        decoder_one, vector_params, 8, core_sum(from_query)
    )
    grad_one = grad_two + grad_input
    grad_mid, encoder_feed_terms, vector_parts[2:4] = feed_backward(
        grad_memory, encoder_mid, vector_params, 2, kept_second, encoder_feed
    )
    decoder_terms, from_query, from_source = attention_backward(
        grad_one, kept_third, decoder_attention, target_valid, True
    )
    grad_input, vector_parts[6], vector_parts[7] = norm_backward(
        target_rows, vector_params, 6, core_sum(from_query + from_source)
    )
    target_grad = swap_chips(own_half((grad_one + grad_input).astype(low))).astype(wide)
    encoder_terms, from_query, from_source = attention_backward(
        grad_mid, kept_first, encoder_attention, source_valid, False
    )
    grad_input, vector_parts[0], vector_parts[1] = norm_backward(
        start_rows, vector_params, 0, core_sum(from_query + from_source)
    )
    grad_start = grad_mid + grad_input
    vector_parts[12] = jnp.sum(jnp.where((flags_all == 1)[:, None], grad_start, 0.0), axis=0)
    vector_parts[13] = jnp.sum(jnp.where((flags_all == 2)[:, None], grad_start, 0.0), axis=0)
    source_grad = swap_chips(own_half(grad_start.astype(low))).astype(wide)
    source_grad = jnp.where((row_flags[0] == 0)[:, None], source_grad, 0.0)

    vector_terms = jnp.stack(vector_parts, axis=1).astype(low)
    vector_terms = jnp.pad(vector_terms, ((0, 0), (0, 128 - vector_terms.shape[1])))
    (encoder_grad, decoder_grad, cross_grad, encoder_feed_grad, decoder_feed_grad, vector_grad) = (
        scatter_groups(
            [
                encoder_terms,
                decoder_terms,
                cross_terms,
                encoder_feed_terms,
                decoder_feed_terms,
                vector_terms,
            ]
        )
    )
    vector_grad = vector_grad[:, :14].T

    def as_matrices(rows, count):
        return rows.reshape(local_rows, count, -1).transpose(1, 0, 2)

    attention_grad = jnp.concatenate(
        [as_matrices(part, 4) for part in (encoder_grad, decoder_grad, cross_grad)], axis=0
    )
    feed_grad = jnp.concatenate(
        [as_matrices(part, 2) for part in (encoder_feed_grad, decoder_feed_grad)], axis=0
    )

    weight_squares = jnp.concatenate(
        [
            jnp.sum(attention_weights * attention_weights, axis=(1, 2)),
            jnp.sum(feed_weights * feed_weights, axis=(1, 2)),
            jnp.sum(rows_attention, axis=1) * 0.5,
            jnp.sum(rows_feed, axis=1) * 0.5,
        ]
    )
    early_sums = data_sum(tensor_sum(weight_squares))
    scale_attention, scale_feed = early_sums[:12], early_sums[12:16]
    rows_total_attention, rows_total_feed = early_sums[16:28], early_sums[28:32]
    attention_square = attention_grad * attention_grad
    feed_square = feed_grad * feed_grad
    row_sums = tensor_sum(
        jnp.concatenate([jnp.sum(attention_square, axis=2), jnp.sum(feed_square, axis=2)], axis=0)
    )
    column_attention = jnp.sum(attention_square, axis=1)
    column_feed = jnp.sum(feed_square, axis=1)
    square_totals = jnp.sum(row_sums, axis=1)
    column_sums = data_sum(
        jnp.concatenate([column_attention.reshape(-1), column_feed.reshape(-1), square_totals])
    )
    column_attention = column_sums[: column_attention.size].reshape(column_attention.shape)
    column_feed = column_sums[column_attention.size : -16].reshape(column_feed.shape)
    square_totals = column_sums[-16:]
    keep, take = decay_rate, 1.0 - decay_rate
    rows_attention_next = keep * rows_attention + take * row_sums[:12] / depth
    rows_feed_next = keep * rows_feed + take * row_sums[12:] / units_all
    total_attention = keep * rows_total_attention + take * square_totals[:12] / depth
    total_feed = keep * rows_total_feed + take * square_totals[12:] / units_all
    columns_attention_next = keep * columns_attention + take * column_attention / depth
    columns_feed_next = keep * columns_feed + take * column_feed / depth
    attention_updated = factored_step(
        attention_weights,
        attention_grad,
        rows_attention_next,
        columns_attention_next,
        total_attention / depth,
        scale_attention / (depth * depth),
    )
    feed_updated = factored_step(
        feed_weights,
        feed_grad,
        rows_feed_next,
        columns_feed_next,
        total_feed / depth,
        scale_feed / (depth * units_all),
    )
    local_width = vector_moments.shape[1]
    place = (lax.axis_index("z") * lax.axis_size("y") + lax.axis_index("y")) * 2 + core
    vector_local = lax.dynamic_slice_in_dim(vector_params, place * local_width, local_width, 1)
    vector_moments_next = keep * vector_moments + take * vector_grad * vector_grad
    vector_scale = jnp.sqrt(jnp.mean(vector_params * vector_params, axis=1))
    vector_updated = vector_local - step_rate * vector_scale[:, None] * vector_grad * lax.rsqrt(
        vector_moments_next
    )
    return (
        decoder_out[None],
        source_grad[None],
        target_grad[None],
        attention_grad,
        feed_grad,
        vector_grad,
        attention_updated,
        feed_updated,
        vector_updated,
        rows_attention_next,
        columns_attention_next,
        rows_feed_next,
        columns_feed_next,
        vector_moments_next,
        vector_grad[10:12],
    )


def solution(mesh):
    groups = mesh.shape["dp"] // 4
    inner = Mesh(mesh.devices.reshape(groups, 2, 2, 2), ("z", "y", "c", "x"))
    data = ("z", "y", "c")
    rows3, rows2 = P(data, "x", None), P(data, "x")
    matrix, row_spec, column_spec = P(None, data, "x"), P(None, data), P(None, "x")
    return jax.shard_map(
        on_device,
        mesh=inner,
        in_specs=(
            rows3,
            rows3,
            rows3,
            rows2,
            P(data, None),
            P(data, None),
            matrix,
            matrix,
            row_spec,
            column_spec,
            row_spec,
            column_spec,
            P(),
            row_spec,
        ),
        out_specs=(
            rows3,
            rows3,
            rows3,
            matrix,
            matrix,
            row_spec,
            matrix,
            matrix,
            row_spec,
            row_spec,
            column_spec,
            row_spec,
            column_spec,
            row_spec,
            row_spec,
        ),
        check_vma=False,
    )
```

```python
import functools

import jax
import jax.numpy as jnp
from jax import lax
from jax.experimental import pallas as pl
from jax.experimental.pallas import tpu as pltpu
from jax.sharding import Mesh
from jax.sharding import PartitionSpec as P

HEAD_DIM = 64
CHUNK = 256
norm_epsilon = 1e-05
decay_rate = 1.0 - 2.0 ** (-0.8)
step_rate = 0.2
masked_score = -1e30
low = jnp.bfloat16
wide = jnp.float32
MESH = pl.DeviceIdType.MESH


def swap_chips(array):
    return lax.ppermute(array, ("c", "x"), [(0, 0), (1, 2), (2, 1), (3, 3)])


def other_core(array):
    return lax.ppermute(array, "c", [(0, 1), (1, 0)])


def both_halves(own_half):
    received = other_core(own_half)
    first = lax.axis_index("c") == 0
    return jnp.concatenate(
        [jnp.where(first, own_half, received), jnp.where(first, received, own_half)], axis=0
    )


def core_sum(partial_rows):
    sent = partial_rows.astype(low)
    return sent.astype(wide) + other_core(sent).astype(wide)


def ring_next(array):
    size = lax.axis_size("z")
    return lax.ppermute(array, "z", [(i, (i + 1) % size) for i in range(size)])


def holds():
    return lax.axis_index("c") == lax.axis_index("x")


def spread_blocks(blocks, order):
    held = blocks[None, None]
    for axis in order:
        if axis == "x":
            received = lax.ppermute(held, ("c", "x"), [(0, 1), (3, 2)])
            held = jnp.where(holds(), held, received)
        elif axis == "y":
            received = lax.ppermute(held, "y", [(0, 1), (1, 0)])
            first = lax.axis_index("y") == 0
            held = jnp.concatenate(
                [jnp.where(first, held, received), jnp.where(first, received, held)], axis=1
            )
        else:
            size = lax.axis_size("z")
            if size != 4:
                held = lax.all_gather(held, "z", axis=0, tiled=True)
                continue
            place = lax.axis_index("z")
            whole = jnp.zeros((size,) + held.shape[1:], held.dtype)
            moving = held
            for step in range(size):
                where_from = lax.rem(place + size - step, size)
                whole = lax.dynamic_update_slice_in_dim(whole, moving, where_from, 0)
                if step < size - 1:
                    moving = ring_next(moving)
            held = whole
    return held


def reduce_blocks(parts, order):
    held = parts
    for position, axis in enumerate(order):
        final = position == len(order) - 1
        kind = wide if final else low
        if axis == "x":
            received = lax.ppermute(held, ("c", "x"), [(1, 0), (2, 3)])
            held = (held.astype(wide) + received.astype(wide)).astype(kind)
        elif axis == "y":
            mine = lax.axis_index("y")
            sent = lax.dynamic_slice_in_dim(held, 1 - mine, 1, 1)
            kept = lax.dynamic_slice_in_dim(held, mine, 1, 1)
            received = lax.ppermute(sent, "y", [(0, 1), (1, 0)])
            held = (kept.astype(wide) + received.astype(wide)).astype(kind)
        else:
            size = lax.axis_size("z")
            if size != 4:
                held = lax.psum_scatter(held, "z", scatter_dimension=0, tiled=True).astype(kind)
                continue
            place = lax.axis_index("z")
            moving = lax.dynamic_slice_in_dim(held, lax.rem(place + size - 1, size), 1, 0)
            for step in range(1, size):
                received = ring_next(moving)
                kept = lax.dynamic_slice_in_dim(held, lax.rem(place + size - 1 - step, size), 1, 0)
                last = step == size - 1
                moving = (kept.astype(wide) + received.astype(wide)).astype(kind if last else low)
            held = moving
    return held[0, 0]


def gather_weights(blocks, order):
    received = lax.ppermute(blocks, ("c", "x"), [(2, 0), (1, 3)])
    first = lax.axis_index("c") == 0
    both = jnp.concatenate(
        [jnp.where(first, blocks, received), jnp.where(first, received, blocks)], axis=0
    )
    spread = spread_blocks(both, order)
    return spread.reshape(-1, spread.shape[-1])


def scatter_gradient(gradient, order):
    depth, columns = gradient.shape
    z_size, y_size = lax.axis_size("z"), lax.axis_size("y")
    rows = depth // (z_size * y_size)
    total = reduce_blocks(gradient.astype(low).reshape(z_size, y_size, rows, columns), order)
    core = lax.axis_index("c")
    half = rows // 2
    kept = lax.dynamic_slice_in_dim(total, core * half, half, 0)
    sent = lax.dynamic_slice_in_dim(total, (1 - core) * half, half, 0)
    received = lax.ppermute(sent, ("c", "x"), [(0, 2), (3, 1)])
    return jnp.where(holds(), kept, received)


def data_sum(values):
    values = values + other_core(values)
    if lax.axis_size("z") != 4:
        return lax.psum(values, ("z", "y"))
    values = values + lax.ppermute(values, "y", [(0, 1), (1, 0)])
    values = values + lax.ppermute(values, "z", [(0, 1), (1, 0), (2, 3), (3, 2)])
    return values + lax.ppermute(values, "z", [(0, 2), (2, 0), (1, 3), (3, 1)])


def tensor_sum(values):
    return values + lax.ppermute(values, "x", [(0, 1), (1, 0)])


def column_cuts(columns):
    tiles = columns // 128
    first = (tiles * 42 + 50) // 100
    second = (tiles * 36 + 50) // 100
    edges = [0, first * 128, (first + second) * 128, columns]
    return list(zip(edges[:-1], edges[1:]))


class Place:
    def __init__(self):
        self.z, self.y, self.c, self.x = (lax.axis_index(name) for name in "zycx")
        self.holds = self.c == self.x

    def block(self, which):
        back, same_y = which
        z = lax.rem(self.z + 4 - back, 4)
        return z * 2 + (self.y if same_y else 1 - self.y)

    def target(self, axis):
        if axis == "z":
            return {"z": lax.rem(self.z + 1, 4)}
        if axis == "z_back":
            return {"z": lax.rem(self.z + 3, 4)}
        return {axis: 1 - getattr(self, axis)}


def greet(place):
    barrier = pltpu.get_barrier_semaphore()
    for axis in ("c", "x", "y", "z", "z_back"):
        pl.semaphore_signal(
            barrier, inc=1, device_id=place.target(axis), device_id_type=MESH
        )
    pl.semaphore_wait(barrier, 5)


def gather_kernel(own_ref, out_ref, local_sem, send_sems, recv_sems):
    place = Place()
    rows = own_ref.shape[0]
    cuts = column_cuts(own_ref.shape[1])
    holds = place.holds
    greet(place)
    own_block = place.block((0, True))
    own_rows = out_ref.at[own_block, pl.ds(place.c * rows, rows), :]
    to_other = pltpu.make_async_remote_copy(
        src_ref=own_ref,
        dst_ref=own_rows,
        send_sem=send_sems.at[72],
        recv_sem=recv_sems.at[24],
        device_id=place.target("c"),
        device_id_type=MESH,
    )
    to_self = pltpu.make_async_copy(own_ref, own_rows, local_sem)
    pl.when(jnp.logical_not(holds))(lambda: to_other.start())

    @pl.when(holds)
    def _():
        to_self.start()
        to_self.wait()
        to_other.wait_recv()

    pending = []

    def copy(group, which, axis):
        begin, end = cuts[group]
        block = place.block(which)
        piece = out_ref.at[block, :, pl.ds(begin, end - begin)]
        number = {"z": 0, "y": 1, "x": 2}[axis]
        return pltpu.make_async_remote_copy(
            src_ref=piece,
            dst_ref=piece,
            send_sem=send_sems.at[(group * 8 + block) * 3 + number],
            recv_sem=recv_sems.at[group * 8 + block],
            device_id=place.target(axis),
            device_id_type=MESH,
        )

    def send(group, which, axis, who):
        copy(group, which, axis).start()
        pending.append((functools.partial(copy, group, which, axis), who))

    def arrive(group, block):
        copy(group, block, "x").wait_recv()

    here, there = (lambda back: (back, True)), (lambda back: (back, False))
    first, second, third = 0, 1, 2

    @pl.when(holds)
    def _():
        send(first, here(0), "x", True)
        send(second, here(0), "y", True)
        send(third, here(0), "z", True)
        send(third, here(0), "y", True)
        send(third, here(0), "x", True)
        send(first, here(0), "z", True)
        send(first, here(0), "y", True)
        send(second, here(0), "z", True)
        send(second, here(0), "x", True)

    @pl.when(jnp.logical_not(holds))
    def _():
        arrive(third, here(0))
        send(third, here(0), "z", False)
        send(third, here(0), "y", False)

    for back in range(1, 5):

        @pl.when(holds)
        def _():
            if back < 4:
                arrive(first, here(back))
                if back < 3:
                    send(first, here(back), "z", True)
                send(first, here(back), "y", True)
                send(first, here(back), "x", True)
                arrive(second, here(back))
                if back < 3:
                    send(second, here(back), "z", True)
                send(second, here(back), "x", True)
                send(second, here(back), "y", True)
            arrive(first, there(back - 1))
            send(first, there(back - 1), "x", True)

        @pl.when(jnp.logical_not(holds))
        def _():
            arrive(second, here(back - 1))
            send(second, here(back - 1), "y", False)

        if back < 4:
            if back == 1:
                arrive(third, there(0))
                send(third, there(0), "z", None)
            arrive(third, here(back))
            if back < 3:
                send(third, here(back), "z", None)
            arrive(third, there(back))
            if back < 3:
                send(third, there(back), "z", None)
    for back in range(4):
        arrive(second, there(back))

    @pl.when(jnp.logical_not(holds))
    def _():
        for back in range(4):
            arrive(first, here(back))
            arrive(first, there(back))
        to_other.wait_send()
        for one, who in pending:
            if who is False:
                one().wait_send()

    @pl.when(holds)
    def _():
        for one, who in pending:
            if who is True:
                one().wait_send()

    for one, who in pending:
        if who is None:
            one().wait_send()


def gather_all(own):
    rows, columns = own.shape
    return pl.pallas_call(
        gather_kernel,
        out_shape=jax.ShapeDtypeStruct((8, 2 * rows, columns), own.dtype),
        in_specs=[pl.BlockSpec(memory_space=pl.ANY)],
        out_specs=pl.BlockSpec(memory_space=pl.ANY),
        scratch_shapes=[
            pltpu.SemaphoreType.DMA,
            pltpu.SemaphoreType.DMA((73,)),
            pltpu.SemaphoreType.DMA((25,)),
        ],
        compiler_params=pltpu.CompilerParams(collective_id=0, has_side_effects=True),
        name="gather_weights",
    )(own)


def scatter_kernel(widths, *refs):
    count = len(widths)
    grads = refs[:count]
    out_ref, total, final = refs[count : count + 3]
    buffers = refs[count + 3 : count + 6]
    load_sems, send_sems, recv_sems, end_sem = refs[count + 6 :]
    place = Place()
    holds = place.holds
    rows = total.shape[1]
    columns = total.shape[2]
    cuts = column_cuts(columns)
    loads = []
    begin = 0
    for number, width in enumerate(widths):
        one = pltpu.make_async_copy(
            grads[number], total.at[:, :, pl.ds(begin, width)], load_sems.at[number]
        )
        one.start()
        loads.append(one)
        begin += width
    greet(place)
    for one in loads:
        one.wait()
    here, there = (lambda back: (back, True)), (lambda back: (back, False))
    pending = []
    slots = {}

    def copy(group, which, slot, axis):
        begin, end = cuts[group]
        block = place.block(which)
        return pltpu.make_async_remote_copy(
            src_ref=total.at[block, :, pl.ds(begin, end - begin)],
            dst_ref=buffers[group].at[slot],
            send_sem=send_sems.at[group * 16 + slot],
            recv_sem=recv_sems.at[group * 16 + slot],
            device_id=place.target(axis),
            device_id_type=MESH,
        )

    def send(group, which, slot, axis, who):
        copy(group, which, slot, axis).start()
        pending.append((functools.partial(copy, group, which, slot, axis), who))

    def add(group, which, slot, last=False):
        copy(group, which, slot, "x").wait_recv()
        block = place.block(which)
        begin, end = cuts[group]
        part = pl.ds(begin, end - begin)

        @pl.loop(0, rows // 16)
        def _(step):
            at = pl.ds(pl.multiple_of(step * 16, 16), 16)
            held = total[block, at, part]
            came = buffers[group][slot, at, :]
            if last:
                final[at, part] = held.astype(wide) + came.astype(wide)
            else:
                total[block, at, part] = held + came

    first, second, third = 0, 1, 2
    for which, offset in ((there, 3), (here, 0)):
        send(third, which(3), offset + 2, "z_back", None)
    for back in (3, 2, 1, 0):
        send(second, there(back), back, "y", None)

    @pl.when(jnp.logical_not(holds))
    def _():
        for back in (3, 2, 1, 0):
            send(first, there(back), 4 + back, "x", False)
            send(first, here(back), back, "x", False)

    for back in (3, 2, 1, 0):
        if back < 3:
            for which, offset in ((there, 3), (here, 0)):
                add(third, which(back), offset + back)
                if back > 0:
                    send(third, which(back), offset + back - 1, "z_back", None)
                elif offset == 3:
                    send(third, which(0), 6, "y", None)
        add(second, here(back), back)

        @pl.when(jnp.logical_not(holds))
        def _():
            send(second, here(back), 4 + back, "x", False)

        @pl.when(holds)
        def _():
            add(first, there(back), 4 + back)
            send(first, there(back), 8 + back, "y", True)
            add(first, here(back), back)
            add(first, here(back), 8 + back, last=False)
            if back < 3:
                add(first, here(back), 12 + back, last=back == 0)
            if back > 0:
                send(first, here(back), 12 + back - 1, "z_back", True)

    add(third, here(0), 6)

    @pl.when(jnp.logical_not(holds))
    def _():
        send(third, here(0), 7, "x", False)

    end_copy = pltpu.make_async_remote_copy(
        src_ref=final.at[pl.ds((1 - place.c) * (rows // 2), rows // 2), :],
        dst_ref=out_ref,
        send_sem=end_sem.at[0],
        recv_sem=end_sem.at[1],
        device_id=place.target("c"),
        device_id_type=MESH,
    )
    keep_copy = pltpu.make_async_copy(
        final.at[pl.ds(place.c * (rows // 2), rows // 2), :], out_ref, end_sem.at[2]
    )

    @pl.when(holds)
    def _():
        for back in (3, 2, 1, 0):
            add(second, here(back), 4 + back)
            if back < 3:
                add(second, here(back), 8 + back, last=back == 0)
            if back > 0:
                send(second, here(back), 8 + back - 1, "z_back", True)
        add(third, here(0), 7, last=True)
        end_copy.start()
        keep_copy.start()
        keep_copy.wait()
        end_copy.wait_send()
        for one, who in pending:
            if who is True:
                one().wait_send()

    @pl.when(jnp.logical_not(holds))
    def _():
        end_copy.wait_recv()
        for one, who in pending:
            if who is False:
                one().wait_send()

    for one, who in pending:
        if who is None:
            one().wait_send()


def scatter_all(parts):
    depth = parts[0].shape[0]
    widths = [part.shape[1] for part in parts]
    columns = sum(widths)
    rows = depth // 8
    cuts = column_cuts(columns)
    return pl.pallas_call(
        functools.partial(scatter_kernel, widths),
        out_shape=jax.ShapeDtypeStruct((rows // 2, columns), wide),
        in_specs=[pl.BlockSpec(memory_space=pl.ANY)] * len(parts),
        out_specs=pl.BlockSpec(memory_space=pl.ANY),
        scratch_shapes=[
            pltpu.VMEM((8, rows, columns), low),
            pltpu.VMEM((rows, columns), wide),
            pltpu.VMEM((15, rows, cuts[0][1] - cuts[0][0]), low),
            pltpu.VMEM((11, rows, cuts[1][1] - cuts[1][0]), low),
            pltpu.VMEM((8, rows, cuts[2][1] - cuts[2][0]), low),
            pltpu.SemaphoreType.DMA((len(parts),)),
            pltpu.SemaphoreType.DMA((48,)),
            pltpu.SemaphoreType.DMA((48,)),
            pltpu.SemaphoreType.DMA((3,)),
        ],
        compiler_params=pltpu.CompilerParams(
            collective_id=1, has_side_effects=True, vmem_limit_bytes=56 << 20
        ),
        name="scatter_gradients",
    )(*[part.reshape(8, rows, part.shape[1]) for part in parts])


def fits_kernels():
    return lax.axis_size("z") == 4


def gather_groups(groups):
    if fits_kernels():
        whole = gather_all(jnp.concatenate(groups, axis=1))
        whole = whole.reshape(-1, whole.shape[2])
        pieces = []
        begin = 0
        for group in groups:
            pieces.append(whole[:, begin : begin + group.shape[1]])
            begin += group.shape[1]
        return pieces
    return [gather_weights(group, "zyx") for group in groups]


def scatter_groups(groups):
    if fits_kernels():
        whole = scatter_all(groups)
        pieces = []
        begin = 0
        for group in groups:
            pieces.append(whole[:, begin : begin + group.shape[1]])
            begin += group.shape[1]
        return pieces
    return [scatter_gradient(group, "xyz") for group in groups]


def dot_nn(left, right):
    return lax.dot_general(left, right, (((1,), (0,)), ((), ())), preferred_element_type=wide)


def dot_nt(left, right):
    return lax.dot_general(left, right, (((1,), (1,)), ((), ())), preferred_element_type=wide)


def turned(block):
    size = block.shape[1]
    row = lax.broadcasted_iota(jnp.int32, (size, size), 0)
    column = lax.broadcasted_iota(jnp.int32, (size, size), 1)
    return dot_nt((row == column).astype(wide).astype(low), block).astype(low)


def turn_into(target, source):
    rows, columns = source.shape
    for at in range(0, columns, 256):
        wide_part = min(256, columns - at)
        target[at : at + wide_part, :] = turned(source[:, at : at + wide_part])


def centre_rows(values):
    centred = values - jnp.mean(values, axis=-1, keepdims=True)
    spread = jnp.mean(centred * centred, axis=-1, keepdims=True)
    return centred * lax.rsqrt(spread + norm_epsilon)


def norm_back(x, gain, grads):
    centred = x - jnp.mean(x, axis=-1, keepdims=True)
    scale = lax.rsqrt(jnp.mean(centred * centred, axis=-1, keepdims=True) + norm_epsilon)
    unit = centred * scale
    inner = grads * gain
    by_unit = inner * unit
    back = scale * (
        inner
        - jnp.mean(inner, axis=-1, keepdims=True)
        - unit * jnp.mean(by_unit, axis=-1, keepdims=True)
    )
    return back, jnp.sum(grads * unit, axis=0, keepdims=True), jnp.sum(grads, axis=0, keepdims=True)


def residual_prologue(norm_row, previous_ref, x_ref, own_ref, other_ref, vec_ref, grad_out, low_ref, vec_out):
    gain = vec_ref[norm_row : norm_row + 1, :]
    vec_out[...] = jnp.zeros_like(vec_out)

    @pl.loop(0, x_ref.shape[0] // CHUNK)
    def _(step):
        at = pl.ds(pl.multiple_of(step * CHUNK, CHUNK), CHUNK)
        grads = own_ref[at, :].astype(wide) + other_ref[at, :].astype(wide)
        back, by_gain, by_shift = norm_back(x_ref[at, :].astype(wide), gain, grads)
        if previous_ref is not None:
            back = back + previous_ref[at, :].astype(wide)
        if grad_out is not None:
            grad_out[at, :] = back
        if low_ref is not None:
            low_ref[at, :] = back.astype(low)
        vec_out[0:1, :] += by_gain
        vec_out[1:2, :] += by_shift


def erf_ratio(values):
    x = jnp.clip(values, -4.0, 4.0)
    square = x * x
    top = jnp.full_like(square, -2.72614225801306e-10)
    for term in (
        2.77068142495902e-08,
        -2.10102402082508e-06,
        -5.69250639462346e-05,
        -7.34990630326855e-04,
        -2.95459980854025e-03,
        -1.60960333262415e-02,
    ):
        top = top * square + term
    low_part = jnp.full_like(square, -1.45660718464996e-05)
    for term in (
        -2.13374055278905e-04,
        -1.68282697438203e-03,
        -7.37332916720468e-03,
        -1.42647390514189e-02,
    ):
        low_part = low_part * square + term
    return x * top / low_part


def gelu_pair(before):
    phi_whole = 0.5 + 0.5 * erf_ratio(before * 0.7071067811865476)
    density = jnp.exp(before * before * -0.5) * 0.3989422804014327
    return before * phi_whole, phi_whole + before * density


def chunks(rows):
    return range(0, rows, CHUNK)


def feed_forward_kernel(
    rows_norm, x_ref, own_ref, other_ref, w_ref, vec_ref, x_out, normed_out, hidden_out, slope_out, part_out
):
    units = w_ref.shape[1] // 2
    gain = vec_ref[rows_norm : rows_norm + 1, :]
    shift = vec_ref[rows_norm + 1 : rows_norm + 2, :]

    @pl.loop(0, x_ref.shape[0] // CHUNK)
    def _(step):
        at = pl.ds(pl.multiple_of(step * CHUNK, CHUNK), CHUNK)
        x = x_ref[at, :] + (own_ref[at, :].astype(wide) + other_ref[at, :].astype(wide))
        x_out[at, :] = x
        normed = (centre_rows(x) * gain + shift).astype(low)
        normed_out[at, :] = normed
        part = jnp.zeros((CHUNK, x.shape[1]), wide)
        for begin in range(0, units, 512):
            before = dot_nn(normed, w_ref[:, begin : begin + 512])
            value, slope = gelu_pair(before)
            hidden = value.astype(low)
            hidden_out[at, begin : begin + 512] = hidden
            slope_out[at, begin : begin + 512] = slope.astype(low)
            part = part + dot_nt(hidden, w_ref[:, units + begin : units + begin + 512])
        part_out[at, :] = part.astype(low)


def params(limit=56):
    return pltpu.CompilerParams(vmem_limit_bytes=limit << 20)


def shaped(rows, columns, kind):
    return jax.ShapeDtypeStruct((rows, columns), kind)


def feed_forward_call(rows_norm, x, own, other, weights, vectors):
    rows, depth = x.shape
    units = weights.shape[1] // 2
    return pl.pallas_call(
        functools.partial(feed_forward_kernel, rows_norm),
        out_shape=(
            shaped(rows, depth, wide),
            shaped(rows, depth, low),
            shaped(rows, units, low),
            shaped(rows, units, low),
            shaped(rows, depth, low),
        ),
        compiler_params=params(),
        name="feed_forward",
    )(x, own, other, weights, vectors)


def feed_backward_body(normed_ref, hidden_ref, slope_in, w_ref, part_out, grad_out, low_ref, slope_ref, turned_ref, turned_low):
    rows, depth = low_ref.shape
    units = w_ref.shape[1] // 2
    turn_into(turned_low, low_ref)
    turn_into(turned_ref, normed_ref)

    @pl.loop(0, rows // CHUNK)
    def _(step):
        at = pl.ds(pl.multiple_of(step * CHUNK, CHUNK), CHUNK)
        grads = low_ref[at, :]
        part = jnp.zeros((CHUNK, depth), wide)
        for begin in range(0, units, 512):
            grad = dot_nn(grads, w_ref[:, units + begin : units + begin + 512])
            grad = (grad * slope_in[at, begin : begin + 512].astype(wide)).astype(low)
            slope_ref[at, begin : begin + 512] = grad
            part = part + dot_nt(grad, w_ref[:, begin : begin + 512])
        part_out[at, :] = part.astype(low)

    for begin in range(0, units, 256):
        grad_out[:, begin : begin + 256] = dot_nn(
            turned_ref[...], slope_ref[:, begin : begin + 256]
        ).astype(low)
        grad_out[:, units + begin : units + begin + 256] = dot_nn(
            turned_low[...], hidden_ref[:, begin : begin + 256]
        ).astype(low)


def feed_backward_scratch(rows, depth, units):
    return [
        pltpu.VMEM((rows, depth), low),
        pltpu.VMEM((rows, units), low),
        pltpu.VMEM((depth, rows), low),
        pltpu.VMEM((depth, rows), low),
    ]


def whole():
    return pl.BlockSpec(memory_space=pltpu.VMEM)


def scalar():
    return pl.BlockSpec(memory_space=pltpu.SMEM)


def last_feed_backward_kernel(
    length_ref, cotangent_ref, normed_ref, hidden_ref, slope_in, w_ref, part_out, grad_out, low_ref, *rest
):
    rows, depth = cotangent_ref.shape
    place = lax.broadcasted_iota(jnp.int32, (CHUNK, depth), 0)

    @pl.loop(0, rows // CHUNK)
    def _(step):
        first_row = pl.multiple_of(step * CHUNK, CHUNK)
        at = pl.ds(first_row, CHUNK)
        rows_here = cotangent_ref[at, :].astype(wide)
        low_ref[at, :] = jnp.where(first_row + place < length_ref[0], rows_here, 0.0).astype(low)

    feed_backward_body(normed_ref, hidden_ref, slope_in, w_ref, part_out, grad_out, low_ref, *rest)


def last_feed_backward_call(length, cotangent, normed, hidden, slope, weights):
    rows, depth = cotangent.shape
    units = hidden.shape[1]
    return pl.pallas_call(
        last_feed_backward_kernel,
        out_shape=(shaped(rows, depth, low), shaped(depth, 2 * units, low), shaped(rows, depth, low)),
        in_specs=[scalar()] + [whole()] * 5,
        scratch_shapes=feed_backward_scratch(rows, depth, units)[1:],
        compiler_params=params(),
        name="last_feed_backward",
    )(length, cotangent, normed, hidden, slope, weights)


def feed_backward_kernel(
    norm_row, x_ref, own_ref, other_ref, vec_ref, normed_ref, hidden_ref, slope_in, w_ref,
    part_out, grad_out, g_out, vec_out, low_ref, *rest
):
    residual_prologue(norm_row, None, x_ref, own_ref, other_ref, vec_ref, g_out, low_ref, vec_out)
    feed_backward_body(normed_ref, hidden_ref, slope_in, w_ref, part_out, grad_out, low_ref, *rest)


def feed_backward_call(norm_row, x, own, other, vectors, normed, hidden, slope, weights):
    rows, depth = x.shape
    units = hidden.shape[1]
    return pl.pallas_call(
        functools.partial(feed_backward_kernel, norm_row),
        out_shape=(
            shaped(rows, depth, low),
            shaped(depth, 2 * units, low),
            shaped(rows, depth, wide),
            shaped(2, depth, wide),
        ),
        scratch_shapes=feed_backward_scratch(rows, depth, units),
        compiler_params=params(),
        name="feed_backward",
    )(x, own, other, vectors, normed, hidden, slope, weights)


def half_lanes(shape):
    return lax.broadcasted_iota(jnp.int32, shape, 1) < 64


def one_head(pair, head):
    first = half_lanes(pair.shape)
    zero = jnp.zeros_like(pair)
    return jnp.where(first, pair, zero) if head == 0 else jnp.where(first, zero, pair)


def key_bias(keys, length, first_row, causal, rows):
    place = lax.broadcasted_iota(jnp.int32, (1, keys), 1)
    if not causal:
        return jnp.where(place < length, 0.0, masked_score)
    place = lax.broadcasted_iota(jnp.int32, (rows, keys), 1)
    row = first_row + lax.broadcasted_iota(jnp.int32, (rows, keys), 0)
    return jnp.where((place < length) & (place <= row), 0.0, masked_score)


def attend_chunk(first_row, length, causal, q_ref, kv_ref, w_ref, attended_out, totals_out, part_out):
    width = q_ref.shape[1]
    keys = kv_ref.shape[0]
    at = pl.ds(first_row, CHUNK)
    bias = key_bias(keys, length, first_row, causal, CHUNK)
    lane = lax.broadcasted_iota(jnp.int32, (CHUNK, 128), 1)
    totals = jnp.zeros((CHUNK, 128), wide)
    for begin in range(0, width, 128):
        pair = q_ref[at, begin : begin + 128]
        key_pair = kv_ref[:, begin : begin + 128]
        value_pair = kv_ref[:, width + begin : width + begin + 128]
        results = []
        for head in range(2):
            scores = dot_nt(one_head(pair, head), key_pair) + bias
            peak = jnp.max(scores, axis=-1, keepdims=True)
            weights = jnp.exp(scores - peak)
            total = jnp.sum(weights, axis=-1, keepdims=True)
            results.append(dot_nn(weights.astype(low), value_pair) * (1.0 / total))
            totals = jnp.where(lane == begin // 64 + head, peak + jnp.log(total), totals)
        attended_out[at, begin : begin + 128] = jnp.where(
            lane < 64, results[0], results[1]
        ).astype(low)
    totals_out[at, :] = totals
    part_out[at, :] = dot_nt(attended_out[at, :], w_ref[:, 3 * width :]).astype(low)


def self_attention_kernel(
    rows_norm, causal, length_ref, x_ref, w_ref, vec_ref, normed_out, q_out, kv_out, attended_out, totals_out, part_out
):
    width = w_ref.shape[1] // 4
    gain = vec_ref[rows_norm : rows_norm + 1, :]
    shift = vec_ref[rows_norm + 1 : rows_norm + 2, :]
    steps = x_ref.shape[0] // CHUNK

    @pl.loop(0, steps)
    def _(step):
        at = pl.ds(pl.multiple_of(step * CHUNK, CHUNK), CHUNK)
        normed = (centre_rows(x_ref[at, :].astype(wide)) * gain + shift).astype(low)
        normed_out[at, :] = normed
        q_out[at, :] = (dot_nn(normed, w_ref[:, :width]).astype(low).astype(wide) * 0.125).astype(low)
        kv_out[at, :] = dot_nn(normed, w_ref[:, width : 3 * width]).astype(low)

    length = length_ref[0]

    @pl.loop(0, steps)
    def _(step):
        attend_chunk(
            pl.multiple_of(step * CHUNK, CHUNK), length, causal, q_out, kv_out, w_ref, attended_out, totals_out, part_out
        )


def self_attention_call(rows_norm, causal, length, x, weights, vectors):
    rows, depth = x.shape
    width = weights.shape[1] // 4
    whole = pl.BlockSpec(memory_space=pltpu.VMEM)
    return pl.pallas_call(
        functools.partial(self_attention_kernel, rows_norm, causal),
        out_shape=(
            shaped(rows, depth, low),
            shaped(rows, width, low),
            shaped(rows, 2 * width, low),
            shaped(rows, width, low),
            shaped(rows, 128, wide),
            shaped(rows, depth, low),
        ),
        in_specs=[pl.BlockSpec(memory_space=pltpu.SMEM), whole, whole, whole],
        compiler_params=params(),
        name="self_attention",
    )(length, x, weights, vectors)


def cross_attention_kernel(
    length_ref, x_ref, own_ref, other_ref, mid_ref, mid_own, mid_other, w_ref, vec_ref,
    x_out, final_out, memory_out, normed_out, q_out, kv_out, attended_out, totals_out, part_out,
):
    width = w_ref.shape[1] // 4

    @pl.loop(0, mid_ref.shape[0] // CHUNK)
    def _(step):
        at = pl.ds(pl.multiple_of(step * CHUNK, CHUNK), CHUNK)
        x = mid_ref[at, :] + (mid_own[at, :].astype(wide) + mid_other[at, :].astype(wide))
        final_out[at, :] = x
        memory = (centre_rows(x) * vec_ref[4:5, :] + vec_ref[5:6, :]).astype(low)
        memory_out[at, :] = memory
        kv_out[at, :] = dot_nn(memory, w_ref[:, width : 3 * width]).astype(low)

    @pl.loop(0, x_ref.shape[0] // CHUNK)
    def _(step):
        at = pl.ds(pl.multiple_of(step * CHUNK, CHUNK), CHUNK)
        x = x_ref[at, :].astype(wide) + (own_ref[at, :].astype(wide) + other_ref[at, :].astype(wide))
        x_out[at, :] = x
        normed = (centre_rows(x) * vec_ref[8:9, :] + vec_ref[9:10, :]).astype(low)
        normed_out[at, :] = normed
        q_out[at, :] = (dot_nn(normed, w_ref[:, :width]).astype(low).astype(wide) * 0.125).astype(low)

    length = length_ref[0]

    @pl.loop(0, x_ref.shape[0] // CHUNK)
    def _(step):
        attend_chunk(
            pl.multiple_of(step * CHUNK, CHUNK), length, False, q_out, kv_out, w_ref, attended_out, totals_out, part_out
        )


def cross_attention_call(length, x, own, other, mid, mid_own, mid_other, weights, vectors):
    rows, depth = x.shape
    keys = mid.shape[0]
    width = weights.shape[1] // 4
    whole = pl.BlockSpec(memory_space=pltpu.VMEM)
    return pl.pallas_call(
        cross_attention_kernel,
        out_shape=(
            shaped(rows, depth, wide),
            shaped(keys, depth, wide),
            shaped(keys, depth, low),
            shaped(rows, depth, low),
            shaped(rows, width, low),
            shaped(keys, 2 * width, low),
            shaped(rows, width, low),
            shaped(rows, 128, wide),
            shaped(rows, depth, low),
        ),
        in_specs=[pl.BlockSpec(memory_space=pltpu.SMEM)] + [whole] * 8,
        compiler_params=params(),
        name="cross_attention",
    )(length, x, own, other, mid, mid_own, mid_other, weights, vectors)


def attention_backward_kernel(
    causal, cross, norm_row, length_ref, previous_ref, x_ref, own_ref, other_ref, vec_ref,
    normed_ref, source_ref, q_ref, kv_ref, attended_ref, totals_ref, w_ref, *rest
):
    outs = 5 if cross else 4
    part_out, g_out, vec_out, grad_out = rest[:4]
    source_part_out = rest[4] if cross else None
    low_ref, grad_q, grad_kv, turned_k, turned_v, turned_low, turned_normed = rest[outs : outs + 7]
    turned_source = rest[outs + 7] if cross else turned_normed
    rows, depth = x_ref.shape
    keys = kv_ref.shape[0]
    width = q_ref.shape[1]
    length = length_ref[0]
    residual_prologue(norm_row, previous_ref, x_ref, own_ref, other_ref, vec_ref, g_out, low_ref, vec_out)
    turned_k[...] = jnp.zeros_like(turned_k)
    turned_v[...] = jnp.zeros_like(turned_v)

    @pl.loop(0, rows // CHUNK)
    def _(step):
        first_row = pl.multiple_of(step * CHUNK, CHUNK)
        at = pl.ds(first_row, CHUNK)
        grad_attended = dot_nn(low_ref[at, :], w_ref[:, 3 * width :]).astype(low)
        bias = key_bias(keys, length, first_row, causal, CHUNK)
        lane = lax.broadcasted_iota(jnp.int32, (CHUNK, 128), 1)
        totals = totals_ref[at, :]
        for begin in range(0, width, 128):
            pair = q_ref[at, begin : begin + 128]
            key_pair = kv_ref[:, begin : begin + 128]
            value_pair = kv_ref[:, width + begin : width + begin + 128]
            grad_pair = grad_attended[:, begin : begin + 128]
            pair_turned = turned(pair)
            grad_turned = turned(grad_pair)
            results = []
            for head in range(2):
                number = begin // 64 + head
                total = jnp.sum(jnp.where(lane == number, totals, 0.0), axis=-1, keepdims=True)
                scores = dot_nt(one_head(pair, head), key_pair) + bias
                weights = jnp.exp(scores - total)
                grad_weights = dot_nt(one_head(grad_pair, head), value_pair)
                row_dot = jnp.sum(weights * grad_weights, axis=-1, keepdims=True)
                grad_scores = (weights * (grad_weights - row_dot)).astype(low)
                results.append(dot_nn(grad_scores, key_pair))
                span = slice(begin + 64 * head, begin + 64 * head + 64)
                local = slice(64 * head, 64 * head + 64)
                turned_k[span, :] += dot_nn(pair_turned[local, :], grad_scores)
                turned_v[span, :] += dot_nn(grad_turned[local, :], weights.astype(low))
            grad_q[at, begin : begin + 128] = (
                jnp.where(lane < 64, results[0], results[1]) * 0.125
            ).astype(low)
        if cross:
            part_out[at, :] = dot_nt(grad_q[at, :], w_ref[:, :width]).astype(low)

    grad_kv[:, :width] = turned(turned_k[...].astype(low))
    grad_kv[:, width:] = turned(turned_v[...].astype(low))

    @pl.loop(0, keys // CHUNK)
    def _(step):
        at = pl.ds(pl.multiple_of(step * CHUNK, CHUNK), CHUNK)
        from_source = dot_nt(grad_kv[at, :], w_ref[:, width : 3 * width])
        if cross:
            source_part_out[at, :] = from_source.astype(low)
        else:
            from_query = dot_nt(grad_q[at, :], w_ref[:, :width])
            part_out[at, :] = (from_source + from_query).astype(low)

    turn_into(turned_low, low_ref)
    turn_into(turned_normed, normed_ref)
    if cross:
        turn_into(turned_source, source_ref)
    grad_out[:, :width] = dot_nn(turned_normed[...], grad_q[...]).astype(low)
    grad_out[:, width : 2 * width] = dot_nn(turned_source[...], grad_kv[:, :width]).astype(low)
    grad_out[:, 2 * width : 3 * width] = dot_nn(turned_source[...], grad_kv[:, width:]).astype(low)
    grad_out[:, 3 * width :] = dot_nn(turned_low[...], attended_ref[...]).astype(low)


def attention_backward_call(
    causal, norm_row, length, previous, x, own, other, vectors, normed, source, q, kv, attended, totals, weights
):
    cross = source is not None
    rows, depth = x.shape
    keys = kv.shape[0]
    width = q.shape[1]
    outs = [
        shaped(rows, depth, low),
        shaped(rows, depth, wide),
        shaped(2, depth, wide),
        shaped(depth, 4 * width, low),
    ]
    if cross:
        outs.append(shaped(keys, depth, low))
    scratch = [
        pltpu.VMEM((rows, depth), low),
        pltpu.VMEM((rows, width), low),
        pltpu.VMEM((keys, 2 * width), low),
        pltpu.VMEM((width, keys), wide),
        pltpu.VMEM((width, keys), wide),
        pltpu.VMEM((depth, rows), low),
        pltpu.VMEM((depth, rows), low),
    ]
    if cross:
        scratch.append(pltpu.VMEM((depth, keys), low))
    operands = [length, previous, x, own, other, vectors, normed]
    if cross:
        operands.append(source)
    operands += [q, kv, attended, totals, weights]

    def kernel(*refs):
        if not cross:
            refs = refs[:7] + (None,) + refs[7:]
        attention_backward_kernel(causal, cross, norm_row, *refs)

    return pl.pallas_call(
        kernel,
        out_shape=tuple(outs),
        in_specs=[scalar()] + [whole()] * (len(operands) - 1),
        scratch_shapes=scratch,
        compiler_params=params(),
        name="attention_backward",
    )(*operands)


def finish_kernel(norm_row, previous_ref, x_ref, own_ref, other_ref, vec_ref, g_out, vec_out):
    residual_prologue(norm_row, previous_ref, x_ref, own_ref, other_ref, vec_ref, g_out, None, vec_out)


def finish_call(norm_row, previous, x, own, other, vectors):
    rows, depth = x.shape
    return pl.pallas_call(
        functools.partial(finish_kernel, norm_row),
        out_shape=(shaped(rows, depth, wide), shaped(2, depth, wide)),
        compiler_params=params(),
        name="finish_norm",
    )(previous, x, own, other, vectors)


def factored_step(weights, grads, rows_next, columns_next, row_level, mean_square):
    estimate = rows_next[:, :, None] * columns_next[:, None, :] / row_level[:, None, None]
    return weights - step_rate * jnp.sqrt(mean_square)[:, None, None] * grads * lax.rsqrt(estimate)


def on_device(
    source_embed,
    target_embed,
    out_cotangent,
    row_flags,
    source_mask,
    target_mask,
    attention_weights,
    feed_weights,
    rows_attention,
    columns_attention,
    rows_feed,
    columns_feed,
    vector_params,
    vector_moments,
):
    core = lax.axis_index("c")
    local_rows, half_width = attention_weights.shape[1:]
    half_units = feed_weights.shape[2]
    depth = vector_params.shape[1]
    units_all = 2 * half_units

    def attention_group(block):
        part = attention_weights[4 * block : 4 * block + 4].astype(low)
        return part.transpose(1, 0, 2).reshape(local_rows, 4 * half_width)

    def feed_group(index):
        part = feed_weights[2 * index : 2 * index + 2].astype(low)
        return part.transpose(1, 0, 2).reshape(local_rows, 2 * half_units)

    source_half = swap_chips(source_embed[0])
    flags_half = swap_chips(row_flags[0])
    source_all = both_halves(source_half)
    flags_all = both_halves(flags_half)
    masks = swap_chips(jnp.concatenate([source_mask[0], target_mask[0]]))
    source_length = jnp.sum(masks[: source_mask.shape[1]]).reshape(1)
    target_length = jnp.sum(masks[source_mask.shape[1] :]).reshape(1)
    target_all = both_halves(swap_chips(target_embed[0]))
    cotangent_all = both_halves(swap_chips(out_cotangent[0]))

    encoder_attention, decoder_attention, cross_attention, encoder_feed, decoder_feed = gather_groups(
        [attention_group(0), attention_group(1), attention_group(2), feed_group(0), feed_group(1)]
    )

    start_rows = jnp.where(
        (flags_all == 1)[:, None],
        vector_params[12][None, :],
        jnp.where((flags_all == 2)[:, None], vector_params[13][None, :], source_all.astype(wide)),
    )
    first_kept = self_attention_call(0, False, source_length, start_rows, encoder_attention, vector_params)
    first_part = first_kept[5]
    first_other = other_core(first_part)
    third_kept = self_attention_call(6, True, target_length, target_all, decoder_attention, vector_params)
    third_part = third_kept[5]
    third_other = other_core(third_part)
    encoder_mid, second_normed, second_hidden, second_slope, second_part = feed_forward_call(
        2, start_rows, first_part, first_other, encoder_feed, vector_params
    )
    second_other = other_core(second_part)
    decoder_one, encoder_final, memory_rows, *fourth_kept, fourth_part = cross_attention_call(
        source_length,
        target_all,
        third_part,
        third_other,
        encoder_mid,
        second_part,
        second_other,
        cross_attention,
        vector_params,
    )
    decoder_two, fifth_normed, fifth_hidden, fifth_slope, fifth_part = feed_forward_call(
        10, decoder_one, fourth_part, other_core(fourth_part), decoder_feed, vector_params
    )
    decoder_three = decoder_two + (fifth_part.astype(wide) + other_core(fifth_part).astype(wide))

    def own_half(rows):
        half = rows.shape[0] // 2
        return lax.dynamic_slice_in_dim(rows, core * half, half, 0)

    decoder_out = swap_chips(own_half(decoder_three).astype(low))

    fifth_back, decoder_feed_terms, grad_three = last_feed_backward_call(
        target_length, cotangent_all, fifth_normed, fifth_hidden, fifth_slope, decoder_feed
    )
    query_back, grad_two, vectors_ten, cross_terms, memory_back = attention_backward_call(
        False,
        10,
        source_length,
        grad_three,
        decoder_two,
        fifth_back,
        other_core(fifth_back),
        vector_params,
        fourth_kept[0],
        memory_rows,
        *fourth_kept[1:],
        cross_attention,
    )
    query_other = other_core(query_back)
    memory_other = other_core(memory_back)
    third_back, grad_one, vectors_eight, decoder_terms = attention_backward_call(
        True,
        8,
        target_length,
        grad_two,
        decoder_one,
        query_back,
        query_other,
        vector_params,
        third_kept[0],
        None,
        *third_kept[1:5],
        decoder_attention,
    )
    third_back_other = other_core(third_back)
    second_back, encoder_feed_terms, grad_final, vectors_four = feed_backward_call(
        4,
        encoder_final,
        memory_back,
        memory_other,
        vector_params,
        second_normed,
        second_hidden,
        second_slope,
        encoder_feed,
    )
    first_back, grad_mid, vectors_two, encoder_terms = attention_backward_call(
        False,
        2,
        source_length,
        grad_final,
        encoder_mid,
        second_back,
        other_core(second_back),
        vector_params,
        first_kept[0],
        None,
        *first_kept[1:5],
        encoder_attention,
    )
    grad_target, vectors_six = finish_call(
        6, grad_one, target_all, third_back, third_back_other, vector_params
    )
    target_grad = swap_chips(own_half(grad_target).astype(low)).astype(wide)
    grad_start, vectors_zero = finish_call(
        0, grad_mid, start_rows, first_back, other_core(first_back), vector_params
    )
    gap_rows = jnp.sum(jnp.where((flags_all == 1)[:, None], grad_start, 0.0), axis=0, keepdims=True)
    mask_rows = jnp.sum(jnp.where((flags_all == 2)[:, None], grad_start, 0.0), axis=0, keepdims=True)
    source_grad = swap_chips(own_half(grad_start).astype(low)).astype(wide)
    source_grad = jnp.where((row_flags[0] == 0)[:, None], source_grad, 0.0)

    vector_terms = jnp.concatenate(
        [
            vectors_zero,
            vectors_two,
            vectors_four,
            vectors_six,
            vectors_eight,
            vectors_ten,
            gap_rows,
            mask_rows,
            jnp.zeros((114, depth), wide),
        ],
        axis=0,
    )
    vector_terms = vector_terms.T.astype(low)
    (encoder_grad, decoder_grad, cross_grad, encoder_feed_grad, decoder_feed_grad, vector_grad) = (
        scatter_groups(
            [
                encoder_terms,
                decoder_terms,
                cross_terms,
                encoder_feed_terms,
                decoder_feed_terms,
                vector_terms,
            ]
        )
    )
    vector_grad = vector_grad[:, :14].T

    def as_matrices(rows, count):
        return rows.reshape(local_rows, count, -1).transpose(1, 0, 2)

    attention_grad = jnp.concatenate(
        [as_matrices(part, 4) for part in (encoder_grad, decoder_grad, cross_grad)], axis=0
    )
    feed_grad = jnp.concatenate(
        [as_matrices(part, 2) for part in (encoder_feed_grad, decoder_feed_grad)], axis=0
    )

    weight_squares = jnp.concatenate(
        [
            jnp.sum(attention_weights * attention_weights, axis=(1, 2)),
            jnp.sum(feed_weights * feed_weights, axis=(1, 2)),
            jnp.sum(rows_attention, axis=1) * 0.5,
            jnp.sum(rows_feed, axis=1) * 0.5,
        ]
    )
    early_sums = data_sum(tensor_sum(weight_squares))
    scale_attention, scale_feed = early_sums[:12], early_sums[12:16]
    rows_total_attention, rows_total_feed = early_sums[16:28], early_sums[28:32]
    attention_square = attention_grad * attention_grad
    feed_square = feed_grad * feed_grad
    row_sums = tensor_sum(
        jnp.concatenate([jnp.sum(attention_square, axis=2), jnp.sum(feed_square, axis=2)], axis=0)
    )
    column_attention = jnp.sum(attention_square, axis=1)
    column_feed = jnp.sum(feed_square, axis=1)
    square_totals = jnp.sum(row_sums, axis=1)
    column_sums = data_sum(
        jnp.concatenate([column_attention.reshape(-1), column_feed.reshape(-1), square_totals])
    )
    column_attention = column_sums[: column_attention.size].reshape(column_attention.shape)
    column_feed = column_sums[column_attention.size : -16].reshape(column_feed.shape)
    square_totals = column_sums[-16:]
    keep, take = decay_rate, 1.0 - decay_rate
    rows_attention_next = keep * rows_attention + take * row_sums[:12] / depth
    rows_feed_next = keep * rows_feed + take * row_sums[12:] / units_all
    total_attention = keep * rows_total_attention + take * square_totals[:12] / depth
    total_feed = keep * rows_total_feed + take * square_totals[12:] / units_all
    columns_attention_next = keep * columns_attention + take * column_attention / depth
    columns_feed_next = keep * columns_feed + take * column_feed / depth
    attention_updated = factored_step(
        attention_weights,
        attention_grad,
        rows_attention_next,
        columns_attention_next,
        total_attention / depth,
        scale_attention / (depth * depth),
    )
    feed_updated = factored_step(
        feed_weights,
        feed_grad,
        rows_feed_next,
        columns_feed_next,
        total_feed / depth,
        scale_feed / (depth * units_all),
    )
    local_width = vector_moments.shape[1]
    place = (lax.axis_index("z") * lax.axis_size("y") + lax.axis_index("y")) * 2 + core
    vector_local = lax.dynamic_slice_in_dim(vector_params, place * local_width, local_width, 1)
    vector_moments_next = keep * vector_moments + take * vector_grad * vector_grad
    vector_scale = jnp.sqrt(jnp.mean(vector_params * vector_params, axis=1))
    vector_updated = vector_local - step_rate * vector_scale[:, None] * vector_grad * lax.rsqrt(
        vector_moments_next
    )
    return (
        decoder_out[None],
        source_grad[None],
        target_grad[None],
        attention_grad,
        feed_grad,
        vector_grad,
        attention_updated,
        feed_updated,
        vector_updated,
        rows_attention_next,
        columns_attention_next,
        rows_feed_next,
        columns_feed_next,
        vector_moments_next,
        vector_grad[10:12],
    )


def solution(mesh):
    groups = mesh.shape["dp"] // 4
    inner = Mesh(mesh.devices.reshape(groups, 2, 2, 2), ("z", "y", "c", "x"))
    data = ("z", "y", "c")
    rows3, rows2 = P(data, "x", None), P(data, "x")
    matrix, row_spec, column_spec = P(None, data, "x"), P(None, data), P(None, "x")
    return jax.shard_map(
        on_device,
        mesh=inner,
        in_specs=(
            rows3,
            rows3,
            rows3,
            rows2,
            P(data, None),
            P(data, None),
            matrix,
            matrix,
            row_spec,
            column_spec,
            row_spec,
            column_spec,
            P(),
            row_spec,
        ),
        out_specs=(
            rows3,
            rows3,
            rows3,
            matrix,
            matrix,
            row_spec,
            matrix,
            matrix,
            row_spec,
            row_spec,
            column_spec,
            row_spec,
            column_spec,
            row_spec,
            row_spec,
        ),
        check_vma=False,
    )
```

```python
import functools

import jax
import jax.numpy as jnp
from jax import lax
from jax.experimental import pallas as pl
from jax.experimental.pallas import tpu as pltpu
from jax.sharding import Mesh
from jax.sharding import PartitionSpec as P

HEAD_DIM = 64
CHUNK = 256
norm_epsilon = 1e-05
decay_rate = 1.0 - 2.0 ** (-0.8)
step_rate = 0.2
masked_score = -1e30
low = jnp.bfloat16
wide = jnp.float32
MESH = pl.DeviceIdType.MESH


def swap_chips(array):
    return lax.ppermute(array, ("c", "x"), [(0, 0), (1, 2), (2, 1), (3, 3)])


def other_core(array):
    return lax.ppermute(array, "c", [(0, 1), (1, 0)])


def both_halves(own_half):
    received = other_core(own_half)
    first = lax.axis_index("c") == 0
    return jnp.concatenate(
        [jnp.where(first, own_half, received), jnp.where(first, received, own_half)], axis=0
    )


def core_sum(partial_rows):
    sent = partial_rows.astype(low)
    return sent.astype(wide) + other_core(sent).astype(wide)


def ring_next(array):
    size = lax.axis_size("z")
    return lax.ppermute(array, "z", [(i, (i + 1) % size) for i in range(size)])


def holds():
    return lax.axis_index("c") == lax.axis_index("x")


def spread_blocks(blocks, order):
    held = blocks[None, None]
    for axis in order:
        if axis == "x":
            received = lax.ppermute(held, ("c", "x"), [(0, 1), (3, 2)])
            held = jnp.where(holds(), held, received)
        elif axis == "y":
            received = lax.ppermute(held, "y", [(0, 1), (1, 0)])
            first = lax.axis_index("y") == 0
            held = jnp.concatenate(
                [jnp.where(first, held, received), jnp.where(first, received, held)], axis=1
            )
        else:
            size = lax.axis_size("z")
            if size != 4:
                held = lax.all_gather(held, "z", axis=0, tiled=True)
                continue
            place = lax.axis_index("z")
            whole = jnp.zeros((size,) + held.shape[1:], held.dtype)
            moving = held
            for step in range(size):
                where_from = lax.rem(place + size - step, size)
                whole = lax.dynamic_update_slice_in_dim(whole, moving, where_from, 0)
                if step < size - 1:
                    moving = ring_next(moving)
            held = whole
    return held


def reduce_blocks(parts, order):
    held = parts
    for position, axis in enumerate(order):
        final = position == len(order) - 1
        kind = wide if final else low
        if axis == "x":
            received = lax.ppermute(held, ("c", "x"), [(1, 0), (2, 3)])
            held = (held.astype(wide) + received.astype(wide)).astype(kind)
        elif axis == "y":
            mine = lax.axis_index("y")
            sent = lax.dynamic_slice_in_dim(held, 1 - mine, 1, 1)
            kept = lax.dynamic_slice_in_dim(held, mine, 1, 1)
            received = lax.ppermute(sent, "y", [(0, 1), (1, 0)])
            held = (kept.astype(wide) + received.astype(wide)).astype(kind)
        else:
            size = lax.axis_size("z")
            if size != 4:
                held = lax.psum_scatter(held, "z", scatter_dimension=0, tiled=True).astype(kind)
                continue
            place = lax.axis_index("z")
            moving = lax.dynamic_slice_in_dim(held, lax.rem(place + size - 1, size), 1, 0)
            for step in range(1, size):
                received = ring_next(moving)
                kept = lax.dynamic_slice_in_dim(held, lax.rem(place + size - 1 - step, size), 1, 0)
                last = step == size - 1
                moving = (kept.astype(wide) + received.astype(wide)).astype(kind if last else low)
            held = moving
    return held[0, 0]


def gather_weights(blocks, order):
    received = lax.ppermute(blocks, ("c", "x"), [(2, 0), (1, 3)])
    first = lax.axis_index("c") == 0
    both = jnp.concatenate(
        [jnp.where(first, blocks, received), jnp.where(first, received, blocks)], axis=0
    )
    spread = spread_blocks(both, order)
    return spread.reshape(-1, spread.shape[-1])


def scatter_gradient(gradient, order):
    depth, columns = gradient.shape
    z_size, y_size = lax.axis_size("z"), lax.axis_size("y")
    rows = depth // (z_size * y_size)
    total = reduce_blocks(gradient.astype(low).reshape(z_size, y_size, rows, columns), order)
    core = lax.axis_index("c")
    half = rows // 2
    kept = lax.dynamic_slice_in_dim(total, core * half, half, 0)
    sent = lax.dynamic_slice_in_dim(total, (1 - core) * half, half, 0)
    received = lax.ppermute(sent, ("c", "x"), [(0, 2), (3, 1)])
    return jnp.where(holds(), kept, received)


def data_sum(values):
    values = values + other_core(values)
    if lax.axis_size("z") != 4:
        return lax.psum(values, ("z", "y"))
    values = values + lax.ppermute(values, "y", [(0, 1), (1, 0)])
    values = values + lax.ppermute(values, "z", [(0, 1), (1, 0), (2, 3), (3, 2)])
    return values + lax.ppermute(values, "z", [(0, 2), (2, 0), (1, 3), (3, 1)])


def tensor_sum(values):
    return values + lax.ppermute(values, "x", [(0, 1), (1, 0)])


def column_cuts(columns):
    tiles = columns // 128
    first = (tiles * 42 + 50) // 100
    second = (tiles * 36 + 50) // 100
    edges = [0, first * 128, (first + second) * 128, columns]
    return list(zip(edges[:-1], edges[1:]))


def place(name):
    return lax.axis_index(name)


def block_at(which):
    back, same = which
    z = lax.rem(place("z") + 4 - back, 4)
    return z * 2 + (place("y") if same else 1 - place("y"))


def target_of(axis):
    if axis == "z":
        return {"z": lax.rem(place("z") + 1, 4)}
    if axis == "z_back":
        return {"z": lax.rem(place("z") + 3, 4)}
    if axis == "x_home":
        return {"c": place("x"), "x": 1 - place("x")}
    return {axis: 1 - place(axis)}


def greet():
    barrier = pltpu.get_barrier_semaphore()
    targets = [target_of(axis) for axis in ("c", "y", "z", "z_back", "x")]
    targets.append({"c": 1 - place("c"), "x": 1 - place("x")})
    for target in targets:
        pl.semaphore_signal(barrier, inc=1, device_id=target, device_id_type=MESH)
    pl.semaphore_wait(barrier, len(targets))


def here(back):
    return (back, True)


def there(back):
    return (back, False)


class Mover:
    def __init__(self, send_sems):
        self.steps = {True: [], False: []}
        self.sent = {True: [], False: []}
        self.done = 0
        self.send_sems = send_sems

    def send(self, home, source, target, recv_sem, device):
        number = len(self.sent[home])

        def copy():
            return pltpu.make_async_remote_copy(
                src_ref=source(),
                dst_ref=target(),
                send_sem=self.send_sems.at[number],
                recv_sem=recv_sem(),
                device_id=device(),
                device_id_type=MESH,
            )

        self.sent[home].append(copy)
        self.steps[home].append(lambda: copy().start())

    def wait(self, home, target, recv_sem):
        def step():
            pltpu.make_async_remote_copy(
                src_ref=target(),
                dst_ref=target(),
                send_sem=self.send_sems.at[0],
                recv_sem=recv_sem(),
                device_id=target_of("c"),
                device_id_type=MESH,
            ).wait_recv()

        self.steps[home].append(step)

    def local(self, home, step):
        self.steps[home].append(step)

    def run(self, part, parts):
        for home in (True, False):
            steps = self.steps[home]
            chosen = steps[len(steps) * part // parts : len(steps) * (part + 1) // parts]
            if not chosen:
                continue
            wanted = place("c") == place("x")

            @pl.when(wanted if home else jnp.logical_not(wanted))
            def _():
                for step in chosen:
                    step()

    def finish(self):
        for home in (True, False):
            wanted = place("c") == place("x")

            @pl.when(wanted if home else jnp.logical_not(wanted))
            def _():
                for copy in self.sent[home]:
                    copy().wait_send()


class Gather(Mover):
    def __init__(self, own_ref, out_ref, stage_ref, local_sem, send_sems, recv_sems):
        super().__init__(send_sems)
        rows, columns = own_ref.shape
        cuts = column_cuts(columns)
        (begin_a, end_a), (begin_b, end_b), (begin_c, end_c) = cuts
        first, second, third = 0, 1, 2

        def out_piece(group, which, parity):
            begin, end = cuts[group]
            return out_ref.at[
                block_at(which), pl.ds(parity() * rows, rows), pl.ds(begin, end - begin)
            ]

        def out_sem(group, which, parity):
            return recv_sems.at[(group * 8 + block_at(which)) * 2 + parity()]

        def stage_piece(group, which):
            begin, end = cuts[group]
            return stage_ref.at[block_at(which), :, pl.ds(begin, end - begin)]

        def stage_sem(group, which):
            return recv_sems.at[48 + group * 8 + block_at(which)]

        def core():
            return place("c")

        def other():
            return 1 - place("c")

        self_copies = {
            True: lambda: pltpu.make_async_copy(
                own_ref, out_ref.at[block_at(here(0)), pl.ds(core() * rows, rows), :], local_sem
            ),
        }

        def own_piece(group):
            begin, end = cuts[group]
            return own_ref.at[:, pl.ds(begin, end - begin)]

        for home in (True, False):
            arrived = set()

            def plane(group, which):
                if which == here(0):
                    return functools.partial(own_piece, group)
                if home:
                    return functools.partial(out_piece, group, which, core)
                return functools.partial(stage_piece, group, which)

            def plane_target(group, which):
                if home:
                    return (
                        functools.partial(out_piece, group, which, core),
                        functools.partial(out_sem, group, which, core),
                    )
                return (
                    functools.partial(stage_piece, group, which),
                    functools.partial(stage_sem, group, which),
                )

            def plane_send(group, which, axis):
                target, sem = plane_target(group, which)
                self.send(home, plane(group, which), target, sem, functools.partial(target_of, axis))

            def plane_wait(group, which):
                if which == here(0):
                    return
                target, sem = plane_target(group, which)
                self.wait(home, target, sem)
                if home:
                    arrived.add((group, which, "core"))

            def deliver(group, which):
                target = functools.partial(out_piece, group, which, core)
                sem = functools.partial(out_sem, group, which, core)
                source = plane(group, which)
                self.send(home, source, target, sem, functools.partial(target_of, "x_home"))
                if not home:
                    self.send(home, source, target, sem, functools.partial(target_of, "c"))

            def core_send(group, which, name, axis):
                parity = core if name == "core" else other
                if home and which == here(0) and name == "core":
                    source = functools.partial(own_piece, group)
                else:
                    source = functools.partial(out_piece, group, which, parity)
                self.send(
                    home,
                    source,
                    functools.partial(out_piece, group, which, parity),
                    functools.partial(out_sem, group, which, parity),
                    functools.partial(target_of, axis),
                )

            def core_wait(group, which, name):
                if home and which == here(0) and name == "core":
                    return
                if (group, which, name) in arrived:
                    return
                arrived.add((group, which, name))
                parity = core if name == "core" else other
                self.wait(
                    home,
                    functools.partial(out_piece, group, which, parity),
                    functools.partial(out_sem, group, which, parity),
                )

            if home:
                self.local(home, lambda: self_copies[True]().start())
            deliver(third, here(0))
            plane_send(first, here(0), "z")
            plane_send(second, here(0), "z")
            plane_send(first, here(0), "y")
            deliver(second, here(0))
            deliver(first, here(0))
            names = ("core", "other") if home else ("other", "core")
            for name in names:
                core_wait(third, here(0), name)
                core_send(third, here(0), name, "z")
                core_send(third, here(0), name, "y")
            for name in names:
                core_wait(second, here(0), name)
                core_send(second, here(0), name, "y")
            for back in (1, 2, 3):
                plane_wait(first, here(back))
                if back < 3:
                    plane_send(first, here(back), "z")
                plane_send(first, here(back), "y")
                plane_wait(second, here(back))
                if back < 3:
                    plane_send(second, here(back), "z")
                deliver(second, here(back))
                deliver(first, here(back))
                plane_wait(first, there(back - 1))
                deliver(first, there(back - 1))
                if back == 1:
                    for name in names:
                        core_wait(third, there(0), name)
                        core_send(third, there(0), name, "z")
                for which in (here(back), there(back)):
                    for name in names:
                        core_wait(third, which, name)
                        if back < 3:
                            core_send(third, which, name, "z")
                for name in names:
                    core_wait(second, here(back), name)
                    core_send(second, here(back), name, "y")
            plane_wait(first, there(3))
            deliver(first, there(3))
            for group in (third, second, first):
                for back in range(4):
                    for which in (here(back), there(back)):
                        for name in ("core", "other"):
                            core_wait(group, which, name)
            if home:
                self.local(home, lambda: self_copies[True]().wait())


GATHER_SENDS = 64


def gather_kernel(own_ref, out_ref, stage_ref, local_sem, send_sems, recv_sems):
    greet()
    mover = Gather(own_ref, out_ref, stage_ref, local_sem, send_sems, recv_sems)
    mover.run(0, 1)
    mover.finish()


def gather_scratch(rows, columns):
    cuts = column_cuts(columns)
    return [
        pltpu.VMEM((8, rows, cuts[1][1]), low),
        pltpu.SemaphoreType.DMA,
        pltpu.SemaphoreType.DMA((GATHER_SENDS,)),
        pltpu.SemaphoreType.DMA((64,)),
    ]


def gather_all(own, number=0):
    rows, columns = own.shape
    return pl.pallas_call(
        gather_kernel,
        out_shape=jax.ShapeDtypeStruct((8, 2 * rows, columns), own.dtype),
        in_specs=[pl.BlockSpec(memory_space=pl.ANY)],
        out_specs=pl.BlockSpec(memory_space=pl.ANY),
        scratch_shapes=gather_scratch(rows, columns),
        compiler_params=pltpu.CompilerParams(
            collective_id=number, has_side_effects=True, vmem_limit_bytes=40 << 20
        ),
        name="gather_weights",
    )(own)


class Scatter(Mover):
    def __init__(self, total, final, stage, x_in, ya_in, yb_in, z_in, zc_in, yc_in, send_sems, recv_sems):
        super().__init__(send_sems)
        rows = total.shape[1] // 2
        columns = total.shape[2]
        cuts = column_cuts(columns)
        first, second, third = 0, 1, 2
        widths = [end - begin for begin, end in cuts]

        def part(group):
            begin, end = cuts[group]
            return pl.ds(begin, end - begin)

        def core_piece(group, which, parity=None):
            if parity is None:
                return total.at[block_at(which), :, part(group)]
            return total.at[block_at(which), pl.ds(parity() * rows, rows), part(group)]

        def slot_of(which):
            return which[0] + (0 if which[1] else 4)

        def x_piece(group, which):
            return x_in.at[slot_of(which), :, part(group)]

        def stage_piece(group, which):
            return stage.at[slot_of(which), :, part(group)]

        def sem(number):
            return lambda: recv_sems.at[number]

        def core():
            return place("c")

        def other():
            return 1 - place("c")

        def add_rows(held_of, came_of, count, final_part=None):
            def step():
                held, came = held_of(), came_of()

                @pl.loop(0, count // 16)
                def _(number):
                    at = pl.ds(pl.multiple_of(number * 16, 16), 16)
                    if final_part is None:
                        held[at, :] = held[at, :] + came[at, :]
                    else:
                        final[at, final_part] = held[at, :].astype(wide) + came[at, :].astype(wide)

            return step

        for home in (True, False):

            def plane(group, which):
                if home:
                    return functools.partial(core_piece, group, which, core)
                return functools.partial(stage_piece, group, which)

            def x_sends(group, which):
                number = group * 8 + slot_of(which)
                if home:
                    self.send(
                        home,
                        functools.partial(core_piece, group, which, other),
                        functools.partial(stage_piece, group, which),
                        sem(24 + number),
                        functools.partial(target_of, "c"),
                    )
                    return
                for parity in (0, 1):
                    self.send(
                        home,
                        functools.partial(core_piece, group, which, functools.partial(parity_value, parity)),
                        functools.partial(x_piece, group, which),
                        sem(number),
                        functools.partial(home_core, parity),
                    )

            def x_add(group, which, last=False):
                number = group * 8 + slot_of(which)
                if not home:
                    self.wait(home, functools.partial(stage_piece, group, which), sem(24 + number))
                self.wait(home, functools.partial(x_piece, group, which), sem(number))
                self.local(
                    home,
                    add_rows(
                        plane(group, which),
                        functools.partial(x_piece, group, which),
                        rows,
                        part(group) if last else None,
                    ),
                )

            def z_slot(group, back):
                return lambda: z_in.at[back, :, part(group)]

            def z_send(group, back):
                self.send(
                    home,
                    plane(group, here(back)),
                    z_slot(group, back - 1),
                    sem(60 + group * 4 + back - 1),
                    functools.partial(target_of, "z_back"),
                )

            def z_add(group, back):
                self.wait(home, z_slot(group, back), sem(60 + group * 4 + back))
                self.local(
                    home,
                    add_rows(
                        plane(group, here(back)),
                        z_slot(group, back),
                        rows,
                        part(group) if back == 0 else None,
                    ),
                )

            def ya_slot(back):
                return lambda: ya_in.at[back]

            def yb_slot(back):
                return lambda: yb_in.at[back]

            def zc_slot(which):
                back, same = which
                return lambda: zc_in.at[back + (0 if same else 3)]

            def zc_send(which):
                back, same = which
                self.send(
                    home,
                    functools.partial(core_piece, third, which),
                    zc_slot((back - 1, same)),
                    sem(72 + back - 1 + (0 if same else 3)),
                    functools.partial(target_of, "z_back"),
                )

            def zc_add(which):
                back, same = which
                self.wait(home, zc_slot(which), sem(72 + back + (0 if same else 3)))
                self.local(
                    home,
                    add_rows(functools.partial(core_piece, third, which), zc_slot(which), 2 * rows),
                )

            def second_steps(back):
                x_add(second, here(back))
                if back < 3:
                    z_add(second, back)
                if back > 0:
                    z_send(second, back)

            zc_send(there(3))
            zc_send(here(3))
            for back in (3, 2, 1, 0):
                self.send(
                    home,
                    functools.partial(core_piece, second, there(back)),
                    yb_slot(back),
                    sem(52 + back),
                    functools.partial(target_of, "y"),
                )
                if back > 1:
                    x_sends(first, there(back))
                    x_sends(first, here(back))
            for back in (3, 2, 1, 0):
                self.wait(home, yb_slot(back), sem(52 + back))
                self.local(
                    home,
                    add_rows(functools.partial(core_piece, second, here(back)), yb_slot(back), 2 * rows),
                )
                x_sends(second, here(back))
                if back > 1:
                    x_sends(first, there(back - 2))
                    x_sends(first, here(back - 2))
                if back < 3:
                    for which in (there(back), here(back)):
                        zc_add(which)
                        if back > 0:
                            zc_send(which)
                        elif not which[1]:
                            self.send(
                                home,
                                functools.partial(core_piece, third, there(0)),
                                lambda: yc_in.at[...],
                                sem(56),
                                functools.partial(target_of, "y"),
                            )
                x_add(first, there(back))
                self.send(
                    home,
                    plane(first, there(back)),
                    ya_slot(back),
                    sem(48 + back),
                    functools.partial(target_of, "y"),
                )
                x_add(first, here(back))
                if back < 3:
                    second_steps(back + 1)
                if back == 0:
                    self.wait(home, lambda: yc_in.at[...], sem(56))
                    self.local(
                        home,
                        add_rows(
                            functools.partial(core_piece, third, here(0)),
                            lambda: yc_in.at[...],
                            2 * rows,
                        ),
                    )
                    x_sends(third, here(0))
                self.wait(home, ya_slot(back), sem(48 + back))
                self.local(home, add_rows(plane(first, here(back)), ya_slot(back), rows))
                if back < 3:
                    z_add(first, back)
                if back > 0:
                    z_send(first, back)
            second_steps(0)
            x_add(third, here(0), last=True)


def parity_value(parity):
    return parity


def home_core(parity):
    return {"c": parity, "x": place("c")}


SCATTER_SENDS = 48


def scatter_scratch(rows, columns):
    cuts = column_cuts(columns)
    widths = [end - begin for begin, end in cuts]
    return [
        pltpu.VMEM((8, 2 * rows, columns), low),
        pltpu.VMEM((8, rows, columns), low),
        pltpu.VMEM((8, rows, columns), low),
        pltpu.VMEM((4, rows, widths[0]), low),
        pltpu.VMEM((4, 2 * rows, widths[1]), low),
        pltpu.VMEM((4, rows, columns), low),
        pltpu.VMEM((6, 2 * rows, widths[2]), low),
        pltpu.VMEM((2 * rows, widths[2]), low),
        pltpu.SemaphoreType.DMA((SCATTER_SENDS,)),
        pltpu.SemaphoreType.DMA((80,)),
    ]


def scatter_kernel(widths, *refs):
    count = len(widths)
    grads = refs[:count]
    final, total = refs[count : count + 2]
    load_sems = refs[-1]
    loads = []
    begin = 0
    for number, width in enumerate(widths):
        one = pltpu.make_async_copy(
            grads[number], total.at[:, :, pl.ds(begin, width)], load_sems.at[number]
        )
        one.start()
        loads.append(one)
        begin += width
    greet()
    for one in loads:
        one.wait()
    mover = Scatter(total, final, *refs[count + 2 : -1])
    mover.run(0, 1)
    mover.finish()


def scatter_all(parts, number=1):
    depth = parts[0].shape[0]
    widths = [part.shape[1] for part in parts]
    columns = sum(widths)
    rows = depth // 16
    return pl.pallas_call(
        functools.partial(scatter_kernel, widths),
        out_shape=jax.ShapeDtypeStruct((rows, columns), wide),
        in_specs=[pl.BlockSpec(memory_space=pl.ANY)] * len(parts),
        out_specs=pl.BlockSpec(memory_space=pltpu.VMEM),
        scratch_shapes=scatter_scratch(rows, columns) + [pltpu.SemaphoreType.DMA((len(parts),))],
        compiler_params=pltpu.CompilerParams(
            collective_id=number, has_side_effects=True, vmem_limit_bytes=58 << 20
        ),
        name="scatter_gradients",
    )(*[part.reshape(8, 2 * rows, part.shape[1]) for part in parts])


class Rider:
    def __init__(self, kind, operand, number):
        self.kind = kind
        self.number = number
        if kind == "gather":
            rows, columns = operand.shape
            self.operand = operand
            self.out = jax.ShapeDtypeStruct((8, 2 * rows, columns), operand.dtype)
            self.out_spec = pl.BlockSpec(memory_space=pl.ANY)
            self.scratch = gather_scratch(rows, columns)
        else:
            depth, columns = operand.shape
            rows = depth // 16
            self.operand = operand.reshape(8, 2 * rows, columns)
            self.out = jax.ShapeDtypeStruct((rows, columns), wide)
            self.out_spec = pl.BlockSpec(memory_space=pltpu.VMEM)
            self.scratch = scatter_scratch(rows, columns) + [pltpu.SemaphoreType.DMA]


class Ticks:
    def __init__(self, rider, operand_ref, out_ref, scratch):
        self.rider = rider
        self.refs = (operand_ref, out_ref, scratch)
        self.mover = None

    def begin(self, parts):
        if self.rider is None:
            return
        operand_ref, out_ref, scratch = self.refs
        self.parts = parts
        if self.rider.kind == "gather":
            self.mover = Gather(operand_ref, out_ref, *scratch)
        else:

            def load():
                return pltpu.make_async_copy(operand_ref, scratch[0], scratch[-1])

            load().start()
            self.mover = Scatter(scratch[0], out_ref, *scratch[1:-1])
            for home in (True, False):
                self.mover.steps[home].insert(0, lambda: load().wait())
        greet()

    def __call__(self, part):
        if self.mover is not None:
            self.mover.run(part, self.parts)

    def in_loop(self, step, steps, offset, stride, inner):
        if self.mover is None:
            return
        for number in range(steps):

            @pl.when(step == number)
            def _():
                self(offset + number * stride + inner)

    def end(self):
        if self.mover is not None:
            self.mover.finish()


def ride_call(body, operands, in_specs, outs, scratch, rider, name):
    count_in, count_out, count_scratch = len(operands), len(outs), len(scratch)
    out_specs = [pl.BlockSpec(memory_space=pltpu.VMEM)] * count_out
    options = dict(vmem_limit_bytes=60 << 20)
    operands, in_specs, outs, scratch = list(operands), list(in_specs), list(outs), list(scratch)
    if rider is not None:
        operands.append(rider.operand)
        in_specs.append(pl.BlockSpec(memory_space=pl.ANY))
        outs.append(rider.out)
        out_specs.append(rider.out_spec)
        scratch += rider.scratch
        options.update(collective_id=rider.number, has_side_effects=True)

    def kernel(*refs):
        ins, rest = refs[:count_in], refs[count_in:]
        operand_ref = out_ref = None
        extra = ()
        if rider is not None:
            operand_ref, rest = rest[0], rest[1:]
        mine, rest = rest[:count_out], rest[count_out:]
        if rider is not None:
            out_ref, rest = rest[0], rest[1:]
        own, extra = rest[:count_scratch], rest[count_scratch:]
        ticks = Ticks(rider, operand_ref, out_ref, extra)
        body(ticks, *ins, *mine, *own)
        ticks.end()

    return pl.pallas_call(
        kernel,
        out_shape=tuple(outs),
        in_specs=in_specs,
        out_specs=tuple(out_specs),
        scratch_shapes=scratch,
        compiler_params=pltpu.CompilerParams(**options),
        name=name,
    )(*operands)


def whole():
    return pl.BlockSpec(memory_space=pltpu.VMEM)


def scalar():
    return pl.BlockSpec(memory_space=pltpu.SMEM)


def weight_spec(weights):
    return pl.BlockSpec(memory_space=pltpu.VMEM)


def shaped(rows, columns, kind):
    return jax.ShapeDtypeStruct((rows, columns), kind)


def dot_nn(left, right):
    return lax.dot_general(left, right, (((1,), (0,)), ((), ())), preferred_element_type=wide)


def dot_nt(left, right):
    return lax.dot_general(left, right, (((1,), (1,)), ((), ())), preferred_element_type=wide)


def turned(block):
    size = block.shape[1]
    row = lax.broadcasted_iota(jnp.int32, (size, size), 0)
    column = lax.broadcasted_iota(jnp.int32, (size, size), 1)
    return dot_nt((row == column).astype(wide).astype(low), block).astype(low)


def turn_into(target, source):
    rows, columns = source.shape
    for at in range(0, columns, 256):
        wide_part = min(256, columns - at)
        target[at : at + wide_part, :] = turned(source[:, at : at + wide_part])


def centre_rows(values):
    centred = values - jnp.mean(values, axis=-1, keepdims=True)
    spread = jnp.mean(centred * centred, axis=-1, keepdims=True)
    return centred * lax.rsqrt(spread + norm_epsilon)


def norm_back(x, gain, grads):
    centred = x - jnp.mean(x, axis=-1, keepdims=True)
    scale = lax.rsqrt(jnp.mean(centred * centred, axis=-1, keepdims=True) + norm_epsilon)
    unit = centred * scale
    inner = grads * gain
    by_unit = inner * unit
    back = scale * (
        inner
        - jnp.mean(inner, axis=-1, keepdims=True)
        - unit * jnp.mean(by_unit, axis=-1, keepdims=True)
    )
    return back, jnp.sum(grads * unit, axis=0, keepdims=True), jnp.sum(grads, axis=0, keepdims=True)


def residual_prologue(norm_row, previous_ref, x_ref, own_ref, other_ref, vec_ref, grad_out, low_ref, vec_out):
    gain = vec_ref[norm_row : norm_row + 1, :]
    vec_out[...] = jnp.zeros_like(vec_out)

    @pl.loop(0, x_ref.shape[0] // CHUNK)
    def _(step):
        at = pl.ds(pl.multiple_of(step * CHUNK, CHUNK), CHUNK)
        grads = own_ref[at, :].astype(wide) + other_ref[at, :].astype(wide)
        back, by_gain, by_shift = norm_back(x_ref[at, :].astype(wide), gain, grads)
        if previous_ref is not None:
            back = back + previous_ref[at, :].astype(wide)
        if grad_out is not None:
            grad_out[at, :] = back
        if low_ref is not None:
            low_ref[at, :] = back.astype(low)
        vec_out[0:1, :] += by_gain
        vec_out[1:2, :] += by_shift


def erf_ratio(values):
    x = jnp.clip(values, -4.0, 4.0)
    square = x * x
    top = jnp.full_like(square, -2.72614225801306e-10)
    for term in (
        2.77068142495902e-08,
        -2.10102402082508e-06,
        -5.69250639462346e-05,
        -7.34990630326855e-04,
        -2.95459980854025e-03,
        -1.60960333262415e-02,
    ):
        top = top * square + term
    low_part = jnp.full_like(square, -1.45660718464996e-05)
    for term in (
        -2.13374055278905e-04,
        -1.68282697438203e-03,
        -7.37332916720468e-03,
        -1.42647390514189e-02,
    ):
        low_part = low_part * square + term
    return x * top / low_part


def gelu_pair(before):
    phi_whole = 0.5 + 0.5 * erf_ratio(before * 0.7071067811865476)
    density = jnp.exp(before * before * -0.5) * 0.3989422804014327
    return before * phi_whole, phi_whole + before * density


def chunks(rows):
    return range(0, rows, CHUNK)


def feed_forward_kernel(
    rows_norm, ticks, x_ref, own_ref, other_ref, w_ref, vec_ref, x_out, normed_out, hidden_out, slope_out, part_out
):
    units = w_ref.shape[1] // 2
    steps = x_ref.shape[0] // CHUNK
    pieces = units // 512
    ticks.begin(steps * pieces)
    gain = vec_ref[rows_norm : rows_norm + 1, :]
    shift = vec_ref[rows_norm + 1 : rows_norm + 2, :]

    @pl.loop(0, x_ref.shape[0] // CHUNK)
    def _(step):
        at = pl.ds(pl.multiple_of(step * CHUNK, CHUNK), CHUNK)
        x = x_ref[at, :] + (own_ref[at, :].astype(wide) + other_ref[at, :].astype(wide))
        x_out[at, :] = x
        normed = (centre_rows(x) * gain + shift).astype(low)
        normed_out[at, :] = normed
        part = jnp.zeros((CHUNK, x.shape[1]), wide)
        for begin in range(0, units, 512):
            ticks.in_loop(step, steps, 0, pieces, begin // 512)
            before = dot_nn(normed, w_ref[:, begin : begin + 512])
            value, slope = gelu_pair(before)
            hidden = value.astype(low)
            hidden_out[at, begin : begin + 512] = hidden
            slope_out[at, begin : begin + 512] = slope.astype(low)
            part = part + dot_nt(hidden, w_ref[:, units + begin : units + begin + 512])
        part_out[at, :] = part.astype(low)


def feed_forward_call(rows_norm, x, own, other, weights, vectors, rider=None):
    rows, depth = x.shape
    units = weights[1] // 2
    return ride_call(
        functools.partial(feed_forward_kernel, rows_norm),
        [x, own, other, weights[0], vectors],
        [whole(), whole(), whole(), weight_spec(weights), whole()],
        [
            shaped(rows, depth, wide),
            shaped(rows, depth, low),
            shaped(rows, units, low),
            shaped(rows, units, low),
            shaped(rows, depth, low),
        ],
        [],
        rider,
        "feed_forward",
    )


def feed_backward_body(ticks, normed_ref, hidden_ref, slope_in, w_ref, part_out, grad_out, low_ref, slope_ref, turned_ref, turned_low):
    rows, depth = low_ref.shape
    units = w_ref.shape[1] // 2
    steps = rows // CHUNK
    pieces = units // 512
    offset = 1 + steps * pieces
    ticks(0)
    turn_into(turned_low, low_ref)
    turn_into(turned_ref, normed_ref)

    @pl.loop(0, rows // CHUNK)
    def _(step):
        at = pl.ds(pl.multiple_of(step * CHUNK, CHUNK), CHUNK)
        grads = low_ref[at, :]
        part = jnp.zeros((CHUNK, depth), wide)
        for begin in range(0, units, 512):
            ticks.in_loop(step, steps, 1, pieces, begin // 512)
            grad = dot_nn(grads, w_ref[:, units + begin : units + begin + 512])
            grad = (grad * slope_in[at, begin : begin + 512].astype(wide)).astype(low)
            slope_ref[at, begin : begin + 512] = grad
            part = part + dot_nt(grad, w_ref[:, begin : begin + 512])
        part_out[at, :] = part.astype(low)

    for begin in range(0, units, 256):
        ticks(offset + begin // 256)
        grad_out[:, begin : begin + 256] = dot_nn(
            turned_ref[...], slope_ref[:, begin : begin + 256]
        ).astype(low)
        grad_out[:, units + begin : units + begin + 256] = dot_nn(
            turned_low[...], hidden_ref[:, begin : begin + 256]
        ).astype(low)


def feed_backward_scratch(rows, depth, units):
    return [
        pltpu.VMEM((rows, depth), low),
        pltpu.VMEM((rows, units), low),
        pltpu.VMEM((depth, rows), low),
        pltpu.VMEM((depth, rows), low),
    ]


def last_feed_backward_kernel(
    ticks, length_ref, cotangent_ref, normed_ref, hidden_ref, slope_in, w_ref, part_out, grad_out, low_ref, *rest
):
    rows, depth = cotangent_ref.shape
    place = lax.broadcasted_iota(jnp.int32, (CHUNK, depth), 0)

    @pl.loop(0, rows // CHUNK)
    def _(step):
        first_row = pl.multiple_of(step * CHUNK, CHUNK)
        at = pl.ds(first_row, CHUNK)
        rows_here = cotangent_ref[at, :].astype(wide)
        low_ref[at, :] = jnp.where(first_row + place < length_ref[0], rows_here, 0.0).astype(low)

    feed_backward_body(ticks, normed_ref, hidden_ref, slope_in, w_ref, part_out, grad_out, low_ref, *rest)


def last_feed_backward_call(length, cotangent, normed, hidden, slope, weights, rider=None):
    rows, depth = cotangent.shape
    units = hidden.shape[1]
    return ride_call(
        last_feed_backward_kernel,
        [length, cotangent, normed, hidden, slope, weights[0]],
        [scalar()] + [whole()] * 4 + [weight_spec(weights)],
        [shaped(rows, depth, low), shaped(depth, 2 * units, low), shaped(rows, depth, low)],
        feed_backward_scratch(rows, depth, units)[1:],
        rider,
        "last_feed_backward",
    )


def feed_backward_kernel(
    norm_row, ticks, x_ref, own_ref, other_ref, vec_ref, normed_ref, hidden_ref, slope_in, w_ref,
    part_out, grad_out, g_out, vec_out, low_ref, *rest
):
    units = w_ref.shape[1] // 2
    ticks.begin(1 + x_ref.shape[0] // CHUNK * (units // 512) + units // 256)
    residual_prologue(norm_row, None, x_ref, own_ref, other_ref, vec_ref, g_out, low_ref, vec_out)
    feed_backward_body(ticks, normed_ref, hidden_ref, slope_in, w_ref, part_out, grad_out, low_ref, *rest)


def feed_backward_call(norm_row, x, own, other, vectors, normed, hidden, slope, weights, rider=None):
    rows, depth = x.shape
    units = hidden.shape[1]
    return ride_call(
        functools.partial(feed_backward_kernel, norm_row),
        [x, own, other, vectors, normed, hidden, slope, weights[0]],
        [whole()] * 7 + [weight_spec(weights)],
        [
            shaped(rows, depth, low),
            shaped(depth, 2 * units, low),
            shaped(rows, depth, wide),
            shaped(2, depth, wide),
        ],
        feed_backward_scratch(rows, depth, units),
        rider,
        "feed_backward",
    )


def half_lanes(shape):
    return lax.broadcasted_iota(jnp.int32, shape, 1) < 64


def one_head(pair, head):
    first = half_lanes(pair.shape)
    zero = jnp.zeros_like(pair)
    return jnp.where(first, pair, zero) if head == 0 else jnp.where(first, zero, pair)


def key_bias(keys, length, first_row, causal, rows):
    place = lax.broadcasted_iota(jnp.int32, (1, keys), 1)
    if not causal:
        return jnp.where(place < length, 0.0, masked_score)
    place = lax.broadcasted_iota(jnp.int32, (rows, keys), 1)
    row = first_row + lax.broadcasted_iota(jnp.int32, (rows, keys), 0)
    return jnp.where((place < length) & (place <= row), 0.0, masked_score)


def attend_chunk(tick, first_row, length, causal, q_ref, kv_ref, w_ref, attended_out, totals_out, part_out):
    width = q_ref.shape[1]
    keys = kv_ref.shape[0]
    at = pl.ds(first_row, CHUNK)
    bias = key_bias(keys, length, first_row, causal, CHUNK)
    lane = lax.broadcasted_iota(jnp.int32, (CHUNK, 128), 1)
    totals = jnp.zeros((CHUNK, 128), wide)
    for begin in range(0, width, 128):
        tick(begin // 128)
        pair = q_ref[at, begin : begin + 128]
        key_pair = kv_ref[:, begin : begin + 128]
        value_pair = kv_ref[:, width + begin : width + begin + 128]
        results = []
        for head in range(2):
            scores = dot_nt(one_head(pair, head), key_pair) + bias
            peak = jnp.max(scores, axis=-1, keepdims=True)
            weights = jnp.exp(scores - peak)
            total = jnp.sum(weights, axis=-1, keepdims=True)
            results.append(dot_nn(weights.astype(low), value_pair) * (1.0 / total))
            totals = jnp.where(lane == begin // 64 + head, peak + jnp.log(total), totals)
        attended_out[at, begin : begin + 128] = jnp.where(
            lane < 64, results[0], results[1]
        ).astype(low)
    totals_out[at, :] = totals
    part_out[at, :] = dot_nt(attended_out[at, :], w_ref[:, 3 * width :]).astype(low)


def self_attention_kernel(
    rows_norm, causal, ticks, length_ref, x_ref, w_ref, vec_ref, normed_out, q_out, kv_out, attended_out, totals_out, part_out
):
    width = w_ref.shape[1] // 4
    gain = vec_ref[rows_norm : rows_norm + 1, :]
    shift = vec_ref[rows_norm + 1 : rows_norm + 2, :]
    steps = x_ref.shape[0] // CHUNK
    pairs = width // 128
    ticks.begin(steps * (pairs + 1))

    @pl.loop(0, steps)
    def _(step):
        ticks.in_loop(step, steps, 0, 1, 0)
        at = pl.ds(pl.multiple_of(step * CHUNK, CHUNK), CHUNK)
        normed = (centre_rows(x_ref[at, :].astype(wide)) * gain + shift).astype(low)
        normed_out[at, :] = normed
        q_out[at, :] = (dot_nn(normed, w_ref[:, :width]).astype(low).astype(wide) * 0.125).astype(low)
        kv_out[at, :] = dot_nn(normed, w_ref[:, width : 3 * width]).astype(low)

    length = length_ref[0]

    @pl.loop(0, steps)
    def _(step):
        attend_chunk(
            functools.partial(ticks.in_loop, step, steps, steps, pairs),
            pl.multiple_of(step * CHUNK, CHUNK), length, causal, q_out, kv_out, w_ref, attended_out, totals_out, part_out
        )


def self_attention_call(rows_norm, causal, length, x, weights, vectors, rider=None):
    rows, depth = x.shape
    width = weights[1] // 4
    return ride_call(
        functools.partial(self_attention_kernel, rows_norm, causal),
        [length, x, weights[0], vectors],
        [scalar(), whole(), weight_spec(weights), whole()],
        [
            shaped(rows, depth, low),
            shaped(rows, width, low),
            shaped(rows, 2 * width, low),
            shaped(rows, width, low),
            shaped(rows, 128, wide),
            shaped(rows, depth, low),
        ],
        [],
        rider,
        "self_attention",
    )


def cross_attention_kernel(
    ticks, length_ref, x_ref, own_ref, other_ref, mid_ref, mid_own, mid_other, w_ref, vec_ref,
    x_out, final_out, memory_out, normed_out, q_out, kv_out, attended_out, totals_out, part_out,
):
    width = w_ref.shape[1] // 4
    first_steps = mid_ref.shape[0] // CHUNK
    steps = x_ref.shape[0] // CHUNK
    pairs = width // 128
    ticks.begin(first_steps + steps * (pairs + 1))

    @pl.loop(0, first_steps)
    def _(step):
        ticks.in_loop(step, first_steps, 0, 1, 0)
        at = pl.ds(pl.multiple_of(step * CHUNK, CHUNK), CHUNK)
        x = mid_ref[at, :] + (mid_own[at, :].astype(wide) + mid_other[at, :].astype(wide))
        final_out[at, :] = x
        memory = (centre_rows(x) * vec_ref[4:5, :] + vec_ref[5:6, :]).astype(low)
        memory_out[at, :] = memory
        kv_out[at, :] = dot_nn(memory, w_ref[:, width : 3 * width]).astype(low)

    @pl.loop(0, steps)
    def _(step):
        ticks.in_loop(step, steps, first_steps, 1, 0)
        at = pl.ds(pl.multiple_of(step * CHUNK, CHUNK), CHUNK)
        x = x_ref[at, :].astype(wide) + (own_ref[at, :].astype(wide) + other_ref[at, :].astype(wide))
        x_out[at, :] = x
        normed = (centre_rows(x) * vec_ref[8:9, :] + vec_ref[9:10, :]).astype(low)
        normed_out[at, :] = normed
        q_out[at, :] = (dot_nn(normed, w_ref[:, :width]).astype(low).astype(wide) * 0.125).astype(low)

    length = length_ref[0]

    @pl.loop(0, steps)
    def _(step):
        attend_chunk(
            functools.partial(ticks.in_loop, step, steps, first_steps + steps, pairs),
            pl.multiple_of(step * CHUNK, CHUNK), length, False, q_out, kv_out, w_ref, attended_out, totals_out, part_out
        )


def cross_attention_call(length, x, own, other, mid, mid_own, mid_other, weights, vectors, rider=None):
    rows, depth = x.shape
    keys = mid.shape[0]
    width = weights[1] // 4
    return ride_call(
        cross_attention_kernel,
        [length, x, own, other, mid, mid_own, mid_other, weights[0], vectors],
        [scalar()] + [whole()] * 6 + [weight_spec(weights), whole()],
        [
            shaped(rows, depth, wide),
            shaped(keys, depth, wide),
            shaped(keys, depth, low),
            shaped(rows, depth, low),
            shaped(rows, width, low),
            shaped(keys, 2 * width, low),
            shaped(rows, width, low),
            shaped(rows, 128, wide),
            shaped(rows, depth, low),
        ],
        [],
        rider,
        "cross_attention",
    )


def attention_backward_kernel(
    causal, cross, norm_row, ticks, length_ref, previous_ref, x_ref, own_ref, other_ref, vec_ref,
    normed_ref, source_ref, q_ref, kv_ref, attended_ref, totals_ref, w_ref, *rest
):
    outs = 5 if cross else 4
    part_out, g_out, vec_out, grad_out = rest[:4]
    source_part_out = rest[4] if cross else None
    low_ref, grad_q, grad_kv, turned_k, turned_v, turned_low, turned_normed = rest[outs : outs + 7]
    turned_source = rest[outs + 7] if cross else turned_normed
    rows, depth = x_ref.shape
    keys = kv_ref.shape[0]
    width = q_ref.shape[1]
    length = length_ref[0]
    steps = rows // CHUNK
    pairs = width // 128
    key_steps = keys // CHUNK
    after = 1 + steps * pairs
    last = after + key_steps
    ticks.begin(last + 5)
    residual_prologue(norm_row, previous_ref, x_ref, own_ref, other_ref, vec_ref, g_out, low_ref, vec_out)
    ticks(0)
    turned_k[...] = jnp.zeros_like(turned_k)
    turned_v[...] = jnp.zeros_like(turned_v)

    @pl.loop(0, rows // CHUNK)
    def _(step):
        first_row = pl.multiple_of(step * CHUNK, CHUNK)
        at = pl.ds(first_row, CHUNK)
        grad_attended = dot_nn(low_ref[at, :], w_ref[:, 3 * width :]).astype(low)
        bias = key_bias(keys, length, first_row, causal, CHUNK)
        lane = lax.broadcasted_iota(jnp.int32, (CHUNK, 128), 1)
        totals = totals_ref[at, :]
        for begin in range(0, width, 128):
            ticks.in_loop(step, steps, 1, pairs, begin // 128)
            pair = q_ref[at, begin : begin + 128]
            key_pair = kv_ref[:, begin : begin + 128]
            value_pair = kv_ref[:, width + begin : width + begin + 128]
            grad_pair = grad_attended[:, begin : begin + 128]
            pair_turned = turned(pair)
            grad_turned = turned(grad_pair)
            results = []
            for head in range(2):
                number = begin // 64 + head
                total = jnp.sum(jnp.where(lane == number, totals, 0.0), axis=-1, keepdims=True)
                scores = dot_nt(one_head(pair, head), key_pair) + bias
                weights = jnp.exp(scores - total)
                grad_weights = dot_nt(one_head(grad_pair, head), value_pair)
                row_dot = jnp.sum(weights * grad_weights, axis=-1, keepdims=True)
                grad_scores = (weights * (grad_weights - row_dot)).astype(low)
                results.append(dot_nn(grad_scores, key_pair))
                span = slice(begin + 64 * head, begin + 64 * head + 64)
                local = slice(64 * head, 64 * head + 64)
                turned_k[span, :] += dot_nn(pair_turned[local, :], grad_scores)
                turned_v[span, :] += dot_nn(grad_turned[local, :], weights.astype(low))
            grad_q[at, begin : begin + 128] = (
                jnp.where(lane < 64, results[0], results[1]) * 0.125
            ).astype(low)
        if cross:
            part_out[at, :] = dot_nt(grad_q[at, :], w_ref[:, :width]).astype(low)

    grad_kv[:, :width] = turned(turned_k[...].astype(low))
    grad_kv[:, width:] = turned(turned_v[...].astype(low))

    @pl.loop(0, keys // CHUNK)
    def _(step):
        ticks.in_loop(step, key_steps, after, 1, 0)
        at = pl.ds(pl.multiple_of(step * CHUNK, CHUNK), CHUNK)
        from_source = dot_nt(grad_kv[at, :], w_ref[:, width : 3 * width])
        if cross:
            source_part_out[at, :] = from_source.astype(low)
        else:
            from_query = dot_nt(grad_q[at, :], w_ref[:, :width])
            part_out[at, :] = (from_source + from_query).astype(low)

    ticks(last)
    turn_into(turned_low, low_ref)
    turn_into(turned_normed, normed_ref)
    if cross:
        turn_into(turned_source, source_ref)
    ticks(last + 1)
    grad_out[:, :width] = dot_nn(turned_normed[...], grad_q[...]).astype(low)
    ticks(last + 2)
    grad_out[:, width : 2 * width] = dot_nn(turned_source[...], grad_kv[:, :width]).astype(low)
    ticks(last + 3)
    grad_out[:, 2 * width : 3 * width] = dot_nn(turned_source[...], grad_kv[:, width:]).astype(low)
    ticks(last + 4)
    grad_out[:, 3 * width :] = dot_nn(turned_low[...], attended_ref[...]).astype(low)


def attention_backward_call(
    causal, norm_row, length, previous, x, own, other, vectors, normed, source, q, kv, attended, totals, weights,
    rider=None,
):
    cross = source is not None
    rows, depth = x.shape
    keys = kv.shape[0]
    width = q.shape[1]
    outs = [
        shaped(rows, depth, low),
        shaped(rows, depth, wide),
        shaped(2, depth, wide),
        shaped(depth, 4 * width, low),
    ]
    if cross:
        outs.append(shaped(keys, depth, low))
    scratch = [
        pltpu.VMEM((rows, depth), low),
        pltpu.VMEM((rows, width), low),
        pltpu.VMEM((keys, 2 * width), low),
        pltpu.VMEM((width, keys), wide),
        pltpu.VMEM((width, keys), wide),
        pltpu.VMEM((depth, rows), low),
        pltpu.VMEM((depth, rows), low),
    ]
    if cross:
        scratch.append(pltpu.VMEM((depth, keys), low))
    operands = [length, previous, x, own, other, vectors, normed]
    if cross:
        operands.append(source)
    operands += [q, kv, attended, totals, weights[0]]

    def body(ticks, *refs):
        if not cross:
            refs = refs[:7] + (None,) + refs[7:]
        attention_backward_kernel(causal, cross, norm_row, ticks, *refs)

    return ride_call(
        body,
        operands,
        [scalar()] + [whole()] * (len(operands) - 2) + [weight_spec(weights)],
        outs,
        scratch,
        rider,
        "attention_backward",
    )


def finish_kernel(norm_row, previous_ref, x_ref, own_ref, other_ref, vec_ref, g_out, vec_out):
    residual_prologue(norm_row, previous_ref, x_ref, own_ref, other_ref, vec_ref, g_out, None, vec_out)


def finish_call(norm_row, previous, x, own, other, vectors):
    rows, depth = x.shape
    return pl.pallas_call(
        functools.partial(finish_kernel, norm_row),
        out_shape=(shaped(rows, depth, wide), shaped(2, depth, wide)),
        compiler_params=pltpu.CompilerParams(vmem_limit_bytes=40 << 20),
        name="finish_norm",
    )(previous, x, own, other, vectors)


def fits_kernels():
    return lax.axis_size("z") == 4


def factored_step(weights, grads, rows_next, columns_next, row_level, mean_square):
    estimate = rows_next[:, :, None] * columns_next[:, None, :] / row_level[:, None, None]
    return weights - step_rate * jnp.sqrt(mean_square)[:, None, None] * grads * lax.rsqrt(estimate)


def on_device(
    source_embed,
    target_embed,
    out_cotangent,
    row_flags,
    source_mask,
    target_mask,
    attention_weights,
    feed_weights,
    rows_attention,
    columns_attention,
    rows_feed,
    columns_feed,
    vector_params,
    vector_moments,
):
    core = lax.axis_index("c")
    local_rows, half_width = attention_weights.shape[1:]
    half_units = feed_weights.shape[2]
    depth = vector_params.shape[1]
    units_all = 2 * half_units

    def attention_group(block):
        part = attention_weights[4 * block : 4 * block + 4].astype(low)
        return part.transpose(1, 0, 2).reshape(local_rows, 4 * half_width)

    def feed_group(index):
        part = feed_weights[2 * index : 2 * index + 2].astype(low)
        return part.transpose(1, 0, 2).reshape(local_rows, 2 * half_units)

    source_half = swap_chips(source_embed[0])
    flags_half = swap_chips(row_flags[0])
    source_all = both_halves(source_half)
    flags_all = both_halves(flags_half)
    masks = swap_chips(jnp.concatenate([source_mask[0], target_mask[0]]))
    source_length = jnp.sum(masks[: source_mask.shape[1]]).reshape(1)
    target_length = jnp.sum(masks[source_mask.shape[1] :]).reshape(1)
    target_all = both_halves(swap_chips(target_embed[0]))
    cotangent_all = both_halves(swap_chips(out_cotangent[0]))

    attention_width, feed_width = 4 * half_width, 2 * half_units
    fits = fits_kernels()

    def flat(gathered):
        return gathered.reshape(-1, gathered.shape[-1])

    def ride(kind, operand, number):
        return Rider(kind, operand, number) if fits else None

    own_groups = [attention_group(0), attention_group(1), attention_group(2), feed_group(0), feed_group(1)]
    if fits:
        encoder_attention = (flat(gather_all(own_groups[0], 0)), attention_width)
    else:
        (encoder_attention, decoder_attention, cross_attention, encoder_feed, decoder_feed) = [
            (gather_weights(group, "zyx"), group.shape[1]) for group in own_groups
        ]

    start_rows = jnp.where(
        (flags_all == 1)[:, None],
        vector_params[12][None, :],
        jnp.where((flags_all == 2)[:, None], vector_params[13][None, :], source_all.astype(wide)),
    )
    first_kept = self_attention_call(
        0, False, source_length, start_rows, encoder_attention, vector_params,
        ride("gather", own_groups[3], 1),
    )
    if fits:
        encoder_feed = (flat(first_kept[6]), feed_width)
    first_part = first_kept[5]
    first_other = other_core(first_part)
    encoder_mid, second_normed, second_hidden, second_slope, second_part, *rest = feed_forward_call(
        2, start_rows, first_part, first_other, encoder_feed, vector_params,
        ride("gather", jnp.concatenate(own_groups[1:3], axis=1), 2),
    )
    if fits:
        decoder_attention = (flat(rest[0])[:, :attention_width], attention_width)
        cross_attention = (flat(rest[0])[:, attention_width:], attention_width)
    second_other = other_core(second_part)
    third_kept = self_attention_call(6, True, target_length, target_all, decoder_attention, vector_params)
    third_part = third_kept[5]
    third_other = other_core(third_part)
    decoder_one, encoder_final, memory_rows, *fourth_kept = cross_attention_call(
        source_length,
        target_all,
        third_part,
        third_other,
        encoder_mid,
        second_part,
        second_other,
        cross_attention,
        vector_params,
        ride("gather", own_groups[4], 3),
    )
    if fits:
        decoder_feed = (flat(fourth_kept[6]), feed_width)
    fourth_part = fourth_kept[5]
    fourth_kept = fourth_kept[:5]
    decoder_two, fifth_normed, fifth_hidden, fifth_slope, fifth_part = feed_forward_call(
        10, decoder_one, fourth_part, other_core(fourth_part), decoder_feed, vector_params
    )
    decoder_three = decoder_two + (fifth_part.astype(wide) + other_core(fifth_part).astype(wide))

    def own_half(rows):
        half = rows.shape[0] // 2
        return lax.dynamic_slice_in_dim(rows, core * half, half, 0)

    decoder_out = swap_chips(own_half(decoder_three).astype(low))

    fifth_back, decoder_feed_terms, grad_three = last_feed_backward_call(
        target_length, cotangent_all, fifth_normed, fifth_hidden, fifth_slope, decoder_feed
    )
    query_back, grad_two, vectors_ten, cross_terms, memory_back, *decoder_feed_grad = attention_backward_call(
        False,
        10,
        source_length,
        grad_three,
        decoder_two,
        fifth_back,
        other_core(fifth_back),
        vector_params,
        fourth_kept[0],
        memory_rows,
        *fourth_kept[1:],
        cross_attention,
        ride("scatter", decoder_feed_terms, 4),
    )
    query_other = other_core(query_back)
    memory_other = other_core(memory_back)
    third_back, grad_one, vectors_eight, decoder_terms, *cross_grad = attention_backward_call(
        True,
        8,
        target_length,
        grad_two,
        decoder_one,
        query_back,
        query_other,
        vector_params,
        third_kept[0],
        None,
        *third_kept[1:5],
        decoder_attention,
        ride("scatter", cross_terms, 5),
    )
    third_back_other = other_core(third_back)
    second_back, encoder_feed_terms, grad_final, vectors_four, *decoder_grad = feed_backward_call(
        4,
        encoder_final,
        memory_back,
        memory_other,
        vector_params,
        second_normed,
        second_hidden,
        second_slope,
        encoder_feed,
        ride("scatter", decoder_terms, 6),
    )
    first_back, grad_mid, vectors_two, encoder_terms, *encoder_feed_grad = attention_backward_call(
        False,
        2,
        source_length,
        grad_final,
        encoder_mid,
        second_back,
        other_core(second_back),
        vector_params,
        first_kept[0],
        None,
        *first_kept[1:5],
        encoder_attention,
        ride("scatter", encoder_feed_terms, 7),
    )
    grad_target, vectors_six = finish_call(
        6, grad_one, target_all, third_back, third_back_other, vector_params
    )
    target_grad = swap_chips(own_half(grad_target).astype(low)).astype(wide)
    grad_start, vectors_zero = finish_call(
        0, grad_mid, start_rows, first_back, other_core(first_back), vector_params
    )
    gap_rows = jnp.sum(jnp.where((flags_all == 1)[:, None], grad_start, 0.0), axis=0, keepdims=True)
    mask_rows = jnp.sum(jnp.where((flags_all == 2)[:, None], grad_start, 0.0), axis=0, keepdims=True)
    source_grad = swap_chips(own_half(grad_start).astype(low)).astype(wide)
    source_grad = jnp.where((row_flags[0] == 0)[:, None], source_grad, 0.0)

    vector_terms = jnp.concatenate(
        [
            vectors_zero,
            vectors_two,
            vectors_four,
            vectors_six,
            vectors_eight,
            vectors_ten,
            gap_rows,
            mask_rows,
            jnp.zeros((114, depth), wide),
        ],
        axis=0,
    )
    vector_terms = vector_terms.T.astype(low)
    if fits:
        (decoder_feed_grad,), (cross_grad,), (decoder_grad,), (encoder_feed_grad,) = (
            decoder_feed_grad, cross_grad, decoder_grad, encoder_feed_grad
        )
        last_grads = scatter_all([encoder_terms, vector_terms], 8)
        encoder_grad, vector_grad = last_grads[:, :attention_width], last_grads[:, attention_width:]
    else:
        (encoder_grad, decoder_grad, cross_grad, encoder_feed_grad, decoder_feed_grad, vector_grad) = [
            scatter_gradient(terms, "xyz")
            for terms in (
                encoder_terms, decoder_terms, cross_terms, encoder_feed_terms, decoder_feed_terms, vector_terms
            )
        ]
    vector_grad = vector_grad[:, :14].T

    def as_matrices(rows, count):
        return rows.reshape(local_rows, count, -1).transpose(1, 0, 2)

    attention_grad = jnp.concatenate(
        [as_matrices(part, 4) for part in (encoder_grad, decoder_grad, cross_grad)], axis=0
    )
    feed_grad = jnp.concatenate(
        [as_matrices(part, 2) for part in (encoder_feed_grad, decoder_feed_grad)], axis=0
    )

    weight_squares = jnp.concatenate(
        [
            jnp.sum(attention_weights * attention_weights, axis=(1, 2)),
            jnp.sum(feed_weights * feed_weights, axis=(1, 2)),
            jnp.sum(rows_attention, axis=1) * 0.5,
            jnp.sum(rows_feed, axis=1) * 0.5,
        ]
    )
    early_sums = data_sum(tensor_sum(weight_squares))
    scale_attention, scale_feed = early_sums[:12], early_sums[12:16]
    rows_total_attention, rows_total_feed = early_sums[16:28], early_sums[28:32]
    attention_square = attention_grad * attention_grad
    feed_square = feed_grad * feed_grad
    row_sums = tensor_sum(
        jnp.concatenate([jnp.sum(attention_square, axis=2), jnp.sum(feed_square, axis=2)], axis=0)
    )
    column_attention = jnp.sum(attention_square, axis=1)
    column_feed = jnp.sum(feed_square, axis=1)
    square_totals = jnp.sum(row_sums, axis=1)
    column_sums = data_sum(
        jnp.concatenate([column_attention.reshape(-1), column_feed.reshape(-1), square_totals])
    )
    column_attention = column_sums[: column_attention.size].reshape(column_attention.shape)
    column_feed = column_sums[column_attention.size : -16].reshape(column_feed.shape)
    square_totals = column_sums[-16:]
    keep, take = decay_rate, 1.0 - decay_rate
    rows_attention_next = keep * rows_attention + take * row_sums[:12] / depth
    rows_feed_next = keep * rows_feed + take * row_sums[12:] / units_all
    total_attention = keep * rows_total_attention + take * square_totals[:12] / depth
    total_feed = keep * rows_total_feed + take * square_totals[12:] / units_all
    columns_attention_next = keep * columns_attention + take * column_attention / depth
    columns_feed_next = keep * columns_feed + take * column_feed / depth
    attention_updated = factored_step(
        attention_weights,
        attention_grad,
        rows_attention_next,
        columns_attention_next,
        total_attention / depth,
        scale_attention / (depth * depth),
    )
    feed_updated = factored_step(
        feed_weights,
        feed_grad,
        rows_feed_next,
        columns_feed_next,
        total_feed / depth,
        scale_feed / (depth * units_all),
    )
    local_width = vector_moments.shape[1]
    place = (lax.axis_index("z") * lax.axis_size("y") + lax.axis_index("y")) * 2 + core
    vector_local = lax.dynamic_slice_in_dim(vector_params, place * local_width, local_width, 1)
    vector_moments_next = keep * vector_moments + take * vector_grad * vector_grad
    vector_scale = jnp.sqrt(jnp.mean(vector_params * vector_params, axis=1))
    vector_updated = vector_local - step_rate * vector_scale[:, None] * vector_grad * lax.rsqrt(
        vector_moments_next
    )
    return (
        decoder_out[None],
        source_grad[None],
        target_grad[None],
        attention_grad,
        feed_grad,
        vector_grad,
        attention_updated,
        feed_updated,
        vector_updated,
        rows_attention_next,
        columns_attention_next,
        rows_feed_next,
        columns_feed_next,
        vector_moments_next,
        vector_grad[10:12],
    )


def solution(mesh):
    groups = mesh.shape["dp"] // 4
    inner = Mesh(mesh.devices.reshape(groups, 2, 2, 2), ("z", "y", "c", "x"))
    data = ("z", "y", "c")
    rows3, rows2 = P(data, "x", None), P(data, "x")
    matrix, row_spec, column_spec = P(None, data, "x"), P(None, data), P(None, "x")
    return jax.shard_map(
        on_device,
        mesh=inner,
        in_specs=(
            rows3,
            rows3,
            rows3,
            rows2,
            P(data, None),
            P(data, None),
            matrix,
            matrix,
            row_spec,
            column_spec,
            row_spec,
            column_spec,
            P(),
            row_spec,
        ),
        out_specs=(
            rows3,
            rows3,
            rows3,
            matrix,
            matrix,
            row_spec,
            matrix,
            matrix,
            row_spec,
            row_spec,
            column_spec,
            row_spec,
            column_spec,
            row_spec,
            row_spec,
        ),
        check_vma=False,
    )
```

```python
import functools

import jax
import jax.numpy as jnp
from jax import lax
from jax.experimental import pallas as pl
from jax.experimental.pallas import tpu as pltpu
from jax.sharding import Mesh
from jax.sharding import PartitionSpec as P

HEAD_DIM = 64
CHUNK = 256
norm_epsilon = 1e-05
decay_rate = 1.0 - 2.0 ** (-0.8)
step_rate = 0.2
masked_score = -1e30
low = jnp.bfloat16
wide = jnp.float32
MESH = pl.DeviceIdType.MESH


def swap_chips(array):
    return lax.ppermute(array, ("c", "x"), [(0, 0), (1, 2), (2, 1), (3, 3)])


def other_core(array):
    return lax.ppermute(array, "c", [(0, 1), (1, 0)])


def both_halves(own_half):
    received = other_core(own_half)
    first = lax.axis_index("c") == 0
    return jnp.concatenate(
        [jnp.where(first, own_half, received), jnp.where(first, received, own_half)], axis=0
    )


def core_sum(partial_rows):
    sent = partial_rows.astype(low)
    return sent.astype(wide) + other_core(sent).astype(wide)


def ring_next(array):
    size = lax.axis_size("z")
    return lax.ppermute(array, "z", [(i, (i + 1) % size) for i in range(size)])


def holds():
    return lax.axis_index("c") == lax.axis_index("x")


def spread_blocks(blocks, order):
    held = blocks[None, None]
    for axis in order:
        if axis == "x":
            received = lax.ppermute(held, ("c", "x"), [(0, 1), (3, 2)])
            held = jnp.where(holds(), held, received)
        elif axis == "y":
            received = lax.ppermute(held, "y", [(0, 1), (1, 0)])
            first = lax.axis_index("y") == 0
            held = jnp.concatenate(
                [jnp.where(first, held, received), jnp.where(first, received, held)], axis=1
            )
        else:
            size = lax.axis_size("z")
            if size != 4:
                held = lax.all_gather(held, "z", axis=0, tiled=True)
                continue
            place = lax.axis_index("z")
            whole = jnp.zeros((size,) + held.shape[1:], held.dtype)
            moving = held
            for step in range(size):
                where_from = lax.rem(place + size - step, size)
                whole = lax.dynamic_update_slice_in_dim(whole, moving, where_from, 0)
                if step < size - 1:
                    moving = ring_next(moving)
            held = whole
    return held


def reduce_blocks(parts, order):
    held = parts
    for position, axis in enumerate(order):
        final = position == len(order) - 1
        kind = wide if final else low
        if axis == "x":
            received = lax.ppermute(held, ("c", "x"), [(1, 0), (2, 3)])
            held = (held.astype(wide) + received.astype(wide)).astype(kind)
        elif axis == "y":
            mine = lax.axis_index("y")
            sent = lax.dynamic_slice_in_dim(held, 1 - mine, 1, 1)
            kept = lax.dynamic_slice_in_dim(held, mine, 1, 1)
            received = lax.ppermute(sent, "y", [(0, 1), (1, 0)])
            held = (kept.astype(wide) + received.astype(wide)).astype(kind)
        else:
            size = lax.axis_size("z")
            if size != 4:
                held = lax.psum_scatter(held, "z", scatter_dimension=0, tiled=True).astype(kind)
                continue
            place = lax.axis_index("z")
            moving = lax.dynamic_slice_in_dim(held, lax.rem(place + size - 1, size), 1, 0)
            for step in range(1, size):
                received = ring_next(moving)
                kept = lax.dynamic_slice_in_dim(held, lax.rem(place + size - 1 - step, size), 1, 0)
                last = step == size - 1
                moving = (kept.astype(wide) + received.astype(wide)).astype(kind if last else low)
            held = moving
    return held[0, 0]


def gather_weights(blocks, order):
    received = lax.ppermute(blocks, ("c", "x"), [(2, 0), (1, 3)])
    first = lax.axis_index("c") == 0
    both = jnp.concatenate(
        [jnp.where(first, blocks, received), jnp.where(first, received, blocks)], axis=0
    )
    spread = spread_blocks(both, order)
    return spread.reshape(-1, spread.shape[-1])


def scatter_gradient(gradient, order):
    depth, columns = gradient.shape
    z_size, y_size = lax.axis_size("z"), lax.axis_size("y")
    rows = depth // (z_size * y_size)
    total = reduce_blocks(gradient.astype(low).reshape(z_size, y_size, rows, columns), order)
    core = lax.axis_index("c")
    half = rows // 2
    kept = lax.dynamic_slice_in_dim(total, core * half, half, 0)
    sent = lax.dynamic_slice_in_dim(total, (1 - core) * half, half, 0)
    received = lax.ppermute(sent, ("c", "x"), [(0, 2), (3, 1)])
    return jnp.where(holds(), kept, received)


def data_sum(values):
    values = values + other_core(values)
    if lax.axis_size("z") != 4:
        return lax.psum(values, ("z", "y"))
    values = values + lax.ppermute(values, "y", [(0, 1), (1, 0)])
    values = values + lax.ppermute(values, "z", [(0, 1), (1, 0), (2, 3), (3, 2)])
    return values + lax.ppermute(values, "z", [(0, 2), (2, 0), (1, 3), (3, 1)])


def tensor_sum(values):
    return values + lax.ppermute(values, "x", [(0, 1), (1, 0)])


def column_cuts(columns):
    tiles = columns // 128
    first = (tiles * 42 + 50) // 100
    second = (tiles * 36 + 50) // 100
    edges = [0, first * 128, (first + second) * 128, columns]
    return list(zip(edges[:-1], edges[1:]))


def gather_cuts(columns):
    tiles = columns // 128
    first = (tiles * 38 + 50) // 100
    second = (tiles * 39 + 50) // 100
    edges = [0, first * 128, (first + second) * 128, columns]
    return list(zip(edges[:-1], edges[1:]))


def place(name):
    return lax.axis_index(name)


def block_at(which):
    back, same = which
    z = lax.rem(place("z") + 4 - back, 4)
    return z * 2 + (place("y") if same else 1 - place("y"))


def target_of(axis):
    if axis == "z":
        return {"z": lax.rem(place("z") + 1, 4)}
    if axis == "z_back":
        return {"z": lax.rem(place("z") + 3, 4)}
    if axis == "x_home":
        return {"c": place("x"), "x": 1 - place("x")}
    return {axis: 1 - place(axis)}


def greet():
    barrier = pltpu.get_barrier_semaphore()
    targets = [target_of(axis) for axis in ("c", "y", "z", "z_back", "x")]
    targets.append({"c": 1 - place("c"), "x": 1 - place("x")})
    for target in targets:
        pl.semaphore_signal(barrier, inc=1, device_id=target, device_id_type=MESH)
    pl.semaphore_wait(barrier, len(targets))


class Part:
    def __init__(self, array, first):
        self.array, self.first = array, first
        self.at = self

    def __getitem__(self, index):
        return self.array.at[self.first + index]


def here(back):
    return (back, True)


def there(back):
    return (back, False)


class Mover:
    def __init__(self, send_sems):
        self.steps = {True: [], False: []}
        self.sent = {True: [], False: []}
        self.done = 0
        self.send_sems = send_sems

    def send(self, home, source, target, recv_sem, device):
        number = len(self.sent[home])

        def copy():
            return pltpu.make_async_remote_copy(
                src_ref=source(),
                dst_ref=target(),
                send_sem=self.send_sems.at[number],
                recv_sem=recv_sem(),
                device_id=device(),
                device_id_type=MESH,
            )

        self.sent[home].append(copy)
        self.steps[home].append(lambda: copy().start())

    def wait(self, home, target, recv_sem):
        def step():
            pltpu.make_async_remote_copy(
                src_ref=target(),
                dst_ref=target(),
                send_sem=self.send_sems.at[0],
                recv_sem=recv_sem(),
                device_id=target_of("c"),
                device_id_type=MESH,
            ).wait_recv()

        self.steps[home].append(step)

    def local(self, home, step):
        self.steps[home].append(step)

    def run(self, part, parts):
        for home in (True, False):
            steps = self.steps[home]
            chosen = steps[len(steps) * part // parts : len(steps) * (part + 1) // parts]
            if not chosen:
                continue
            wanted = place("c") == place("x")

            @pl.when(wanted if home else jnp.logical_not(wanted))
            def _():
                for step in chosen:
                    step()

    def finish(self):
        for home in (True, False):
            wanted = place("c") == place("x")

            @pl.when(wanted if home else jnp.logical_not(wanted))
            def _():
                for copy in self.sent[home]:
                    copy().wait_send()


class Gather(Mover):
    def __init__(self, own_ref, out_ref, stage_ref, local_sem, send_sems, recv_sems):
        super().__init__(send_sems)
        rows, columns = own_ref.shape
        cuts = gather_cuts(columns)
        (begin_a, end_a), (begin_b, end_b), (begin_c, end_c) = cuts
        first, second, third = 0, 1, 2

        def out_piece(group, which, parity):
            begin, end = cuts[group]
            first_row = (block_at(which) * 2 + parity()) * rows
            return out_ref.at[pl.ds(first_row, rows), pl.ds(begin, end - begin)]

        def out_sem(group, which, parity):
            return recv_sems.at[(group * 8 + block_at(which)) * 2 + parity()]

        def stage_piece(group, which):
            begin, end = cuts[group]
            return stage_ref.at[block_at(which), :, pl.ds(begin, end - begin)]

        def stage_sem(group, which):
            return recv_sems.at[48 + group * 8 + block_at(which)]

        def core():
            return place("c")

        def other():
            return 1 - place("c")

        self_copies = {
            True: lambda: pltpu.make_async_copy(
                own_ref, out_ref.at[pl.ds((block_at(here(0)) * 2 + core()) * rows, rows), :], local_sem
            ),
        }

        def own_piece(group):
            begin, end = cuts[group]
            return own_ref.at[:, pl.ds(begin, end - begin)]

        for home in (True, False):
            arrived = set()

            def plane(group, which):
                if which == here(0):
                    return functools.partial(own_piece, group)
                if home:
                    return functools.partial(out_piece, group, which, core)
                return functools.partial(stage_piece, group, which)

            def plane_target(group, which):
                if home:
                    return (
                        functools.partial(out_piece, group, which, core),
                        functools.partial(out_sem, group, which, core),
                    )
                return (
                    functools.partial(stage_piece, group, which),
                    functools.partial(stage_sem, group, which),
                )

            def plane_send(group, which, axis):
                target, sem = plane_target(group, which)
                self.send(home, plane(group, which), target, sem, functools.partial(target_of, axis))

            def plane_wait(group, which):
                if which == here(0):
                    return
                target, sem = plane_target(group, which)
                self.wait(home, target, sem)
                if home:
                    arrived.add((group, which, "core"))

            def deliver(group, which):
                target = functools.partial(out_piece, group, which, core)
                sem = functools.partial(out_sem, group, which, core)
                source = plane(group, which)
                self.send(home, source, target, sem, functools.partial(target_of, "x_home"))
                if not home:
                    self.send(home, source, target, sem, functools.partial(target_of, "c"))

            def core_send(group, which, name, axis):
                parity = core if name == "core" else other
                if home and which == here(0) and name == "core":
                    source = functools.partial(own_piece, group)
                else:
                    source = functools.partial(out_piece, group, which, parity)
                self.send(
                    home,
                    source,
                    functools.partial(out_piece, group, which, parity),
                    functools.partial(out_sem, group, which, parity),
                    functools.partial(target_of, axis),
                )

            def core_wait(group, which, name):
                if home and which == here(0) and name == "core":
                    return
                if (group, which, name) in arrived:
                    return
                arrived.add((group, which, name))
                parity = core if name == "core" else other
                self.wait(
                    home,
                    functools.partial(out_piece, group, which, parity),
                    functools.partial(out_sem, group, which, parity),
                )

            if home:
                self.local(home, lambda: self_copies[True]().start())
            deliver(third, here(0))
            plane_send(first, here(0), "z")
            plane_send(second, here(0), "z")
            plane_send(first, here(0), "y")
            deliver(second, here(0))
            deliver(first, here(0))
            names = ("core", "other") if home else ("other", "core")
            for name in names:
                core_wait(third, here(0), name)
                core_send(third, here(0), name, "z")
                core_send(third, here(0), name, "y")
            for name in names:
                core_wait(second, here(0), name)
                core_send(second, here(0), name, "y")
            for back in (1, 2, 3):
                plane_wait(first, here(back))
                if back < 3:
                    plane_send(first, here(back), "z")
                plane_send(first, here(back), "y")
                plane_wait(second, here(back))
                if back < 3:
                    plane_send(second, here(back), "z")
                deliver(second, here(back))
                deliver(first, here(back))
                plane_wait(first, there(back - 1))
                deliver(first, there(back - 1))
                if back == 1:
                    for name in names:
                        core_wait(third, there(0), name)
                        core_send(third, there(0), name, "z")
                for which in (here(back), there(back)):
                    for name in names:
                        core_wait(third, which, name)
                        if back < 3:
                            core_send(third, which, name, "z")
                for name in names:
                    core_wait(second, here(back), name)
                    core_send(second, here(back), name, "y")
            plane_wait(first, there(3))
            deliver(first, there(3))
            for group in (third, second, first):
                for back in range(4):
                    for which in (here(back), there(back)):
                        for name in ("core", "other"):
                            core_wait(group, which, name)
            if home:
                self.local(home, lambda: self_copies[True]().wait())


GATHER_SENDS = 64


class Scatter(Mover):
    def __init__(self, buffers, final, send_sems, recv_sems):
        super().__init__(send_sems)
        total, stages, x_ins, z_ins = buffers[0], buffers[1:4], buffers[4:7], buffers[7:9]
        ya_in, yb_in, zc_in, yc_in = buffers[9:]
        rows = total.shape[1] // 2
        columns = total.shape[2]
        cuts = column_cuts(columns)
        first, second, third = 0, 1, 2
        widths = [end - begin for begin, end in cuts]

        def part(group):
            begin, end = cuts[group]
            return pl.ds(begin, end - begin)

        def core_piece(group, which, parity=None):
            if parity is None:
                return total.at[block_at(which), :, part(group)]
            return total.at[block_at(which), pl.ds(parity() * rows, rows), part(group)]

        def slot_of(which):
            return which[0] + (0 if which[1] else 4)

        def x_piece(group, which):
            return x_ins[group].at[slot_of(which)]

        def stage_piece(group, which):
            return stages[group].at[slot_of(which)]

        def sem(number):
            return lambda: recv_sems.at[number]

        def core():
            return place("c")

        def other():
            return 1 - place("c")

        def add_rows(held_of, came_of, count, final_part=None):
            def step():
                held, came = held_of(), came_of()

                @pl.loop(0, count // 16)
                def _(number):
                    at = pl.ds(pl.multiple_of(number * 16, 16), 16)
                    if final_part is None:
                        held[at, :] = held[at, :] + came[at, :]
                    else:
                        final[at, final_part] = held[at, :].astype(wide) + came[at, :].astype(wide)

            return step

        for home in (True, False):

            def plane(group, which):
                if home:
                    return functools.partial(core_piece, group, which, core)
                return functools.partial(stage_piece, group, which)

            def x_sends(group, which):
                if widths[group] == 0:
                    return
                number = group * 8 + slot_of(which)
                if home:
                    self.send(
                        home,
                        functools.partial(core_piece, group, which, other),
                        functools.partial(stage_piece, group, which),
                        sem(24 + number),
                        functools.partial(target_of, "c"),
                    )
                    return
                for parity in (0, 1):
                    self.send(
                        home,
                        functools.partial(core_piece, group, which, functools.partial(parity_value, parity)),
                        functools.partial(x_piece, group, which),
                        sem(number),
                        functools.partial(home_core, parity),
                    )

            def x_add(group, which, last=False):
                if widths[group] == 0:
                    return
                number = group * 8 + slot_of(which)
                if not home:
                    self.wait(home, functools.partial(stage_piece, group, which), sem(24 + number))
                self.wait(home, functools.partial(x_piece, group, which), sem(number))
                self.local(
                    home,
                    add_rows(
                        plane(group, which),
                        functools.partial(x_piece, group, which),
                        rows,
                        part(group) if last else None,
                    ),
                )

            def z_slot(group, back):
                return lambda: z_ins[group].at[back]

            def z_send(group, back):
                if widths[group] == 0:
                    return
                self.send(
                    home,
                    plane(group, here(back)),
                    z_slot(group, back - 1),
                    sem(60 + group * 4 + back - 1),
                    functools.partial(target_of, "z_back"),
                )

            def z_add(group, back):
                if widths[group] == 0:
                    return
                self.wait(home, z_slot(group, back), sem(60 + group * 4 + back))
                self.local(
                    home,
                    add_rows(
                        plane(group, here(back)),
                        z_slot(group, back),
                        rows,
                        part(group) if back == 0 else None,
                    ),
                )

            def ya_slot(back):
                return lambda: ya_in.at[back]

            def yb_slot(back):
                return lambda: yb_in.at[back]

            def zc_slot(which):
                back, same = which
                return lambda: zc_in.at[back + (0 if same else 3)]

            def zc_send(which):
                back, same = which
                self.send(
                    home,
                    functools.partial(core_piece, third, which),
                    zc_slot((back - 1, same)),
                    sem(72 + back - 1 + (0 if same else 3)),
                    functools.partial(target_of, "z_back"),
                )

            def zc_add(which):
                back, same = which
                self.wait(home, zc_slot(which), sem(72 + back + (0 if same else 3)))
                self.local(
                    home,
                    add_rows(functools.partial(core_piece, third, which), zc_slot(which), 2 * rows),
                )

            def second_steps(back):
                x_add(second, here(back))
                if back < 3:
                    z_add(second, back)
                if back > 0:
                    z_send(second, back)

            zc_send(there(3))
            zc_send(here(3))
            for back in (3, 2, 1, 0):
                if widths[second]:
                    self.send(
                        home,
                        functools.partial(core_piece, second, there(back)),
                        yb_slot(back),
                        sem(52 + back),
                        functools.partial(target_of, "y"),
                    )
                if back > 1:
                    x_sends(first, there(back))
                    x_sends(first, here(back))
            for back in (3, 2, 1, 0):
                if widths[second]:
                    self.wait(home, yb_slot(back), sem(52 + back))
                    self.local(
                        home,
                        add_rows(
                            functools.partial(core_piece, second, here(back)), yb_slot(back), 2 * rows
                        ),
                    )
                x_sends(second, here(back))
                if back > 1:
                    x_sends(first, there(back - 2))
                    x_sends(first, here(back - 2))
                if back < 3:
                    for which in (there(back), here(back)):
                        zc_add(which)
                        if back > 0:
                            zc_send(which)
                        elif not which[1]:
                            self.send(
                                home,
                                functools.partial(core_piece, third, there(0)),
                                lambda: yc_in.at[...],
                                sem(56),
                                functools.partial(target_of, "y"),
                            )
                x_add(first, there(back))
                if widths[first]:
                    self.send(
                        home,
                        plane(first, there(back)),
                        ya_slot(back),
                        sem(48 + back),
                        functools.partial(target_of, "y"),
                    )
                x_add(first, here(back))
                if back < 3:
                    second_steps(back + 1)
                if back == 0:
                    self.wait(home, lambda: yc_in.at[...], sem(56))
                    self.local(
                        home,
                        add_rows(
                            functools.partial(core_piece, third, here(0)),
                            lambda: yc_in.at[...],
                            2 * rows,
                        ),
                    )
                    x_sends(third, here(0))
                if widths[first]:
                    self.wait(home, ya_slot(back), sem(48 + back))
                    self.local(home, add_rows(plane(first, here(back)), ya_slot(back), rows))
                if back < 3:
                    z_add(first, back)
                if back > 0:
                    z_send(first, back)
            second_steps(0)
            x_add(third, here(0), last=True)


def parity_value(parity):
    return parity


def home_core(parity):
    return {"c": parity, "x": place("c")}


SCATTER_SENDS = 48


SCATTER_BUFFERS = 13


def scatter_buffers(rows, columns):
    first, second, third = [max(end - begin, 128) for begin, end in column_cuts(columns)]
    return [
        pltpu.VMEM((8, 2 * rows, columns), low),
        pltpu.VMEM((8, rows, first), low),
        pltpu.VMEM((4, rows, second), low),
        pltpu.VMEM((1, rows, third), low),
        pltpu.VMEM((8, rows, first), low),
        pltpu.VMEM((4, rows, second), low),
        pltpu.VMEM((1, rows, third), low),
        pltpu.VMEM((3, rows, first), low),
        pltpu.VMEM((3, rows, second), low),
        pltpu.VMEM((4, rows, first), low),
        pltpu.VMEM((4, 2 * rows, second), low),
        pltpu.VMEM((6, 2 * rows, third), low),
        pltpu.VMEM((2 * rows, third), low),
    ]

def ride_call(body, operands, in_specs, outs, scratch, rider, name):
    def kernel(*refs):
        body(Nothing(), *refs)

    return pl.pallas_call(
        kernel,
        out_shape=tuple(outs),
        in_specs=list(in_specs),
        scratch_shapes=list(scratch),
        compiler_params=pltpu.CompilerParams(vmem_limit_bytes=60 << 20),
        name=name,
    )(*operands)


def whole():
    return pl.BlockSpec(memory_space=pltpu.VMEM)


def weight_spec(weights):
    return pl.BlockSpec(memory_space=pltpu.VMEM)


def shaped(rows, columns, kind):
    return jax.ShapeDtypeStruct((rows, columns), kind)


def dot_nn(left, right):
    return lax.dot_general(left, right, (((1,), (0,)), ((), ())), preferred_element_type=wide)


def dot_nt(left, right):
    return lax.dot_general(left, right, (((1,), (1,)), ((), ())), preferred_element_type=wide)


def turned(block):
    size = block.shape[1]
    row = lax.broadcasted_iota(jnp.int32, (size, size), 0)
    column = lax.broadcasted_iota(jnp.int32, (size, size), 1)
    return dot_nt((row == column).astype(wide).astype(low), block).astype(low)


def turn_into(target, source):
    rows, columns = source.shape
    for at in range(0, columns, 256):
        wide_part = min(256, columns - at)
        target[at : at + wide_part, :] = turned(source[:, at : at + wide_part])


def centre_rows(values):
    centred = values - jnp.mean(values, axis=-1, keepdims=True)
    spread = jnp.mean(centred * centred, axis=-1, keepdims=True)
    return centred * lax.rsqrt(spread + norm_epsilon)


def norm_back(x, gain, grads):
    centred = x - jnp.mean(x, axis=-1, keepdims=True)
    scale = lax.rsqrt(jnp.mean(centred * centred, axis=-1, keepdims=True) + norm_epsilon)
    unit = centred * scale
    inner = grads * gain
    by_unit = inner * unit
    back = scale * (
        inner
        - jnp.mean(inner, axis=-1, keepdims=True)
        - unit * jnp.mean(by_unit, axis=-1, keepdims=True)
    )
    return back, jnp.sum(grads * unit, axis=0, keepdims=True), jnp.sum(grads, axis=0, keepdims=True)


def residual_prologue(norm_row, previous_ref, x_ref, own_ref, other_ref, vec_ref, grad_out, low_ref, vec_out, ticks=None):
    ticks = ticks or Nothing()
    steps = x_ref.shape[0] // CHUNK
    ticks.begin(steps)
    gain = vec_ref[norm_row : norm_row + 1, :]
    vec_out[...] = jnp.zeros_like(vec_out)

    @pl.loop(0, x_ref.shape[0] // CHUNK)
    def _(step):
        at = pl.ds(pl.multiple_of(step * CHUNK, CHUNK), CHUNK)
        ticks.in_loop(step, steps, 0, 1, 0)
        grads = own_ref[at, :].astype(wide) + other_ref[at, :].astype(wide)
        back, by_gain, by_shift = norm_back(x_ref[at, :].astype(wide), gain, grads)
        if previous_ref is not None:
            back = back + previous_ref[at, :].astype(wide)
        if grad_out is not None:
            grad_out[at, :] = back.astype(grad_out.dtype)
        if low_ref is not None:
            low_ref[at, :] = back.astype(low)
        vec_out[0:1, :] += by_gain
        vec_out[1:2, :] += by_shift


def erf_ratio(values):
    x = jnp.clip(values, -4.0, 4.0)
    square = x * x
    top = jnp.full_like(square, -2.72614225801306e-10)
    for term in (
        2.77068142495902e-08,
        -2.10102402082508e-06,
        -5.69250639462346e-05,
        -7.34990630326855e-04,
        -2.95459980854025e-03,
        -1.60960333262415e-02,
    ):
        top = top * square + term
    low_part = jnp.full_like(square, -1.45660718464996e-05)
    for term in (
        -2.13374055278905e-04,
        -1.68282697438203e-03,
        -7.37332916720468e-03,
        -1.42647390514189e-02,
    ):
        low_part = low_part * square + term
    return x * top / low_part


def gelu_pair(before):
    phi_whole = 0.5 + 0.5 * erf_ratio(before * 0.7071067811865476)
    density = jnp.exp(before * before * -0.5) * 0.3989422804014327
    return before * phi_whole, phi_whole + before * density


def chunks(rows):
    return range(0, rows, CHUNK)


def feed_forward_kernel(
    rows_norm, ticks, x_ref, own_ref, other_ref, w_ref, vec_ref, x_out, normed_out, hidden_out, slope_out, part_out
):
    units = w_ref.shape[1] // 2
    steps = x_ref.shape[0] // CHUNK
    pieces = units // 512
    ticks.begin(steps * pieces)
    gain = vec_ref[rows_norm : rows_norm + 1, :]
    shift = vec_ref[rows_norm + 1 : rows_norm + 2, :]

    @pl.loop(0, x_ref.shape[0] // CHUNK)
    def _(step):
        at = pl.ds(pl.multiple_of(step * CHUNK, CHUNK), CHUNK)
        x = x_ref[at, :] + (own_ref[at, :].astype(wide) + other_ref[at, :].astype(wide))
        x_out[at, :] = x
        normed = (centre_rows(x) * gain + shift).astype(low)
        normed_out[at, :] = normed
        part = jnp.zeros((CHUNK, x.shape[1]), wide)
        for begin in range(0, units, 512):
            ticks.in_loop(step, steps, 0, pieces, begin // 512)
            before = dot_nn(normed, w_ref[:, begin : begin + 512])
            value, slope = gelu_pair(before)
            hidden = value.astype(low)
            hidden_out[at, begin : begin + 512] = hidden
            slope_out[at, begin : begin + 512] = slope.astype(low)
            part = part + dot_nt(hidden, w_ref[:, units + begin : units + begin + 512])
        part_out[at, :] = part.astype(low)


def feed_forward_call(rows_norm, x, own, other, weights, vectors, rider=None):
    rows, depth = x.shape
    units = weights[1] // 2
    return ride_call(
        functools.partial(feed_forward_kernel, rows_norm),
        [x, own, other, weights[0], vectors],
        [whole(), whole(), whole(), weight_spec(weights), whole()],
        [
            shaped(rows, depth, wide),
            shaped(rows, depth, low),
            shaped(rows, units, low),
            shaped(rows, units, low),
            shaped(rows, depth, low),
        ],
        [],
        rider,
        "feed_forward",
    )


def store_grad(target, begin, value):
    value = value.astype(low)
    span = slice(begin, begin + value.shape[1])
    if len(target.shape) == 2:
        target[:, span] = value
    else:
        target[:, :, span] = value.reshape(target.shape[0], target.shape[1], value.shape[1])


def feed_backward_ticks(rows, units):
    return 1 + rows // CHUNK * (units // 512) + units // 256


def feed_backward_body(ticks, normed_ref, hidden_ref, slope_in, w_ref, part_out, grad_out, low_ref, slope_ref, turned_ref, turned_low):
    rows, depth = low_ref.shape
    units = w_ref.shape[1] // 2
    steps = rows // CHUNK
    pieces = units // 512
    offset = 1 + steps * pieces
    ticks(0)
    turn_into(turned_low, low_ref)
    turn_into(turned_ref, normed_ref)

    @pl.loop(0, rows // CHUNK)
    def _(step):
        at = pl.ds(pl.multiple_of(step * CHUNK, CHUNK), CHUNK)
        grads = low_ref[at, :]
        part = jnp.zeros((CHUNK, depth), wide)
        for begin in range(0, units, 512):
            ticks.in_loop(step, steps, 1, pieces, begin // 512)
            grad = dot_nn(grads, w_ref[:, units + begin : units + begin + 512])
            grad = (grad * slope_in[at, begin : begin + 512].astype(wide)).astype(low)
            slope_ref[at, begin : begin + 512] = grad
            part = part + dot_nt(grad, w_ref[:, begin : begin + 512])
        part_out[at, :] = part.astype(low)

    for begin in range(0, units, 256):
        ticks(offset + begin // 256)
        store_grad(grad_out, begin, dot_nn(turned_ref[...], slope_ref[:, begin : begin + 256]))
        store_grad(
            grad_out, units + begin, dot_nn(turned_low[...], hidden_ref[:, begin : begin + 256])
        )


def feed_backward_scratch(rows, depth, units):
    return [
        pltpu.VMEM((rows, depth), low),
        pltpu.VMEM((rows, units), low),
        pltpu.VMEM((depth, rows), low),
        pltpu.VMEM((depth, rows), low),
    ]


def last_feed_backward_kernel(
    ticks, length_ref, cotangent_ref, normed_ref, hidden_ref, slope_in, w_ref, part_out, grad_out, low_ref, *rest
):
    rows, depth = cotangent_ref.shape

    @pl.loop(0, rows // CHUNK)
    def _(step):
        first_row = pl.multiple_of(step * CHUNK, CHUNK)
        at = pl.ds(first_row, CHUNK)
        rows_here = cotangent_ref[at, :].astype(wide)
        kept = column_of(length_ref, first_row) > 0
        low_ref[at, :] = jnp.where(kept, rows_here, 0.0).astype(low)

    feed_backward_body(ticks, normed_ref, hidden_ref, slope_in, w_ref, part_out, grad_out, low_ref, *rest)


def last_feed_backward_call(length, cotangent, normed, hidden, slope, weights, rider=None):
    rows, depth = cotangent.shape
    units = hidden.shape[1]
    return ride_call(
        last_feed_backward_kernel,
        [length, cotangent, normed, hidden, slope, weights[0]],
        [whole()] + [whole()] * 4 + [weight_spec(weights)],
        [shaped(rows, depth, low), shaped(depth, 2 * units, low), shaped(rows, depth, low)],
        feed_backward_scratch(rows, depth, units)[1:],
        rider,
        "last_feed_backward",
    )


def feed_backward_kernel(
    norm_row, ticks, x_ref, own_ref, other_ref, vec_ref, normed_ref, hidden_ref, slope_in, w_ref,
    part_out, grad_out, g_out, vec_out, low_ref, *rest
):
    units = w_ref.shape[1] // 2
    ticks.begin(1 + x_ref.shape[0] // CHUNK * (units // 512) + units // 256)
    residual_prologue(norm_row, None, x_ref, own_ref, other_ref, vec_ref, g_out, low_ref, vec_out)
    feed_backward_body(ticks, normed_ref, hidden_ref, slope_in, w_ref, part_out, grad_out, low_ref, *rest)


def feed_backward_call(norm_row, x, own, other, vectors, normed, hidden, slope, weights, rider=None):
    rows, depth = x.shape
    units = hidden.shape[1]
    return ride_call(
        functools.partial(feed_backward_kernel, norm_row),
        [x, own, other, vectors, normed, hidden, slope, weights[0]],
        [whole()] * 7 + [weight_spec(weights)],
        [
            shaped(rows, depth, low),
            shaped(depth, 2 * units, low),
            shaped(rows, depth, wide),
            shaped(2, depth, wide),
        ],
        feed_backward_scratch(rows, depth, units),
        rider,
        "feed_backward",
    )


def half_lanes(shape):
    return lax.broadcasted_iota(jnp.int32, shape, 1) < 64


def one_head(pair, head):
    first = half_lanes(pair.shape)
    zero = jnp.zeros_like(pair)
    return jnp.where(first, pair, zero) if head == 0 else jnp.where(first, zero, pair)


def key_bias(keys, mask_row, first_row, causal, rows):
    allowed = jnp.where(mask_row[...] > 0, 0.0, masked_score)
    if not causal:
        return allowed
    column = lax.broadcasted_iota(jnp.int32, (rows, keys), 1)
    row = first_row + lax.broadcasted_iota(jnp.int32, (rows, keys), 0)
    return jnp.where(column <= row, allowed, masked_score)


def attend_chunk(tick, first_row, length, causal, q_ref, kv_ref, w_ref, attended_out, totals_out, part_out):
    width = q_ref.shape[1]
    keys = kv_ref.shape[0]
    at = pl.ds(first_row, CHUNK)
    bias = key_bias(keys, length, first_row, causal, CHUNK)
    lane = lax.broadcasted_iota(jnp.int32, (CHUNK, 128), 1)
    totals = jnp.zeros((CHUNK, 128), wide)
    for begin in range(0, width, 128):
        tick(begin // 128)
        pair = q_ref[at, begin : begin + 128]
        key_pair = kv_ref[:, begin : begin + 128]
        value_pair = kv_ref[:, width + begin : width + begin + 128]
        results = []
        for head in range(2):
            scores = dot_nt(one_head(pair, head), key_pair) + bias
            peak = jnp.max(scores, axis=-1, keepdims=True)
            weights = jnp.exp(scores - peak)
            total = jnp.sum(weights, axis=-1, keepdims=True)
            results.append(dot_nn(weights.astype(low), value_pair) * (1.0 / total))
            totals = jnp.where(lane == begin // 64 + head, peak + jnp.log(total), totals)
        attended_out[at, begin : begin + 128] = jnp.where(
            lane < 64, results[0], results[1]
        ).astype(low)
    totals_out[at, :] = totals
    part_out[at, :] = dot_nt(attended_out[at, :], w_ref[:, 3 * width :]).astype(low)


def self_attention_kernel(
    rows_norm, causal, ticks, length_ref, x_ref, w_ref, vec_ref, normed_out, q_out, kv_out, attended_out, totals_out, part_out
):
    width = w_ref.shape[1] // 4
    gain = vec_ref[rows_norm : rows_norm + 1, :]
    shift = vec_ref[rows_norm + 1 : rows_norm + 2, :]
    steps = x_ref.shape[0] // CHUNK
    pairs = width // 128
    ticks.begin(steps * (pairs + 1))

    @pl.loop(0, steps)
    def _(step):
        ticks.in_loop(step, steps, 0, 1, 0)
        at = pl.ds(pl.multiple_of(step * CHUNK, CHUNK), CHUNK)
        normed = (centre_rows(x_ref[at, :].astype(wide)) * gain + shift).astype(low)
        normed_out[at, :] = normed
        q_out[at, :] = (dot_nn(normed, w_ref[:, :width]).astype(low).astype(wide) * 0.125).astype(low)
        kv_out[at, :] = dot_nn(normed, w_ref[:, width : 3 * width]).astype(low)

    length = length_ref

    @pl.loop(0, steps)
    def _(step):
        attend_chunk(
            functools.partial(ticks.in_loop, step, steps, steps, pairs),
            pl.multiple_of(step * CHUNK, CHUNK), length, causal, q_out, kv_out, w_ref, attended_out, totals_out, part_out
        )


def self_attention_call(rows_norm, causal, length, x, weights, vectors, rider=None):
    rows, depth = x.shape
    width = weights[1] // 4
    return ride_call(
        functools.partial(self_attention_kernel, rows_norm, causal),
        [length, x, weights[0], vectors],
        [whole(), whole(), weight_spec(weights), whole()],
        [
            shaped(rows, depth, low),
            shaped(rows, width, low),
            shaped(rows, 2 * width, low),
            shaped(rows, width, low),
            shaped(rows, 128, wide),
            shaped(rows, depth, low),
        ],
        [],
        rider,
        "self_attention",
    )


def cross_attention_kernel(
    ticks, length_ref, x_ref, own_ref, other_ref, mid_ref, mid_own, mid_other, w_ref, vec_ref,
    x_out, final_out, memory_out, normed_out, q_out, kv_out, attended_out, totals_out, part_out,
):
    width = w_ref.shape[1] // 4
    first_steps = mid_ref.shape[0] // CHUNK
    steps = x_ref.shape[0] // CHUNK
    pairs = width // 128
    ticks.begin(first_steps + steps * (pairs + 1))

    @pl.loop(0, first_steps)
    def _(step):
        ticks.in_loop(step, first_steps, 0, 1, 0)
        at = pl.ds(pl.multiple_of(step * CHUNK, CHUNK), CHUNK)
        x = mid_ref[at, :] + (mid_own[at, :].astype(wide) + mid_other[at, :].astype(wide))
        final_out[at, :] = x
        memory = (centre_rows(x) * vec_ref[4:5, :] + vec_ref[5:6, :]).astype(low)
        memory_out[at, :] = memory
        kv_out[at, :] = dot_nn(memory, w_ref[:, width : 3 * width]).astype(low)

    @pl.loop(0, steps)
    def _(step):
        ticks.in_loop(step, steps, first_steps, 1, 0)
        at = pl.ds(pl.multiple_of(step * CHUNK, CHUNK), CHUNK)
        x = x_ref[at, :].astype(wide) + (own_ref[at, :].astype(wide) + other_ref[at, :].astype(wide))
        x_out[at, :] = x
        normed = (centre_rows(x) * vec_ref[8:9, :] + vec_ref[9:10, :]).astype(low)
        normed_out[at, :] = normed
        q_out[at, :] = (dot_nn(normed, w_ref[:, :width]).astype(low).astype(wide) * 0.125).astype(low)

    length = length_ref

    @pl.loop(0, steps)
    def _(step):
        attend_chunk(
            functools.partial(ticks.in_loop, step, steps, first_steps + steps, pairs),
            pl.multiple_of(step * CHUNK, CHUNK), length, False, q_out, kv_out, w_ref, attended_out, totals_out, part_out
        )


def cross_attention_call(length, x, own, other, mid, mid_own, mid_other, weights, vectors, rider=None):
    rows, depth = x.shape
    keys = mid.shape[0]
    width = weights[1] // 4
    return ride_call(
        cross_attention_kernel,
        [length, x, own, other, mid, mid_own, mid_other, weights[0], vectors],
        [whole()] + [whole()] * 6 + [weight_spec(weights), whole()],
        [
            shaped(rows, depth, wide),
            shaped(keys, depth, wide),
            shaped(keys, depth, low),
            shaped(rows, depth, low),
            shaped(rows, width, low),
            shaped(keys, 2 * width, low),
            shaped(rows, width, low),
            shaped(rows, 128, wide),
            shaped(rows, depth, low),
        ],
        [],
        rider,
        "cross_attention",
    )


def attention_backward_kernel(
    causal, cross, norm_row, ticks, length_ref, previous_ref, x_ref, own_ref, other_ref, vec_ref,
    normed_ref, source_ref, q_ref, kv_ref, attended_ref, totals_ref, w_ref, *rest
):
    outs = 5 if cross else 4
    part_out, g_out, vec_out, grad_out = rest[:4]
    source_part_out = rest[4] if cross else None
    low_ref, scratch = rest[outs], rest[outs + 1 :]
    residual_prologue(norm_row, previous_ref, x_ref, own_ref, other_ref, vec_ref, g_out, low_ref, vec_out)
    attention_backward_main(
        causal, cross, ticks, length_ref, low_ref, normed_ref, source_ref, q_ref, kv_ref, attended_ref, totals_ref,
        w_ref, part_out, grad_out, source_part_out, *scratch,
    )


def attention_backward_main(
    causal, cross, ticks, length, low_ref, normed_ref, source_ref, q_ref, kv_ref, attended_ref, totals_ref, w_ref,
    part_out, grad_out, source_part_out, grad_q, grad_kv, turned_k, turned_v, turned_low, turned_normed, *rest
):
    turned_source = rest[0] if cross else turned_normed
    rows, depth = low_ref.shape
    keys = kv_ref.shape[0]
    width = q_ref.shape[1]
    steps = rows // CHUNK
    pairs = width // 128
    key_steps = keys // CHUNK
    after = 1 + steps * pairs
    last = after + key_steps
    ticks.begin(last + 5)
    ticks(0)
    turned_k[...] = jnp.zeros_like(turned_k)
    turned_v[...] = jnp.zeros_like(turned_v)

    @pl.loop(0, rows // CHUNK)
    def _(step):
        first_row = pl.multiple_of(step * CHUNK, CHUNK)
        at = pl.ds(first_row, CHUNK)
        grad_attended = dot_nn(low_ref[at, :], w_ref[:, 3 * width :]).astype(low)
        bias = key_bias(keys, length, first_row, causal, CHUNK)
        lane = lax.broadcasted_iota(jnp.int32, (CHUNK, 128), 1)
        totals = totals_ref[at, :]
        for begin in range(0, width, 128):
            ticks.in_loop(step, steps, 1, pairs, begin // 128)
            pair = q_ref[at, begin : begin + 128]
            key_pair = kv_ref[:, begin : begin + 128]
            value_pair = kv_ref[:, width + begin : width + begin + 128]
            grad_pair = grad_attended[:, begin : begin + 128]
            pair_turned = turned(pair)
            grad_turned = turned(grad_pair)
            results = []
            for head in range(2):
                number = begin // 64 + head
                total = jnp.sum(jnp.where(lane == number, totals, 0.0), axis=-1, keepdims=True)
                scores = dot_nt(one_head(pair, head), key_pair) + bias
                weights = jnp.exp(scores - total)
                grad_weights = dot_nt(one_head(grad_pair, head), value_pair)
                row_dot = jnp.sum(weights * grad_weights, axis=-1, keepdims=True)
                grad_scores = (weights * (grad_weights - row_dot)).astype(low)
                results.append(dot_nn(grad_scores, key_pair))
                span = slice(begin + 64 * head, begin + 64 * head + 64)
                local = slice(64 * head, 64 * head + 64)
                turned_k[span, :] += dot_nn(pair_turned[local, :], grad_scores)
                turned_v[span, :] += dot_nn(grad_turned[local, :], weights.astype(low))
            grad_q[at, begin : begin + 128] = (
                jnp.where(lane < 64, results[0], results[1]) * 0.125
            ).astype(low)
        if cross:
            part_out[at, :] = dot_nt(grad_q[at, :], w_ref[:, :width]).astype(low)

    grad_kv[:, :width] = turned(turned_k[...].astype(low))
    grad_kv[:, width:] = turned(turned_v[...].astype(low))

    @pl.loop(0, keys // CHUNK)
    def _(step):
        ticks.in_loop(step, key_steps, after, 1, 0)
        at = pl.ds(pl.multiple_of(step * CHUNK, CHUNK), CHUNK)
        from_source = dot_nt(grad_kv[at, :], w_ref[:, width : 3 * width])
        if cross:
            source_part_out[at, :] = from_source.astype(low)
        else:
            from_query = dot_nt(grad_q[at, :], w_ref[:, :width])
            part_out[at, :] = (from_source + from_query).astype(low)

    ticks(last)
    turn_into(turned_low, low_ref)
    turn_into(turned_normed, normed_ref)
    if cross:
        turn_into(turned_source, source_ref)
    ticks(last + 1)
    store_grad(grad_out, 0, dot_nn(turned_normed[...], grad_q[...]))
    ticks(last + 2)
    store_grad(grad_out, width, dot_nn(turned_source[...], grad_kv[:, :width]))
    ticks(last + 3)
    store_grad(grad_out, 2 * width, dot_nn(turned_source[...], grad_kv[:, width:]))
    ticks(last + 4)
    store_grad(grad_out, 3 * width, dot_nn(turned_low[...], attended_ref[...]))


def attention_backward_scratch(rows, keys, depth, width, cross):
    scratch = [
        pltpu.VMEM((rows, depth), low),
        pltpu.VMEM((rows, width), low),
        pltpu.VMEM((keys, 2 * width), low),
        pltpu.VMEM((width, keys), wide),
        pltpu.VMEM((width, keys), wide),
        pltpu.VMEM((depth, rows), low),
        pltpu.VMEM((depth, rows), low),
    ]
    if cross:
        scratch.append(pltpu.VMEM((depth, keys), low))
    return scratch


def attention_backward_call(
    causal, norm_row, length, previous, x, own, other, vectors, normed, source, q, kv, attended, totals, weights,
    rider=None,
):
    cross = source is not None
    rows, depth = x.shape
    keys = kv.shape[0]
    width = q.shape[1]
    outs = [
        shaped(rows, depth, low),
        shaped(rows, depth, wide),
        shaped(2, depth, wide),
        shaped(depth, 4 * width, low),
    ]
    if cross:
        outs.append(shaped(keys, depth, low))
    scratch = attention_backward_scratch(rows, keys, depth, width, cross)
    operands = [length, previous, x, own, other, vectors, normed]
    if cross:
        operands.append(source)
    operands += [q, kv, attended, totals, weights[0]]

    def body(ticks, *refs):
        if not cross:
            refs = refs[:7] + (None,) + refs[7:]
        attention_backward_kernel(causal, cross, norm_row, ticks, *refs)

    return ride_call(
        body,
        operands,
        [whole()] + [whole()] * (len(operands) - 2) + [weight_spec(weights)],
        outs,
        scratch,
        rider,
        "attention_backward",
    )


def finish_kernel(norm_row, previous_ref, x_ref, own_ref, other_ref, vec_ref, g_out, vec_out):
    residual_prologue(norm_row, previous_ref, x_ref, own_ref, other_ref, vec_ref, g_out, None, vec_out)


def finish_call(norm_row, previous, x, own, other, vectors):
    rows, depth = x.shape
    return pl.pallas_call(
        functools.partial(finish_kernel, norm_row),
        out_shape=(shaped(rows, depth, wide), shaped(2, depth, wide)),
        compiler_params=pltpu.CompilerParams(vmem_limit_bytes=40 << 20),
        name="finish_norm",
    )(previous, x, own, other, vectors)


class Stream:
    def __init__(self):
        self.steps = {True: [], False: []}
        self.begins, self.ends = [], []
        self.position = {True: 0, False: 0}
        self.movers = []

    def add(self, mover, overlap=0.0):
        self.movers.append(mover)
        begin, end = {}, {}
        for home in (True, False):
            had, new = self.steps[home], mover.steps[home]
            shared = min(int(len(new) * overlap), len(had))
            kept = len(had) - shared
            merged = had[:kept]
            for one, two in zip(had[kept:], new[:shared]):
                merged += [one, two]
            merged += new[shared:]
            for mark in self.ends:
                if mark[home] > kept:
                    mark[home] = kept + 2 * (mark[home] - kept)
            self.steps[home] = merged
            begin[home], end[home] = kept, len(merged)
        self.begins.append(begin)
        self.ends.append(end)

    def between(self, one, two, share):
        return {home: one[home] + int((two[home] - one[home]) * share) for home in (True, False)}

    def plan(self, marks, shares=(1.0,)):
        windows, done, start = [], 0.0, dict(self.position)
        for share in shares:
            done += share / sum(shares)
            end = {
                home: max(
                    self.position[home],
                    start[home] + round((marks[home] - start[home]) * done),
                )
                for home in (True, False)
            }
            windows.append(Window(self, dict(self.position), end))
            self.position = end
        return windows

    def run(self, chosen):
        for home in (True, False):
            if not chosen[home]:
                continue
            wanted = place("c") == place("x")

            @pl.when(wanted if home else jnp.logical_not(wanted))
            def _():
                for step in chosen[home]:
                    step()

    def finish(self):
        for mover in self.movers:
            mover.finish()


class Window:
    def __init__(self, stream, start, end):
        self.stream, self.start, self.end = stream, start, end
        self.parts = 1

    def begin(self, parts):
        self.parts = parts

    def __call__(self, part=0):
        chosen = {}
        for home in (True, False):
            start, size = self.start[home], self.end[home] - self.start[home]
            first = start + size * part // self.parts
            chosen[home] = self.stream.steps[home][first : start + size * (part + 1) // self.parts]
        self.stream.run(chosen)

    def in_loop(self, step, steps, offset, stride, inner):
        if all(self.start[home] == self.end[home] for home in (True, False)):
            return
        for number in range(steps):

            @pl.when(step == number)
            def _():
                self(offset + number * stride + inner)


class Bag:
    def __init__(self, **entries):
        self.__dict__.update(entries)

    def names(self):
        return list(self.__dict__)

    def values(self):
        return list(self.__dict__.values())

    def joined(self, other):
        return Bag(**self.__dict__, **other.__dict__)


def filled(names, values):
    return Bag(**dict(zip(names, values)))


class Nothing:
    def begin(self, parts):
        pass

    def __call__(self, part=0):
        pass

    def in_loop(self, *unused):
        pass


nothing = Nothing()


def vmem_like(ref):
    return pltpu.VMEM(ref.shape, ref.dtype)


class Direct:
    def __init__(self, ref):
        self.ref = ref


class Swap:
    def __init__(self, target, send_sem, recv_sem):
        self.target, self.send_sem, self.recv_sem = target, send_sem, recv_sem

    def copy(self, source):
        return pltpu.make_async_remote_copy(
            src_ref=source,
            dst_ref=self.target,
            send_sem=self.send_sem,
            recv_sem=self.recv_sem,
            device_id=target_of("c"),
            device_id_type=MESH,
        )

    def arrive(self):
        self.copy(self.target).wait_recv()


def run_phase(body, sems, ins, outs, scratch=(), swaps=(), before=nothing, after=nothing):
    moved_in = [ref for ref in ins if not isinstance(ref, Direct)]
    moved_out = [ref for ref in outs if not isinstance(ref, Direct)]

    def scoped(*refs):
        own_in, rest = refs[: len(moved_in)], refs[len(moved_in) :]
        own_out, own_scratch = rest[: len(moved_out)], rest[len(moved_out) :]
        copies = [
            pltpu.make_async_copy(ref, own, sems.at[number])
            for number, (ref, own) in enumerate(zip(moved_in, own_in))
        ]
        for copy in copies:
            copy.start()
        before()
        for copy in copies:
            copy.wait()
        own_in, own_out = iter(own_in), iter(own_out)
        all_in = [ref.ref if isinstance(ref, Direct) else next(own_in) for ref in ins]
        all_out = [ref.ref if isinstance(ref, Direct) else next(own_out) for ref in outs]
        body(*all_in, *all_out, *own_scratch)
        copies = []
        for number, swap in swaps:
            swap.copy(all_out[number]).start()
        for ref, own in zip(outs, all_out):
            if not isinstance(ref, Direct):
                copy = pltpu.make_async_copy(own, ref, sems.at[16 + len(copies)])
                copy.start()
                copies.append(copy)
        after()
        for copy in copies:
            copy.wait()
        for number, swap in swaps:
            swap.copy(all_out[number]).wait_send()

    allocations = [vmem_like(ref) for ref in moved_in] + [vmem_like(ref) for ref in moved_out]
    pl.run_scoped(scoped, *allocations, *scratch)


def column_of(row_ref, first_row):
    size = row_ref.shape[1]
    lane = lax.broadcasted_iota(jnp.int32, (CHUNK, size), 1)
    row = first_row + lax.broadcasted_iota(jnp.int32, (CHUNK, size), 0)
    return jnp.sum(jnp.where(lane == row, row_ref[...], 0), axis=-1, keepdims=True)


class Inputs(Mover):
    def __init__(self, send_sems, recv_sems, local_sems):
        super().__init__(send_sems)
        self.recv_sems, self.local_sems = recv_sems, local_sems
        self.count = 0

    def taken(self):
        steps = self.steps
        self.steps = {True: [], False: []}
        return steps

    def swap(self, source, target):
        number = self.count
        self.count += 1

        def diagonal():
            return {"c": 1 - place("c"), "x": 1 - place("x")}

        def local():
            return pltpu.make_async_copy(source(), target(True), self.local_sems.at[number])

        self.local(True, lambda: local().start())
        self.send(
            False,
            source,
            functools.partial(target, False),
            lambda: self.recv_sems.at[number],
            diagonal,
        )

        def arrive():
            self.local(True, lambda: local().wait())
            self.wait(False, functools.partial(target, True), lambda: self.recv_sems.at[number])

        return arrive

    def share(self, piece):
        number = self.count
        self.count += 1

        def sem():
            return self.recv_sems.at[number]

        for home in (True, False):
            self.send(
                home,
                functools.partial(piece, True),
                functools.partial(piece, True),
                sem,
                functools.partial(target_of, "c"),
            )

        def arrive():
            for home in (True, False):
                self.wait(home, functools.partial(piece, False), sem)

        return arrive


def half_of(ref, own):
    size = ref.shape[0] // 2
    core = place("c") if own else 1 - place("c")
    return ref.at[pl.ds(core * size, size), :]


def half_lanes_of(ref, own):
    size = ref.shape[1] // 2
    core = place("c") if own else 1 - place("c")
    return ref.at[:, pl.ds(core * size, size)]


def source_mask(marks_row):
    quarter = marks_row.shape[1] // 4
    return marks_row.at[:, pl.ds(quarter, 2 * quarter)]


def target_mask(marks_row):
    quarter = marks_row.shape[1] // 4
    return marks_row.at[:, pl.ds(3 * quarter, quarter)]


def any_space():
    return pl.BlockSpec(memory_space=pl.ANY)


def spliced(one, two, at):
    return {home: one[home][: at[home]] + two[home] + one[home][at[home] :] for home in (True, False)}


def shares_of(steps, share):
    return {home: int(len(steps[home]) * share) for home in (True, False)}


def forward_kernel(names_in, names_out, *refs):
    count_in, count_out = len(names_in), len(names_out)
    i = filled(names_in, refs[:count_in])
    o = filled(names_out, refs[count_in : count_in + count_out])
    (marks_row, flags_row, *rest) = refs[count_in + count_out :]
    stages, rest = rest[:5], rest[5:]
    sems, group_send, group_recv, group_local, in_send, in_recv, in_local, swap_sems = rest
    vec = i.vectors
    greet()

    start = Inputs(Part(in_send, 0), Part(in_recv, 0), Part(in_local, 0))
    marks_here = start.swap(lambda: i.marks, lambda own: marks_row)
    source_here = start.swap(lambda: i.source, functools.partial(half_of, o.source_all))
    opening = start.taken()
    marks_here()
    flags_size = flags_row.shape[1] // 2

    def flags_piece(own):
        return half_lanes_of(flags_row, own)

    def flags_local():
        return pltpu.make_async_copy(
            marks_row.at[:, pl.ds(0, flags_size)], flags_piece(True), in_local.at[8]
        )

    for home in (True, False):
        start.local(home, lambda: flags_local().start())
        start.local(home, lambda: flags_local().wait())
    flags_there = start.share(flags_piece)
    source_here()
    source_there = start.share(functools.partial(half_of, o.source_all))
    middle = start.taken()
    flags_there()
    source_there()
    closing = start.taken()

    owns = (i.own_1, i.own_3, i.own_2, i.own_4, i.own_5)
    alls = (o.all_1, o.all_3, o.all_2, o.all_4, o.all_5)
    gathers = []
    for number, (own, gathered) in enumerate(zip(owns, alls)):
        gathers.append(
            Gather(
                own,
                gathered,
                stages[number],
                group_local.at[number],
                Part(group_send, number * GATHER_SENDS),
                Part(group_recv, number * 64),
            )
        )
    first, second, last = gathers[0], gathers[1], gathers[4]
    steps = spliced(first.steps, middle, shares_of(first.steps, 0.6))
    first.steps = {home: opening[home] + steps[home] + closing[home] for home in (True, False)}

    def bring(source, target, first_send, first_recv, first_local):
        mover = Inputs(Part(in_send, first_send), Part(in_recv, first_recv), Part(in_local, first_local))
        here_now = mover.swap(lambda: source, functools.partial(half_of, target))
        begin = mover.taken()
        here_now()
        there_now = mover.share(functools.partial(half_of, target))
        there_now()
        return mover, begin, mover.taken()

    target_mover, begin, rest = bring(i.target, o.target_all, 16, 8, 9)
    steps = spliced(second.steps, rest, shares_of(second.steps, 0.4))
    second.steps = {home: begin[home] + steps[home] for home in (True, False)}
    cotangent_mover, begin, rest = bring(i.cotangent, o.cotangent_all, 24, 12, 13)
    steps = spliced(last.steps, begin, shares_of(last.steps, 0.7))
    last.steps = {home: steps[home] + rest[home] for home in (True, False)}
    stream = Stream()
    stream.movers += [start, target_mover, cotangent_mover]
    for number, mover in enumerate(gathers):
        stream.add(mover, 0.4 if number > 1 else 0.0)
    ends = stream.ends

    swap_refs = (o.other_1, o.other_2, o.other_3, o.other_4, o.other_5)
    swaps = [
        Swap(ref, swap_sems.at[number], swap_sems.at[8 + number])
        for number, ref in enumerate(swap_refs)
    ]

    stream.plan(ends[0])[0]()

    one, ticks, two = stream.plan(stream.between(ends[1], ends[2], 0.25), (1, 7, 1))

    def encoder_attention_body(source_ref, w_ref, x_out, *outs):
        @pl.loop(0, x_out.shape[0] // CHUNK)
        def _(step):
            first_row = pl.multiple_of(step * CHUNK, CHUNK)
            at = pl.ds(first_row, CHUNK)
            kind = column_of(flags_row, first_row)
            x_out[at, :] = jnp.where(
                kind == 1, vec[12:13, :], jnp.where(kind == 2, vec[13:14, :], source_ref[at, :].astype(wide))
            )

        self_attention_kernel(0, False, ticks, source_mask(marks_row), x_out, w_ref, vec, *outs)

    run_phase(
        encoder_attention_body,
        sems,
        [o.source_all, o.all_1],
        [o.start, o.normed_1, o.query_1, o.kv_1, o.attended_1, o.totals_1, o.part_1],
        swaps=[(6, swaps[0])],
        before=one,
        after=two,
    )
    one, ticks_two, two = stream.plan(stream.between(ends[1], ends[2], 0.6), (1, 6, 1))

    def decoder_attention_body(x_ref, w_ref, *outs):
        self_attention_kernel(6, True, ticks_two, target_mask(marks_row), x_ref, w_ref, vec, *outs)

    run_phase(
        decoder_attention_body,
        sems,
        [o.target_all, o.all_3],
        [o.normed_3, o.query_3, o.kv_3, o.attended_3, o.totals_3, o.part_3],
        swaps=[(5, swaps[2])],
        before=one,
        after=two,
    )
    stream.plan(ends[2])[0]()
    swaps[0].arrive()
    one, ticks_three, two = stream.plan(stream.between(ends[3], ends[4], 0.2), (1, 5, 1))

    def encoder_feed_body(x_ref, own_ref, other_ref, w_ref, *outs):
        feed_forward_kernel(2, ticks_three, x_ref, own_ref, other_ref, w_ref, vec, *outs)

    run_phase(
        encoder_feed_body,
        sems,
        [o.start, o.part_1, o.other_1, o.all_2],
        [o.mid, o.normed_2, o.hidden_2, o.slope_2, o.part_2],
        swaps=[(4, swaps[1])],
        before=one,
        after=two,
    )
    stream.plan(ends[3])[0]()
    swaps[2].arrive()
    swaps[1].arrive()
    one, ticks_four, two = stream.plan(ends[4], (1, 5, 1))

    def cross_attention_body(x_ref, own_ref, other_ref, mid_ref, mid_own, mid_other, w_ref, *outs):
        cross_attention_kernel(
            ticks_four, source_mask(marks_row), x_ref, own_ref, other_ref, mid_ref, mid_own, mid_other, w_ref, vec, *outs
        )

    run_phase(
        cross_attention_body,
        sems,
        [o.target_all, o.part_3, o.other_3, o.mid, o.part_2, o.other_2, o.all_4],
        [o.one, o.final, o.memory, o.normed_4, o.query_4, o.kv_4, o.attended_4, o.totals_4, o.part_4],
        swaps=[(8, swaps[3])],
        before=one,
        after=two,
    )
    swaps[3].arrive()

    def decoder_feed_body(x_ref, own_ref, other_ref, w_ref, *outs):
        feed_forward_kernel(10, nothing, x_ref, own_ref, other_ref, w_ref, vec, *outs)

    run_phase(
        decoder_feed_body,
        sems,
        [o.one, o.part_4, o.other_4, o.all_5],
        [o.two, o.normed_5, o.hidden_5, o.slope_5, o.part_5],
        swaps=[(4, swaps[4])],
    )
    o.marks_all[...] = marks_row[...]
    o.flags_all[...] = flags_row[...]
    swaps[4].arrive()
    stream.finish()


def attention_kept(rows, keys, depth, width):
    return (
        shaped(rows, depth, low),
        shaped(rows, width, low),
        shaped(keys, 2 * width, low),
        shaped(rows, width, low),
        shaped(rows, 128, wide),
    )


def feed_kept(rows, depth, units):
    return shaped(rows, depth, low), shaped(rows, units, low), shaped(rows, units, low)


def specs_of(near, far):
    return [whole() for unused in near.values()] + [any_space() for unused in far.values()]


def dma(count):
    return pltpu.SemaphoreType.DMA((count,))


def forward_call(source, target, cotangent, marks, vectors, groups):
    depth = vectors.shape[1]
    rows, few = 2 * source.shape[0], 2 * target.shape[0]
    block = groups[0].shape[0]
    width, units = groups[0].shape[1] // 4, groups[1].shape[1] // 2
    near_in = Bag(marks=marks, vectors=vectors)
    far_in = Bag(source=source, target=target, cotangent=cotangent)
    far_in.own_1, far_in.own_2, far_in.own_3, far_in.own_4, far_in.own_5 = groups
    near_out = Bag(
        marks_all=jax.ShapeDtypeStruct(marks.shape, marks.dtype),
        flags_all=jax.ShapeDtypeStruct((1, rows), marks.dtype),
    )
    far_out = Bag(
        source_all=shaped(rows, depth, low),
        target_all=shaped(few, depth, low),
        cotangent_all=shaped(few, depth, low),
        start=shaped(rows, depth, wide),
        mid=shaped(rows, depth, wide),
        final=shaped(rows, depth, wide),
        memory=shaped(rows, depth, low),
        one=shaped(few, depth, wide),
        two=shaped(few, depth, wide),
    )
    f = far_out
    f.normed_1, f.query_1, f.kv_1, f.attended_1, f.totals_1 = attention_kept(rows, rows, depth, width)
    f.normed_3, f.query_3, f.kv_3, f.attended_3, f.totals_3 = attention_kept(few, few, depth, width)
    f.normed_4, f.query_4, f.kv_4, f.attended_4, f.totals_4 = attention_kept(few, rows, depth, width)
    f.normed_2, f.hidden_2, f.slope_2 = feed_kept(rows, depth, units)
    f.normed_5, f.hidden_5, f.slope_5 = feed_kept(few, depth, units)
    f.part_1 = f.other_1 = f.part_2 = f.other_2 = shaped(rows, depth, low)
    f.part_3 = f.other_3 = f.part_4 = f.other_4 = f.part_5 = f.other_5 = shaped(few, depth, low)
    f.all_1, f.all_2, f.all_3, f.all_4, f.all_5 = [
        shaped(16 * block, group.shape[1], low) for group in groups
    ]
    ins, outs = near_in.joined(far_in), near_out.joined(far_out)
    order = (0, 2, 1, 3, 4)
    stage = [
        pltpu.VMEM((8, block, gather_cuts(groups[number].shape[1])[1][1]), low) for number in order
    ]
    results = pl.pallas_call(
        functools.partial(forward_kernel, ins.names(), outs.names()),
        out_shape=tuple(outs.values()),
        in_specs=specs_of(near_in, far_in),
        out_specs=tuple(specs_of(near_out, far_out)),
        scratch_shapes=[
            pltpu.VMEM(marks.shape, marks.dtype),
            pltpu.VMEM((1, rows), marks.dtype),
            *stage,
            dma(32),
            dma(5 * GATHER_SENDS),
            dma(5 * 64),
            dma(5),
            dma(32),
            dma(16),
            dma(18),
            dma(16),
        ],
        compiler_params=pltpu.CompilerParams(
            collective_id=0, has_side_effects=True, vmem_limit_bytes=60 << 20
        ),
        name="forward_pass",
    )(*ins.values())
    return filled(outs.names(), results)


def backward_kernel(names_in, names_out, *refs):
    count_in, count_out = len(names_in), len(names_out)
    i = filled(names_in, refs[:count_in])
    o = filled(names_out, refs[count_in : count_in + count_out])
    rest = refs[count_in + count_out :]
    vectors_of, rest = dict(zip((0, 2, 4, 6, 8, 10, 12), rest[:7])), rest[7:]
    vector_rows, rest = rest[0], rest[1:]
    buffers = []
    for unused in range(6):
        buffers.append(rest[:SCATTER_BUFFERS])
        rest = rest[SCATTER_BUFFERS:]
    sems, group_send, group_recv, in_send, in_recv, in_local, swap_sems = rest
    vec, marks_row, flags_row = i.vectors, i.marks_all, i.flags_all
    finals = (o.final_5, o.final_4, o.final_3, o.final_2, o.final_1, o.final_vectors)
    greet()
    stream = Stream()
    for number in range(6):
        mover = Scatter(
            buffers[number],
            finals[number],
            Part(group_send, number * SCATTER_SENDS),
            Part(group_recv, number * 80),
        )
        stream.add(mover, (0.0, 0.15, 0.15, 0.15, 0.1, 0.0)[number])
    begins, ends = stream.begins, stream.ends
    swap_refs = (o.other_6, o.other_7, o.other_8, o.other_9, o.other_10, o.other_11)
    swaps = [
        Swap(ref, swap_sems.at[number], swap_sems.at[8 + number])
        for number, ref in enumerate(swap_refs)
    ]

    def total_of(number):
        return Direct(buffers[number][0])

    moves = Inputs(Part(in_send, 0), Part(in_recv, 0), Part(in_local, 0))

    swaps_before = []

    def result_body(x_ref, own_ref, other_ref, out):
        total = own_ref[...].astype(wide) + other_ref[...].astype(wide)
        out[...] = (x_ref[...] + total).astype(low)

    def last_feed_body(*refs):
        last_feed_backward_kernel(nothing, target_mask(marks_row), *refs)

    rows, depth = i.cotangent_all.shape
    units = i.hidden_5.shape[1]
    run_phase(
        last_feed_body,
        sems,
        [i.cotangent_all, i.normed_5, i.hidden_5, i.slope_5, i.all_5],
        [o.part_6, total_of(0), o.grad_three],
        feed_backward_scratch(rows, depth, units)[1:],
        swaps=[(0, swaps[0])],
    )
    run_phase(
        result_body,
        sems,
        [i.two, i.part_5, i.other_5],
        [o.three],
        before=stream.plan(stream.between(stream.position, begins[1], 0.15))[0],
    )
    result_here = moves.swap(functools.partial(half_of, o.three, True), lambda own: o.decoder_out)
    stream.run(moves.taken())
    swaps[0].arrive()

    def residual(norm_row, previous, x, own, other, grad_out, low_ref, before=nothing, ticks=nothing, after=nothing):
        ins = [x, own, other] + ([previous] if previous is not None else [])

        def body(*refs):
            if previous is None:
                x_ref, own_ref, other_ref, grad_ref = refs
                previous_ref = None
            else:
                x_ref, own_ref, other_ref, previous_ref, grad_ref = refs
            residual_prologue(
                norm_row, previous_ref, x_ref, own_ref, other_ref, vec, grad_ref, low_ref, vectors_of[norm_row], ticks
            )

        run_phase(body, sems, ins, [grad_out], before=before, after=after)

    def attention(number, causal, marks, norm_row, previous, x, own, other, grad_out, parts, mask_row, source, kept):
        rows, depth = x.shape
        keys, width = kept[2].shape[0], kept[1].shape[1]
        cross = source is not None
        early, prologue, late, main_in, ticks, main_out = stream.plan(marks, (1, 1, 1, 1, 8, 1))

        def inner(low_ref):
            residual(norm_row, previous, x, own, other, grad_out, low_ref, early, prologue, late)
            ins = [kept[0]] + ([source] if cross else []) + list(kept[1:])
            outs = [part for part, swap in parts] + [total_of(number)]

            def body(*refs):
                normed_ref, refs = refs[0], refs[1:]
                source_ref = None
                if cross:
                    source_ref, refs = refs[0], refs[1:]
                held, refs = refs[:5], refs[5:]
                part_out, refs = refs[0], refs[1:]
                source_part = None
                if cross:
                    source_part, refs = refs[0], refs[1:]
                grad_total, scratch = refs[0], refs[1:]
                attention_backward_main(
                    causal, cross, ticks, mask_row, low_ref, normed_ref, source_ref, *held,
                    part_out, grad_total, source_part, *scratch,
                )

            run_phase(
                body,
                sems,
                ins,
                outs,
                attention_backward_scratch(rows, keys, depth, width, cross)[1:],
                swaps=[(at, swap) for at, (part, swap) in enumerate(parts)],
                before=main_in,
                after=main_out,
            )

        pl.run_scoped(inner, pltpu.VMEM((rows, depth), low))

    attention(
        1, False, begins[1], 10, o.grad_three, i.two, o.part_6, o.other_6, o.grad_two,
        [(o.part_7, swaps[1]), (o.part_8, swaps[2])], source_mask(marks_row), i.memory,
        (i.normed_4, i.query_4, i.kv_4, i.attended_4, i.totals_4, i.all_4),
    )
    swaps[1].arrive()
    attention(
        2, True, begins[2], 8, o.grad_two, i.one, o.part_7, o.other_7, o.grad_one,
        [(o.part_9, swaps[3])], target_mask(marks_row), None,
        (i.normed_3, i.query_3, i.kv_3, i.attended_3, i.totals_3, i.all_3),
    )
    swaps[2].arrive()
    rows, depth = i.final.shape
    early, prologue, late, main_in, ticks, main_out = stream.plan(begins[3], (1, 1, 1, 1, 6, 1))

    def feed(low_ref):
        residual(4, None, i.final, o.part_8, o.other_8, o.grad_final, low_ref, early, prologue, late)

        def body(normed_ref, hidden_ref, slope_ref, w_ref, part_out, grad_total, turned_ref, turned_low):
            ticks.begin(feed_backward_ticks(rows, units))
            feed_backward_body(
                ticks, normed_ref, hidden_ref, slope_ref, w_ref, part_out, grad_total, low_ref, slope_ref,
                turned_ref, turned_low,
            )

        run_phase(
            body,
            sems,
            [i.normed_2, i.hidden_2, i.slope_2, i.all_2],
            [o.part_10, total_of(3)],
            feed_backward_scratch(rows, depth, units)[2:],
            swaps=[(0, swaps[4])],
            before=main_in,
            after=main_out,
        )

    pl.run_scoped(feed, pltpu.VMEM((rows, depth), low))
    swaps[3].arrive()
    residual(
        6, o.grad_one, i.target_all, o.part_9, o.other_9, o.target_low, None,
        stream.plan(stream.between(stream.position, begins[4], 0.1))[0],
    )
    target_here = moves.swap(functools.partial(half_of, o.target_low, True), lambda own: o.target_grad)
    stream.run(moves.taken())
    swaps[4].arrive()
    attention(
        4, False, begins[4], 2, o.grad_final, i.mid, o.part_10, o.other_10, o.grad_mid,
        [(o.part_11, swaps[5])], source_mask(marks_row), None,
        (i.normed_1, i.query_1, i.kv_1, i.attended_1, i.totals_1, i.all_1),
    )
    one, two, three = stream.plan(stream.between(stream.position, ends[4], 0.5), (2, 2, 1))
    one()
    swaps[5].arrive()

    def finish_body(previous_ref, x_ref, own_ref, other_ref, grad_out):
        norms, kinds = vectors_of[0], vectors_of[12]
        norms[...] = jnp.zeros_like(norms)
        kinds[...] = jnp.zeros_like(kinds)

        @pl.loop(0, x_ref.shape[0] // CHUNK)
        def _(step):
            first_row = pl.multiple_of(step * CHUNK, CHUNK)
            at = pl.ds(first_row, CHUNK)
            grads = own_ref[at, :].astype(wide) + other_ref[at, :].astype(wide)
            back, by_gain, by_shift = norm_back(x_ref[at, :], vec[0:1, :], grads)
            back = back + previous_ref[at, :]
            grad_out[at, :] = back.astype(low)
            norms[0:1, :] += by_gain
            norms[1:2, :] += by_shift
            kind = column_of(flags_row, first_row)
            kinds[0:1, :] += jnp.sum(jnp.where(kind == 1, back, 0.0), axis=0, keepdims=True)
            kinds[1:2, :] += jnp.sum(jnp.where(kind == 2, back, 0.0), axis=0, keepdims=True)

        vector_rows[...] = jnp.zeros_like(vector_rows)
        for first, pair in vectors_of.items():
            vector_rows[first : first + 2, :] = pair[...]
        every = jnp.concatenate([vector_rows[...], jnp.zeros((112, depth), wide)], axis=0)
        store_grad(buffers[5][0], 0, turned(every.astype(low)))

    run_phase(
        finish_body,
        sems,
        [o.grad_mid, i.start, o.part_11, o.other_11],
        [o.source_low],
        before=two,
        after=three,
    )
    source_here = moves.swap(functools.partial(half_of, o.source_low, True), lambda own: o.source_grad)
    stream.run(moves.taken())
    rest = {}
    for home in (True, False):
        late = stream.steps[home][stream.position[home] : ends[4][home]]
        few = stream.steps[home][ends[4][home] :]
        merged = []
        for number in range(max(len(late), len(few))):
            merged += few[number : number + 1] + late[number : number + 1]
        rest[home] = merged
    stream.run(rest)
    result_here()
    target_here()
    source_here()
    stream.run(moves.taken())
    moves.finish()
    stream.finish()


def backward_call(kept, vectors):
    rows, depth = kept.start.shape
    few = kept.one.shape[0]
    block = depth // 16
    near_in = Bag(vectors=vectors, marks_all=kept.marks_all, flags_all=kept.flags_all)
    far_in = Bag(**kept.__dict__)
    del far_in.marks_all, far_in.flags_all
    columns = [
        kept.all_5.shape[1], kept.all_4.shape[1], kept.all_3.shape[1], kept.all_2.shape[1], kept.all_1.shape[1], 128
    ]
    near_out = Bag()
    n = near_out
    n.final_5, n.final_4, n.final_3, n.final_2, n.final_1, n.final_vectors = [
        shaped(block, count, wide) for count in columns
    ]
    far_out = Bag(
        grad_three=shaped(few, depth, low),
        grad_two=shaped(few, depth, wide),
        grad_one=shaped(few, depth, wide),
        grad_final=shaped(rows, depth, wide),
        grad_mid=shaped(rows, depth, wide),
        target_low=shaped(few, depth, low),
        source_low=shaped(rows, depth, low),
        target_grad=shaped(few // 2, depth, low),
        source_grad=shaped(rows // 2, depth, low),
        three=shaped(few, depth, low),
        decoder_out=shaped(few // 2, depth, low),
    )
    f = far_out
    f.part_6 = f.other_6 = f.part_7 = f.other_7 = f.part_9 = f.other_9 = shaped(few, depth, low)
    f.part_8 = f.other_8 = f.part_10 = f.other_10 = f.part_11 = f.other_11 = shaped(rows, depth, low)
    ins, outs = near_in.joined(far_in), near_out.joined(far_out)
    scratch = [pltpu.VMEM((2, depth), wide)] * 7 + [pltpu.VMEM((16, depth), wide)]
    for count in columns:
        scratch += scatter_buffers(block, count)
    results = pl.pallas_call(
        functools.partial(backward_kernel, ins.names(), outs.names()),
        out_shape=tuple(outs.values()),
        in_specs=specs_of(near_in, far_in),
        out_specs=tuple(specs_of(near_out, far_out)),
        scratch_shapes=scratch
        + [dma(32), dma(6 * SCATTER_SENDS), dma(6 * 80), dma(8), dma(8), dma(8), dma(16)],
        compiler_params=pltpu.CompilerParams(
            collective_id=1, has_side_effects=True, vmem_limit_bytes=61 << 20
        ),
        name="backward_pass",
    )(*ins.values())
    return filled(outs.names(), results)


def fits_kernels():
    return lax.axis_size("z") == 4


def factored_step(weights, grads, rows_next, columns_next, row_level, mean_square):
    estimate = rows_next[:, :, None] * columns_next[:, None, :] / row_level[:, None, None]
    return weights - step_rate * jnp.sqrt(mean_square)[:, None, None] * grads * lax.rsqrt(estimate)


def plain_pass(source, target, cotangent, marks, vectors, own_groups):
    core = lax.axis_index("c")
    depth = vectors.shape[1]
    source_half = swap_chips(source)
    flags_half = swap_chips(marks[:source.shape[0]])
    source_all = both_halves(source_half)
    flags_all = both_halves(flags_half)
    masks = swap_chips(marks[source.shape[0] :])
    source_length = masks[None, : 2 * source.shape[0]]
    target_length = masks[None, 2 * source.shape[0] :]
    target_all = both_halves(swap_chips(target))
    cotangent_all = both_halves(swap_chips(cotangent))

    (encoder_attention, encoder_feed, decoder_attention, cross_attention, decoder_feed) = [
        (gather_weights(group, "zyx"), group.shape[1]) for group in own_groups
    ]

    start_rows = jnp.where(
        (flags_all == 1)[:, None],
        vectors[12][None, :],
        jnp.where((flags_all == 2)[:, None], vectors[13][None, :], source_all.astype(wide)),
    )
    first_kept = self_attention_call(
        0, False, source_length, start_rows, encoder_attention, vectors,
    )
    first_part = first_kept[5]
    first_other = other_core(first_part)
    encoder_mid, second_normed, second_hidden, second_slope, second_part, *rest = feed_forward_call(
        2, start_rows, first_part, first_other, encoder_feed, vectors,
    )
    second_other = other_core(second_part)
    third_kept = self_attention_call(6, True, target_length, target_all, decoder_attention, vectors)
    third_part = third_kept[5]
    third_other = other_core(third_part)
    decoder_one, encoder_final, memory_rows, *fourth_kept = cross_attention_call(
        source_length,
        target_all,
        third_part,
        third_other,
        encoder_mid,
        second_part,
        second_other,
        cross_attention,
        vectors,
    )
    fourth_part = fourth_kept[5]
    fourth_kept = fourth_kept[:5]
    decoder_two, fifth_normed, fifth_hidden, fifth_slope, fifth_part = feed_forward_call(
        10, decoder_one, fourth_part, other_core(fourth_part), decoder_feed, vectors
    )
    decoder_three = decoder_two + (fifth_part.astype(wide) + other_core(fifth_part).astype(wide))

    def own_half(rows):
        half = rows.shape[0] // 2
        return lax.dynamic_slice_in_dim(rows, core * half, half, 0)

    decoder_out = swap_chips(own_half(decoder_three).astype(low))

    fifth_back, decoder_feed_terms, grad_three = last_feed_backward_call(
        target_length, cotangent_all, fifth_normed, fifth_hidden, fifth_slope, decoder_feed
    )
    query_back, grad_two, vectors_ten, cross_terms, memory_back, *decoder_feed_grad = attention_backward_call(
        False,
        10,
        source_length,
        grad_three,
        decoder_two,
        fifth_back,
        other_core(fifth_back),
        vectors,
        fourth_kept[0],
        memory_rows,
        *fourth_kept[1:],
        cross_attention,
    )
    query_other = other_core(query_back)
    memory_other = other_core(memory_back)
    third_back, grad_one, vectors_eight, decoder_terms, *cross_grad = attention_backward_call(
        True,
        8,
        target_length,
        grad_two,
        decoder_one,
        query_back,
        query_other,
        vectors,
        third_kept[0],
        None,
        *third_kept[1:5],
        decoder_attention,
    )
    third_back_other = other_core(third_back)
    second_back, encoder_feed_terms, grad_final, vectors_four, *decoder_grad = feed_backward_call(
        4,
        encoder_final,
        memory_back,
        memory_other,
        vectors,
        second_normed,
        second_hidden,
        second_slope,
        encoder_feed,
    )
    first_back, grad_mid, vectors_two, encoder_terms, *encoder_feed_grad = attention_backward_call(
        False,
        2,
        source_length,
        grad_final,
        encoder_mid,
        second_back,
        other_core(second_back),
        vectors,
        first_kept[0],
        None,
        *first_kept[1:5],
        encoder_attention,
    )
    grad_target, vectors_six = finish_call(
        6, grad_one, target_all, third_back, third_back_other, vectors
    )
    target_grad = swap_chips(own_half(grad_target).astype(low)).astype(wide)
    grad_start, vectors_zero = finish_call(
        0, grad_mid, start_rows, first_back, other_core(first_back), vectors
    )
    gap_rows = jnp.sum(jnp.where((flags_all == 1)[:, None], grad_start, 0.0), axis=0, keepdims=True)
    mask_rows = jnp.sum(jnp.where((flags_all == 2)[:, None], grad_start, 0.0), axis=0, keepdims=True)
    source_grad = swap_chips(own_half(grad_start).astype(low)).astype(wide)

    vector_terms = jnp.concatenate(
        [
            vectors_zero,
            vectors_two,
            vectors_four,
            vectors_six,
            vectors_eight,
            vectors_ten,
            gap_rows,
            mask_rows,
            jnp.zeros((114, depth), wide),
        ],
        axis=0,
    )
    vector_terms = vector_terms.T.astype(low)
    grads = [
        scatter_gradient(terms, "xyz")
        for terms in (
            encoder_terms, decoder_terms, cross_terms, encoder_feed_terms, decoder_feed_terms, vector_terms
        )
    ]
    return (decoder_out, source_grad, target_grad, *grads)


def on_device(
    source_embed,
    target_embed,
    out_cotangent,
    row_flags,
    source_mask,
    target_mask,
    attention_weights,
    feed_weights,
    rows_attention,
    columns_attention,
    rows_feed,
    columns_feed,
    vector_params,
    vector_moments,
):
    core = lax.axis_index("c")
    local_rows, half_width = attention_weights.shape[1:]
    half_units = feed_weights.shape[2]
    depth = vector_params.shape[1]
    units_all = 2 * half_units

    def attention_group(block):
        part = attention_weights[4 * block : 4 * block + 4].astype(low)
        return part.transpose(1, 0, 2).reshape(local_rows, 4 * half_width)

    def feed_group(index):
        part = feed_weights[2 * index : 2 * index + 2].astype(low)
        return part.transpose(1, 0, 2).reshape(local_rows, 2 * half_units)

    own_groups = [attention_group(0), feed_group(0), attention_group(1), attention_group(2), feed_group(1)]
    marks = jnp.concatenate([row_flags[0], source_mask[0], target_mask[0]])
    if fits_kernels():
        kept = forward_call(
            source_embed[0], target_embed[0], out_cotangent[0], marks[None], vector_params, own_groups
        )
        back = backward_call(kept, vector_params)
        decoder_out = back.decoder_out
        target_grad = back.target_grad.astype(wide)
        source_grad = back.source_grad.astype(wide)
        decoder_feed_grad, cross_grad, decoder_grad = back.final_5, back.final_4, back.final_3
        encoder_feed_grad, encoder_grad, vector_grad = back.final_2, back.final_1, back.final_vectors
    else:
        (
            decoder_out, source_grad, target_grad,
            encoder_grad, decoder_grad, cross_grad, encoder_feed_grad, decoder_feed_grad, vector_grad,
        ) = plain_pass(source_embed[0], target_embed[0], out_cotangent[0], marks, vector_params, own_groups)
    source_grad = jnp.where((row_flags[0] == 0)[:, None], source_grad, 0.0)
    vector_grad = vector_grad[:, :14].T

    def as_matrices(rows, count):
        return rows.reshape(local_rows, count, -1).transpose(1, 0, 2)

    attention_grad = jnp.concatenate(
        [as_matrices(part, 4) for part in (encoder_grad, decoder_grad, cross_grad)], axis=0
    )
    feed_grad = jnp.concatenate(
        [as_matrices(part, 2) for part in (encoder_feed_grad, decoder_feed_grad)], axis=0
    )

    weight_squares = jnp.concatenate(
        [
            jnp.sum(attention_weights * attention_weights, axis=(1, 2)),
            jnp.sum(feed_weights * feed_weights, axis=(1, 2)),
            jnp.sum(rows_attention, axis=1) * 0.5,
            jnp.sum(rows_feed, axis=1) * 0.5,
        ]
    )
    early_sums = data_sum(tensor_sum(weight_squares))
    scale_attention, scale_feed = early_sums[:12], early_sums[12:16]
    rows_total_attention, rows_total_feed = early_sums[16:28], early_sums[28:32]
    attention_square = attention_grad * attention_grad
    feed_square = feed_grad * feed_grad
    row_sums = tensor_sum(
        jnp.concatenate([jnp.sum(attention_square, axis=2), jnp.sum(feed_square, axis=2)], axis=0)
    )
    column_attention = jnp.sum(attention_square, axis=1)
    column_feed = jnp.sum(feed_square, axis=1)
    square_totals = jnp.sum(row_sums, axis=1)
    column_sums = data_sum(
        jnp.concatenate([column_attention.reshape(-1), column_feed.reshape(-1), square_totals])
    )
    column_attention = column_sums[: column_attention.size].reshape(column_attention.shape)
    column_feed = column_sums[column_attention.size : -16].reshape(column_feed.shape)
    square_totals = column_sums[-16:]
    keep, take = decay_rate, 1.0 - decay_rate
    rows_attention_next = keep * rows_attention + take * row_sums[:12] / depth
    rows_feed_next = keep * rows_feed + take * row_sums[12:] / units_all
    total_attention = keep * rows_total_attention + take * square_totals[:12] / depth
    total_feed = keep * rows_total_feed + take * square_totals[12:] / units_all
    columns_attention_next = keep * columns_attention + take * column_attention / depth
    columns_feed_next = keep * columns_feed + take * column_feed / depth
    attention_updated = factored_step(
        attention_weights,
        attention_grad,
        rows_attention_next,
        columns_attention_next,
        total_attention / depth,
        scale_attention / (depth * depth),
    )
    feed_updated = factored_step(
        feed_weights,
        feed_grad,
        rows_feed_next,
        columns_feed_next,
        total_feed / depth,
        scale_feed / (depth * units_all),
    )
    local_width = vector_moments.shape[1]
    place = (lax.axis_index("z") * lax.axis_size("y") + lax.axis_index("y")) * 2 + core
    vector_local = lax.dynamic_slice_in_dim(vector_params, place * local_width, local_width, 1)
    vector_moments_next = keep * vector_moments + take * vector_grad * vector_grad
    vector_scale = jnp.sqrt(jnp.mean(vector_params * vector_params, axis=1))
    vector_updated = vector_local - step_rate * vector_scale[:, None] * vector_grad * lax.rsqrt(
        vector_moments_next
    )
    return (
        decoder_out[None],
        source_grad[None],
        target_grad[None],
        attention_grad,
        feed_grad,
        vector_grad,
        attention_updated,
        feed_updated,
        vector_updated,
        rows_attention_next,
        columns_attention_next,
        rows_feed_next,
        columns_feed_next,
        vector_moments_next,
        vector_grad[10:12],
    )


def solution(mesh):
    groups = mesh.shape["dp"] // 4
    inner = Mesh(mesh.devices.reshape(groups, 2, 2, 2), ("z", "y", "c", "x"))
    data = ("z", "y", "c")
    rows3, rows2 = P(data, "x", None), P(data, "x")
    matrix, row_spec, column_spec = P(None, data, "x"), P(None, data), P(None, "x")
    return jax.shard_map(
        on_device,
        mesh=inner,
        in_specs=(
            rows3,
            rows3,
            rows3,
            rows2,
            P(data, None),
            P(data, None),
            matrix,
            matrix,
            row_spec,
            column_spec,
            row_spec,
            column_spec,
            P(),
            row_spec,
        ),
        out_specs=(
            rows3,
            rows3,
            rows3,
            matrix,
            matrix,
            row_spec,
            matrix,
            matrix,
            row_spec,
            row_spec,
            column_spec,
            row_spec,
            column_spec,
            row_spec,
            row_spec,
        ),
        check_vma=False,
    )
```

```python
import functools

import jax
import jax.numpy as jnp
from jax import lax
from jax.experimental import pallas as pl
from jax.experimental.pallas import tpu as pltpu
from jax.sharding import Mesh
from jax.sharding import PartitionSpec as P

HEAD_DIM = 64
CHUNK = 256
norm_epsilon = 1e-05
decay_rate = 1.0 - 2.0 ** (-0.8)
step_rate = 0.2
masked_score = -1e30
low = jnp.bfloat16
wide = jnp.float32
MESH = pl.DeviceIdType.MESH


def swap_chips(array):
    return lax.ppermute(array, ("c", "x"), [(0, 0), (1, 2), (2, 1), (3, 3)])


def other_core(array):
    return lax.ppermute(array, "c", [(0, 1), (1, 0)])


def both_halves(own_half):
    received = other_core(own_half)
    first = lax.axis_index("c") == 0
    return jnp.concatenate(
        [jnp.where(first, own_half, received), jnp.where(first, received, own_half)], axis=0
    )


def core_sum(partial_rows):
    sent = partial_rows.astype(low)
    return sent.astype(wide) + other_core(sent).astype(wide)


def ring_next(array):
    size = lax.axis_size("z")
    return lax.ppermute(array, "z", [(i, (i + 1) % size) for i in range(size)])


def holds():
    return lax.axis_index("c") == lax.axis_index("x")


def spread_blocks(blocks, order):
    held = blocks[None, None]
    for axis in order:
        if axis == "x":
            received = lax.ppermute(held, ("c", "x"), [(0, 1), (3, 2)])
            held = jnp.where(holds(), held, received)
        elif axis == "y":
            received = lax.ppermute(held, "y", [(0, 1), (1, 0)])
            first = lax.axis_index("y") == 0
            held = jnp.concatenate(
                [jnp.where(first, held, received), jnp.where(first, received, held)], axis=1
            )
        else:
            size = lax.axis_size("z")
            if size != 4:
                held = lax.all_gather(held, "z", axis=0, tiled=True)
                continue
            place = lax.axis_index("z")
            whole = jnp.zeros((size,) + held.shape[1:], held.dtype)
            moving = held
            for step in range(size):
                where_from = lax.rem(place + size - step, size)
                whole = lax.dynamic_update_slice_in_dim(whole, moving, where_from, 0)
                if step < size - 1:
                    moving = ring_next(moving)
            held = whole
    return held


def reduce_blocks(parts, order):
    held = parts
    for position, axis in enumerate(order):
        final = position == len(order) - 1
        kind = wide if final else low
        if axis == "x":
            received = lax.ppermute(held, ("c", "x"), [(1, 0), (2, 3)])
            held = (held.astype(wide) + received.astype(wide)).astype(kind)
        elif axis == "y":
            mine = lax.axis_index("y")
            sent = lax.dynamic_slice_in_dim(held, 1 - mine, 1, 1)
            kept = lax.dynamic_slice_in_dim(held, mine, 1, 1)
            received = lax.ppermute(sent, "y", [(0, 1), (1, 0)])
            held = (kept.astype(wide) + received.astype(wide)).astype(kind)
        else:
            size = lax.axis_size("z")
            if size != 4:
                held = lax.psum_scatter(held, "z", scatter_dimension=0, tiled=True).astype(kind)
                continue
            place = lax.axis_index("z")
            moving = lax.dynamic_slice_in_dim(held, lax.rem(place + size - 1, size), 1, 0)
            for step in range(1, size):
                received = ring_next(moving)
                kept = lax.dynamic_slice_in_dim(held, lax.rem(place + size - 1 - step, size), 1, 0)
                last = step == size - 1
                moving = (kept.astype(wide) + received.astype(wide)).astype(kind if last else low)
            held = moving
    return held[0, 0]


def gather_weights(blocks, order):
    received = lax.ppermute(blocks, ("c", "x"), [(2, 0), (1, 3)])
    first = lax.axis_index("c") == 0
    both = jnp.concatenate(
        [jnp.where(first, blocks, received), jnp.where(first, received, blocks)], axis=0
    )
    spread = spread_blocks(both, order)
    return spread.reshape(-1, spread.shape[-1])


def scatter_gradient(gradient, order):
    depth, columns = gradient.shape
    z_size, y_size = lax.axis_size("z"), lax.axis_size("y")
    rows = depth // (z_size * y_size)
    total = reduce_blocks(gradient.astype(low).reshape(z_size, y_size, rows, columns), order)
    core = lax.axis_index("c")
    half = rows // 2
    kept = lax.dynamic_slice_in_dim(total, core * half, half, 0)
    sent = lax.dynamic_slice_in_dim(total, (1 - core) * half, half, 0)
    received = lax.ppermute(sent, ("c", "x"), [(0, 2), (3, 1)])
    return jnp.where(holds(), kept, received)


def data_sum(values):
    values = values + other_core(values)
    if lax.axis_size("z") != 4:
        return lax.psum(values, ("z", "y"))
    values = values + lax.ppermute(values, "y", [(0, 1), (1, 0)])
    values = values + lax.ppermute(values, "z", [(0, 1), (1, 0), (2, 3), (3, 2)])
    return values + lax.ppermute(values, "z", [(0, 2), (2, 0), (1, 3), (3, 1)])


def tensor_sum(values):
    return values + lax.ppermute(values, "x", [(0, 1), (1, 0)])


def column_cuts(columns):
    tiles = columns // 128
    first = (tiles * 42 + 50) // 100
    second = (tiles * 36 + 50) // 100
    edges = [0, first * 128, (first + second) * 128, columns]
    return list(zip(edges[:-1], edges[1:]))


def gather_cuts(columns):
    tiles = columns // 128
    first = (tiles * 38 + 50) // 100
    second = (tiles * 39 + 50) // 100
    edges = [0, first * 128, (first + second) * 128, columns]
    return list(zip(edges[:-1], edges[1:]))


def place(name):
    return lax.axis_index(name)


def block_at(which):
    back, same = which
    z = lax.rem(place("z") + 4 - back, 4)
    return z * 2 + (place("y") if same else 1 - place("y"))


def target_of(axis):
    if axis == "z":
        return {"z": lax.rem(place("z") + 1, 4)}
    if axis == "z_back":
        return {"z": lax.rem(place("z") + 3, 4)}
    if axis == "x_home":
        return {"c": place("x"), "x": 1 - place("x")}
    return {axis: 1 - place(axis)}


def greet():
    barrier = pltpu.get_barrier_semaphore()
    targets = [target_of(axis) for axis in ("c", "y", "z", "z_back", "x")]
    targets.append({"c": 1 - place("c"), "x": 1 - place("x")})
    for target in targets:
        pl.semaphore_signal(barrier, inc=1, device_id=target, device_id_type=MESH)
    pl.semaphore_wait(barrier, len(targets))


class Part:
    def __init__(self, array, first):
        self.array, self.first = array, first
        self.at = self

    def __getitem__(self, index):
        return self.array.at[self.first + index]


def here(back):
    return (back, True)


def there(back):
    return (back, False)


class Mover:
    def __init__(self, send_sems):
        self.steps = {True: [], False: []}
        self.sent = {True: [], False: []}
        self.done = 0
        self.send_sems = send_sems

    def send(self, home, source, target, recv_sem, device):
        number = len(self.sent[home])

        def copy():
            return pltpu.make_async_remote_copy(
                src_ref=source(),
                dst_ref=target(),
                send_sem=self.send_sems.at[number],
                recv_sem=recv_sem(),
                device_id=device(),
                device_id_type=MESH,
            )

        self.sent[home].append(copy)
        self.steps[home].append(lambda: copy().start())

    def wait(self, home, target, recv_sem):
        def step():
            pltpu.make_async_remote_copy(
                src_ref=target(),
                dst_ref=target(),
                send_sem=self.send_sems.at[0],
                recv_sem=recv_sem(),
                device_id=target_of("c"),
                device_id_type=MESH,
            ).wait_recv()

        self.steps[home].append(step)

    def local(self, home, step):
        self.steps[home].append(step)

    def run(self, part, parts):
        for home in (True, False):
            steps = self.steps[home]
            chosen = steps[len(steps) * part // parts : len(steps) * (part + 1) // parts]
            if not chosen:
                continue
            wanted = place("c") == place("x")

            @pl.when(wanted if home else jnp.logical_not(wanted))
            def _():
                for step in chosen:
                    step()

    def finish(self):
        for home in (True, False):
            wanted = place("c") == place("x")

            @pl.when(wanted if home else jnp.logical_not(wanted))
            def _():
                for copy in self.sent[home]:
                    copy().wait_send()


class Gather(Mover):
    def __init__(self, own_ref, out_ref, stage_ref, local_sem, send_sems, recv_sems):
        super().__init__(send_sems)
        rows, columns = own_ref.shape
        cuts = gather_cuts(columns)
        (begin_a, end_a), (begin_b, end_b), (begin_c, end_c) = cuts
        first, second, third = 0, 1, 2

        def out_piece(group, which, parity):
            begin, end = cuts[group]
            first_row = (block_at(which) * 2 + parity()) * rows
            return out_ref.at[pl.ds(first_row, rows), pl.ds(begin, end - begin)]

        def out_sem(group, which, parity):
            return recv_sems.at[(group * 8 + block_at(which)) * 2 + parity()]

        def stage_piece(group, which):
            begin, end = cuts[group]
            return stage_ref.at[block_at(which), :, pl.ds(begin, end - begin)]

        def stage_sem(group, which):
            return recv_sems.at[48 + group * 8 + block_at(which)]

        def core():
            return place("c")

        def other():
            return 1 - place("c")

        self_copies = {
            True: lambda: pltpu.make_async_copy(
                own_ref, out_ref.at[pl.ds((block_at(here(0)) * 2 + core()) * rows, rows), :], local_sem
            ),
        }

        def own_piece(group):
            begin, end = cuts[group]
            return own_ref.at[:, pl.ds(begin, end - begin)]

        for home in (True, False):
            arrived = set()

            def plane(group, which):
                if which == here(0):
                    return functools.partial(own_piece, group)
                if home:
                    return functools.partial(out_piece, group, which, core)
                return functools.partial(stage_piece, group, which)

            def plane_target(group, which):
                if home:
                    return (
                        functools.partial(out_piece, group, which, core),
                        functools.partial(out_sem, group, which, core),
                    )
                return (
                    functools.partial(stage_piece, group, which),
                    functools.partial(stage_sem, group, which),
                )

            def plane_send(group, which, axis):
                target, sem = plane_target(group, which)
                self.send(home, plane(group, which), target, sem, functools.partial(target_of, axis))

            def plane_wait(group, which):
                if which == here(0):
                    return
                target, sem = plane_target(group, which)
                self.wait(home, target, sem)
                if home:
                    arrived.add((group, which, "core"))

            def deliver(group, which):
                target = functools.partial(out_piece, group, which, core)
                sem = functools.partial(out_sem, group, which, core)
                source = plane(group, which)
                self.send(home, source, target, sem, functools.partial(target_of, "x_home"))
                if not home:
                    self.send(home, source, target, sem, functools.partial(target_of, "c"))

            def core_send(group, which, name, axis):
                parity = core if name == "core" else other
                if home and which == here(0) and name == "core":
                    source = functools.partial(own_piece, group)
                else:
                    source = functools.partial(out_piece, group, which, parity)
                self.send(
                    home,
                    source,
                    functools.partial(out_piece, group, which, parity),
                    functools.partial(out_sem, group, which, parity),
                    functools.partial(target_of, axis),
                )

            def core_wait(group, which, name):
                if home and which == here(0) and name == "core":
                    return
                if (group, which, name) in arrived:
                    return
                arrived.add((group, which, name))
                parity = core if name == "core" else other
                self.wait(
                    home,
                    functools.partial(out_piece, group, which, parity),
                    functools.partial(out_sem, group, which, parity),
                )

            if home:
                self.local(home, lambda: self_copies[True]().start())
            deliver(third, here(0))
            plane_send(first, here(0), "z")
            plane_send(second, here(0), "z")
            plane_send(first, here(0), "y")
            deliver(second, here(0))
            deliver(first, here(0))
            names = ("core", "other") if home else ("other", "core")
            for name in names:
                core_wait(third, here(0), name)
                core_send(third, here(0), name, "z")
                core_send(third, here(0), name, "y")
            for name in names:
                core_wait(second, here(0), name)
                core_send(second, here(0), name, "y")
            for back in (1, 2, 3):
                plane_wait(first, here(back))
                if back < 3:
                    plane_send(first, here(back), "z")
                plane_send(first, here(back), "y")
                plane_wait(second, here(back))
                if back < 3:
                    plane_send(second, here(back), "z")
                deliver(second, here(back))
                deliver(first, here(back))
                plane_wait(first, there(back - 1))
                deliver(first, there(back - 1))
                if back == 1:
                    for name in names:
                        core_wait(third, there(0), name)
                        core_send(third, there(0), name, "z")
                for which in (here(back), there(back)):
                    for name in names:
                        core_wait(third, which, name)
                        if back < 3:
                            core_send(third, which, name, "z")
                for name in names:
                    core_wait(second, here(back), name)
                    core_send(second, here(back), name, "y")
            plane_wait(first, there(3))
            deliver(first, there(3))
            for group in (third, second, first):
                for back in range(4):
                    for which in (here(back), there(back)):
                        for name in ("core", "other"):
                            core_wait(group, which, name)
            if home:
                self.local(home, lambda: self_copies[True]().wait())


GATHER_SENDS = 64


class Scatter(Mover):
    def __init__(self, buffers, final, send_sems, recv_sems):
        super().__init__(send_sems)
        total, stages, x_ins, z_ins = buffers[0], buffers[1:4], buffers[4:7], buffers[7:9]
        ya_in, yb_in, zc_in, yc_in = buffers[9:]
        rows = total.shape[1] // 2
        columns = total.shape[2]
        cuts = column_cuts(columns)
        first, second, third = 0, 1, 2
        widths = [end - begin for begin, end in cuts]

        def part(group):
            begin, end = cuts[group]
            return pl.ds(begin, end - begin)

        def core_piece(group, which, parity=None):
            if parity is None:
                return total.at[block_at(which), :, part(group)]
            return total.at[block_at(which), pl.ds(parity() * rows, rows), part(group)]

        def slot_of(which):
            return which[0] + (0 if which[1] else 4)

        def x_piece(group, which):
            return x_ins[group].at[slot_of(which)]

        def stage_piece(group, which):
            return stages[group].at[slot_of(which)]

        def sem(number):
            return lambda: recv_sems.at[number]

        def core():
            return place("c")

        def other():
            return 1 - place("c")

        def add_rows(held_of, came_of, count, final_part=None):
            def step():
                held, came = held_of(), came_of()

                @pl.loop(0, count // 16)
                def _(number):
                    at = pl.ds(pl.multiple_of(number * 16, 16), 16)
                    if final_part is None:
                        held[at, :] = held[at, :] + came[at, :]
                    else:
                        final[at, final_part] = held[at, :].astype(wide) + came[at, :].astype(wide)

            return step

        for home in (True, False):

            def plane(group, which):
                if home:
                    return functools.partial(core_piece, group, which, core)
                return functools.partial(stage_piece, group, which)

            def x_sends(group, which):
                if widths[group] == 0:
                    return
                number = group * 8 + slot_of(which)
                if home:
                    self.send(
                        home,
                        functools.partial(core_piece, group, which, other),
                        functools.partial(stage_piece, group, which),
                        sem(24 + number),
                        functools.partial(target_of, "c"),
                    )
                    return
                for parity in (0, 1):
                    self.send(
                        home,
                        functools.partial(core_piece, group, which, functools.partial(parity_value, parity)),
                        functools.partial(x_piece, group, which),
                        sem(number),
                        functools.partial(home_core, parity),
                    )

            def x_add(group, which, last=False):
                if widths[group] == 0:
                    return
                number = group * 8 + slot_of(which)
                if not home:
                    self.wait(home, functools.partial(stage_piece, group, which), sem(24 + number))
                self.wait(home, functools.partial(x_piece, group, which), sem(number))
                self.local(
                    home,
                    add_rows(
                        plane(group, which),
                        functools.partial(x_piece, group, which),
                        rows,
                        part(group) if last else None,
                    ),
                )

            def z_slot(group, back):
                return lambda: z_ins[group].at[back]

            def z_send(group, back):
                if widths[group] == 0:
                    return
                self.send(
                    home,
                    plane(group, here(back)),
                    z_slot(group, back - 1),
                    sem(60 + group * 4 + back - 1),
                    functools.partial(target_of, "z_back"),
                )

            def z_add(group, back):
                if widths[group] == 0:
                    return
                self.wait(home, z_slot(group, back), sem(60 + group * 4 + back))
                self.local(
                    home,
                    add_rows(
                        plane(group, here(back)),
                        z_slot(group, back),
                        rows,
                        part(group) if back == 0 else None,
                    ),
                )

            def ya_slot(back):
                return lambda: ya_in.at[back]

            def yb_slot(back):
                return lambda: yb_in.at[back]

            def zc_slot(which):
                back, same = which
                return lambda: zc_in.at[back + (0 if same else 3)]

            def zc_send(which):
                back, same = which
                self.send(
                    home,
                    functools.partial(core_piece, third, which),
                    zc_slot((back - 1, same)),
                    sem(72 + back - 1 + (0 if same else 3)),
                    functools.partial(target_of, "z_back"),
                )

            def zc_add(which):
                back, same = which
                self.wait(home, zc_slot(which), sem(72 + back + (0 if same else 3)))
                self.local(
                    home,
                    add_rows(functools.partial(core_piece, third, which), zc_slot(which), 2 * rows),
                )

            zc_send(there(3))
            zc_send(here(3))
            for back in (3, 2, 1, 0):
                if widths[second]:
                    self.send(
                        home,
                        functools.partial(core_piece, second, there(back)),
                        yb_slot(back),
                        sem(52 + back),
                        functools.partial(target_of, "y"),
                    )
                if back > 1:
                    x_sends(first, there(back))
                    x_sends(first, here(back))
            for turn in range(7):
                back = 3 - turn
                if back >= 0:
                    if widths[second]:
                        self.wait(home, yb_slot(back), sem(52 + back))
                        self.local(
                            home,
                            add_rows(
                                functools.partial(core_piece, second, here(back)), yb_slot(back), 2 * rows
                            ),
                        )
                    x_sends(second, here(back))
                    if back > 1:
                        x_sends(first, there(back - 2))
                        x_sends(first, here(back - 2))
                    if back < 3:
                        for which in (there(back), here(back)):
                            zc_add(which)
                            if back > 0:
                                zc_send(which)
                            elif not which[1]:
                                self.send(
                                    home,
                                    functools.partial(core_piece, third, there(0)),
                                    lambda: yc_in.at[...],
                                    sem(56),
                                    functools.partial(target_of, "y"),
                                )
                    x_add(first, there(back))
                    if widths[first]:
                        self.send(
                            home,
                            plane(first, there(back)),
                            ya_slot(back),
                            sem(48 + back),
                            functools.partial(target_of, "y"),
                        )
                if back == -1:
                    self.wait(home, lambda: yc_in.at[...], sem(56))
                    self.local(
                        home,
                        add_rows(
                            functools.partial(core_piece, third, here(0)),
                            lambda: yc_in.at[...],
                            2 * rows,
                        ),
                    )
                    x_sends(third, here(0))
                back = 4 - turn
                if 0 <= back < 4:
                    x_add(first, here(back))
                    if widths[first]:
                        self.wait(home, ya_slot(back), sem(48 + back))
                        self.local(home, add_rows(plane(first, here(back)), ya_slot(back), rows))
                    if back == 3:
                        z_send(first, back)
                back = 5 - turn
                if 0 <= back < 3:
                    z_add(first, back)
                    if back > 0:
                        z_send(first, back)
                if 0 <= back < 4:
                    x_add(second, here(back))
                    if back == 3:
                        z_send(second, back)
                back = 6 - turn
                if 0 <= back < 3:
                    z_add(second, back)
                    if back > 0:
                        z_send(second, back)
            x_add(third, here(0), last=True)


def parity_value(parity):
    return parity


def home_core(parity):
    return {"c": parity, "x": place("c")}


SCATTER_SENDS = 48


SCATTER_BUFFERS = 13


def scatter_buffers(rows, columns):
    first, second, third = [max(end - begin, 128) for begin, end in column_cuts(columns)]
    return [
        pltpu.VMEM((8, 2 * rows, columns), low),
        pltpu.VMEM((8, rows, first), low),
        pltpu.VMEM((4, rows, second), low),
        pltpu.VMEM((1, rows, third), low),
        pltpu.VMEM((8, rows, first), low),
        pltpu.VMEM((4, rows, second), low),
        pltpu.VMEM((1, rows, third), low),
        pltpu.VMEM((3, rows, first), low),
        pltpu.VMEM((3, rows, second), low),
        pltpu.VMEM((4, rows, first), low),
        pltpu.VMEM((4, 2 * rows, second), low),
        pltpu.VMEM((6, 2 * rows, third), low),
        pltpu.VMEM((2 * rows, third), low),
    ]

def ride_call(body, operands, in_specs, outs, scratch, rider, name):
    def kernel(*refs):
        body(Nothing(), *refs)

    return pl.pallas_call(
        kernel,
        out_shape=tuple(outs),
        in_specs=list(in_specs),
        scratch_shapes=list(scratch),
        compiler_params=pltpu.CompilerParams(vmem_limit_bytes=60 << 20),
        name=name,
    )(*operands)


def whole():
    return pl.BlockSpec(memory_space=pltpu.VMEM)


def weight_spec(weights):
    return pl.BlockSpec(memory_space=pltpu.VMEM)


def shaped(rows, columns, kind):
    return jax.ShapeDtypeStruct((rows, columns), kind)


def dot_nn(left, right):
    return lax.dot_general(left, right, (((1,), (0,)), ((), ())), preferred_element_type=wide)


def dot_nt(left, right):
    return lax.dot_general(left, right, (((1,), (1,)), ((), ())), preferred_element_type=wide)


def turned(block):
    size = block.shape[1]
    row = lax.broadcasted_iota(jnp.int32, (size, size), 0)
    column = lax.broadcasted_iota(jnp.int32, (size, size), 1)
    return dot_nt((row == column).astype(wide).astype(low), block).astype(low)


def turn_into(target, source):
    rows, columns = source.shape
    for at in range(0, columns, 256):
        wide_part = min(256, columns - at)
        target[at : at + wide_part, :] = turned(source[:, at : at + wide_part])


def centre_rows(values):
    centred = values - jnp.mean(values, axis=-1, keepdims=True)
    spread = jnp.mean(centred * centred, axis=-1, keepdims=True)
    return centred * lax.rsqrt(spread + norm_epsilon)


def norm_back(x, gain, grads):
    centred = x - jnp.mean(x, axis=-1, keepdims=True)
    scale = lax.rsqrt(jnp.mean(centred * centred, axis=-1, keepdims=True) + norm_epsilon)
    unit = centred * scale
    inner = grads * gain
    by_unit = inner * unit
    back = scale * (
        inner
        - jnp.mean(inner, axis=-1, keepdims=True)
        - unit * jnp.mean(by_unit, axis=-1, keepdims=True)
    )
    return back, jnp.sum(grads * unit, axis=0, keepdims=True), jnp.sum(grads, axis=0, keepdims=True)


def residual_prologue(norm_row, previous_ref, x_ref, own_ref, other_ref, vec_ref, grad_out, low_ref, vec_out, ticks=None):
    ticks = ticks or Nothing()
    steps = x_ref.shape[0] // CHUNK
    ticks.begin(steps)
    gain = vec_ref[norm_row : norm_row + 1, :]
    vec_out[...] = jnp.zeros_like(vec_out)

    @pl.loop(0, x_ref.shape[0] // CHUNK)
    def _(step):
        at = pl.ds(pl.multiple_of(step * CHUNK, CHUNK), CHUNK)
        ticks.in_loop(step, steps, 0, 1, 0)
        grads = own_ref[at, :].astype(wide) + other_ref[at, :].astype(wide)
        back, by_gain, by_shift = norm_back(x_ref[at, :].astype(wide), gain, grads)
        if previous_ref is not None:
            back = back + previous_ref[at, :].astype(wide)
        if grad_out is not None:
            grad_out[at, :] = back.astype(grad_out.dtype)
        if low_ref is not None:
            low_ref[at, :] = back.astype(low)
        vec_out[0:1, :] += by_gain
        vec_out[1:2, :] += by_shift


def erf_ratio(values):
    x = jnp.clip(values, -4.0, 4.0)
    square = x * x
    top = jnp.full_like(square, -2.72614225801306e-10)
    for term in (
        2.77068142495902e-08,
        -2.10102402082508e-06,
        -5.69250639462346e-05,
        -7.34990630326855e-04,
        -2.95459980854025e-03,
        -1.60960333262415e-02,
    ):
        top = top * square + term
    low_part = jnp.full_like(square, -1.45660718464996e-05)
    for term in (
        -2.13374055278905e-04,
        -1.68282697438203e-03,
        -7.37332916720468e-03,
        -1.42647390514189e-02,
    ):
        low_part = low_part * square + term
    return x * top / low_part


def gelu_pair(before):
    phi_whole = 0.5 + 0.5 * erf_ratio(before * 0.7071067811865476)
    density = jnp.exp(before * before * -0.5) * 0.3989422804014327
    return before * phi_whole, phi_whole + before * density


def chunks(rows):
    return range(0, rows, CHUNK)


def feed_forward_kernel(
    rows_norm, ticks, x_ref, own_ref, other_ref, w_ref, vec_ref, x_out, normed_out, hidden_out, slope_out, part_out
):
    units = w_ref.shape[1] // 2
    steps = x_ref.shape[0] // CHUNK
    pieces = units // 512
    ticks.begin(steps * pieces)
    gain = vec_ref[rows_norm : rows_norm + 1, :]
    shift = vec_ref[rows_norm + 1 : rows_norm + 2, :]

    @pl.loop(0, x_ref.shape[0] // CHUNK)
    def _(step):
        at = pl.ds(pl.multiple_of(step * CHUNK, CHUNK), CHUNK)
        x = x_ref[at, :] + (own_ref[at, :].astype(wide) + other_ref[at, :].astype(wide))
        x_out[at, :] = x
        normed = (centre_rows(x) * gain + shift).astype(low)
        normed_out[at, :] = normed
        part = jnp.zeros((CHUNK, x.shape[1]), wide)
        for begin in range(0, units, 512):
            ticks.in_loop(step, steps, 0, pieces, begin // 512)
            before = dot_nn(normed, w_ref[:, begin : begin + 512])
            value, slope = gelu_pair(before)
            hidden = value.astype(low)
            hidden_out[at, begin : begin + 512] = hidden
            slope_out[at, begin : begin + 512] = slope.astype(low)
            part = part + dot_nt(hidden, w_ref[:, units + begin : units + begin + 512])
        part_out[at, :] = part.astype(low)


def feed_forward_call(rows_norm, x, own, other, weights, vectors, rider=None):
    rows, depth = x.shape
    units = weights[1] // 2
    return ride_call(
        functools.partial(feed_forward_kernel, rows_norm),
        [x, own, other, weights[0], vectors],
        [whole(), whole(), whole(), weight_spec(weights), whole()],
        [
            shaped(rows, depth, wide),
            shaped(rows, depth, low),
            shaped(rows, units, low),
            shaped(rows, units, low),
            shaped(rows, depth, low),
        ],
        [],
        rider,
        "feed_forward",
    )


def store_grad(target, begin, value):
    value = value.astype(low)
    span = slice(begin, begin + value.shape[1])
    if len(target.shape) == 2:
        target[:, span] = value
    else:
        target[:, :, span] = value.reshape(target.shape[0], target.shape[1], value.shape[1])


def feed_backward_ticks(rows, units):
    return 1 + rows // CHUNK * (units // 512) + units // 256


def feed_backward_body(ticks, normed_ref, hidden_ref, slope_in, w_ref, part_out, grad_out, low_ref, slope_ref, turned_ref, turned_low):
    rows, depth = low_ref.shape
    units = w_ref.shape[1] // 2
    steps = rows // CHUNK
    pieces = units // 512
    offset = 1 + steps * pieces
    ticks(0)
    turn_into(turned_low, low_ref)
    turn_into(turned_ref, normed_ref)

    @pl.loop(0, rows // CHUNK)
    def _(step):
        at = pl.ds(pl.multiple_of(step * CHUNK, CHUNK), CHUNK)
        grads = low_ref[at, :]
        part = jnp.zeros((CHUNK, depth), wide)
        for begin in range(0, units, 512):
            ticks.in_loop(step, steps, 1, pieces, begin // 512)
            grad = dot_nn(grads, w_ref[:, units + begin : units + begin + 512])
            grad = (grad * slope_in[at, begin : begin + 512].astype(wide)).astype(low)
            slope_ref[at, begin : begin + 512] = grad
            part = part + dot_nt(grad, w_ref[:, begin : begin + 512])
        part_out[at, :] = part.astype(low)

    for begin in range(0, units, 256):
        ticks(offset + begin // 256)
        store_grad(grad_out, begin, dot_nn(turned_ref[...], slope_ref[:, begin : begin + 256]))
        store_grad(
            grad_out, units + begin, dot_nn(turned_low[...], hidden_ref[:, begin : begin + 256])
        )


def feed_backward_scratch(rows, depth, units):
    return [
        pltpu.VMEM((rows, depth), low),
        pltpu.VMEM((rows, units), low),
        pltpu.VMEM((depth, rows), low),
        pltpu.VMEM((depth, rows), low),
    ]


def last_feed_backward_kernel(
    ticks, length_ref, cotangent_ref, normed_ref, hidden_ref, slope_in, w_ref, part_out, grad_out, low_ref, *rest
):
    rows, depth = cotangent_ref.shape

    @pl.loop(0, rows // CHUNK)
    def _(step):
        first_row = pl.multiple_of(step * CHUNK, CHUNK)
        at = pl.ds(first_row, CHUNK)
        rows_here = cotangent_ref[at, :].astype(wide)
        kept = column_of(length_ref, first_row) > 0
        low_ref[at, :] = jnp.where(kept, rows_here, 0.0).astype(low)

    feed_backward_body(ticks, normed_ref, hidden_ref, slope_in, w_ref, part_out, grad_out, low_ref, *rest)


def last_feed_backward_call(length, cotangent, normed, hidden, slope, weights, rider=None):
    rows, depth = cotangent.shape
    units = hidden.shape[1]
    return ride_call(
        last_feed_backward_kernel,
        [length, cotangent, normed, hidden, slope, weights[0]],
        [whole()] + [whole()] * 4 + [weight_spec(weights)],
        [shaped(rows, depth, low), shaped(depth, 2 * units, low), shaped(rows, depth, low)],
        feed_backward_scratch(rows, depth, units)[1:],
        rider,
        "last_feed_backward",
    )


def feed_backward_kernel(
    norm_row, ticks, x_ref, own_ref, other_ref, vec_ref, normed_ref, hidden_ref, slope_in, w_ref,
    part_out, grad_out, g_out, vec_out, low_ref, *rest
):
    units = w_ref.shape[1] // 2
    ticks.begin(1 + x_ref.shape[0] // CHUNK * (units // 512) + units // 256)
    residual_prologue(norm_row, None, x_ref, own_ref, other_ref, vec_ref, g_out, low_ref, vec_out)
    feed_backward_body(ticks, normed_ref, hidden_ref, slope_in, w_ref, part_out, grad_out, low_ref, *rest)


def feed_backward_call(norm_row, x, own, other, vectors, normed, hidden, slope, weights, rider=None):
    rows, depth = x.shape
    units = hidden.shape[1]
    return ride_call(
        functools.partial(feed_backward_kernel, norm_row),
        [x, own, other, vectors, normed, hidden, slope, weights[0]],
        [whole()] * 7 + [weight_spec(weights)],
        [
            shaped(rows, depth, low),
            shaped(depth, 2 * units, low),
            shaped(rows, depth, wide),
            shaped(2, depth, wide),
        ],
        feed_backward_scratch(rows, depth, units),
        rider,
        "feed_backward",
    )


def half_lanes(shape):
    return lax.broadcasted_iota(jnp.int32, shape, 1) < 64


def one_head(pair, head):
    first = half_lanes(pair.shape)
    zero = jnp.zeros_like(pair)
    return jnp.where(first, pair, zero) if head == 0 else jnp.where(first, zero, pair)


def key_bias(keys, mask_row, first_row, causal, rows):
    allowed = jnp.where(mask_row[...] > 0, 0.0, masked_score)
    if not causal:
        return allowed
    column = lax.broadcasted_iota(jnp.int32, (rows, keys), 1)
    row = first_row + lax.broadcasted_iota(jnp.int32, (rows, keys), 0)
    return jnp.where(column <= row, allowed, masked_score)


def attend_chunk(tick, first_row, length, causal, q_ref, kv_ref, w_ref, attended_out, totals_out, part_out):
    width = q_ref.shape[1]
    keys = kv_ref.shape[0]
    at = pl.ds(first_row, CHUNK)
    bias = key_bias(keys, length, first_row, causal, CHUNK)
    lane = lax.broadcasted_iota(jnp.int32, (CHUNK, 128), 1)
    totals = jnp.zeros((CHUNK, 128), wide)
    for begin in range(0, width, 128):
        tick(begin // 128)
        pair = q_ref[at, begin : begin + 128]
        key_pair = kv_ref[:, begin : begin + 128]
        value_pair = kv_ref[:, width + begin : width + begin + 128]
        results = []
        for head in range(2):
            scores = dot_nt(one_head(pair, head), key_pair) + bias
            peak = jnp.max(scores, axis=-1, keepdims=True)
            weights = jnp.exp(scores - peak)
            total = jnp.sum(weights, axis=-1, keepdims=True)
            results.append(dot_nn(weights.astype(low), value_pair) * (1.0 / total))
            totals = jnp.where(lane == begin // 64 + head, peak + jnp.log(total), totals)
        attended_out[at, begin : begin + 128] = jnp.where(
            lane < 64, results[0], results[1]
        ).astype(low)
    totals_out[at, :] = totals
    part_out[at, :] = dot_nt(attended_out[at, :], w_ref[:, 3 * width :]).astype(low)


def self_attention_kernel(
    rows_norm, causal, ticks, length_ref, x_ref, w_ref, vec_ref, normed_out, q_out, kv_out, attended_out, totals_out, part_out
):
    width = w_ref.shape[1] // 4
    gain = vec_ref[rows_norm : rows_norm + 1, :]
    shift = vec_ref[rows_norm + 1 : rows_norm + 2, :]
    steps = x_ref.shape[0] // CHUNK
    pairs = width // 128
    ticks.begin(steps * (pairs + 1))

    @pl.loop(0, steps)
    def _(step):
        ticks.in_loop(step, steps, 0, 1, 0)
        at = pl.ds(pl.multiple_of(step * CHUNK, CHUNK), CHUNK)
        normed = (centre_rows(x_ref[at, :].astype(wide)) * gain + shift).astype(low)
        normed_out[at, :] = normed
        q_out[at, :] = (dot_nn(normed, w_ref[:, :width]).astype(low).astype(wide) * 0.125).astype(low)
        kv_out[at, :] = dot_nn(normed, w_ref[:, width : 3 * width]).astype(low)

    length = length_ref

    @pl.loop(0, steps)
    def _(step):
        attend_chunk(
            functools.partial(ticks.in_loop, step, steps, steps, pairs),
            pl.multiple_of(step * CHUNK, CHUNK), length, causal, q_out, kv_out, w_ref, attended_out, totals_out, part_out
        )


def self_attention_call(rows_norm, causal, length, x, weights, vectors, rider=None):
    rows, depth = x.shape
    width = weights[1] // 4
    return ride_call(
        functools.partial(self_attention_kernel, rows_norm, causal),
        [length, x, weights[0], vectors],
        [whole(), whole(), weight_spec(weights), whole()],
        [
            shaped(rows, depth, low),
            shaped(rows, width, low),
            shaped(rows, 2 * width, low),
            shaped(rows, width, low),
            shaped(rows, 128, wide),
            shaped(rows, depth, low),
        ],
        [],
        rider,
        "self_attention",
    )


def cross_attention_kernel(
    ticks, length_ref, x_ref, own_ref, other_ref, mid_ref, mid_own, mid_other, w_ref, vec_ref,
    x_out, final_out, memory_out, normed_out, q_out, kv_out, attended_out, totals_out, part_out,
):
    width = w_ref.shape[1] // 4
    first_steps = mid_ref.shape[0] // CHUNK
    steps = x_ref.shape[0] // CHUNK
    pairs = width // 128
    ticks.begin(first_steps + steps * (pairs + 1))

    @pl.loop(0, first_steps)
    def _(step):
        ticks.in_loop(step, first_steps, 0, 1, 0)
        at = pl.ds(pl.multiple_of(step * CHUNK, CHUNK), CHUNK)
        x = mid_ref[at, :] + (mid_own[at, :].astype(wide) + mid_other[at, :].astype(wide))
        final_out[at, :] = x
        memory = (centre_rows(x) * vec_ref[4:5, :] + vec_ref[5:6, :]).astype(low)
        memory_out[at, :] = memory
        kv_out[at, :] = dot_nn(memory, w_ref[:, width : 3 * width]).astype(low)

    @pl.loop(0, steps)
    def _(step):
        ticks.in_loop(step, steps, first_steps, 1, 0)
        at = pl.ds(pl.multiple_of(step * CHUNK, CHUNK), CHUNK)
        x = x_ref[at, :].astype(wide) + (own_ref[at, :].astype(wide) + other_ref[at, :].astype(wide))
        x_out[at, :] = x
        normed = (centre_rows(x) * vec_ref[8:9, :] + vec_ref[9:10, :]).astype(low)
        normed_out[at, :] = normed
        q_out[at, :] = (dot_nn(normed, w_ref[:, :width]).astype(low).astype(wide) * 0.125).astype(low)

    length = length_ref

    @pl.loop(0, steps)
    def _(step):
        attend_chunk(
            functools.partial(ticks.in_loop, step, steps, first_steps + steps, pairs),
            pl.multiple_of(step * CHUNK, CHUNK), length, False, q_out, kv_out, w_ref, attended_out, totals_out, part_out
        )


def cross_attention_call(length, x, own, other, mid, mid_own, mid_other, weights, vectors, rider=None):
    rows, depth = x.shape
    keys = mid.shape[0]
    width = weights[1] // 4
    return ride_call(
        cross_attention_kernel,
        [length, x, own, other, mid, mid_own, mid_other, weights[0], vectors],
        [whole()] + [whole()] * 6 + [weight_spec(weights), whole()],
        [
            shaped(rows, depth, wide),
            shaped(keys, depth, wide),
            shaped(keys, depth, low),
            shaped(rows, depth, low),
            shaped(rows, width, low),
            shaped(keys, 2 * width, low),
            shaped(rows, width, low),
            shaped(rows, 128, wide),
            shaped(rows, depth, low),
        ],
        [],
        rider,
        "cross_attention",
    )


def attention_backward_kernel(
    causal, cross, norm_row, ticks, length_ref, previous_ref, x_ref, own_ref, other_ref, vec_ref,
    normed_ref, source_ref, q_ref, kv_ref, attended_ref, totals_ref, w_ref, *rest
):
    outs = 5 if cross else 4
    part_out, g_out, vec_out, grad_out = rest[:4]
    source_part_out = rest[4] if cross else None
    low_ref, scratch = rest[outs], rest[outs + 1 :]
    residual_prologue(norm_row, previous_ref, x_ref, own_ref, other_ref, vec_ref, g_out, low_ref, vec_out)
    attention_backward_main(
        causal, cross, ticks, length_ref, low_ref, normed_ref, source_ref, q_ref, kv_ref, attended_ref, totals_ref,
        w_ref, part_out, grad_out, source_part_out, *scratch,
    )


def attention_backward_main(
    causal, cross, ticks, length, low_ref, normed_ref, source_ref, q_ref, kv_ref, attended_ref, totals_ref, w_ref,
    part_out, grad_out, source_part_out, grad_q, grad_kv, turned_k, turned_v, turned_low, turned_normed, *rest
):
    turned_source = rest[0] if cross else turned_normed
    rows, depth = low_ref.shape
    keys = kv_ref.shape[0]
    width = q_ref.shape[1]
    steps = rows // CHUNK
    pairs = width // 128
    key_steps = keys // CHUNK
    after = 1 + steps * pairs
    last = after + key_steps
    ticks.begin(last + 5)
    ticks(0)
    turned_k[...] = jnp.zeros_like(turned_k)
    turned_v[...] = jnp.zeros_like(turned_v)

    @pl.loop(0, rows // CHUNK)
    def _(step):
        first_row = pl.multiple_of(step * CHUNK, CHUNK)
        at = pl.ds(first_row, CHUNK)
        grad_attended = dot_nn(low_ref[at, :], w_ref[:, 3 * width :]).astype(low)
        bias = key_bias(keys, length, first_row, causal, CHUNK)
        lane = lax.broadcasted_iota(jnp.int32, (CHUNK, 128), 1)
        totals = totals_ref[at, :]
        for begin in range(0, width, 128):
            ticks.in_loop(step, steps, 1, pairs, begin // 128)
            pair = q_ref[at, begin : begin + 128]
            key_pair = kv_ref[:, begin : begin + 128]
            value_pair = kv_ref[:, width + begin : width + begin + 128]
            grad_pair = grad_attended[:, begin : begin + 128]
            pair_turned = turned(pair)
            grad_turned = turned(grad_pair)
            results = []
            for head in range(2):
                number = begin // 64 + head
                total = jnp.sum(jnp.where(lane == number, totals, 0.0), axis=-1, keepdims=True)
                scores = dot_nt(one_head(pair, head), key_pair) + bias
                weights = jnp.exp(scores - total)
                grad_weights = dot_nt(one_head(grad_pair, head), value_pair)
                row_dot = jnp.sum(weights * grad_weights, axis=-1, keepdims=True)
                grad_scores = (weights * (grad_weights - row_dot)).astype(low)
                results.append(dot_nn(grad_scores, key_pair))
                span = slice(begin + 64 * head, begin + 64 * head + 64)
                local = slice(64 * head, 64 * head + 64)
                turned_k[span, :] += dot_nn(pair_turned[local, :], grad_scores)
                turned_v[span, :] += dot_nn(grad_turned[local, :], weights.astype(low))
            grad_q[at, begin : begin + 128] = (
                jnp.where(lane < 64, results[0], results[1]) * 0.125
            ).astype(low)
        if cross:
            part_out[at, :] = dot_nt(grad_q[at, :], w_ref[:, :width]).astype(low)

    grad_kv[:, :width] = turned(turned_k[...].astype(low))
    grad_kv[:, width:] = turned(turned_v[...].astype(low))

    @pl.loop(0, keys // CHUNK)
    def _(step):
        ticks.in_loop(step, key_steps, after, 1, 0)
        at = pl.ds(pl.multiple_of(step * CHUNK, CHUNK), CHUNK)
        from_source = dot_nt(grad_kv[at, :], w_ref[:, width : 3 * width])
        if cross:
            source_part_out[at, :] = from_source.astype(low)
        else:
            from_query = dot_nt(grad_q[at, :], w_ref[:, :width])
            part_out[at, :] = (from_source + from_query).astype(low)

    ticks(last)
    turn_into(turned_low, low_ref)
    turn_into(turned_normed, normed_ref)
    if cross:
        turn_into(turned_source, source_ref)
    ticks(last + 1)
    store_grad(grad_out, 0, dot_nn(turned_normed[...], grad_q[...]))
    ticks(last + 2)
    store_grad(grad_out, width, dot_nn(turned_source[...], grad_kv[:, :width]))
    ticks(last + 3)
    store_grad(grad_out, 2 * width, dot_nn(turned_source[...], grad_kv[:, width:]))
    ticks(last + 4)
    store_grad(grad_out, 3 * width, dot_nn(turned_low[...], attended_ref[...]))


def attention_backward_scratch(rows, keys, depth, width, cross):
    scratch = [
        pltpu.VMEM((rows, depth), low),
        pltpu.VMEM((rows, width), low),
        pltpu.VMEM((keys, 2 * width), low),
        pltpu.VMEM((width, keys), wide),
        pltpu.VMEM((width, keys), wide),
        pltpu.VMEM((depth, rows), low),
        pltpu.VMEM((depth, rows), low),
    ]
    if cross:
        scratch.append(pltpu.VMEM((depth, keys), low))
    return scratch


def attention_backward_call(
    causal, norm_row, length, previous, x, own, other, vectors, normed, source, q, kv, attended, totals, weights,
    rider=None,
):
    cross = source is not None
    rows, depth = x.shape
    keys = kv.shape[0]
    width = q.shape[1]
    outs = [
        shaped(rows, depth, low),
        shaped(rows, depth, wide),
        shaped(2, depth, wide),
        shaped(depth, 4 * width, low),
    ]
    if cross:
        outs.append(shaped(keys, depth, low))
    scratch = attention_backward_scratch(rows, keys, depth, width, cross)
    operands = [length, previous, x, own, other, vectors, normed]
    if cross:
        operands.append(source)
    operands += [q, kv, attended, totals, weights[0]]

    def body(ticks, *refs):
        if not cross:
            refs = refs[:7] + (None,) + refs[7:]
        attention_backward_kernel(causal, cross, norm_row, ticks, *refs)

    return ride_call(
        body,
        operands,
        [whole()] + [whole()] * (len(operands) - 2) + [weight_spec(weights)],
        outs,
        scratch,
        rider,
        "attention_backward",
    )


def finish_kernel(norm_row, previous_ref, x_ref, own_ref, other_ref, vec_ref, g_out, vec_out):
    residual_prologue(norm_row, previous_ref, x_ref, own_ref, other_ref, vec_ref, g_out, None, vec_out)


def finish_call(norm_row, previous, x, own, other, vectors):
    rows, depth = x.shape
    return pl.pallas_call(
        functools.partial(finish_kernel, norm_row),
        out_shape=(shaped(rows, depth, wide), shaped(2, depth, wide)),
        compiler_params=pltpu.CompilerParams(vmem_limit_bytes=40 << 20),
        name="finish_norm",
    )(previous, x, own, other, vectors)


class Stream:
    def __init__(self):
        self.steps = {True: [], False: []}
        self.begins, self.ends = [], []
        self.position = {True: 0, False: 0}
        self.movers = []

    def add(self, mover, overlap=0.0):
        self.movers.append(mover)
        begin, end = {}, {}
        for home in (True, False):
            had, new = self.steps[home], mover.steps[home]
            shared = min(int(len(new) * overlap), len(had))
            kept = len(had) - shared
            merged = had[:kept]
            for one, two in zip(had[kept:], new[:shared]):
                merged += [one, two]
            merged += new[shared:]
            for mark in self.ends:
                if mark[home] > kept:
                    mark[home] = kept + 2 * (mark[home] - kept)
            self.steps[home] = merged
            begin[home], end[home] = kept, len(merged)
        self.begins.append(begin)
        self.ends.append(end)

    def between(self, one, two, share):
        return {home: one[home] + int((two[home] - one[home]) * share) for home in (True, False)}

    def plan(self, marks, shares=(1.0,)):
        windows, done, start = [], 0.0, dict(self.position)
        for share in shares:
            done += share / sum(shares)
            end = {
                home: max(
                    self.position[home],
                    start[home] + round((marks[home] - start[home]) * done),
                )
                for home in (True, False)
            }
            windows.append(Window(self, dict(self.position), end))
            self.position = end
        return windows

    def run(self, chosen):
        for home in (True, False):
            if not chosen[home]:
                continue
            wanted = place("c") == place("x")

            @pl.when(wanted if home else jnp.logical_not(wanted))
            def _():
                for step in chosen[home]:
                    step()

    def finish(self):
        for mover in self.movers:
            mover.finish()


class Window:
    def __init__(self, stream, start, end):
        self.stream, self.start, self.end = stream, start, end
        self.parts = 1

    def begin(self, parts):
        self.parts = parts

    def __call__(self, part=0):
        chosen = {}
        for home in (True, False):
            start, size = self.start[home], self.end[home] - self.start[home]
            first = start + size * part // self.parts
            chosen[home] = self.stream.steps[home][first : start + size * (part + 1) // self.parts]
        self.stream.run(chosen)

    def in_loop(self, step, steps, offset, stride, inner):
        if all(self.start[home] == self.end[home] for home in (True, False)):
            return
        for number in range(steps):

            @pl.when(step == number)
            def _():
                self(offset + number * stride + inner)


class Bag:
    def __init__(self, **entries):
        self.__dict__.update(entries)

    def names(self):
        return list(self.__dict__)

    def values(self):
        return list(self.__dict__.values())

    def joined(self, other):
        return Bag(**self.__dict__, **other.__dict__)


def filled(names, values):
    return Bag(**dict(zip(names, values)))


class Nothing:
    def begin(self, parts):
        pass

    def __call__(self, part=0):
        pass

    def in_loop(self, *unused):
        pass


nothing = Nothing()


def vmem_like(ref):
    return pltpu.VMEM(ref.shape, ref.dtype)


class Direct:
    def __init__(self, ref):
        self.ref = ref


class Swap:
    def __init__(self, target, send_sem, recv_sem):
        self.target, self.send_sem, self.recv_sem = target, send_sem, recv_sem

    def copy(self, source):
        return pltpu.make_async_remote_copy(
            src_ref=source,
            dst_ref=self.target,
            send_sem=self.send_sem,
            recv_sem=self.recv_sem,
            device_id=target_of("c"),
            device_id_type=MESH,
        )

    def arrive(self):
        self.copy(self.target).wait_recv()


def run_phase(body, sems, ins, outs, scratch=(), swaps=(), before=nothing, after=nothing):
    moved_in = [ref for ref in ins if not isinstance(ref, Direct)]
    moved_out = [ref for ref in outs if not isinstance(ref, Direct)]

    def scoped(*refs):
        own_in, rest = refs[: len(moved_in)], refs[len(moved_in) :]
        own_out, own_scratch = rest[: len(moved_out)], rest[len(moved_out) :]
        copies = [
            pltpu.make_async_copy(ref, own, sems.at[number])
            for number, (ref, own) in enumerate(zip(moved_in, own_in))
        ]
        for copy in copies:
            copy.start()
        before()
        for copy in copies:
            copy.wait()
        own_in, own_out = iter(own_in), iter(own_out)
        all_in = [ref.ref if isinstance(ref, Direct) else next(own_in) for ref in ins]
        all_out = [ref.ref if isinstance(ref, Direct) else next(own_out) for ref in outs]
        body(*all_in, *all_out, *own_scratch)
        copies = []
        for number, swap in swaps:
            swap.copy(all_out[number]).start()
        for ref, own in zip(outs, all_out):
            if not isinstance(ref, Direct):
                copy = pltpu.make_async_copy(own, ref, sems.at[16 + len(copies)])
                copy.start()
                copies.append(copy)
        after()
        for copy in copies:
            copy.wait()
        for number, swap in swaps:
            swap.copy(all_out[number]).wait_send()

    allocations = [vmem_like(ref) for ref in moved_in] + [vmem_like(ref) for ref in moved_out]
    pl.run_scoped(scoped, *allocations, *scratch)


def prefetched(sems, ins, use):
    def scoped(*own):
        copies = [
            pltpu.make_async_copy(ref, one, sems.at[32 + number])
            for number, (ref, one) in enumerate(zip(ins, own))
        ]
        for copy in copies:
            copy.start()

        def wait():
            for copy in copies:
                copy.wait()

        use([Direct(one) for one in own], wait)

    pl.run_scoped(scoped, *[vmem_like(ref) for ref in ins])


def column_of(row_ref, first_row):
    size = row_ref.shape[1]
    lane = lax.broadcasted_iota(jnp.int32, (CHUNK, size), 1)
    row = first_row + lax.broadcasted_iota(jnp.int32, (CHUNK, size), 0)
    return jnp.sum(jnp.where(lane == row, row_ref[...], 0), axis=-1, keepdims=True)


class Inputs(Mover):
    def __init__(self, send_sems, recv_sems, local_sems):
        super().__init__(send_sems)
        self.recv_sems, self.local_sems = recv_sems, local_sems
        self.count = 0

    def taken(self):
        steps = self.steps
        self.steps = {True: [], False: []}
        return steps

    def swap(self, source, target):
        number = self.count
        self.count += 1

        def diagonal():
            return {"c": 1 - place("c"), "x": 1 - place("x")}

        def local():
            return pltpu.make_async_copy(source(), target(True), self.local_sems.at[number])

        self.local(True, lambda: local().start())
        self.send(
            False,
            source,
            functools.partial(target, False),
            lambda: self.recv_sems.at[number],
            diagonal,
        )

        def arrive():
            self.local(True, lambda: local().wait())
            self.wait(False, functools.partial(target, True), lambda: self.recv_sems.at[number])

        return arrive

    def share(self, piece):
        number = self.count
        self.count += 1

        def sem():
            return self.recv_sems.at[number]

        for home in (True, False):
            self.send(
                home,
                functools.partial(piece, True),
                functools.partial(piece, True),
                sem,
                functools.partial(target_of, "c"),
            )

        def arrive():
            for home in (True, False):
                self.wait(home, functools.partial(piece, False), sem)

        return arrive


def half_of(ref, own):
    size = ref.shape[0] // 2
    core = place("c") if own else 1 - place("c")
    return ref.at[pl.ds(core * size, size), :]


def half_lanes_of(ref, own):
    size = ref.shape[1] // 2
    core = place("c") if own else 1 - place("c")
    return ref.at[:, pl.ds(core * size, size)]


def source_mask(marks_row):
    quarter = marks_row.shape[1] // 4
    return marks_row.at[:, pl.ds(quarter, 2 * quarter)]


def target_mask(marks_row):
    quarter = marks_row.shape[1] // 4
    return marks_row.at[:, pl.ds(3 * quarter, quarter)]


def any_space():
    return pl.BlockSpec(memory_space=pl.ANY)


def spliced(one, two, at):
    return {home: one[home][: at[home]] + two[home] + one[home][at[home] :] for home in (True, False)}


def shares_of(steps, share):
    return {home: int(len(steps[home]) * share) for home in (True, False)}


def forward_kernel(names_in, names_out, *refs):
    count_in, count_out = len(names_in), len(names_out)
    i = filled(names_in, refs[:count_in])
    o = filled(names_out, refs[count_in : count_in + count_out])
    (marks_row, flags_row, *rest) = refs[count_in + count_out :]
    stages, rest = rest[:5], rest[5:]
    sems, group_send, group_recv, group_local, in_send, in_recv, in_local, swap_sems = rest
    vec = i.vectors
    greet()

    start = Inputs(Part(in_send, 0), Part(in_recv, 0), Part(in_local, 0))
    marks_here = start.swap(lambda: i.marks, lambda own: marks_row)
    source_here = start.swap(lambda: i.source, functools.partial(half_of, o.source_all))
    opening = start.taken()
    marks_here()
    flags_size = flags_row.shape[1] // 2

    def flags_piece(own):
        return half_lanes_of(flags_row, own)

    def flags_local():
        return pltpu.make_async_copy(
            marks_row.at[:, pl.ds(0, flags_size)], flags_piece(True), in_local.at[8]
        )

    for home in (True, False):
        start.local(home, lambda: flags_local().start())
        start.local(home, lambda: flags_local().wait())
    flags_there = start.share(flags_piece)
    source_here()
    source_there = start.share(functools.partial(half_of, o.source_all))
    middle = start.taken()
    flags_there()
    source_there()
    closing = start.taken()

    owns = (i.own_1, i.own_3, i.own_2, i.own_4, i.own_5)
    alls = (o.all_1, o.all_3, o.all_2, o.all_4, o.all_5)
    gathers = []
    for number, (own, gathered) in enumerate(zip(owns, alls)):
        gathers.append(
            Gather(
                own,
                gathered,
                stages[number],
                group_local.at[number],
                Part(group_send, number * GATHER_SENDS),
                Part(group_recv, number * 64),
            )
        )
    first, second, last = gathers[0], gathers[1], gathers[4]
    steps = spliced(first.steps, middle, shares_of(first.steps, 0.6))
    first.steps = {home: opening[home] + steps[home] + closing[home] for home in (True, False)}

    def bring(source, target, first_send, first_recv, first_local):
        mover = Inputs(Part(in_send, first_send), Part(in_recv, first_recv), Part(in_local, first_local))
        here_now = mover.swap(lambda: source, functools.partial(half_of, target))
        begin = mover.taken()
        here_now()
        there_now = mover.share(functools.partial(half_of, target))
        there_now()
        return mover, begin, mover.taken()

    target_mover, begin, rest = bring(i.target, o.target_all, 16, 8, 9)
    steps = spliced(second.steps, rest, shares_of(second.steps, 0.4))
    second.steps = {home: begin[home] + steps[home] for home in (True, False)}
    cotangent_mover, begin, rest = bring(i.cotangent, o.cotangent_all, 24, 12, 13)
    steps = spliced(last.steps, begin, shares_of(last.steps, 0.7))
    last.steps = {home: steps[home] + rest[home] for home in (True, False)}
    stream = Stream()
    stream.movers += [start, target_mover, cotangent_mover]
    for number, mover in enumerate(gathers):
        stream.add(mover, 0.4 if number > 1 else 0.0)
    ends = stream.ends

    swap_refs = (o.other_1, o.other_2, o.other_3, o.other_4, o.other_5)
    swaps = [
        Swap(ref, swap_sems.at[number], swap_sems.at[8 + number])
        for number, ref in enumerate(swap_refs)
    ]

    stream.plan(ends[0])[0]()

    one, ticks, two = stream.plan(stream.between(ends[1], ends[2], 0.25), (1, 7, 1))

    def encoder_attention_body(source_ref, w_ref, x_out, *outs):
        @pl.loop(0, x_out.shape[0] // CHUNK)
        def _(step):
            first_row = pl.multiple_of(step * CHUNK, CHUNK)
            at = pl.ds(first_row, CHUNK)
            kind = column_of(flags_row, first_row)
            x_out[at, :] = jnp.where(
                kind == 1, vec[12:13, :], jnp.where(kind == 2, vec[13:14, :], source_ref[at, :].astype(wide))
            )

        self_attention_kernel(0, False, ticks, source_mask(marks_row), x_out, w_ref, vec, *outs)

    run_phase(
        encoder_attention_body,
        sems,
        [o.source_all, o.all_1],
        [o.start, o.normed_1, o.query_1, o.kv_1, o.attended_1, o.totals_1, o.part_1],
        swaps=[(6, swaps[0])],
        before=one,
        after=two,
    )
    one, ticks_two, two = stream.plan(stream.between(ends[1], ends[2], 0.6), (1, 6, 1))

    def decoder_attention_body(x_ref, w_ref, *outs):
        self_attention_kernel(6, True, ticks_two, target_mask(marks_row), x_ref, w_ref, vec, *outs)

    run_phase(
        decoder_attention_body,
        sems,
        [o.target_all, o.all_3],
        [o.normed_3, o.query_3, o.kv_3, o.attended_3, o.totals_3, o.part_3],
        swaps=[(5, swaps[2])],
        before=one,
        after=two,
    )
    stream.plan(ends[2])[0]()
    swaps[0].arrive()
    one, ticks_three, two = stream.plan(stream.between(ends[3], ends[4], 0.2), (1, 5, 1))

    def encoder_feed_body(x_ref, own_ref, other_ref, w_ref, *outs):
        feed_forward_kernel(2, ticks_three, x_ref, own_ref, other_ref, w_ref, vec, *outs)

    run_phase(
        encoder_feed_body,
        sems,
        [o.start, o.part_1, o.other_1, o.all_2],
        [o.mid, o.normed_2, o.hidden_2, o.slope_2, o.part_2],
        swaps=[(4, swaps[1])],
        before=one,
        after=two,
    )
    stream.plan(ends[3])[0]()
    swaps[2].arrive()
    swaps[1].arrive()
    one, ticks_four, two = stream.plan(ends[4], (1, 5, 1))

    def cross_attention_body(x_ref, own_ref, other_ref, mid_ref, mid_own, mid_other, w_ref, *outs):
        cross_attention_kernel(
            ticks_four, source_mask(marks_row), x_ref, own_ref, other_ref, mid_ref, mid_own, mid_other, w_ref, vec, *outs
        )

    run_phase(
        cross_attention_body,
        sems,
        [o.target_all, o.part_3, o.other_3, o.mid, o.part_2, o.other_2, o.all_4],
        [o.one, o.final, o.memory, o.normed_4, o.query_4, o.kv_4, o.attended_4, o.totals_4, o.part_4],
        swaps=[(8, swaps[3])],
        before=one,
        after=two,
    )
    swaps[3].arrive()

    def decoder_feed_body(x_ref, own_ref, other_ref, w_ref, *outs):
        feed_forward_kernel(10, nothing, x_ref, own_ref, other_ref, w_ref, vec, *outs)

    run_phase(
        decoder_feed_body,
        sems,
        [o.one, o.part_4, o.other_4, o.all_5],
        [o.two, o.normed_5, o.hidden_5, o.slope_5, o.part_5],
        swaps=[(4, swaps[4])],
    )
    o.marks_all[...] = marks_row[...]
    o.flags_all[...] = flags_row[...]
    swaps[4].arrive()
    stream.finish()


def attention_kept(rows, keys, depth, width):
    return (
        shaped(rows, depth, low),
        shaped(rows, width, low),
        shaped(keys, 2 * width, low),
        shaped(rows, width, low),
        shaped(rows, 128, wide),
    )


def feed_kept(rows, depth, units):
    return shaped(rows, depth, low), shaped(rows, units, low), shaped(rows, units, low)


def specs_of(near, far):
    return [whole() for unused in near.values()] + [any_space() for unused in far.values()]


def dma(count):
    return pltpu.SemaphoreType.DMA((count,))


def forward_call(source, target, cotangent, marks, vectors, groups):
    depth = vectors.shape[1]
    rows, few = 2 * source.shape[0], 2 * target.shape[0]
    block = groups[0].shape[0]
    width, units = groups[0].shape[1] // 4, groups[1].shape[1] // 2
    near_in = Bag(marks=marks, vectors=vectors)
    far_in = Bag(source=source, target=target, cotangent=cotangent)
    far_in.own_1, far_in.own_2, far_in.own_3, far_in.own_4, far_in.own_5 = groups
    near_out = Bag(
        marks_all=jax.ShapeDtypeStruct(marks.shape, marks.dtype),
        flags_all=jax.ShapeDtypeStruct((1, rows), marks.dtype),
    )
    far_out = Bag(
        source_all=shaped(rows, depth, low),
        target_all=shaped(few, depth, low),
        cotangent_all=shaped(few, depth, low),
        start=shaped(rows, depth, wide),
        mid=shaped(rows, depth, wide),
        final=shaped(rows, depth, wide),
        memory=shaped(rows, depth, low),
        one=shaped(few, depth, wide),
        two=shaped(few, depth, wide),
    )
    f = far_out
    f.normed_1, f.query_1, f.kv_1, f.attended_1, f.totals_1 = attention_kept(rows, rows, depth, width)
    f.normed_3, f.query_3, f.kv_3, f.attended_3, f.totals_3 = attention_kept(few, few, depth, width)
    f.normed_4, f.query_4, f.kv_4, f.attended_4, f.totals_4 = attention_kept(few, rows, depth, width)
    f.normed_2, f.hidden_2, f.slope_2 = feed_kept(rows, depth, units)
    f.normed_5, f.hidden_5, f.slope_5 = feed_kept(few, depth, units)
    f.part_1 = f.other_1 = f.part_2 = f.other_2 = shaped(rows, depth, low)
    f.part_3 = f.other_3 = f.part_4 = f.other_4 = f.part_5 = f.other_5 = shaped(few, depth, low)
    f.all_1, f.all_2, f.all_3, f.all_4, f.all_5 = [
        shaped(16 * block, group.shape[1], low) for group in groups
    ]
    ins, outs = near_in.joined(far_in), near_out.joined(far_out)
    order = (0, 2, 1, 3, 4)
    stage = [
        pltpu.VMEM((8, block, gather_cuts(groups[number].shape[1])[1][1]), low) for number in order
    ]
    results = pl.pallas_call(
        functools.partial(forward_kernel, ins.names(), outs.names()),
        out_shape=tuple(outs.values()),
        in_specs=specs_of(near_in, far_in),
        out_specs=tuple(specs_of(near_out, far_out)),
        scratch_shapes=[
            pltpu.VMEM(marks.shape, marks.dtype),
            pltpu.VMEM((1, rows), marks.dtype),
            *stage,
            dma(32),
            dma(5 * GATHER_SENDS),
            dma(5 * 64),
            dma(5),
            dma(32),
            dma(16),
            dma(18),
            dma(16),
        ],
        compiler_params=pltpu.CompilerParams(
            collective_id=0, has_side_effects=True, vmem_limit_bytes=60 << 20
        ),
        name="forward_pass",
    )(*ins.values())
    return filled(outs.names(), results)


def backward_kernel(names_in, names_out, *refs):
    count_in, count_out = len(names_in), len(names_out)
    i = filled(names_in, refs[:count_in])
    o = filled(names_out, refs[count_in : count_in + count_out])
    rest = refs[count_in + count_out :]
    vectors_of, rest = dict(zip((0, 2, 4, 6, 8, 10, 12), rest[:7])), rest[7:]
    vector_rows, rest = rest[0], rest[1:]
    buffers = []
    for unused in range(6):
        buffers.append(rest[:SCATTER_BUFFERS])
        rest = rest[SCATTER_BUFFERS:]
    sems, group_send, group_recv, in_send, in_recv, in_local, swap_sems = rest
    vec, marks_row, flags_row = i.vectors, i.marks_all, i.flags_all
    finals = (o.final_5, o.final_4, o.final_3, o.final_2, o.final_1, o.final_vectors)
    greet()
    stream = Stream()
    for number in range(6):
        mover = Scatter(
            buffers[number],
            finals[number],
            Part(group_send, number * SCATTER_SENDS),
            Part(group_recv, number * 80),
        )
        stream.add(mover, (0.0, 0.85, 0.85, 0.85, 0.5, 0.0)[number])
    begins, ends = stream.begins, stream.ends
    swap_refs = (o.other_6, o.other_7, o.other_8, o.other_9, o.other_10, o.other_11)
    swaps = [
        Swap(ref, swap_sems.at[number], swap_sems.at[8 + number])
        for number, ref in enumerate(swap_refs)
    ]

    def total_of(number):
        return Direct(buffers[number][0])

    moves = Inputs(Part(in_send, 0), Part(in_recv, 0), Part(in_local, 0))

    swaps_before = []

    def result_body(x_ref, own_ref, other_ref, out):
        total = own_ref[...].astype(wide) + other_ref[...].astype(wide)
        out[...] = (x_ref[...] + total).astype(low)

    def last_feed_body(*refs):
        last_feed_backward_kernel(nothing, target_mask(marks_row), *refs)

    rows, depth = i.cotangent_all.shape
    units = i.hidden_5.shape[1]
    run_phase(
        last_feed_body,
        sems,
        [i.cotangent_all, i.normed_5, i.hidden_5, i.slope_5, i.all_5],
        [o.part_6, total_of(0), o.grad_three],
        feed_backward_scratch(rows, depth, units)[1:],
        swaps=[(0, swaps[0])],
    )
    run_phase(
        result_body,
        sems,
        [i.two, i.part_5, i.other_5],
        [o.three],
        before=stream.plan(stream.between(stream.position, begins[1], 0.15))[0],
    )
    result_here = moves.swap(functools.partial(half_of, o.three, True), lambda own: o.decoder_out)
    stream.run(moves.taken())
    swaps[0].arrive()

    def residual(norm_row, previous, x, own, other, grad_out, low_ref, before=nothing, ticks=nothing, after=nothing):
        ins = [x, own, other] + ([previous] if previous is not None else [])

        def body(*refs):
            if previous is None:
                x_ref, own_ref, other_ref, grad_ref = refs
                previous_ref = None
            else:
                x_ref, own_ref, other_ref, previous_ref, grad_ref = refs
            residual_prologue(
                norm_row, previous_ref, x_ref, own_ref, other_ref, vec, grad_ref, low_ref, vectors_of[norm_row], ticks
            )

        run_phase(body, sems, ins, [grad_out], before=before, after=after)

    def attention(number, causal, marks, norm_row, previous, x, own, other, grad_out, parts, mask_row, source, kept):
        rows, depth = x.shape
        keys, width = kept[2].shape[0], kept[1].shape[1]
        cross = source is not None
        early, prologue, late, main_in, ticks, main_out = stream.plan(marks, (1, 1, 1, 1, 8, 1))

        def inner(low_ref, ins, wait):
            residual(norm_row, previous, x, own, other, grad_out, low_ref, early, prologue, late)
            wait()
            ins = [kept[0]] + ([source] if cross else []) + ins
            outs = [part for part, swap in parts] + [total_of(number)]

            def body(*refs):
                normed_ref, refs = refs[0], refs[1:]
                source_ref = None
                if cross:
                    source_ref, refs = refs[0], refs[1:]
                held, refs = refs[:5], refs[5:]
                part_out, refs = refs[0], refs[1:]
                source_part = None
                if cross:
                    source_part, refs = refs[0], refs[1:]
                grad_total, scratch = refs[0], refs[1:]
                attention_backward_main(
                    causal, cross, ticks, mask_row, low_ref, normed_ref, source_ref, *held,
                    part_out, grad_total, source_part, *scratch,
                )

            run_phase(
                body,
                sems,
                ins,
                outs,
                attention_backward_scratch(rows, keys, depth, width, cross)[1:],
                swaps=[(at, swap) for at, (part, swap) in enumerate(parts)],
                before=main_in,
                after=main_out,
            )

        pl.run_scoped(
            lambda low_ref: prefetched(sems, kept[1:], functools.partial(inner, low_ref)),
            pltpu.VMEM((rows, depth), low),
        )

    attention(
        1, False, begins[1], 10, o.grad_three, i.two, o.part_6, o.other_6, o.grad_two,
        [(o.part_7, swaps[1]), (o.part_8, swaps[2])], source_mask(marks_row), i.memory,
        (i.normed_4, i.query_4, i.kv_4, i.attended_4, i.totals_4, i.all_4),
    )
    swaps[1].arrive()
    attention(
        2, True, begins[2], 8, o.grad_two, i.one, o.part_7, o.other_7, o.grad_one,
        [(o.part_9, swaps[3])], target_mask(marks_row), None,
        (i.normed_3, i.query_3, i.kv_3, i.attended_3, i.totals_3, i.all_3),
    )
    swaps[2].arrive()
    rows, depth = i.final.shape
    early, prologue, late, main_in, ticks, main_out = stream.plan(begins[3], (1, 1, 1, 1, 6, 1))

    def feed(low_ref, ins, wait):
        residual(4, None, i.final, o.part_8, o.other_8, o.grad_final, low_ref, early, prologue, late)
        wait()

        def body(normed_ref, hidden_ref, slope_ref, w_ref, part_out, grad_total, turned_ref, turned_low):
            ticks.begin(feed_backward_ticks(rows, units))
            feed_backward_body(
                ticks, normed_ref, hidden_ref, slope_ref, w_ref, part_out, grad_total, low_ref, slope_ref,
                turned_ref, turned_low,
            )

        run_phase(
            body,
            sems,
            [ins[0], i.hidden_2, i.slope_2, ins[1]],
            [o.part_10, total_of(3)],
            feed_backward_scratch(rows, depth, units)[2:],
            swaps=[(0, swaps[4])],
            before=main_in,
            after=main_out,
        )

    feed_ins = [i.normed_2, i.all_2]
    pl.run_scoped(
        lambda low_ref: prefetched(sems, feed_ins, functools.partial(feed, low_ref)),
        pltpu.VMEM((rows, depth), low),
    )
    swaps[3].arrive()
    residual(
        6, o.grad_one, i.target_all, o.part_9, o.other_9, o.target_low, None,
        stream.plan(stream.between(stream.position, begins[4], 0.1))[0],
    )
    target_here = moves.swap(functools.partial(half_of, o.target_low, True), lambda own: o.target_grad)
    stream.run(moves.taken())
    swaps[4].arrive()
    attention(
        4, False, begins[4], 2, o.grad_final, i.mid, o.part_10, o.other_10, o.grad_mid,
        [(o.part_11, swaps[5])], source_mask(marks_row), None,
        (i.normed_1, i.query_1, i.kv_1, i.attended_1, i.totals_1, i.all_1),
    )
    one, two, three = stream.plan(stream.between(stream.position, ends[4], 0.5), (2, 2, 1))
    one()
    swaps[5].arrive()

    def finish_body(previous_ref, x_ref, own_ref, other_ref, grad_out):
        norms, kinds = vectors_of[0], vectors_of[12]
        norms[...] = jnp.zeros_like(norms)
        kinds[...] = jnp.zeros_like(kinds)

        @pl.loop(0, x_ref.shape[0] // CHUNK)
        def _(step):
            first_row = pl.multiple_of(step * CHUNK, CHUNK)
            at = pl.ds(first_row, CHUNK)
            grads = own_ref[at, :].astype(wide) + other_ref[at, :].astype(wide)
            back, by_gain, by_shift = norm_back(x_ref[at, :], vec[0:1, :], grads)
            back = back + previous_ref[at, :]
            grad_out[at, :] = back.astype(low)
            norms[0:1, :] += by_gain
            norms[1:2, :] += by_shift
            kind = column_of(flags_row, first_row)
            kinds[0:1, :] += jnp.sum(jnp.where(kind == 1, back, 0.0), axis=0, keepdims=True)
            kinds[1:2, :] += jnp.sum(jnp.where(kind == 2, back, 0.0), axis=0, keepdims=True)

        vector_rows[...] = jnp.zeros_like(vector_rows)
        for first, pair in vectors_of.items():
            vector_rows[first : first + 2, :] = pair[...]
        every = jnp.concatenate([vector_rows[...], jnp.zeros((112, depth), wide)], axis=0)
        store_grad(buffers[5][0], 0, turned(every.astype(low)))

    run_phase(
        finish_body,
        sems,
        [o.grad_mid, i.start, o.part_11, o.other_11],
        [o.source_low],
        before=two,
        after=three,
    )
    source_here = moves.swap(functools.partial(half_of, o.source_low, True), lambda own: o.source_grad)
    stream.run(moves.taken())
    rest = {}
    for home in (True, False):
        late = stream.steps[home][stream.position[home] : ends[4][home]]
        few = stream.steps[home][ends[4][home] :]
        merged = []
        for number in range(max(len(late), len(few))):
            merged += few[number : number + 1] + late[number : number + 1]
        rest[home] = merged
    stream.run(rest)
    result_here()
    target_here()
    source_here()
    stream.run(moves.taken())
    moves.finish()
    stream.finish()


def backward_call(kept, vectors):
    rows, depth = kept.start.shape
    few = kept.one.shape[0]
    block = depth // 16
    near_in = Bag(vectors=vectors, marks_all=kept.marks_all, flags_all=kept.flags_all)
    far_in = Bag(**kept.__dict__)
    del far_in.marks_all, far_in.flags_all
    columns = [
        kept.all_5.shape[1], kept.all_4.shape[1], kept.all_3.shape[1], kept.all_2.shape[1], kept.all_1.shape[1], 128
    ]
    near_out = Bag()
    n = near_out
    n.final_5, n.final_4, n.final_3, n.final_2, n.final_1, n.final_vectors = [
        shaped(block, count, wide) for count in columns
    ]
    far_out = Bag(
        grad_three=shaped(few, depth, low),
        grad_two=shaped(few, depth, wide),
        grad_one=shaped(few, depth, wide),
        grad_final=shaped(rows, depth, wide),
        grad_mid=shaped(rows, depth, wide),
        target_low=shaped(few, depth, low),
        source_low=shaped(rows, depth, low),
        target_grad=shaped(few // 2, depth, low),
        source_grad=shaped(rows // 2, depth, low),
        three=shaped(few, depth, low),
        decoder_out=shaped(few // 2, depth, low),
    )
    f = far_out
    f.part_6 = f.other_6 = f.part_7 = f.other_7 = f.part_9 = f.other_9 = shaped(few, depth, low)
    f.part_8 = f.other_8 = f.part_10 = f.other_10 = f.part_11 = f.other_11 = shaped(rows, depth, low)
    ins, outs = near_in.joined(far_in), near_out.joined(far_out)
    scratch = [pltpu.VMEM((2, depth), wide)] * 7 + [pltpu.VMEM((16, depth), wide)]
    for count in columns:
        scratch += scatter_buffers(block, count)
    results = pl.pallas_call(
        functools.partial(backward_kernel, ins.names(), outs.names()),
        out_shape=tuple(outs.values()),
        in_specs=specs_of(near_in, far_in),
        out_specs=tuple(specs_of(near_out, far_out)),
        scratch_shapes=scratch
        + [dma(48), dma(6 * SCATTER_SENDS), dma(6 * 80), dma(8), dma(8), dma(8), dma(16)],
        compiler_params=pltpu.CompilerParams(
            collective_id=1, has_side_effects=True, vmem_limit_bytes=61 << 20
        ),
        name="backward_pass",
    )(*ins.values())
    return filled(outs.names(), results)


def lane_slot(number):
    return number if number < 12 else number + 4


def update_kernel(
    f1, f2, f3, f4, f5, fv, aw, fw, ra, ca, rf, cf, vp, vl, vm,
    ag, fg, vg, au, fu, vu, ran, can, rfn, cfn, vmn, fng,
    square, other_square, mine, theirs, line, line_in, send_sems, recv_sems,
):
    rows = f1.shape[0]
    depth = 16 * rows
    width, units = aw.shape[2], fw.shape[2]
    barrier = pltpu.get_barrier_semaphore()
    z = place("z")
    near = z + 1 - 2 * lax.rem(z, 2)
    far = lax.rem(z + 2, 4)
    partners = [target_of("x"), target_of("c"), target_of("y"), {"z": near}, {"z": far}]
    for partner in partners:
        pl.semaphore_signal(barrier, inc=1, device_id=partner, device_id_type=MESH)
    keep, take = decay_rate, 1.0 - decay_rate
    finals = (f1, f3, f4, f2, f5)
    matrices = []
    for number in range(16):
        if number < 12:
            final, at, size = finals[number // 4], number % 4 * width, width
            held = (aw, ag, au, number, ca, can)
        else:
            final, at, size = finals[3 + (number - 12) // 2], (number - 12) % 2 * units, units
            held = (fw, fg, fu, number - 12, cf, cfn)
        matrices.append((final, at, size, number * width if number < 12 else 12 * width + (number - 12) * units, held))
    columns = 12 * width + 4 * units

    square[...] = jnp.zeros_like(square)
    square[0:12, 0:rows] = ra[...]
    square[16:20, 0:rows] = rf[...]
    moments = jnp.transpose(square[...])[0:rows, :]
    other_square[...] = jnp.ones_like(other_square)
    other_square[0:14, 0:rows] = vm[...]
    other_square[16:30, 0:rows] = vl[...]
    scale = jnp.sqrt(jnp.mean(vp[...] * vp[...], axis=1, keepdims=True))
    other_square[16:30, rows : rows + 128 - rows] = jnp.broadcast_to(scale, (14, 128 - rows))
    turned_vectors = jnp.transpose(other_square[...])
    vector_moments = turned_vectors[0:rows, :]
    shifted = pltpu.roll(turned_vectors, 112, 1)
    vector_local, vector_scale = shifted[0:rows, :], shifted[rows : rows + 1, :]

    lane = lax.broadcasted_iota(jnp.int32, (rows, 128), 1)
    one_lane = lax.broadcasted_iota(jnp.int32, (1, 128), 1)
    row_sums = jnp.zeros((rows, 128), wide)
    totals = pltpu.roll(jnp.sum(moments, axis=0, keepdims=True) * 0.5, 64, 1)
    for number, (final, at, size, begin, held) in enumerate(matrices):
        grads = final[:, at : at + size]
        squares = grads * grads
        by_row = jnp.sum(squares, axis=1, keepdims=True)
        line[:, begin : begin + size] = jnp.sum(squares, axis=0, keepdims=True)
        weights = held[0][held[3]]
        by_weight = jnp.sum(jnp.sum(weights * weights, axis=1, keepdims=True), axis=0, keepdims=True)
        slot = lane_slot(number)
        row_sums = jnp.where(lane == slot, by_row, row_sums)
        totals = jnp.where(one_lane == slot, jnp.sum(by_row, axis=0, keepdims=True), totals)
        totals = jnp.where(one_lane == slot + 32, by_weight, totals)
        held[1][held[3]] = grads
    mine[0:rows, :] = row_sums
    mine[rows : rows + 8, :] = jnp.broadcast_to(totals, (8, 128))
    pl.semaphore_wait(barrier, len(partners))

    def exchange(source, target, number):
        copy = pltpu.make_async_remote_copy(
            src_ref=source,
            dst_ref=target,
            send_sem=send_sems.at[number],
            recv_sem=recv_sems.at[number],
            device_id=partners[number],
            device_id_type=MESH,
        )
        copy.start()
        copy.wait()

    exchange(mine, theirs, 0)
    row_sums = mine[0:rows, :] + theirs[0:rows, :]
    line[:, columns : columns + 128] = mine[rows : rows + 1, :] + theirs[rows : rows + 1, :]
    for number in range(1, 5):
        exchange(line, line_in.at[number - 1], number)
        line[...] += line_in[number - 1]

    totals = line[:, columns : columns + 128]
    across = jnp.where(one_lane < 16, float(2 * width), float(2 * units))
    level = (keep * pltpu.roll(totals, 64, 1) + take * totals / across) / depth
    size_of = jnp.sqrt(pltpu.roll(totals, 96, 1) / (across * depth))
    rows_next = keep * moments + take * row_sums / across

    def pick(row, slot):
        return jnp.sum(jnp.where(lane[0 : row.shape[0], :] == slot, row, 0.0), axis=1, keepdims=True)

    for number, (final, at, size, begin, held) in enumerate(matrices):
        slot = lane_slot(number)
        index = held[3]
        columns_next = keep * held[4][index : index + 1, :] + take * line[:, begin : begin + size] / depth
        held[5][index : index + 1, :] = columns_next
        estimate = pick(rows_next, slot) * columns_next / pick(level, slot)
        step = step_rate * pick(size_of, slot)
        held[2][index] = held[0][index] - step * final[:, at : at + size] * lax.rsqrt(estimate)

    grads = fv[...]
    moments_next = keep * vector_moments + take * grads * grads
    vectors_next = vector_local - step_rate * vector_scale * grads * lax.rsqrt(moments_next)
    small = jnp.where(lane < 32, rows_next, pltpu.roll(grads, 32, 1))
    small = jnp.where(lane < 48, small, pltpu.roll(moments_next, 48, 1))
    small = jnp.where(lane < 64, small, pltpu.roll(vectors_next, 64, 1))
    small = jnp.where(lane < 80, small, pltpu.roll(grads, 70, 1))
    square[0:rows, :] = small
    turned_small = jnp.transpose(square[...])
    ran[...] = turned_small[0:12, 0:rows]
    rfn[...] = turned_small[16:20, 0:rows]
    vg[...] = turned_small[32:46, 0:rows]
    vmn[...] = turned_small[48:62, 0:rows]
    vu[...] = turned_small[64:78, 0:rows]
    fng[...] = turned_small[80:82, 0:rows]


def update_call(finals, aw, fw, ra, ca, rf, cf, vp, vl, vm):
    rows = finals[0].shape[0]
    columns = 12 * aw.shape[2] + 4 * fw.shape[2]

    def same(array):
        return jax.ShapeDtypeStruct(array.shape, wide)

    pair = jax.ShapeDtypeStruct((2, rows), wide)
    return pl.pallas_call(
        update_kernel,
        out_shape=tuple(same(a) for a in (aw, fw, vm, aw, fw, vm, ra, ca, rf, cf, vm)) + (pair,),
        in_specs=[whole()] * 15,
        out_specs=tuple([whole()] * 12),
        scratch_shapes=[
            pltpu.VMEM((128, 128), wide),
            pltpu.VMEM((128, 128), wide),
            pltpu.VMEM((rows + 8, 128), wide),
            pltpu.VMEM((rows + 8, 128), wide),
            pltpu.VMEM((1, columns + 128), wide),
            pltpu.VMEM((4, 1, columns + 128), wide),
            dma(5),
            dma(5),
        ],
        compiler_params=pltpu.CompilerParams(
            collective_id=2, has_side_effects=True, vmem_limit_bytes=40 << 20
        ),
        name="update",
    )(*finals, aw, fw, ra, ca, rf, cf, vp, vl, vm)


def fits_kernels():
    return lax.axis_size("z") == 4


def factored_step(weights, grads, rows_next, columns_next, row_level, mean_square):
    estimate = rows_next[:, :, None] * columns_next[:, None, :] / row_level[:, None, None]
    return weights - step_rate * jnp.sqrt(mean_square)[:, None, None] * grads * lax.rsqrt(estimate)


def plain_pass(source, target, cotangent, marks, vectors, own_groups):
    core = lax.axis_index("c")
    depth = vectors.shape[1]
    source_half = swap_chips(source)
    flags_half = swap_chips(marks[:source.shape[0]])
    source_all = both_halves(source_half)
    flags_all = both_halves(flags_half)
    masks = swap_chips(marks[source.shape[0] :])
    source_length = masks[None, : 2 * source.shape[0]]
    target_length = masks[None, 2 * source.shape[0] :]
    target_all = both_halves(swap_chips(target))
    cotangent_all = both_halves(swap_chips(cotangent))

    (encoder_attention, encoder_feed, decoder_attention, cross_attention, decoder_feed) = [
        (gather_weights(group, "zyx"), group.shape[1]) for group in own_groups
    ]

    start_rows = jnp.where(
        (flags_all == 1)[:, None],
        vectors[12][None, :],
        jnp.where((flags_all == 2)[:, None], vectors[13][None, :], source_all.astype(wide)),
    )
    first_kept = self_attention_call(
        0, False, source_length, start_rows, encoder_attention, vectors,
    )
    first_part = first_kept[5]
    first_other = other_core(first_part)
    encoder_mid, second_normed, second_hidden, second_slope, second_part, *rest = feed_forward_call(
        2, start_rows, first_part, first_other, encoder_feed, vectors,
    )
    second_other = other_core(second_part)
    third_kept = self_attention_call(6, True, target_length, target_all, decoder_attention, vectors)
    third_part = third_kept[5]
    third_other = other_core(third_part)
    decoder_one, encoder_final, memory_rows, *fourth_kept = cross_attention_call(
        source_length,
        target_all,
        third_part,
        third_other,
        encoder_mid,
        second_part,
        second_other,
        cross_attention,
        vectors,
    )
    fourth_part = fourth_kept[5]
    fourth_kept = fourth_kept[:5]
    decoder_two, fifth_normed, fifth_hidden, fifth_slope, fifth_part = feed_forward_call(
        10, decoder_one, fourth_part, other_core(fourth_part), decoder_feed, vectors
    )
    decoder_three = decoder_two + (fifth_part.astype(wide) + other_core(fifth_part).astype(wide))

    def own_half(rows):
        half = rows.shape[0] // 2
        return lax.dynamic_slice_in_dim(rows, core * half, half, 0)

    decoder_out = swap_chips(own_half(decoder_three).astype(low))

    fifth_back, decoder_feed_terms, grad_three = last_feed_backward_call(
        target_length, cotangent_all, fifth_normed, fifth_hidden, fifth_slope, decoder_feed
    )
    query_back, grad_two, vectors_ten, cross_terms, memory_back, *decoder_feed_grad = attention_backward_call(
        False,
        10,
        source_length,
        grad_three,
        decoder_two,
        fifth_back,
        other_core(fifth_back),
        vectors,
        fourth_kept[0],
        memory_rows,
        *fourth_kept[1:],
        cross_attention,
    )
    query_other = other_core(query_back)
    memory_other = other_core(memory_back)
    third_back, grad_one, vectors_eight, decoder_terms, *cross_grad = attention_backward_call(
        True,
        8,
        target_length,
        grad_two,
        decoder_one,
        query_back,
        query_other,
        vectors,
        third_kept[0],
        None,
        *third_kept[1:5],
        decoder_attention,
    )
    third_back_other = other_core(third_back)
    second_back, encoder_feed_terms, grad_final, vectors_four, *decoder_grad = feed_backward_call(
        4,
        encoder_final,
        memory_back,
        memory_other,
        vectors,
        second_normed,
        second_hidden,
        second_slope,
        encoder_feed,
    )
    first_back, grad_mid, vectors_two, encoder_terms, *encoder_feed_grad = attention_backward_call(
        False,
        2,
        source_length,
        grad_final,
        encoder_mid,
        second_back,
        other_core(second_back),
        vectors,
        first_kept[0],
        None,
        *first_kept[1:5],
        encoder_attention,
    )
    grad_target, vectors_six = finish_call(
        6, grad_one, target_all, third_back, third_back_other, vectors
    )
    target_grad = swap_chips(own_half(grad_target).astype(low)).astype(wide)
    grad_start, vectors_zero = finish_call(
        0, grad_mid, start_rows, first_back, other_core(first_back), vectors
    )
    gap_rows = jnp.sum(jnp.where((flags_all == 1)[:, None], grad_start, 0.0), axis=0, keepdims=True)
    mask_rows = jnp.sum(jnp.where((flags_all == 2)[:, None], grad_start, 0.0), axis=0, keepdims=True)
    source_grad = swap_chips(own_half(grad_start).astype(low)).astype(wide)

    vector_terms = jnp.concatenate(
        [
            vectors_zero,
            vectors_two,
            vectors_four,
            vectors_six,
            vectors_eight,
            vectors_ten,
            gap_rows,
            mask_rows,
            jnp.zeros((114, depth), wide),
        ],
        axis=0,
    )
    vector_terms = vector_terms.T.astype(low)
    grads = [
        scatter_gradient(terms, "xyz")
        for terms in (
            encoder_terms, decoder_terms, cross_terms, encoder_feed_terms, decoder_feed_terms, vector_terms
        )
    ]
    return (decoder_out, source_grad, target_grad, *grads)


def on_device(
    source_embed,
    target_embed,
    out_cotangent,
    row_flags,
    source_mask,
    target_mask,
    attention_weights,
    feed_weights,
    rows_attention,
    columns_attention,
    rows_feed,
    columns_feed,
    vector_params,
    vector_moments,
):
    core = lax.axis_index("c")
    local_rows, half_width = attention_weights.shape[1:]
    half_units = feed_weights.shape[2]
    depth = vector_params.shape[1]
    units_all = 2 * half_units

    def attention_group(block):
        part = attention_weights[4 * block : 4 * block + 4].astype(low)
        return part.transpose(1, 0, 2).reshape(local_rows, 4 * half_width)

    def feed_group(index):
        part = feed_weights[2 * index : 2 * index + 2].astype(low)
        return part.transpose(1, 0, 2).reshape(local_rows, 2 * half_units)

    own_groups = [attention_group(0), feed_group(0), attention_group(1), attention_group(2), feed_group(1)]
    marks = jnp.concatenate([row_flags[0], source_mask[0], target_mask[0]])
    if fits_kernels():
        kept = forward_call(
            source_embed[0], target_embed[0], out_cotangent[0], marks[None], vector_params, own_groups
        )
        back = backward_call(kept, vector_params)
        decoder_out = back.decoder_out
        target_grad = back.target_grad.astype(wide)
        source_grad = back.source_grad.astype(wide)
        source_grad = jnp.where((row_flags[0] == 0)[:, None], source_grad, 0.0)
        local_width = vector_moments.shape[1]
        number = (lax.axis_index("z") * 2 + lax.axis_index("y")) * 2 + core
        vector_local = lax.dynamic_slice_in_dim(vector_params, number * local_width, local_width, 1)
        updates = update_call(
            [back.final_1, back.final_2, back.final_3, back.final_4, back.final_5, back.final_vectors],
            attention_weights, feed_weights, rows_attention, columns_attention, rows_feed, columns_feed,
            vector_params, vector_local, vector_moments,
        )
        return decoder_out[None], source_grad[None], target_grad[None], *updates
    (
        decoder_out, source_grad, target_grad,
        encoder_grad, decoder_grad, cross_grad, encoder_feed_grad, decoder_feed_grad, vector_grad,
    ) = plain_pass(source_embed[0], target_embed[0], out_cotangent[0], marks, vector_params, own_groups)
    source_grad = jnp.where((row_flags[0] == 0)[:, None], source_grad, 0.0)
    vector_grad = vector_grad[:, :14].T

    def as_matrices(rows, count):
        return rows.reshape(local_rows, count, -1).transpose(1, 0, 2)

    attention_grad = jnp.concatenate(
        [as_matrices(part, 4) for part in (encoder_grad, decoder_grad, cross_grad)], axis=0
    )
    feed_grad = jnp.concatenate(
        [as_matrices(part, 2) for part in (encoder_feed_grad, decoder_feed_grad)], axis=0
    )

    weight_squares = jnp.concatenate(
        [
            jnp.sum(attention_weights * attention_weights, axis=(1, 2)),
            jnp.sum(feed_weights * feed_weights, axis=(1, 2)),
            jnp.sum(rows_attention, axis=1) * 0.5,
            jnp.sum(rows_feed, axis=1) * 0.5,
        ]
    )
    early_sums = data_sum(tensor_sum(weight_squares))
    scale_attention, scale_feed = early_sums[:12], early_sums[12:16]
    rows_total_attention, rows_total_feed = early_sums[16:28], early_sums[28:32]
    attention_square = attention_grad * attention_grad
    feed_square = feed_grad * feed_grad
    row_sums = tensor_sum(
        jnp.concatenate([jnp.sum(attention_square, axis=2), jnp.sum(feed_square, axis=2)], axis=0)
    )
    column_attention = jnp.sum(attention_square, axis=1)
    column_feed = jnp.sum(feed_square, axis=1)
    square_totals = jnp.sum(row_sums, axis=1)
    column_sums = data_sum(
        jnp.concatenate([column_attention.reshape(-1), column_feed.reshape(-1), square_totals])
    )
    column_attention = column_sums[: column_attention.size].reshape(column_attention.shape)
    column_feed = column_sums[column_attention.size : -16].reshape(column_feed.shape)
    square_totals = column_sums[-16:]
    keep, take = decay_rate, 1.0 - decay_rate
    rows_attention_next = keep * rows_attention + take * row_sums[:12] / depth
    rows_feed_next = keep * rows_feed + take * row_sums[12:] / units_all
    total_attention = keep * rows_total_attention + take * square_totals[:12] / depth
    total_feed = keep * rows_total_feed + take * square_totals[12:] / units_all
    columns_attention_next = keep * columns_attention + take * column_attention / depth
    columns_feed_next = keep * columns_feed + take * column_feed / depth
    attention_updated = factored_step(
        attention_weights,
        attention_grad,
        rows_attention_next,
        columns_attention_next,
        total_attention / depth,
        scale_attention / (depth * depth),
    )
    feed_updated = factored_step(
        feed_weights,
        feed_grad,
        rows_feed_next,
        columns_feed_next,
        total_feed / depth,
        scale_feed / (depth * units_all),
    )
    local_width = vector_moments.shape[1]
    place = (lax.axis_index("z") * lax.axis_size("y") + lax.axis_index("y")) * 2 + core
    vector_local = lax.dynamic_slice_in_dim(vector_params, place * local_width, local_width, 1)
    vector_moments_next = keep * vector_moments + take * vector_grad * vector_grad
    vector_scale = jnp.sqrt(jnp.mean(vector_params * vector_params, axis=1))
    vector_updated = vector_local - step_rate * vector_scale[:, None] * vector_grad * lax.rsqrt(
        vector_moments_next
    )
    return (
        decoder_out[None],
        source_grad[None],
        target_grad[None],
        attention_grad,
        feed_grad,
        vector_grad,
        attention_updated,
        feed_updated,
        vector_updated,
        rows_attention_next,
        columns_attention_next,
        rows_feed_next,
        columns_feed_next,
        vector_moments_next,
        vector_grad[10:12],
    )


def solution(mesh):
    groups = mesh.shape["dp"] // 4
    inner = Mesh(mesh.devices.reshape(groups, 2, 2, 2), ("z", "y", "c", "x"))
    data = ("z", "y", "c")
    rows3, rows2 = P(data, "x", None), P(data, "x")
    matrix, row_spec, column_spec = P(None, data, "x"), P(None, data), P(None, "x")
    return jax.shard_map(
        on_device,
        mesh=inner,
        in_specs=(
            rows3,
            rows3,
            rows3,
            rows2,
            P(data, None),
            P(data, None),
            matrix,
            matrix,
            row_spec,
            column_spec,
            row_spec,
            column_spec,
            P(),
            row_spec,
        ),
        out_specs=(
            rows3,
            rows3,
            rows3,
            matrix,
            matrix,
            row_spec,
            matrix,
            matrix,
            row_spec,
            row_spec,
            column_spec,
            row_spec,
            column_spec,
            row_spec,
            row_spec,
        ),
        check_vma=False,
    )
```

```python
import functools

import jax
import jax.numpy as jnp
from jax import lax
from jax.experimental import pallas as pl
from jax.experimental.pallas import tpu as pltpu
from jax.sharding import Mesh
from jax.sharding import PartitionSpec as P

HEAD_DIM = 64
CHUNK = 256
norm_epsilon = 1e-05
decay_rate = 1.0 - 2.0 ** (-0.8)
step_rate = 0.2
masked_score = -1e30
low = jnp.bfloat16
wide = jnp.float32
MESH = pl.DeviceIdType.MESH


def swap_chips(array):
    return lax.ppermute(array, ("c", "x"), [(0, 0), (1, 2), (2, 1), (3, 3)])


def other_core(array):
    return lax.ppermute(array, "c", [(0, 1), (1, 0)])


def both_halves(own_half):
    received = other_core(own_half)
    first = lax.axis_index("c") == 0
    return jnp.concatenate(
        [jnp.where(first, own_half, received), jnp.where(first, received, own_half)], axis=0
    )


def core_sum(partial_rows):
    sent = partial_rows.astype(low)
    return sent.astype(wide) + other_core(sent).astype(wide)


def ring_next(array):
    size = lax.axis_size("z")
    return lax.ppermute(array, "z", [(i, (i + 1) % size) for i in range(size)])


def holds():
    return lax.axis_index("c") == lax.axis_index("x")


def spread_blocks(blocks, order):
    held = blocks[None, None]
    for axis in order:
        if axis == "x":
            received = lax.ppermute(held, ("c", "x"), [(0, 1), (3, 2)])
            held = jnp.where(holds(), held, received)
        elif axis == "y":
            received = lax.ppermute(held, "y", [(0, 1), (1, 0)])
            first = lax.axis_index("y") == 0
            held = jnp.concatenate(
                [jnp.where(first, held, received), jnp.where(first, received, held)], axis=1
            )
        else:
            size = lax.axis_size("z")
            if size != 4:
                held = lax.all_gather(held, "z", axis=0, tiled=True)
                continue
            place = lax.axis_index("z")
            whole = jnp.zeros((size,) + held.shape[1:], held.dtype)
            moving = held
            for step in range(size):
                where_from = lax.rem(place + size - step, size)
                whole = lax.dynamic_update_slice_in_dim(whole, moving, where_from, 0)
                if step < size - 1:
                    moving = ring_next(moving)
            held = whole
    return held


def reduce_blocks(parts, order):
    held = parts
    for position, axis in enumerate(order):
        final = position == len(order) - 1
        kind = wide if final else low
        if axis == "x":
            received = lax.ppermute(held, ("c", "x"), [(1, 0), (2, 3)])
            held = (held.astype(wide) + received.astype(wide)).astype(kind)
        elif axis == "y":
            mine = lax.axis_index("y")
            sent = lax.dynamic_slice_in_dim(held, 1 - mine, 1, 1)
            kept = lax.dynamic_slice_in_dim(held, mine, 1, 1)
            received = lax.ppermute(sent, "y", [(0, 1), (1, 0)])
            held = (kept.astype(wide) + received.astype(wide)).astype(kind)
        else:
            size = lax.axis_size("z")
            if size != 4:
                held = lax.psum_scatter(held, "z", scatter_dimension=0, tiled=True).astype(kind)
                continue
            place = lax.axis_index("z")
            moving = lax.dynamic_slice_in_dim(held, lax.rem(place + size - 1, size), 1, 0)
            for step in range(1, size):
                received = ring_next(moving)
                kept = lax.dynamic_slice_in_dim(held, lax.rem(place + size - 1 - step, size), 1, 0)
                last = step == size - 1
                moving = (kept.astype(wide) + received.astype(wide)).astype(kind if last else low)
            held = moving
    return held[0, 0]


def gather_weights(blocks, order):
    received = lax.ppermute(blocks, ("c", "x"), [(2, 0), (1, 3)])
    first = lax.axis_index("c") == 0
    both = jnp.concatenate(
        [jnp.where(first, blocks, received), jnp.where(first, received, blocks)], axis=0
    )
    spread = spread_blocks(both, order)
    return spread.reshape(-1, spread.shape[-1])


def scatter_gradient(gradient, order):
    depth, columns = gradient.shape
    z_size, y_size = lax.axis_size("z"), lax.axis_size("y")
    rows = depth // (z_size * y_size)
    total = reduce_blocks(gradient.astype(low).reshape(z_size, y_size, rows, columns), order)
    core = lax.axis_index("c")
    half = rows // 2
    kept = lax.dynamic_slice_in_dim(total, core * half, half, 0)
    sent = lax.dynamic_slice_in_dim(total, (1 - core) * half, half, 0)
    received = lax.ppermute(sent, ("c", "x"), [(0, 2), (3, 1)])
    return jnp.where(holds(), kept, received)


def data_sum(values):
    values = values + other_core(values)
    if lax.axis_size("z") != 4:
        return lax.psum(values, ("z", "y"))
    values = values + lax.ppermute(values, "y", [(0, 1), (1, 0)])
    values = values + lax.ppermute(values, "z", [(0, 1), (1, 0), (2, 3), (3, 2)])
    return values + lax.ppermute(values, "z", [(0, 2), (2, 0), (1, 3), (3, 1)])


def tensor_sum(values):
    return values + lax.ppermute(values, "x", [(0, 1), (1, 0)])


def column_cuts(columns):
    tiles = columns // 128
    first = (tiles * 42 + 50) // 100
    second = (tiles * 36 + 50) // 100
    edges = [0, first * 128, (first + second) * 128, columns]
    return list(zip(edges[:-1], edges[1:]))


def gather_cuts(columns):
    tiles = columns // 128
    first = (tiles * 38 + 50) // 100
    second = (tiles * 39 + 50) // 100
    edges = [0, first * 128, (first + second) * 128, columns]
    return list(zip(edges[:-1], edges[1:]))


def place(name):
    return lax.axis_index(name)


def block_at(which):
    back, same = which
    z = lax.rem(place("z") + 4 - back, 4)
    return z * 2 + (place("y") if same else 1 - place("y"))


def target_of(axis):
    if axis == "z":
        return {"z": lax.rem(place("z") + 1, 4)}
    if axis == "z_back":
        return {"z": lax.rem(place("z") + 3, 4)}
    if axis == "x_home":
        return {"c": place("x"), "x": 1 - place("x")}
    return {axis: 1 - place(axis)}


def greet_others():
    barrier = pltpu.get_barrier_semaphore()
    targets = [target_of(axis) for axis in ("c", "y", "z", "z_back", "x")]
    targets.append({"c": 1 - place("c"), "x": 1 - place("x")})
    for target in targets:
        pl.semaphore_signal(barrier, inc=1, device_id=target, device_id_type=MESH)


def greeted():
    pl.semaphore_wait(pltpu.get_barrier_semaphore(), 6)


def greet():
    greet_others()
    greeted()


class Part:
    def __init__(self, array, first):
        self.array, self.first = array, first
        self.at = self

    def __getitem__(self, index):
        return self.array.at[self.first + index]


def here(back):
    return (back, True)


def there(back):
    return (back, False)


class Mover:
    def __init__(self, send_sems):
        self.steps = {True: [], False: []}
        self.sent = {True: [], False: []}
        self.done = 0
        self.send_sems = send_sems

    def send(self, home, source, target, recv_sem, device):
        number = len(self.sent[home])

        def copy():
            return pltpu.make_async_remote_copy(
                src_ref=source(),
                dst_ref=target(),
                send_sem=self.send_sems.at[number],
                recv_sem=recv_sem(),
                device_id=device(),
                device_id_type=MESH,
            )

        self.sent[home].append(copy)
        self.steps[home].append(lambda: copy().start())

    def wait(self, home, target, recv_sem):
        def step():
            pltpu.make_async_remote_copy(
                src_ref=target(),
                dst_ref=target(),
                send_sem=self.send_sems.at[0],
                recv_sem=recv_sem(),
                device_id=target_of("c"),
                device_id_type=MESH,
            ).wait_recv()

        self.steps[home].append(step)

    def local(self, home, step):
        self.steps[home].append(step)

    def run(self, part, parts):
        for home in (True, False):
            steps = self.steps[home]
            chosen = steps[len(steps) * part // parts : len(steps) * (part + 1) // parts]
            if not chosen:
                continue
            wanted = place("c") == place("x")

            @pl.when(wanted if home else jnp.logical_not(wanted))
            def _():
                for step in chosen:
                    step()

    def finish(self):
        for home in (True, False):
            wanted = place("c") == place("x")

            @pl.when(wanted if home else jnp.logical_not(wanted))
            def _():
                for copy in self.sent[home]:
                    copy().wait_send()


class Gather(Mover):
    def __init__(self, own_ref, out_ref, stage_ref, local_sem, send_sems, recv_sems, first_column, columns):
        super().__init__(send_sems)
        rows = own_ref.shape[0]
        cuts = gather_cuts(columns)
        (begin_a, end_a), (begin_b, end_b), (begin_c, end_c) = cuts
        first, second, third = 0, 1, 2

        def out_piece(group, which, parity):
            begin, end = cuts[group]
            first_row = (block_at(which) * 2 + parity()) * rows
            return out_ref.at[pl.ds(first_row, rows), pl.ds(first_column + begin, end - begin)]

        def out_sem(group, which, parity):
            return recv_sems.at[(group * 8 + block_at(which)) * 2 + parity()]

        def stage_piece(group, which):
            begin, end = cuts[group]
            return stage_ref.at[block_at(which), :, pl.ds(begin, end - begin)]

        def stage_sem(group, which):
            return recv_sems.at[48 + group * 8 + block_at(which)]

        def core():
            return place("c")

        def other():
            return 1 - place("c")

        self_copies = {
            True: lambda: pltpu.make_async_copy(
                own_ref.at[:, pl.ds(first_column, columns)],
                out_ref.at[
                    pl.ds((block_at(here(0)) * 2 + core()) * rows, rows), pl.ds(first_column, columns)
                ],
                local_sem,
            ),
        }

        def own_piece(group):
            begin, end = cuts[group]
            return own_ref.at[:, pl.ds(first_column + begin, end - begin)]

        for home in (True, False):
            arrived = set()

            def plane(group, which):
                if which == here(0):
                    return functools.partial(own_piece, group)
                if home:
                    return functools.partial(out_piece, group, which, core)
                return functools.partial(stage_piece, group, which)

            def plane_target(group, which):
                if home:
                    return (
                        functools.partial(out_piece, group, which, core),
                        functools.partial(out_sem, group, which, core),
                    )
                return (
                    functools.partial(stage_piece, group, which),
                    functools.partial(stage_sem, group, which),
                )

            def plane_send(group, which, axis):
                target, sem = plane_target(group, which)
                self.send(home, plane(group, which), target, sem, functools.partial(target_of, axis))

            def plane_wait(group, which):
                if which == here(0):
                    return
                target, sem = plane_target(group, which)
                self.wait(home, target, sem)
                if home:
                    arrived.add((group, which, "core"))

            def deliver(group, which):
                target = functools.partial(out_piece, group, which, core)
                sem = functools.partial(out_sem, group, which, core)
                source = plane(group, which)
                self.send(home, source, target, sem, functools.partial(target_of, "x_home"))
                if not home:
                    self.send(home, source, target, sem, functools.partial(target_of, "c"))

            def core_send(group, which, name, axis):
                parity = core if name == "core" else other
                if home and which == here(0) and name == "core":
                    source = functools.partial(own_piece, group)
                else:
                    source = functools.partial(out_piece, group, which, parity)
                self.send(
                    home,
                    source,
                    functools.partial(out_piece, group, which, parity),
                    functools.partial(out_sem, group, which, parity),
                    functools.partial(target_of, axis),
                )

            def core_wait(group, which, name):
                if home and which == here(0) and name == "core":
                    return
                if (group, which, name) in arrived:
                    return
                arrived.add((group, which, name))
                parity = core if name == "core" else other
                self.wait(
                    home,
                    functools.partial(out_piece, group, which, parity),
                    functools.partial(out_sem, group, which, parity),
                )

            if home:
                self.local(home, lambda: self_copies[True]().start())
            deliver(third, here(0))
            plane_send(first, here(0), "z")
            plane_send(second, here(0), "z")
            plane_send(first, here(0), "y")
            deliver(second, here(0))
            deliver(first, here(0))
            names = ("core", "other") if home else ("other", "core")
            for name in names:
                core_wait(third, here(0), name)
                core_send(third, here(0), name, "z")
                core_send(third, here(0), name, "y")
            for name in names:
                core_wait(second, here(0), name)
                core_send(second, here(0), name, "y")
            for back in (1, 2, 3):
                plane_wait(first, here(back))
                if back < 3:
                    plane_send(first, here(back), "z")
                plane_send(first, here(back), "y")
                plane_wait(second, here(back))
                if back < 3:
                    plane_send(second, here(back), "z")
                deliver(second, here(back))
                deliver(first, here(back))
                plane_wait(first, there(back - 1))
                deliver(first, there(back - 1))
                if back == 1:
                    for name in names:
                        core_wait(third, there(0), name)
                        core_send(third, there(0), name, "z")
                for which in (here(back), there(back)):
                    for name in names:
                        core_wait(third, which, name)
                        if back < 3:
                            core_send(third, which, name, "z")
                for name in names:
                    core_wait(second, here(back), name)
                    core_send(second, here(back), name, "y")
            plane_wait(first, there(3))
            deliver(first, there(3))
            for group in (third, second, first):
                for back in range(4):
                    for which in (here(back), there(back)):
                        for name in ("core", "other"):
                            core_wait(group, which, name)
            if home:
                self.local(home, lambda: self_copies[True]().wait())


GATHER_SENDS = 64


class Scatter(Mover):
    def __init__(self, buffers, final, send_sems, recv_sems):
        super().__init__(send_sems)
        total, stages, x_ins, z_ins = buffers[0], buffers[1:4], buffers[4:7], buffers[7:9]
        ya_in, yb_in, zc_in, yc_in = buffers[9:]
        rows = total.shape[1] // 2
        columns = total.shape[2]
        cuts = column_cuts(columns)
        first, second, third = 0, 1, 2
        widths = [end - begin for begin, end in cuts]

        def part(group):
            begin, end = cuts[group]
            return pl.ds(begin, end - begin)

        def core_piece(group, which, parity=None):
            if parity is None:
                return total.at[block_at(which), :, part(group)]
            return total.at[block_at(which), pl.ds(parity() * rows, rows), part(group)]

        def slot_of(which):
            return which[0] + (0 if which[1] else 4)

        def x_piece(group, which):
            return x_ins[group].at[slot_of(which)]

        def stage_piece(group, which):
            return stages[group].at[slot_of(which)]

        def sem(number):
            return lambda: recv_sems.at[number]

        def core():
            return place("c")

        def other():
            return 1 - place("c")

        def add_rows(held_of, came_of, count, final_part=None):
            def step():
                held, came = held_of(), came_of()

                @pl.loop(0, count // 16)
                def _(number):
                    at = pl.ds(pl.multiple_of(number * 16, 16), 16)
                    if final_part is None:
                        held[at, :] = held[at, :] + came[at, :]
                    else:
                        final[at, final_part] = held[at, :].astype(wide) + came[at, :].astype(wide)

            return step

        for home in (True, False):

            def plane(group, which):
                if home:
                    return functools.partial(core_piece, group, which, core)
                return functools.partial(stage_piece, group, which)

            def x_sends(group, which):
                if widths[group] == 0:
                    return
                number = group * 8 + slot_of(which)
                if home:
                    self.send(
                        home,
                        functools.partial(core_piece, group, which, other),
                        functools.partial(stage_piece, group, which),
                        sem(24 + number),
                        functools.partial(target_of, "c"),
                    )
                    return
                for parity in (0, 1):
                    self.send(
                        home,
                        functools.partial(core_piece, group, which, functools.partial(parity_value, parity)),
                        functools.partial(x_piece, group, which),
                        sem(number),
                        functools.partial(home_core, parity),
                    )

            def x_add(group, which, last=False):
                if widths[group] == 0:
                    return
                number = group * 8 + slot_of(which)
                if not home:
                    self.wait(home, functools.partial(stage_piece, group, which), sem(24 + number))
                self.wait(home, functools.partial(x_piece, group, which), sem(number))
                self.local(
                    home,
                    add_rows(
                        plane(group, which),
                        functools.partial(x_piece, group, which),
                        rows,
                        part(group) if last else None,
                    ),
                )

            def z_slot(group, back):
                return lambda: z_ins[group].at[back]

            def z_send(group, back):
                if widths[group] == 0:
                    return
                self.send(
                    home,
                    plane(group, here(back)),
                    z_slot(group, back - 1),
                    sem(60 + group * 4 + back - 1),
                    functools.partial(target_of, "z_back"),
                )

            def z_add(group, back):
                if widths[group] == 0:
                    return
                self.wait(home, z_slot(group, back), sem(60 + group * 4 + back))
                self.local(
                    home,
                    add_rows(
                        plane(group, here(back)),
                        z_slot(group, back),
                        rows,
                        part(group) if back == 0 else None,
                    ),
                )

            def ya_slot(back):
                return lambda: ya_in.at[back]

            def yb_slot(back):
                return lambda: yb_in.at[back]

            def zc_slot(which):
                back, same = which
                return lambda: zc_in.at[back + (0 if same else 3)]

            def zc_send(which):
                back, same = which
                self.send(
                    home,
                    functools.partial(core_piece, third, which),
                    zc_slot((back - 1, same)),
                    sem(72 + back - 1 + (0 if same else 3)),
                    functools.partial(target_of, "z_back"),
                )

            def zc_add(which):
                back, same = which
                self.wait(home, zc_slot(which), sem(72 + back + (0 if same else 3)))
                self.local(
                    home,
                    add_rows(functools.partial(core_piece, third, which), zc_slot(which), 2 * rows),
                )

            zc_send(there(3))
            zc_send(here(3))
            for back in (3, 2, 1, 0):
                if widths[second]:
                    self.send(
                        home,
                        functools.partial(core_piece, second, there(back)),
                        yb_slot(back),
                        sem(52 + back),
                        functools.partial(target_of, "y"),
                    )
                if back > 1:
                    x_sends(first, there(back))
                    x_sends(first, here(back))
            for turn in range(7):
                back = 3 - turn
                if back >= 0:
                    if widths[second]:
                        self.wait(home, yb_slot(back), sem(52 + back))
                        self.local(
                            home,
                            add_rows(
                                functools.partial(core_piece, second, here(back)), yb_slot(back), 2 * rows
                            ),
                        )
                    x_sends(second, here(back))
                    if back > 1:
                        x_sends(first, there(back - 2))
                        x_sends(first, here(back - 2))
                    if back < 3:
                        for which in (there(back), here(back)):
                            zc_add(which)
                            if back > 0:
                                zc_send(which)
                            elif not which[1]:
                                self.send(
                                    home,
                                    functools.partial(core_piece, third, there(0)),
                                    lambda: yc_in.at[...],
                                    sem(56),
                                    functools.partial(target_of, "y"),
                                )
                    x_add(first, there(back))
                    if widths[first]:
                        self.send(
                            home,
                            plane(first, there(back)),
                            ya_slot(back),
                            sem(48 + back),
                            functools.partial(target_of, "y"),
                        )
                if back == -1:
                    self.wait(home, lambda: yc_in.at[...], sem(56))
                    self.local(
                        home,
                        add_rows(
                            functools.partial(core_piece, third, here(0)),
                            lambda: yc_in.at[...],
                            2 * rows,
                        ),
                    )
                    x_sends(third, here(0))
                back = 4 - turn
                if 0 <= back < 4:
                    x_add(first, here(back))
                    if widths[first]:
                        self.wait(home, ya_slot(back), sem(48 + back))
                        self.local(home, add_rows(plane(first, here(back)), ya_slot(back), rows))
                    if back == 3:
                        z_send(first, back)
                back = 5 - turn
                if 0 <= back < 3:
                    z_add(first, back)
                    if back > 0:
                        z_send(first, back)
                if 0 <= back < 4:
                    x_add(second, here(back))
                    if back == 3:
                        z_send(second, back)
                back = 6 - turn
                if 0 <= back < 3:
                    z_add(second, back)
                    if back > 0:
                        z_send(second, back)
            x_add(third, here(0), last=True)


def parity_value(parity):
    return parity


def home_core(parity):
    return {"c": parity, "x": place("c")}


SCATTER_SENDS = 48


SCATTER_BUFFERS = 13


def scatter_buffers(rows, columns):
    first, second, third = [max(end - begin, 128) for begin, end in column_cuts(columns)]
    return [
        pltpu.VMEM((8, 2 * rows, columns), low),
        pltpu.VMEM((8, rows, first), low),
        pltpu.VMEM((4, rows, second), low),
        pltpu.VMEM((1, rows, third), low),
        pltpu.VMEM((8, rows, first), low),
        pltpu.VMEM((4, rows, second), low),
        pltpu.VMEM((1, rows, third), low),
        pltpu.VMEM((3, rows, first), low),
        pltpu.VMEM((3, rows, second), low),
        pltpu.VMEM((4, rows, first), low),
        pltpu.VMEM((4, 2 * rows, second), low),
        pltpu.VMEM((6, 2 * rows, third), low),
        pltpu.VMEM((2 * rows, third), low),
    ]

def ride_call(body, operands, in_specs, outs, scratch, rider, name):
    def kernel(*refs):
        body(Nothing(), *refs)

    return pl.pallas_call(
        kernel,
        out_shape=tuple(outs),
        in_specs=list(in_specs),
        scratch_shapes=list(scratch),
        compiler_params=pltpu.CompilerParams(vmem_limit_bytes=60 << 20),
        name=name,
    )(*operands)


def whole():
    return pl.BlockSpec(memory_space=pltpu.VMEM)


def weight_spec(weights):
    return pl.BlockSpec(memory_space=pltpu.VMEM)


def shaped(rows, columns, kind):
    return jax.ShapeDtypeStruct((rows, columns), kind)


def dot_nn(left, right):
    return lax.dot_general(left, right, (((1,), (0,)), ((), ())), preferred_element_type=wide)


def dot_nt(left, right):
    return lax.dot_general(left, right, (((1,), (1,)), ((), ())), preferred_element_type=wide)


def turned(block):
    size = block.shape[1]
    row = lax.broadcasted_iota(jnp.int32, (size, size), 0)
    column = lax.broadcasted_iota(jnp.int32, (size, size), 1)
    return dot_nt((row == column).astype(wide).astype(low), block).astype(low)


def turn_into(target, source):
    rows, columns = source.shape
    for at in range(0, columns, 256):
        wide_part = min(256, columns - at)
        target[at : at + wide_part, :] = turned(source[:, at : at + wide_part])


def centre_rows(values):
    centred = values - jnp.mean(values, axis=-1, keepdims=True)
    spread = jnp.mean(centred * centred, axis=-1, keepdims=True)
    return centred * lax.rsqrt(spread + norm_epsilon)


def norm_back(x, gain, grads):
    centred = x - jnp.mean(x, axis=-1, keepdims=True)
    scale = lax.rsqrt(jnp.mean(centred * centred, axis=-1, keepdims=True) + norm_epsilon)
    unit = centred * scale
    inner = grads * gain
    by_unit = inner * unit
    back = scale * (
        inner
        - jnp.mean(inner, axis=-1, keepdims=True)
        - unit * jnp.mean(by_unit, axis=-1, keepdims=True)
    )
    return back, jnp.sum(grads * unit, axis=0, keepdims=True), jnp.sum(grads, axis=0, keepdims=True)


def residual_prologue(norm_row, previous_ref, x_ref, own_ref, other_ref, vec_ref, grad_out, low_ref, vec_out, ticks=None):
    ticks = ticks or Nothing()
    steps = x_ref.shape[0] // CHUNK
    ticks.begin(steps)
    gain = vec_ref[norm_row : norm_row + 1, :]
    vec_out[...] = jnp.zeros_like(vec_out)

    @pl.loop(0, x_ref.shape[0] // CHUNK)
    def _(step):
        at = pl.ds(pl.multiple_of(step * CHUNK, CHUNK), CHUNK)
        ticks.in_loop(step, steps, 0, 1, 0)
        grads = own_ref[at, :].astype(wide) + other_ref[at, :].astype(wide)
        back, by_gain, by_shift = norm_back(x_ref[at, :].astype(wide), gain, grads)
        if previous_ref is not None:
            back = back + previous_ref[at, :].astype(wide)
        if grad_out is not None:
            grad_out[at, :] = back.astype(grad_out.dtype)
        if low_ref is not None:
            low_ref[at, :] = back.astype(low)
        vec_out[0:1, :] += by_gain
        vec_out[1:2, :] += by_shift


def erf_ratio(values):
    x = jnp.clip(values, -4.0, 4.0)
    square = x * x
    top = jnp.full_like(square, -2.72614225801306e-10)
    for term in (
        2.77068142495902e-08,
        -2.10102402082508e-06,
        -5.69250639462346e-05,
        -7.34990630326855e-04,
        -2.95459980854025e-03,
        -1.60960333262415e-02,
    ):
        top = top * square + term
    low_part = jnp.full_like(square, -1.45660718464996e-05)
    for term in (
        -2.13374055278905e-04,
        -1.68282697438203e-03,
        -7.37332916720468e-03,
        -1.42647390514189e-02,
    ):
        low_part = low_part * square + term
    return x * top / low_part


def gelu_pair(before):
    phi_whole = 0.5 + 0.5 * erf_ratio(before * 0.7071067811865476)
    density = jnp.exp(before * before * -0.5) * 0.3989422804014327
    return before * phi_whole, phi_whole + before * density


def chunks(rows):
    return range(0, rows, CHUNK)


def feed_forward_kernel(
    rows_norm, ticks, x_ref, own_ref, other_ref, w_ref, vec_ref, x_out, normed_out, hidden_out, slope_out, part_out
):
    units = w_ref.shape[1] // 2
    steps = x_ref.shape[0] // CHUNK
    pieces = units // 512
    ticks.begin(steps * pieces)
    gain = vec_ref[rows_norm : rows_norm + 1, :]
    shift = vec_ref[rows_norm + 1 : rows_norm + 2, :]

    @pl.loop(0, x_ref.shape[0] // CHUNK)
    def _(step):
        at = pl.ds(pl.multiple_of(step * CHUNK, CHUNK), CHUNK)
        x = x_ref[at, :] + (own_ref[at, :].astype(wide) + other_ref[at, :].astype(wide))
        x_out[at, :] = x
        normed = (centre_rows(x) * gain + shift).astype(low)
        normed_out[at, :] = normed
        part = jnp.zeros((CHUNK, x.shape[1]), wide)
        for begin in range(0, units, 512):
            ticks.in_loop(step, steps, 0, pieces, begin // 512)
            before = dot_nn(normed, w_ref[:, begin : begin + 512])
            value, slope = gelu_pair(before)
            hidden = value.astype(low)
            hidden_out[at, begin : begin + 512] = hidden
            slope_out[at, begin : begin + 512] = slope.astype(low)
            part = part + dot_nt(hidden, w_ref[:, units + begin : units + begin + 512])
        part_out[at, :] = part.astype(low)


def feed_forward_call(rows_norm, x, own, other, weights, vectors, rider=None):
    rows, depth = x.shape
    units = weights[1] // 2
    return ride_call(
        functools.partial(feed_forward_kernel, rows_norm),
        [x, own, other, weights[0], vectors],
        [whole(), whole(), whole(), weight_spec(weights), whole()],
        [
            shaped(rows, depth, wide),
            shaped(rows, depth, low),
            shaped(rows, units, low),
            shaped(rows, units, low),
            shaped(rows, depth, low),
        ],
        [],
        rider,
        "feed_forward",
    )


def store_grad(target, begin, value):
    value = value.astype(low)
    span = slice(begin, begin + value.shape[1])
    if len(target.shape) == 2:
        target[:, span] = value
    else:
        target[:, :, span] = value.reshape(target.shape[0], target.shape[1], value.shape[1])


def feed_backward_ticks(rows, units):
    return 1 + rows // CHUNK * (units // 512) + units // 256


def feed_backward_body(ticks, normed_ref, hidden_ref, slope_in, w_ref, part_out, grad_out, low_ref, slope_ref, turned_ref, turned_low):
    rows, depth = low_ref.shape
    units = w_ref.shape[1] // 2
    steps = rows // CHUNK
    pieces = units // 512
    offset = 1 + steps * pieces
    ticks(0)
    turn_into(turned_low, low_ref)
    turn_into(turned_ref, normed_ref)

    @pl.loop(0, rows // CHUNK)
    def _(step):
        at = pl.ds(pl.multiple_of(step * CHUNK, CHUNK), CHUNK)
        grads = low_ref[at, :]
        part = jnp.zeros((CHUNK, depth), wide)
        for begin in range(0, units, 512):
            ticks.in_loop(step, steps, 1, pieces, begin // 512)
            grad = dot_nn(grads, w_ref[:, units + begin : units + begin + 512])
            grad = (grad * slope_in[at, begin : begin + 512].astype(wide)).astype(low)
            slope_ref[at, begin : begin + 512] = grad
            part = part + dot_nt(grad, w_ref[:, begin : begin + 512])
        part_out[at, :] = part.astype(low)

    for begin in range(0, units, 256):
        ticks(offset + begin // 256)
        store_grad(grad_out, begin, dot_nn(turned_ref[...], slope_ref[:, begin : begin + 256]))
        store_grad(
            grad_out, units + begin, dot_nn(turned_low[...], hidden_ref[:, begin : begin + 256])
        )


def feed_backward_scratch(rows, depth, units):
    return [
        pltpu.VMEM((rows, depth), low),
        pltpu.VMEM((rows, units), low),
        pltpu.VMEM((depth, rows), low),
        pltpu.VMEM((depth, rows), low),
    ]


def last_feed_backward_kernel(
    ticks, length_ref, cotangent_ref, normed_ref, hidden_ref, slope_in, w_ref, part_out, grad_out, low_ref, *rest
):
    rows, depth = cotangent_ref.shape

    @pl.loop(0, rows // CHUNK)
    def _(step):
        first_row = pl.multiple_of(step * CHUNK, CHUNK)
        at = pl.ds(first_row, CHUNK)
        rows_here = cotangent_ref[at, :].astype(wide)
        kept = column_of(length_ref, first_row) > 0
        low_ref[at, :] = jnp.where(kept, rows_here, 0.0).astype(low)

    feed_backward_body(ticks, normed_ref, hidden_ref, slope_in, w_ref, part_out, grad_out, low_ref, *rest)


def last_feed_backward_call(length, cotangent, normed, hidden, slope, weights, rider=None):
    rows, depth = cotangent.shape
    units = hidden.shape[1]
    return ride_call(
        last_feed_backward_kernel,
        [length, cotangent, normed, hidden, slope, weights[0]],
        [whole()] + [whole()] * 4 + [weight_spec(weights)],
        [shaped(rows, depth, low), shaped(depth, 2 * units, low), shaped(rows, depth, low)],
        feed_backward_scratch(rows, depth, units)[1:],
        rider,
        "last_feed_backward",
    )


def feed_backward_kernel(
    norm_row, ticks, x_ref, own_ref, other_ref, vec_ref, normed_ref, hidden_ref, slope_in, w_ref,
    part_out, grad_out, g_out, vec_out, low_ref, *rest
):
    units = w_ref.shape[1] // 2
    ticks.begin(1 + x_ref.shape[0] // CHUNK * (units // 512) + units // 256)
    residual_prologue(norm_row, None, x_ref, own_ref, other_ref, vec_ref, g_out, low_ref, vec_out)
    feed_backward_body(ticks, normed_ref, hidden_ref, slope_in, w_ref, part_out, grad_out, low_ref, *rest)


def feed_backward_call(norm_row, x, own, other, vectors, normed, hidden, slope, weights, rider=None):
    rows, depth = x.shape
    units = hidden.shape[1]
    return ride_call(
        functools.partial(feed_backward_kernel, norm_row),
        [x, own, other, vectors, normed, hidden, slope, weights[0]],
        [whole()] * 7 + [weight_spec(weights)],
        [
            shaped(rows, depth, low),
            shaped(depth, 2 * units, low),
            shaped(rows, depth, wide),
            shaped(2, depth, wide),
        ],
        feed_backward_scratch(rows, depth, units),
        rider,
        "feed_backward",
    )


def half_lanes(shape):
    return lax.broadcasted_iota(jnp.int32, shape, 1) < 64


def one_head(pair, head):
    first = half_lanes(pair.shape)
    zero = jnp.zeros_like(pair)
    return jnp.where(first, pair, zero) if head == 0 else jnp.where(first, zero, pair)


def key_bias(keys, mask_row, first_row, causal, rows):
    allowed = jnp.where(mask_row[...] > 0, 0.0, masked_score)
    if not causal:
        return allowed
    column = lax.broadcasted_iota(jnp.int32, (rows, keys), 1)
    row = first_row + lax.broadcasted_iota(jnp.int32, (rows, keys), 0)
    return jnp.where(column <= row, allowed, masked_score)


def attend_chunk(tick, first_row, length, causal, q_ref, kv_ref, w_ref, attended_out, totals_out, part_out):
    width = q_ref.shape[1]
    keys = kv_ref.shape[0]
    at = pl.ds(first_row, CHUNK)
    bias = key_bias(keys, length, first_row, causal, CHUNK)
    lane = lax.broadcasted_iota(jnp.int32, (CHUNK, 128), 1)
    totals = jnp.zeros((CHUNK, 128), wide)
    for begin in range(0, width, 128):
        tick(begin // 128)
        pair = q_ref[at, begin : begin + 128]
        key_pair = kv_ref[:, begin : begin + 128]
        value_pair = kv_ref[:, width + begin : width + begin + 128]
        results = []
        for head in range(2):
            scores = dot_nt(one_head(pair, head), key_pair) + bias
            peak = jnp.max(scores, axis=-1, keepdims=True)
            weights = jnp.exp(scores - peak)
            total = jnp.sum(weights, axis=-1, keepdims=True)
            results.append(dot_nn(weights.astype(low), value_pair) * (1.0 / total))
            totals = jnp.where(lane == begin // 64 + head, peak + jnp.log(total), totals)
        attended_out[at, begin : begin + 128] = jnp.where(
            lane < 64, results[0], results[1]
        ).astype(low)
    totals_out[at, :] = totals
    part_out[at, :] = dot_nt(attended_out[at, :], w_ref[:, 3 * width :]).astype(low)


def self_attention_kernel(
    rows_norm, causal, ticks, length_ref, x_ref, w_ref, vec_ref, normed_out, q_out, kv_out, attended_out, totals_out, part_out
):
    width = w_ref.shape[1] // 4
    gain = vec_ref[rows_norm : rows_norm + 1, :]
    shift = vec_ref[rows_norm + 1 : rows_norm + 2, :]
    steps = x_ref.shape[0] // CHUNK
    pairs = width // 128
    ticks.begin(steps * (pairs + 1))

    @pl.loop(0, steps)
    def _(step):
        ticks.in_loop(step, steps, 0, 1, 0)
        at = pl.ds(pl.multiple_of(step * CHUNK, CHUNK), CHUNK)
        normed = (centre_rows(x_ref[at, :].astype(wide)) * gain + shift).astype(low)
        normed_out[at, :] = normed
        q_out[at, :] = (dot_nn(normed, w_ref[:, :width]).astype(low).astype(wide) * 0.125).astype(low)
        kv_out[at, :] = dot_nn(normed, w_ref[:, width : 3 * width]).astype(low)

    length = length_ref

    @pl.loop(0, steps)
    def _(step):
        attend_chunk(
            functools.partial(ticks.in_loop, step, steps, steps, pairs),
            pl.multiple_of(step * CHUNK, CHUNK), length, causal, q_out, kv_out, w_ref, attended_out, totals_out, part_out
        )


def self_attention_call(rows_norm, causal, length, x, weights, vectors, rider=None):
    rows, depth = x.shape
    width = weights[1] // 4
    return ride_call(
        functools.partial(self_attention_kernel, rows_norm, causal),
        [length, x, weights[0], vectors],
        [whole(), whole(), weight_spec(weights), whole()],
        [
            shaped(rows, depth, low),
            shaped(rows, width, low),
            shaped(rows, 2 * width, low),
            shaped(rows, width, low),
            shaped(rows, 128, wide),
            shaped(rows, depth, low),
        ],
        [],
        rider,
        "self_attention",
    )


def cross_attention_kernel(
    ticks, length_ref, x_ref, own_ref, other_ref, mid_ref, mid_own, mid_other, w_ref, vec_ref,
    x_out, final_out, memory_out, normed_out, q_out, kv_out, attended_out, totals_out, part_out,
):
    width = w_ref.shape[1] // 4
    first_steps = mid_ref.shape[0] // CHUNK
    steps = x_ref.shape[0] // CHUNK
    pairs = width // 128
    ticks.begin(first_steps + steps * (pairs + 1))

    @pl.loop(0, first_steps)
    def _(step):
        ticks.in_loop(step, first_steps, 0, 1, 0)
        at = pl.ds(pl.multiple_of(step * CHUNK, CHUNK), CHUNK)
        x = mid_ref[at, :] + (mid_own[at, :].astype(wide) + mid_other[at, :].astype(wide))
        final_out[at, :] = x
        memory = (centre_rows(x) * vec_ref[4:5, :] + vec_ref[5:6, :]).astype(low)
        memory_out[at, :] = memory
        kv_out[at, :] = dot_nn(memory, w_ref[:, width : 3 * width]).astype(low)

    @pl.loop(0, steps)
    def _(step):
        ticks.in_loop(step, steps, first_steps, 1, 0)
        at = pl.ds(pl.multiple_of(step * CHUNK, CHUNK), CHUNK)
        x = x_ref[at, :].astype(wide) + (own_ref[at, :].astype(wide) + other_ref[at, :].astype(wide))
        x_out[at, :] = x
        normed = (centre_rows(x) * vec_ref[8:9, :] + vec_ref[9:10, :]).astype(low)
        normed_out[at, :] = normed
        q_out[at, :] = (dot_nn(normed, w_ref[:, :width]).astype(low).astype(wide) * 0.125).astype(low)

    length = length_ref

    @pl.loop(0, steps)
    def _(step):
        attend_chunk(
            functools.partial(ticks.in_loop, step, steps, first_steps + steps, pairs),
            pl.multiple_of(step * CHUNK, CHUNK), length, False, q_out, kv_out, w_ref, attended_out, totals_out, part_out
        )


def cross_attention_call(length, x, own, other, mid, mid_own, mid_other, weights, vectors, rider=None):
    rows, depth = x.shape
    keys = mid.shape[0]
    width = weights[1] // 4
    return ride_call(
        cross_attention_kernel,
        [length, x, own, other, mid, mid_own, mid_other, weights[0], vectors],
        [whole()] + [whole()] * 6 + [weight_spec(weights), whole()],
        [
            shaped(rows, depth, wide),
            shaped(keys, depth, wide),
            shaped(keys, depth, low),
            shaped(rows, depth, low),
            shaped(rows, width, low),
            shaped(keys, 2 * width, low),
            shaped(rows, width, low),
            shaped(rows, 128, wide),
            shaped(rows, depth, low),
        ],
        [],
        rider,
        "cross_attention",
    )


def attention_backward_kernel(
    causal, cross, norm_row, ticks, length_ref, previous_ref, x_ref, own_ref, other_ref, vec_ref,
    normed_ref, source_ref, q_ref, kv_ref, attended_ref, totals_ref, w_ref, *rest
):
    outs = 5 if cross else 4
    part_out, g_out, vec_out, grad_out = rest[:4]
    source_part_out = rest[4] if cross else None
    low_ref, scratch = rest[outs], rest[outs + 1 :]
    residual_prologue(norm_row, previous_ref, x_ref, own_ref, other_ref, vec_ref, g_out, low_ref, vec_out)
    attention_backward_main(
        causal, cross, ticks, length_ref, low_ref, normed_ref, source_ref, q_ref, kv_ref, attended_ref, totals_ref,
        w_ref, part_out, grad_out, source_part_out, *scratch,
    )


def attention_backward_main(
    causal, cross, ticks, length, low_ref, normed_ref, source_ref, q_ref, kv_ref, attended_ref, totals_ref, w_ref,
    part_out, grad_out, source_part_out, grad_q, grad_kv, turned_k, turned_v, turned_low, turned_normed, *rest
):
    turned_source = rest[0] if cross else turned_normed
    rows, depth = low_ref.shape
    keys = kv_ref.shape[0]
    width = q_ref.shape[1]
    steps = rows // CHUNK
    pairs = width // 128
    key_steps = keys // CHUNK
    after = 1 + steps * pairs
    last = after + key_steps
    ticks.begin(last + 5)
    ticks(0)
    turned_k[...] = jnp.zeros_like(turned_k)
    turned_v[...] = jnp.zeros_like(turned_v)

    @pl.loop(0, rows // CHUNK)
    def _(step):
        first_row = pl.multiple_of(step * CHUNK, CHUNK)
        at = pl.ds(first_row, CHUNK)
        grad_attended = dot_nn(low_ref[at, :], w_ref[:, 3 * width :]).astype(low)
        bias = key_bias(keys, length, first_row, causal, CHUNK)
        lane = lax.broadcasted_iota(jnp.int32, (CHUNK, 128), 1)
        totals = totals_ref[at, :]
        for begin in range(0, width, 128):
            ticks.in_loop(step, steps, 1, pairs, begin // 128)
            pair = q_ref[at, begin : begin + 128]
            key_pair = kv_ref[:, begin : begin + 128]
            value_pair = kv_ref[:, width + begin : width + begin + 128]
            grad_pair = grad_attended[:, begin : begin + 128]
            pair_turned = turned(pair)
            grad_turned = turned(grad_pair)
            results = []
            for head in range(2):
                number = begin // 64 + head
                total = jnp.sum(jnp.where(lane == number, totals, 0.0), axis=-1, keepdims=True)
                scores = dot_nt(one_head(pair, head), key_pair) + bias
                weights = jnp.exp(scores - total)
                grad_weights = dot_nt(one_head(grad_pair, head), value_pair)
                row_dot = jnp.sum(weights * grad_weights, axis=-1, keepdims=True)
                grad_scores = (weights * (grad_weights - row_dot)).astype(low)
                results.append(dot_nn(grad_scores, key_pair))
                span = slice(begin + 64 * head, begin + 64 * head + 64)
                local = slice(64 * head, 64 * head + 64)
                turned_k[span, :] += dot_nn(pair_turned[local, :], grad_scores)
                turned_v[span, :] += dot_nn(grad_turned[local, :], weights.astype(low))
            grad_q[at, begin : begin + 128] = (
                jnp.where(lane < 64, results[0], results[1]) * 0.125
            ).astype(low)
        if cross:
            part_out[at, :] = dot_nt(grad_q[at, :], w_ref[:, :width]).astype(low)

    grad_kv[:, :width] = turned(turned_k[...].astype(low))
    grad_kv[:, width:] = turned(turned_v[...].astype(low))

    @pl.loop(0, keys // CHUNK)
    def _(step):
        ticks.in_loop(step, key_steps, after, 1, 0)
        at = pl.ds(pl.multiple_of(step * CHUNK, CHUNK), CHUNK)
        from_source = dot_nt(grad_kv[at, :], w_ref[:, width : 3 * width])
        if cross:
            source_part_out[at, :] = from_source.astype(low)
        else:
            from_query = dot_nt(grad_q[at, :], w_ref[:, :width])
            part_out[at, :] = (from_source + from_query).astype(low)

    ticks(last)
    turn_into(turned_low, low_ref)
    turn_into(turned_normed, normed_ref)
    if cross:
        turn_into(turned_source, source_ref)
    ticks(last + 1)
    store_grad(grad_out, 0, dot_nn(turned_normed[...], grad_q[...]))
    ticks(last + 2)
    store_grad(grad_out, width, dot_nn(turned_source[...], grad_kv[:, :width]))
    ticks(last + 3)
    store_grad(grad_out, 2 * width, dot_nn(turned_source[...], grad_kv[:, width:]))
    ticks(last + 4)
    store_grad(grad_out, 3 * width, dot_nn(turned_low[...], attended_ref[...]))


def attention_backward_scratch(rows, keys, depth, width, cross):
    scratch = [
        pltpu.VMEM((rows, depth), low),
        pltpu.VMEM((rows, width), low),
        pltpu.VMEM((keys, 2 * width), low),
        pltpu.VMEM((width, keys), wide),
        pltpu.VMEM((width, keys), wide),
        pltpu.VMEM((depth, rows), low),
        pltpu.VMEM((depth, rows), low),
    ]
    if cross:
        scratch.append(pltpu.VMEM((depth, keys), low))
    return scratch


def attention_backward_call(
    causal, norm_row, length, previous, x, own, other, vectors, normed, source, q, kv, attended, totals, weights,
    rider=None,
):
    cross = source is not None
    rows, depth = x.shape
    keys = kv.shape[0]
    width = q.shape[1]
    outs = [
        shaped(rows, depth, low),
        shaped(rows, depth, wide),
        shaped(2, depth, wide),
        shaped(depth, 4 * width, low),
    ]
    if cross:
        outs.append(shaped(keys, depth, low))
    scratch = attention_backward_scratch(rows, keys, depth, width, cross)
    operands = [length, previous, x, own, other, vectors, normed]
    if cross:
        operands.append(source)
    operands += [q, kv, attended, totals, weights[0]]

    def body(ticks, *refs):
        if not cross:
            refs = refs[:7] + (None,) + refs[7:]
        attention_backward_kernel(causal, cross, norm_row, ticks, *refs)

    return ride_call(
        body,
        operands,
        [whole()] + [whole()] * (len(operands) - 2) + [weight_spec(weights)],
        outs,
        scratch,
        rider,
        "attention_backward",
    )


def finish_kernel(norm_row, previous_ref, x_ref, own_ref, other_ref, vec_ref, g_out, vec_out):
    residual_prologue(norm_row, previous_ref, x_ref, own_ref, other_ref, vec_ref, g_out, None, vec_out)


def finish_call(norm_row, previous, x, own, other, vectors):
    rows, depth = x.shape
    return pl.pallas_call(
        functools.partial(finish_kernel, norm_row),
        out_shape=(shaped(rows, depth, wide), shaped(2, depth, wide)),
        compiler_params=pltpu.CompilerParams(vmem_limit_bytes=40 << 20),
        name="finish_norm",
    )(previous, x, own, other, vectors)


class Stream:
    def __init__(self):
        self.steps = {True: [], False: []}
        self.begins, self.ends = [], []
        self.position = {True: 0, False: 0}
        self.movers = []

    def add(self, mover, overlap=0.0):
        self.movers.append(mover)
        begin, end = {}, {}
        for home in (True, False):
            had, new = self.steps[home], mover.steps[home]
            shared = min(int(len(new) * overlap), len(had))
            kept = len(had) - shared
            merged = had[:kept]
            for one, two in zip(had[kept:], new[:shared]):
                merged += [one, two]
            merged += new[shared:]
            for mark in self.ends:
                if mark[home] > kept:
                    mark[home] = kept + 2 * (mark[home] - kept)
            self.steps[home] = merged
            begin[home], end[home] = kept, len(merged)
        self.begins.append(begin)
        self.ends.append(end)

    def between(self, one, two, share):
        return {home: one[home] + int((two[home] - one[home]) * share) for home in (True, False)}

    def plan(self, marks, shares=(1.0,)):
        windows, done, start = [], 0.0, dict(self.position)
        for share in shares:
            done += share / sum(shares)
            end = {
                home: max(
                    self.position[home],
                    start[home] + round((marks[home] - start[home]) * done),
                )
                for home in (True, False)
            }
            windows.append(Window(self, dict(self.position), end))
            self.position = end
        return windows

    def run(self, chosen):
        for home in (True, False):
            if not chosen[home]:
                continue
            wanted = place("c") == place("x")

            @pl.when(wanted if home else jnp.logical_not(wanted))
            def _():
                for step in chosen[home]:
                    step()

    def finish(self):
        for mover in self.movers:
            mover.finish()


class Window:
    def __init__(self, stream, start, end):
        self.stream, self.start, self.end = stream, start, end
        self.parts = 1

    def begin(self, parts):
        self.parts = parts

    def __call__(self, part=0):
        chosen = {}
        for home in (True, False):
            start, size = self.start[home], self.end[home] - self.start[home]
            first = start + size * part // self.parts
            chosen[home] = self.stream.steps[home][first : start + size * (part + 1) // self.parts]
        self.stream.run(chosen)

    def in_loop(self, step, steps, offset, stride, inner):
        if all(self.start[home] == self.end[home] for home in (True, False)):
            return
        for number in range(steps):

            @pl.when(step == number)
            def _():
                self(offset + number * stride + inner)


class Bag:
    def __init__(self, **entries):
        self.__dict__.update(entries)

    def names(self):
        return list(self.__dict__)

    def values(self):
        return list(self.__dict__.values())

    def joined(self, other):
        return Bag(**self.__dict__, **other.__dict__)


def filled(names, values):
    return Bag(**dict(zip(names, values)))


class Nothing:
    def begin(self, parts):
        pass

    def __call__(self, part=0):
        pass

    def in_loop(self, *unused):
        pass


nothing = Nothing()


def vmem_like(ref):
    return pltpu.VMEM(ref.shape, ref.dtype)


class Direct:
    def __init__(self, ref):
        self.ref = ref


class Swap:
    def __init__(self, target, send_sem, recv_sem):
        self.target, self.send_sem, self.recv_sem = target, send_sem, recv_sem

    def copy(self, source):
        return pltpu.make_async_remote_copy(
            src_ref=source,
            dst_ref=self.target,
            send_sem=self.send_sem,
            recv_sem=self.recv_sem,
            device_id=target_of("c"),
            device_id_type=MESH,
        )

    def arrive(self):
        self.copy(self.target).wait_recv()


def run_phase(body, sems, ins, outs, scratch=(), swaps=(), before=nothing, after=nothing):
    moved_in = [ref for ref in ins if not isinstance(ref, Direct)]
    moved_out = [ref for ref in outs if not isinstance(ref, Direct)]

    def scoped(*refs):
        own_in, rest = refs[: len(moved_in)], refs[len(moved_in) :]
        own_out, own_scratch = rest[: len(moved_out)], rest[len(moved_out) :]
        copies = [
            pltpu.make_async_copy(ref, own, sems.at[number])
            for number, (ref, own) in enumerate(zip(moved_in, own_in))
        ]
        for copy in copies:
            copy.start()
        before()
        for copy in copies:
            copy.wait()
        own_in, own_out = iter(own_in), iter(own_out)
        all_in = [ref.ref if isinstance(ref, Direct) else next(own_in) for ref in ins]
        all_out = [ref.ref if isinstance(ref, Direct) else next(own_out) for ref in outs]
        body(*all_in, *all_out, *own_scratch)
        copies = []
        for number, swap in swaps:
            swap.copy(all_out[number]).start()
        for ref, own in zip(outs, all_out):
            if not isinstance(ref, Direct):
                copy = pltpu.make_async_copy(own, ref, sems.at[16 + len(copies)])
                copy.start()
                copies.append(copy)
        after()
        for copy in copies:
            copy.wait()
        for number, swap in swaps:
            swap.copy(all_out[number]).wait_send()

    allocations = [vmem_like(ref) for ref in moved_in] + [vmem_like(ref) for ref in moved_out]
    pl.run_scoped(scoped, *allocations, *scratch)


def prefetched(sems, ins, use):
    def scoped(*own):
        copies = [
            pltpu.make_async_copy(ref, one, sems.at[32 + number])
            for number, (ref, one) in enumerate(zip(ins, own))
        ]
        for copy in copies:
            copy.start()

        def wait():
            for copy in copies:
                copy.wait()

        use([Direct(one) for one in own], wait)

    pl.run_scoped(scoped, *[vmem_like(ref) for ref in ins])


def column_of(row_ref, first_row):
    size = row_ref.shape[1]
    lane = lax.broadcasted_iota(jnp.int32, (CHUNK, size), 1)
    row = first_row + lax.broadcasted_iota(jnp.int32, (CHUNK, size), 0)
    return jnp.sum(jnp.where(lane == row, row_ref[...], 0), axis=-1, keepdims=True)


class Inputs(Mover):
    def __init__(self, send_sems, recv_sems, local_sems):
        super().__init__(send_sems)
        self.recv_sems, self.local_sems = recv_sems, local_sems
        self.count = 0

    def taken(self):
        steps = self.steps
        self.steps = {True: [], False: []}
        return steps

    def swap(self, source, target):
        number = self.count
        self.count += 1

        def diagonal():
            return {"c": 1 - place("c"), "x": 1 - place("x")}

        def local():
            return pltpu.make_async_copy(source(), target(True), self.local_sems.at[number])

        self.local(True, lambda: local().start())
        self.send(
            False,
            source,
            functools.partial(target, False),
            lambda: self.recv_sems.at[number],
            diagonal,
        )

        def arrive():
            self.local(True, lambda: local().wait())
            self.wait(False, functools.partial(target, True), lambda: self.recv_sems.at[number])

        return arrive

    def share(self, piece):
        number = self.count
        self.count += 1

        def sem():
            return self.recv_sems.at[number]

        for home in (True, False):
            self.send(
                home,
                functools.partial(piece, True),
                functools.partial(piece, True),
                sem,
                functools.partial(target_of, "c"),
            )

        def arrive():
            for home in (True, False):
                self.wait(home, functools.partial(piece, False), sem)

        return arrive


def half_of(ref, own):
    size = ref.shape[0] // 2
    core = place("c") if own else 1 - place("c")
    return ref.at[pl.ds(core * size, size), :]


def half_lanes_of(ref, own):
    size = ref.shape[1] // 2
    core = place("c") if own else 1 - place("c")
    return ref.at[:, pl.ds(core * size, size)]


def source_mask(marks_row):
    quarter = marks_row.shape[1] // 4
    return marks_row.at[:, pl.ds(quarter, 2 * quarter)]


def target_mask(marks_row):
    quarter = marks_row.shape[1] // 4
    return marks_row.at[:, pl.ds(3 * quarter, quarter)]


def any_space():
    return pl.BlockSpec(memory_space=pl.ANY)


def spliced(one, two, at):
    return {home: one[home][: at[home]] + two[home] + one[home][at[home] :] for home in (True, False)}


def shares_of(steps, share):
    return {home: int(len(steps[home]) * share) for home in (True, False)}


def forward_kernel(names_in, names_out, *refs):
    count_in, count_out = len(names_in), len(names_out)
    i = filled(names_in, refs[:count_in])
    o = filled(names_out, refs[count_in : count_in + count_out])
    (marks_row, flags_row, *rest) = refs[count_in + count_out :]
    stages, owns, rest = rest[:5], rest[5:10], rest[10:]
    sems, group_send, group_recv, group_local, in_send, in_recv, in_local, swap_sems = rest
    vec = i.vectors
    greet_others()
    for number in range(12):
        width = i.attention.shape[2]
        at = number % 4 * width
        owns[number // 4][:, at : at + width] = i.attention[number].astype(low)
    for number in range(4):
        width = i.feed.shape[2]
        at = number % 2 * width
        owns[3 + number // 2][:, at : at + width] = i.feed[number].astype(low)
    greeted()

    start = Inputs(Part(in_send, 0), Part(in_recv, 0), Part(in_local, 0))
    marks_here = start.swap(lambda: i.marks, lambda own: marks_row)
    source_here = start.swap(lambda: i.source, functools.partial(half_of, o.source_all))
    opening = start.taken()
    marks_here()
    flags_size = flags_row.shape[1] // 2

    def flags_piece(own):
        return half_lanes_of(flags_row, own)

    def flags_local():
        return pltpu.make_async_copy(
            marks_row.at[:, pl.ds(0, flags_size)], flags_piece(True), in_local.at[8]
        )

    for home in (True, False):
        start.local(home, lambda: flags_local().start())
        start.local(home, lambda: flags_local().wait())
    flags_there = start.share(flags_piece)
    source_here()
    source_there = start.share(functools.partial(half_of, o.source_all))
    middle = start.taken()
    flags_there()
    source_there()
    closing = start.taken()

    units = i.feed.shape[2]
    gathers = []
    for number, (own, gathered, first_column, columns) in enumerate(
        (
            (owns[0], o.all_1, 0, owns[0].shape[1]),
            (owns[1], o.all_3, 0, owns[1].shape[1]),
            (owns[3], o.all_2, 0, 2 * units),
            (owns[2], o.all_4, 0, owns[2].shape[1]),
            (owns[4], o.all_5, 0, 2 * units),
        )
    ):
        gathers.append(
            Gather(
                own,
                gathered,
                stages[number],
                group_local.at[number],
                Part(group_send, number * GATHER_SENDS),
                Part(group_recv, number * 64),
                first_column,
                columns,
            )
        )
    first, second, last = gathers[0], gathers[1], gathers[4]
    steps = spliced(first.steps, middle, shares_of(first.steps, 0.6))
    first.steps = {home: opening[home] + steps[home] + closing[home] for home in (True, False)}

    def bring(source, target, first_send, first_recv, first_local):
        mover = Inputs(Part(in_send, first_send), Part(in_recv, first_recv), Part(in_local, first_local))
        here_now = mover.swap(lambda: source, functools.partial(half_of, target))
        begin = mover.taken()
        here_now()
        there_now = mover.share(functools.partial(half_of, target))
        there_now()
        return mover, begin, mover.taken()

    target_mover, begin, rest = bring(i.target, o.target_all, 16, 8, 9)
    steps = spliced(second.steps, rest, shares_of(second.steps, 0.4))
    second.steps = {home: begin[home] + steps[home] for home in (True, False)}
    cotangent_mover, begin, late_steps = bring(i.cotangent, o.cotangent_all, 24, 12, 13)
    last.steps = spliced(last.steps, begin, shares_of(last.steps, 0.95))
    stream = Stream()
    stream.movers += [start, target_mover, cotangent_mover]
    for number, mover in enumerate(gathers):
        stream.add(mover, 0.4 if number > 1 else 0.0)
    ends = stream.ends

    swap_refs = (o.other_1, o.other_2, o.other_3, o.other_4, o.other_5)
    swaps = [
        Swap(ref, swap_sems.at[number], swap_sems.at[8 + number])
        for number, ref in enumerate(swap_refs)
    ]

    stream.plan(ends[0])[0]()

    one, ticks, two = stream.plan(stream.between(ends[1], ends[2], 0.25), (1, 7, 1))

    def encoder_attention_body(source_ref, w_ref, x_out, *outs):
        @pl.loop(0, x_out.shape[0] // CHUNK)
        def _(step):
            first_row = pl.multiple_of(step * CHUNK, CHUNK)
            at = pl.ds(first_row, CHUNK)
            kind = column_of(flags_row, first_row)
            x_out[at, :] = jnp.where(
                kind == 1, vec[12:13, :], jnp.where(kind == 2, vec[13:14, :], source_ref[at, :].astype(wide))
            )

        self_attention_kernel(0, False, ticks, source_mask(marks_row), x_out, w_ref, vec, *outs)

    run_phase(
        encoder_attention_body,
        sems,
        [o.source_all, o.all_1],
        [o.start, o.normed_1, o.query_1, o.kv_1, o.attended_1, o.totals_1, o.part_1],
        swaps=[(6, swaps[0])],
        before=one,
        after=two,
    )
    one, ticks_two, two = stream.plan(stream.between(ends[1], ends[2], 0.6), (1, 6, 1))

    def decoder_attention_body(x_ref, w_ref, *outs):
        self_attention_kernel(6, True, ticks_two, target_mask(marks_row), x_ref, w_ref, vec, *outs)

    run_phase(
        decoder_attention_body,
        sems,
        [o.target_all, o.all_3],
        [o.normed_3, o.query_3, o.kv_3, o.attended_3, o.totals_3, o.part_3],
        swaps=[(5, swaps[2])],
        before=one,
        after=two,
    )
    stream.plan(ends[2])[0]()
    swaps[0].arrive()
    one, ticks_three, two = stream.plan(stream.between(ends[3], ends[4], 0.2), (1, 5, 1))

    def encoder_feed_body(x_ref, own_ref, other_ref, w_ref, *outs):
        feed_forward_kernel(2, ticks_three, x_ref, own_ref, other_ref, w_ref, vec, *outs)

    run_phase(
        encoder_feed_body,
        sems,
        [o.start, o.part_1, o.other_1, o.all_2],
        [o.mid, o.normed_2, o.hidden_2, o.slope_2, o.part_2],
        swaps=[(4, swaps[1])],
        before=one,
        after=two,
    )
    stream.plan(ends[3])[0]()
    swaps[2].arrive()
    swaps[1].arrive()
    one, ticks_four, two = stream.plan(ends[4], (1, 5, 1))

    def cross_attention_body(x_ref, own_ref, other_ref, mid_ref, mid_own, mid_other, w_ref, *outs):
        cross_attention_kernel(
            ticks_four, source_mask(marks_row), x_ref, own_ref, other_ref, mid_ref, mid_own, mid_other, w_ref, vec, *outs
        )

    run_phase(
        cross_attention_body,
        sems,
        [o.target_all, o.part_3, o.other_3, o.mid, o.part_2, o.other_2, o.all_4],
        [o.one, o.final, o.memory, o.normed_4, o.query_4, o.kv_4, o.attended_4, o.totals_4, o.part_4],
        swaps=[(8, swaps[3])],
        before=one,
        after=two,
    )
    swaps[3].arrive()

    def decoder_feed_body(x_ref, own_ref, other_ref, w_ref, *outs):
        feed_forward_kernel(10, nothing, x_ref, own_ref, other_ref, w_ref, vec, *outs)

    run_phase(
        decoder_feed_body,
        sems,
        [o.one, o.part_4, o.other_4, o.all_5],
        [o.two, o.normed_5, o.hidden_5, o.slope_5, o.part_5],
        swaps=[(4, swaps[4])],
    )
    stream.run(late_steps)
    o.marks_all[...] = marks_row[...]
    o.flags_all[...] = flags_row[...]
    swaps[4].arrive()
    stream.finish()


def attention_kept(rows, keys, depth, width):
    return (
        shaped(rows, depth, low),
        shaped(rows, width, low),
        shaped(keys, 2 * width, low),
        shaped(rows, width, low),
        shaped(rows, 128, wide),
    )


def feed_kept(rows, depth, units):
    return shaped(rows, depth, low), shaped(rows, units, low), shaped(rows, units, low)


def specs_of(near, far):
    return [whole() for unused in near.values()] + [any_space() for unused in far.values()]


def dma(count):
    return pltpu.SemaphoreType.DMA((count,))


def forward_call(source, target, cotangent, marks, vectors, attention, feed):
    depth = vectors.shape[1]
    rows, few = 2 * source.shape[0], 2 * target.shape[0]
    block, width, units = attention.shape[1], attention.shape[2], feed.shape[2]
    near_in = Bag(marks=marks, vectors=vectors, attention=attention, feed=feed)
    far_in = Bag(source=source, target=target, cotangent=cotangent)
    near_out = Bag(
        marks_all=jax.ShapeDtypeStruct(marks.shape, marks.dtype),
        flags_all=jax.ShapeDtypeStruct((1, rows), marks.dtype),
    )
    far_out = Bag(
        source_all=shaped(rows, depth, low),
        target_all=shaped(few, depth, low),
        cotangent_all=shaped(few, depth, low),
        start=shaped(rows, depth, wide),
        mid=shaped(rows, depth, wide),
        final=shaped(rows, depth, wide),
        memory=shaped(rows, depth, low),
        one=shaped(few, depth, wide),
        two=shaped(few, depth, wide),
    )
    f = far_out
    f.normed_1, f.query_1, f.kv_1, f.attended_1, f.totals_1 = attention_kept(rows, rows, depth, width)
    f.normed_3, f.query_3, f.kv_3, f.attended_3, f.totals_3 = attention_kept(few, few, depth, width)
    f.normed_4, f.query_4, f.kv_4, f.attended_4, f.totals_4 = attention_kept(few, rows, depth, width)
    f.normed_2, f.hidden_2, f.slope_2 = feed_kept(rows, depth, units)
    f.normed_5, f.hidden_5, f.slope_5 = feed_kept(few, depth, units)
    f.part_1 = f.other_1 = f.part_2 = f.other_2 = shaped(rows, depth, low)
    f.part_3 = f.other_3 = f.part_4 = f.other_4 = f.part_5 = f.other_5 = shaped(few, depth, low)
    f.all_1 = f.all_3 = f.all_4 = shaped(16 * block, 4 * width, low)
    f.all_2 = f.all_5 = shaped(16 * block, 2 * units, low)
    ins, outs = near_in.joined(far_in), near_out.joined(far_out)
    stage = [
        pltpu.VMEM((8, block, gather_cuts(columns)[1][1]), low)
        for columns in (4 * width, 4 * width, 2 * units, 4 * width, 2 * units)
    ]
    stage += [pltpu.VMEM((block, columns), low) for columns in [4 * width] * 3 + [2 * units] * 2]
    results = pl.pallas_call(
        functools.partial(forward_kernel, ins.names(), outs.names()),
        out_shape=tuple(outs.values()),
        in_specs=specs_of(near_in, far_in),
        out_specs=tuple(specs_of(near_out, far_out)),
        scratch_shapes=[
            pltpu.VMEM(marks.shape, marks.dtype),
            pltpu.VMEM((1, rows), marks.dtype),
            *stage,
            dma(32),
            dma(6 * GATHER_SENDS),
            dma(6 * 64),
            dma(6),
            dma(32),
            dma(16),
            dma(18),
            dma(16),
        ],
        compiler_params=pltpu.CompilerParams(
            collective_id=0, has_side_effects=True, vmem_limit_bytes=60 << 20
        ),
        name="forward_pass",
    )(*ins.values())
    return filled(outs.names(), results)


def backward_kernel(names_in, names_out, *refs):
    count_in, count_out = len(names_in), len(names_out)
    i = filled(names_in, refs[:count_in])
    o = filled(names_out, refs[count_in : count_in + count_out])
    rest = refs[count_in + count_out :]
    vectors_of, rest = dict(zip((0, 2, 4, 6, 8, 10, 12), rest[:7])), rest[7:]
    vector_rows, rest = rest[0], rest[1:]
    buffers = []
    for unused in range(6):
        buffers.append(rest[:SCATTER_BUFFERS])
        rest = rest[SCATTER_BUFFERS:]
    sems, group_send, group_recv, in_send, in_recv, in_local, swap_sems = rest
    vec, marks_row, flags_row = i.vectors, i.marks_all, i.flags_all
    finals = (o.final_5, o.final_4, o.final_3, o.final_2, o.final_1, o.final_vectors)
    greet()
    stream = Stream()
    for number in range(6):
        mover = Scatter(
            buffers[number],
            finals[number],
            Part(group_send, number * SCATTER_SENDS),
            Part(group_recv, number * 80),
        )
        stream.add(mover, (0.0, 0.85, 0.85, 0.85, 0.5, 0.0)[number])
    begins, ends = stream.begins, stream.ends
    swap_refs = (o.other_6, o.other_7, o.other_8, o.other_9, o.other_10, o.other_11)
    swaps = [
        Swap(ref, swap_sems.at[number], swap_sems.at[8 + number])
        for number, ref in enumerate(swap_refs)
    ]

    def total_of(number):
        return Direct(buffers[number][0])

    moves = Inputs(Part(in_send, 0), Part(in_recv, 0), Part(in_local, 0))

    swaps_before = []

    def result_body(x_ref, own_ref, other_ref, out):
        total = own_ref[...].astype(wide) + other_ref[...].astype(wide)
        out[...] = (x_ref[...] + total).astype(low)

    def last_feed_body(*refs):
        last_feed_backward_kernel(nothing, target_mask(marks_row), *refs)

    rows, depth = i.cotangent_all.shape
    units = i.hidden_5.shape[1]
    run_phase(
        last_feed_body,
        sems,
        [i.cotangent_all, i.normed_5, i.hidden_5, i.slope_5, i.all_5],
        [o.part_6, total_of(0), o.grad_three],
        feed_backward_scratch(rows, depth, units)[1:],
        swaps=[(0, swaps[0])],
    )
    run_phase(
        result_body,
        sems,
        [i.two, i.part_5, i.other_5],
        [o.three],
        before=stream.plan(stream.between(stream.position, begins[1], 0.15))[0],
    )
    result_here = moves.swap(functools.partial(half_of, o.three, True), lambda own: o.decoder_out)
    stream.run(moves.taken())
    swaps[0].arrive()

    def residual(norm_row, previous, x, own, other, grad_out, low_ref, before=nothing, ticks=nothing, after=nothing):
        ins = [x, own, other] + ([previous] if previous is not None else [])

        def body(*refs):
            if previous is None:
                x_ref, own_ref, other_ref, grad_ref = refs
                previous_ref = None
            else:
                x_ref, own_ref, other_ref, previous_ref, grad_ref = refs
            residual_prologue(
                norm_row, previous_ref, x_ref, own_ref, other_ref, vec, grad_ref, low_ref, vectors_of[norm_row], ticks
            )

        run_phase(body, sems, ins, [grad_out], before=before, after=after)

    def attention(number, causal, marks, norm_row, previous, x, own, other, grad_out, parts, mask_row, source, kept):
        rows, depth = x.shape
        keys, width = kept[2].shape[0], kept[1].shape[1]
        cross = source is not None
        early, prologue, late, main_in, ticks, main_out = stream.plan(marks, (1, 1, 1, 1, 8, 1))

        def inner(low_ref, ins, wait):
            residual(norm_row, previous, x, own, other, grad_out, low_ref, early, prologue, late)
            wait()
            ins = [kept[0]] + ([source] if cross else []) + ins
            outs = [part for part, swap in parts] + [total_of(number)]

            def body(*refs):
                normed_ref, refs = refs[0], refs[1:]
                source_ref = None
                if cross:
                    source_ref, refs = refs[0], refs[1:]
                held, refs = refs[:5], refs[5:]
                part_out, refs = refs[0], refs[1:]
                source_part = None
                if cross:
                    source_part, refs = refs[0], refs[1:]
                grad_total, scratch = refs[0], refs[1:]
                attention_backward_main(
                    causal, cross, ticks, mask_row, low_ref, normed_ref, source_ref, *held,
                    part_out, grad_total, source_part, *scratch,
                )

            run_phase(
                body,
                sems,
                ins,
                outs,
                attention_backward_scratch(rows, keys, depth, width, cross)[1:],
                swaps=[(at, swap) for at, (part, swap) in enumerate(parts)],
                before=main_in,
                after=main_out,
            )

        pl.run_scoped(
            lambda low_ref: prefetched(sems, kept[1:], functools.partial(inner, low_ref)),
            pltpu.VMEM((rows, depth), low),
        )

    attention(
        1, False, begins[1], 10, o.grad_three, i.two, o.part_6, o.other_6, o.grad_two,
        [(o.part_7, swaps[1]), (o.part_8, swaps[2])], source_mask(marks_row), i.memory,
        (i.normed_4, i.query_4, i.kv_4, i.attended_4, i.totals_4, i.all_4),
    )
    swaps[1].arrive()
    attention(
        2, True, begins[2], 8, o.grad_two, i.one, o.part_7, o.other_7, o.grad_one,
        [(o.part_9, swaps[3])], target_mask(marks_row), None,
        (i.normed_3, i.query_3, i.kv_3, i.attended_3, i.totals_3, i.all_3),
    )
    swaps[2].arrive()
    rows, depth = i.final.shape
    early, prologue, late, main_in, ticks, main_out = stream.plan(begins[3], (1, 1, 1, 1, 6, 1))

    def feed(low_ref, ins, wait):
        residual(4, None, i.final, o.part_8, o.other_8, o.grad_final, low_ref, early, prologue, late)
        wait()

        def body(normed_ref, hidden_ref, slope_ref, w_ref, part_out, grad_total, turned_ref, turned_low):
            ticks.begin(feed_backward_ticks(rows, units))
            feed_backward_body(
                ticks, normed_ref, hidden_ref, slope_ref, w_ref, part_out, grad_total, low_ref, slope_ref,
                turned_ref, turned_low,
            )

        run_phase(
            body,
            sems,
            [ins[0], i.hidden_2, i.slope_2, ins[1]],
            [o.part_10, total_of(3)],
            feed_backward_scratch(rows, depth, units)[2:],
            swaps=[(0, swaps[4])],
            before=main_in,
            after=main_out,
        )

    feed_ins = [i.normed_2, i.all_2]
    pl.run_scoped(
        lambda low_ref: prefetched(sems, feed_ins, functools.partial(feed, low_ref)),
        pltpu.VMEM((rows, depth), low),
    )
    swaps[3].arrive()
    residual(
        6, o.grad_one, i.target_all, o.part_9, o.other_9, o.target_low, None,
        stream.plan(stream.between(stream.position, begins[4], 0.1))[0],
    )
    target_here = moves.swap(functools.partial(half_of, o.target_low, True), lambda own: o.target_grad)
    stream.run(moves.taken())
    swaps[4].arrive()
    attention(
        4, False, begins[4], 2, o.grad_final, i.mid, o.part_10, o.other_10, o.grad_mid,
        [(o.part_11, swaps[5])], source_mask(marks_row), None,
        (i.normed_1, i.query_1, i.kv_1, i.attended_1, i.totals_1, i.all_1),
    )
    one, two, three = stream.plan(stream.between(stream.position, ends[4], 0.5), (2, 2, 1))
    one()
    swaps[5].arrive()

    def finish_body(previous_ref, x_ref, own_ref, other_ref, grad_out):
        norms, kinds = vectors_of[0], vectors_of[12]
        norms[...] = jnp.zeros_like(norms)
        kinds[...] = jnp.zeros_like(kinds)

        @pl.loop(0, x_ref.shape[0] // CHUNK)
        def _(step):
            first_row = pl.multiple_of(step * CHUNK, CHUNK)
            at = pl.ds(first_row, CHUNK)
            grads = own_ref[at, :].astype(wide) + other_ref[at, :].astype(wide)
            back, by_gain, by_shift = norm_back(x_ref[at, :], vec[0:1, :], grads)
            back = back + previous_ref[at, :]
            grad_out[at, :] = back.astype(low)
            norms[0:1, :] += by_gain
            norms[1:2, :] += by_shift
            kind = column_of(flags_row, first_row)
            kinds[0:1, :] += jnp.sum(jnp.where(kind == 1, back, 0.0), axis=0, keepdims=True)
            kinds[1:2, :] += jnp.sum(jnp.where(kind == 2, back, 0.0), axis=0, keepdims=True)

        vector_rows[...] = jnp.zeros_like(vector_rows)
        for first, pair in vectors_of.items():
            vector_rows[first : first + 2, :] = pair[...]
        every = jnp.concatenate([vector_rows[...], jnp.zeros((112, depth), wide)], axis=0)
        store_grad(buffers[5][0], 0, turned(every.astype(low)))

    run_phase(
        finish_body,
        sems,
        [o.grad_mid, i.start, o.part_11, o.other_11],
        [o.source_low],
        before=two,
        after=three,
    )
    source_here = moves.swap(functools.partial(half_of, o.source_low, True), lambda own: o.source_grad)
    stream.run(moves.taken())
    rest = {}
    for home in (True, False):
        late = stream.steps[home][stream.position[home] : ends[4][home]]
        few = stream.steps[home][ends[4][home] :]
        merged = []
        for number in range(max(len(late), len(few))):
            merged += few[number : number + 1] + late[number : number + 1]
        rest[home] = merged
    stream.run(rest)
    result_here()
    target_here()
    source_here()
    stream.run(moves.taken())
    moves.finish()
    stream.finish()


def backward_call(kept, vectors):
    rows, depth = kept.start.shape
    few = kept.one.shape[0]
    block = depth // 16
    near_in = Bag(vectors=vectors, marks_all=kept.marks_all, flags_all=kept.flags_all)
    far_in = Bag(**kept.__dict__)
    del far_in.marks_all, far_in.flags_all
    columns = [
        kept.all_5.shape[1], kept.all_4.shape[1], kept.all_3.shape[1], kept.all_2.shape[1], kept.all_1.shape[1], 128
    ]
    near_out = Bag()
    n = near_out
    n.final_5, n.final_4, n.final_3, n.final_2, n.final_1, n.final_vectors = [
        shaped(block, count, wide) for count in columns
    ]
    far_out = Bag(
        grad_three=shaped(few, depth, low),
        grad_two=shaped(few, depth, wide),
        grad_one=shaped(few, depth, wide),
        grad_final=shaped(rows, depth, wide),
        grad_mid=shaped(rows, depth, wide),
        target_low=shaped(few, depth, low),
        source_low=shaped(rows, depth, low),
        target_grad=shaped(few // 2, depth, low),
        source_grad=shaped(rows // 2, depth, low),
        three=shaped(few, depth, low),
        decoder_out=shaped(few // 2, depth, low),
    )
    f = far_out
    f.part_6 = f.other_6 = f.part_7 = f.other_7 = f.part_9 = f.other_9 = shaped(few, depth, low)
    f.part_8 = f.other_8 = f.part_10 = f.other_10 = f.part_11 = f.other_11 = shaped(rows, depth, low)
    ins, outs = near_in.joined(far_in), near_out.joined(far_out)
    scratch = [pltpu.VMEM((2, depth), wide)] * 7 + [pltpu.VMEM((16, depth), wide)]
    for count in columns:
        scratch += scatter_buffers(block, count)
    results = pl.pallas_call(
        functools.partial(backward_kernel, ins.names(), outs.names()),
        out_shape=tuple(outs.values()),
        in_specs=specs_of(near_in, far_in),
        out_specs=tuple(specs_of(near_out, far_out)),
        scratch_shapes=scratch
        + [dma(48), dma(6 * SCATTER_SENDS), dma(6 * 80), dma(8), dma(8), dma(8), dma(16)],
        compiler_params=pltpu.CompilerParams(
            collective_id=1, has_side_effects=True, vmem_limit_bytes=61 << 20
        ),
        name="backward_pass",
    )(*ins.values())
    return filled(outs.names(), results)


def lane_slot(number):
    return number if number < 12 else number + 4


def update_kernel(
    f1_far, f2_far, f3_far, f4_far, f5_far, aw_far, fw_far, fv, ra, ca, rf, cf, vp, vl, vm,
    ag, fg, vg, au, fu, vu, ran, can, rfn, cfn, vmn, fng,
    f1, f2, f3, f4, f5, aw, fw, square, other_square, mine, theirs, line, line_in, send_sems, recv_sems, load_sems,
):
    loads = [
        pltpu.make_async_copy(source, target, load_sems.at[number])
        for number, (source, target) in enumerate(
            (
                (f1_far, f1), (f2_far, f2), (f3_far, f3), (f4_far, f4), (f5_far, f5), (aw_far, aw), (fw_far, fw),
            )
        )
    ]
    for load in loads:
        load.start()
    rows = f1.shape[0]
    depth = 16 * rows
    width, units = aw.shape[2], fw.shape[2]
    barrier = pltpu.get_barrier_semaphore()
    z = place("z")
    near = z + 1 - 2 * lax.rem(z, 2)
    far = lax.rem(z + 2, 4)
    partners = [target_of("x"), target_of("c"), target_of("y"), {"z": near}, {"z": far}]
    for partner in partners:
        pl.semaphore_signal(barrier, inc=1, device_id=partner, device_id_type=MESH)
    keep, take = decay_rate, 1.0 - decay_rate
    finals = (f1, f3, f4, f2, f5)
    matrices = []
    for number in range(16):
        if number < 12:
            final, at, size = finals[number // 4], number % 4 * width, width
            held = (aw, ag, au, number, ca, can)
        else:
            final, at, size = finals[3 + (number - 12) // 2], (number - 12) % 2 * units, units
            held = (fw, fg, fu, number - 12, cf, cfn)
        matrices.append((final, at, size, number * width if number < 12 else 12 * width + (number - 12) * units, held))
    columns = 12 * width + 4 * units

    square[...] = jnp.zeros_like(square)
    square[0:12, 0:rows] = ra[...]
    square[16:20, 0:rows] = rf[...]
    moments = jnp.transpose(square[...])[0:rows, :]
    other_square[...] = jnp.ones_like(other_square)
    other_square[0:14, 0:rows] = vm[...]
    other_square[16:30, 0:rows] = vl[...]
    scale = jnp.sqrt(jnp.mean(vp[...] * vp[...], axis=1, keepdims=True))
    other_square[16:30, rows : rows + 128 - rows] = jnp.broadcast_to(scale, (14, 128 - rows))
    turned_vectors = jnp.transpose(other_square[...])
    vector_moments = turned_vectors[0:rows, :]
    shifted = pltpu.roll(turned_vectors, 112, 1)
    vector_local, vector_scale = shifted[0:rows, :], shifted[rows : rows + 1, :]

    for load in loads:
        load.wait()
    lane = lax.broadcasted_iota(jnp.int32, (rows, 128), 1)
    one_lane = lax.broadcasted_iota(jnp.int32, (1, 128), 1)
    row_sums = jnp.zeros((rows, 128), wide)
    totals = pltpu.roll(jnp.sum(moments, axis=0, keepdims=True) * 0.5, 64, 1)
    for number, (final, at, size, begin, held) in enumerate(matrices):
        grads = final[:, at : at + size]
        squares = grads * grads
        by_row = jnp.sum(squares, axis=1, keepdims=True)
        line[:, begin : begin + size] = jnp.sum(squares, axis=0, keepdims=True)
        weights = held[0][held[3]]
        by_weight = jnp.sum(jnp.sum(weights * weights, axis=1, keepdims=True), axis=0, keepdims=True)
        slot = lane_slot(number)
        row_sums = jnp.where(lane == slot, by_row, row_sums)
        totals = jnp.where(one_lane == slot, jnp.sum(by_row, axis=0, keepdims=True), totals)
        totals = jnp.where(one_lane == slot + 32, by_weight, totals)
        held[1][held[3]] = grads
    mine[0:rows, :] = row_sums
    mine[rows : rows + 8, :] = jnp.broadcast_to(totals, (8, 128))
    pl.semaphore_wait(barrier, len(partners))

    def exchange(source, target, number):
        copy = pltpu.make_async_remote_copy(
            src_ref=source,
            dst_ref=target,
            send_sem=send_sems.at[number],
            recv_sem=recv_sems.at[number],
            device_id=partners[number],
            device_id_type=MESH,
        )
        copy.start()
        copy.wait()

    exchange(mine, theirs, 0)
    row_sums = mine[0:rows, :] + theirs[0:rows, :]
    line[:, columns : columns + 128] = mine[rows : rows + 1, :] + theirs[rows : rows + 1, :]
    for number in range(1, 5):
        exchange(line, line_in.at[number - 1], number)
        line[...] += line_in[number - 1]

    totals = line[:, columns : columns + 128]
    across = jnp.where(one_lane < 16, float(2 * width), float(2 * units))
    level = (keep * pltpu.roll(totals, 64, 1) + take * totals / across) / depth
    size_of = jnp.sqrt(pltpu.roll(totals, 96, 1) / (across * depth))
    rows_next = keep * moments + take * row_sums / across

    def pick(row, slot):
        return jnp.sum(jnp.where(lane[0 : row.shape[0], :] == slot, row, 0.0), axis=1, keepdims=True)

    for number, (final, at, size, begin, held) in enumerate(matrices):
        slot = lane_slot(number)
        index = held[3]
        columns_next = keep * held[4][index : index + 1, :] + take * line[:, begin : begin + size] / depth
        held[5][index : index + 1, :] = columns_next
        estimate = pick(rows_next, slot) * columns_next / pick(level, slot)
        step = step_rate * pick(size_of, slot)
        held[2][index] = held[0][index] - step * final[:, at : at + size] * lax.rsqrt(estimate)

    grads = fv[...]
    moments_next = keep * vector_moments + take * grads * grads
    vectors_next = vector_local - step_rate * vector_scale * grads * lax.rsqrt(moments_next)
    small = jnp.where(lane < 32, rows_next, pltpu.roll(grads, 32, 1))
    small = jnp.where(lane < 48, small, pltpu.roll(moments_next, 48, 1))
    small = jnp.where(lane < 64, small, pltpu.roll(vectors_next, 64, 1))
    small = jnp.where(lane < 80, small, pltpu.roll(grads, 70, 1))
    square[0:rows, :] = small
    turned_small = jnp.transpose(square[...])
    ran[...] = turned_small[0:12, 0:rows]
    rfn[...] = turned_small[16:20, 0:rows]
    vg[...] = turned_small[32:46, 0:rows]
    vmn[...] = turned_small[48:62, 0:rows]
    vu[...] = turned_small[64:78, 0:rows]
    fng[...] = turned_small[80:82, 0:rows]


def update_call(finals, aw, fw, ra, ca, rf, cf, vp, vl, vm):
    rows = finals[0].shape[0]
    columns = 12 * aw.shape[2] + 4 * fw.shape[2]

    def same(array):
        return jax.ShapeDtypeStruct(array.shape, wide)

    pair = jax.ShapeDtypeStruct((2, rows), wide)
    far = [*finals[:5], aw, fw]
    return pl.pallas_call(
        update_kernel,
        out_shape=tuple(same(a) for a in (aw, fw, vm, aw, fw, vm, ra, ca, rf, cf, vm)) + (pair,),
        in_specs=[any_space()] * 7 + [whole()] * 8,
        out_specs=tuple([whole()] * 12),
        scratch_shapes=[vmem_like(array) for array in far]
        + [
            pltpu.VMEM((128, 128), wide),
            pltpu.VMEM((128, 128), wide),
            pltpu.VMEM((rows + 8, 128), wide),
            pltpu.VMEM((rows + 8, 128), wide),
            pltpu.VMEM((1, columns + 128), wide),
            pltpu.VMEM((4, 1, columns + 128), wide),
            dma(5),
            dma(5),
            dma(7),
        ],
        compiler_params=pltpu.CompilerParams(
            collective_id=2, has_side_effects=True, vmem_limit_bytes=60 << 20
        ),
        name="update",
    )(*far, finals[5], ra, ca, rf, cf, vp, vl, vm)


def fits_kernels():
    return lax.axis_size("z") == 4


def factored_step(weights, grads, rows_next, columns_next, row_level, mean_square):
    estimate = rows_next[:, :, None] * columns_next[:, None, :] / row_level[:, None, None]
    return weights - step_rate * jnp.sqrt(mean_square)[:, None, None] * grads * lax.rsqrt(estimate)


def plain_pass(source, target, cotangent, marks, vectors, own_groups):
    core = lax.axis_index("c")
    depth = vectors.shape[1]
    source_half = swap_chips(source)
    flags_half = swap_chips(marks[:source.shape[0]])
    source_all = both_halves(source_half)
    flags_all = both_halves(flags_half)
    masks = swap_chips(marks[source.shape[0] :])
    source_length = masks[None, : 2 * source.shape[0]]
    target_length = masks[None, 2 * source.shape[0] :]
    target_all = both_halves(swap_chips(target))
    cotangent_all = both_halves(swap_chips(cotangent))

    (encoder_attention, encoder_feed, decoder_attention, cross_attention, decoder_feed) = [
        (gather_weights(group, "zyx"), group.shape[1]) for group in own_groups
    ]

    start_rows = jnp.where(
        (flags_all == 1)[:, None],
        vectors[12][None, :],
        jnp.where((flags_all == 2)[:, None], vectors[13][None, :], source_all.astype(wide)),
    )
    first_kept = self_attention_call(
        0, False, source_length, start_rows, encoder_attention, vectors,
    )
    first_part = first_kept[5]
    first_other = other_core(first_part)
    encoder_mid, second_normed, second_hidden, second_slope, second_part, *rest = feed_forward_call(
        2, start_rows, first_part, first_other, encoder_feed, vectors,
    )
    second_other = other_core(second_part)
    third_kept = self_attention_call(6, True, target_length, target_all, decoder_attention, vectors)
    third_part = third_kept[5]
    third_other = other_core(third_part)
    decoder_one, encoder_final, memory_rows, *fourth_kept = cross_attention_call(
        source_length,
        target_all,
        third_part,
        third_other,
        encoder_mid,
        second_part,
        second_other,
        cross_attention,
        vectors,
    )
    fourth_part = fourth_kept[5]
    fourth_kept = fourth_kept[:5]
    decoder_two, fifth_normed, fifth_hidden, fifth_slope, fifth_part = feed_forward_call(
        10, decoder_one, fourth_part, other_core(fourth_part), decoder_feed, vectors
    )
    decoder_three = decoder_two + (fifth_part.astype(wide) + other_core(fifth_part).astype(wide))

    def own_half(rows):
        half = rows.shape[0] // 2
        return lax.dynamic_slice_in_dim(rows, core * half, half, 0)

    decoder_out = swap_chips(own_half(decoder_three).astype(low))

    fifth_back, decoder_feed_terms, grad_three = last_feed_backward_call(
        target_length, cotangent_all, fifth_normed, fifth_hidden, fifth_slope, decoder_feed
    )
    query_back, grad_two, vectors_ten, cross_terms, memory_back, *decoder_feed_grad = attention_backward_call(
        False,
        10,
        source_length,
        grad_three,
        decoder_two,
        fifth_back,
        other_core(fifth_back),
        vectors,
        fourth_kept[0],
        memory_rows,
        *fourth_kept[1:],
        cross_attention,
    )
    query_other = other_core(query_back)
    memory_other = other_core(memory_back)
    third_back, grad_one, vectors_eight, decoder_terms, *cross_grad = attention_backward_call(
        True,
        8,
        target_length,
        grad_two,
        decoder_one,
        query_back,
        query_other,
        vectors,
        third_kept[0],
        None,
        *third_kept[1:5],
        decoder_attention,
    )
    third_back_other = other_core(third_back)
    second_back, encoder_feed_terms, grad_final, vectors_four, *decoder_grad = feed_backward_call(
        4,
        encoder_final,
        memory_back,
        memory_other,
        vectors,
        second_normed,
        second_hidden,
        second_slope,
        encoder_feed,
    )
    first_back, grad_mid, vectors_two, encoder_terms, *encoder_feed_grad = attention_backward_call(
        False,
        2,
        source_length,
        grad_final,
        encoder_mid,
        second_back,
        other_core(second_back),
        vectors,
        first_kept[0],
        None,
        *first_kept[1:5],
        encoder_attention,
    )
    grad_target, vectors_six = finish_call(
        6, grad_one, target_all, third_back, third_back_other, vectors
    )
    target_grad = swap_chips(own_half(grad_target).astype(low)).astype(wide)
    grad_start, vectors_zero = finish_call(
        0, grad_mid, start_rows, first_back, other_core(first_back), vectors
    )
    gap_rows = jnp.sum(jnp.where((flags_all == 1)[:, None], grad_start, 0.0), axis=0, keepdims=True)
    mask_rows = jnp.sum(jnp.where((flags_all == 2)[:, None], grad_start, 0.0), axis=0, keepdims=True)
    source_grad = swap_chips(own_half(grad_start).astype(low)).astype(wide)

    vector_terms = jnp.concatenate(
        [
            vectors_zero,
            vectors_two,
            vectors_four,
            vectors_six,
            vectors_eight,
            vectors_ten,
            gap_rows,
            mask_rows,
            jnp.zeros((114, depth), wide),
        ],
        axis=0,
    )
    vector_terms = vector_terms.T.astype(low)
    grads = [
        scatter_gradient(terms, "xyz")
        for terms in (
            encoder_terms, decoder_terms, cross_terms, encoder_feed_terms, decoder_feed_terms, vector_terms
        )
    ]
    return (decoder_out, source_grad, target_grad, *grads)


def on_device(
    source_embed,
    target_embed,
    out_cotangent,
    row_flags,
    source_mask,
    target_mask,
    attention_weights,
    feed_weights,
    rows_attention,
    columns_attention,
    rows_feed,
    columns_feed,
    vector_params,
    vector_moments,
):
    core = lax.axis_index("c")
    local_rows, half_width = attention_weights.shape[1:]
    half_units = feed_weights.shape[2]
    depth = vector_params.shape[1]
    units_all = 2 * half_units

    def attention_group(block):
        part = attention_weights[4 * block : 4 * block + 4].astype(low)
        return part.transpose(1, 0, 2).reshape(local_rows, 4 * half_width)

    def feed_group(index):
        part = feed_weights[2 * index : 2 * index + 2].astype(low)
        return part.transpose(1, 0, 2).reshape(local_rows, 2 * half_units)

    marks = jnp.concatenate([row_flags[0], source_mask[0], target_mask[0]])
    if fits_kernels():
        kept = forward_call(
            source_embed[0], target_embed[0], out_cotangent[0], marks[None], vector_params, attention_weights, feed_weights
        )
        back = backward_call(kept, vector_params)
        decoder_out = back.decoder_out
        target_grad = back.target_grad.astype(wide)
        source_grad = back.source_grad.astype(wide)
        source_grad = jnp.where((row_flags[0] == 0)[:, None], source_grad, 0.0)
        local_width = vector_moments.shape[1]
        number = (lax.axis_index("z") * 2 + lax.axis_index("y")) * 2 + core
        vector_local = lax.dynamic_slice_in_dim(vector_params, number * local_width, local_width, 1)
        updates = update_call(
            [back.final_1, back.final_2, back.final_3, back.final_4, back.final_5, back.final_vectors],
            attention_weights, feed_weights, rows_attention, columns_attention, rows_feed, columns_feed,
            vector_params, vector_local, vector_moments,
        )
        return decoder_out[None], source_grad[None], target_grad[None], *updates
    own_groups = [attention_group(0), feed_group(0), attention_group(1), attention_group(2), feed_group(1)]
    (
        decoder_out, source_grad, target_grad,
        encoder_grad, decoder_grad, cross_grad, encoder_feed_grad, decoder_feed_grad, vector_grad,
    ) = plain_pass(source_embed[0], target_embed[0], out_cotangent[0], marks, vector_params, own_groups)
    source_grad = jnp.where((row_flags[0] == 0)[:, None], source_grad, 0.0)
    vector_grad = vector_grad[:, :14].T

    def as_matrices(rows, count):
        return rows.reshape(local_rows, count, -1).transpose(1, 0, 2)

    attention_grad = jnp.concatenate(
        [as_matrices(part, 4) for part in (encoder_grad, decoder_grad, cross_grad)], axis=0
    )
    feed_grad = jnp.concatenate(
        [as_matrices(part, 2) for part in (encoder_feed_grad, decoder_feed_grad)], axis=0
    )

    weight_squares = jnp.concatenate(
        [
            jnp.sum(attention_weights * attention_weights, axis=(1, 2)),
            jnp.sum(feed_weights * feed_weights, axis=(1, 2)),
            jnp.sum(rows_attention, axis=1) * 0.5,
            jnp.sum(rows_feed, axis=1) * 0.5,
        ]
    )
    early_sums = data_sum(tensor_sum(weight_squares))
    scale_attention, scale_feed = early_sums[:12], early_sums[12:16]
    rows_total_attention, rows_total_feed = early_sums[16:28], early_sums[28:32]
    attention_square = attention_grad * attention_grad
    feed_square = feed_grad * feed_grad
    row_sums = tensor_sum(
        jnp.concatenate([jnp.sum(attention_square, axis=2), jnp.sum(feed_square, axis=2)], axis=0)
    )
    column_attention = jnp.sum(attention_square, axis=1)
    column_feed = jnp.sum(feed_square, axis=1)
    square_totals = jnp.sum(row_sums, axis=1)
    column_sums = data_sum(
        jnp.concatenate([column_attention.reshape(-1), column_feed.reshape(-1), square_totals])
    )
    column_attention = column_sums[: column_attention.size].reshape(column_attention.shape)
    column_feed = column_sums[column_attention.size : -16].reshape(column_feed.shape)
    square_totals = column_sums[-16:]
    keep, take = decay_rate, 1.0 - decay_rate
    rows_attention_next = keep * rows_attention + take * row_sums[:12] / depth
    rows_feed_next = keep * rows_feed + take * row_sums[12:] / units_all
    total_attention = keep * rows_total_attention + take * square_totals[:12] / depth
    total_feed = keep * rows_total_feed + take * square_totals[12:] / units_all
    columns_attention_next = keep * columns_attention + take * column_attention / depth
    columns_feed_next = keep * columns_feed + take * column_feed / depth
    attention_updated = factored_step(
        attention_weights,
        attention_grad,
        rows_attention_next,
        columns_attention_next,
        total_attention / depth,
        scale_attention / (depth * depth),
    )
    feed_updated = factored_step(
        feed_weights,
        feed_grad,
        rows_feed_next,
        columns_feed_next,
        total_feed / depth,
        scale_feed / (depth * units_all),
    )
    local_width = vector_moments.shape[1]
    place = (lax.axis_index("z") * lax.axis_size("y") + lax.axis_index("y")) * 2 + core
    vector_local = lax.dynamic_slice_in_dim(vector_params, place * local_width, local_width, 1)
    vector_moments_next = keep * vector_moments + take * vector_grad * vector_grad
    vector_scale = jnp.sqrt(jnp.mean(vector_params * vector_params, axis=1))
    vector_updated = vector_local - step_rate * vector_scale[:, None] * vector_grad * lax.rsqrt(
        vector_moments_next
    )
    return (
        decoder_out[None],
        source_grad[None],
        target_grad[None],
        attention_grad,
        feed_grad,
        vector_grad,
        attention_updated,
        feed_updated,
        vector_updated,
        rows_attention_next,
        columns_attention_next,
        rows_feed_next,
        columns_feed_next,
        vector_moments_next,
        vector_grad[10:12],
    )


def solution(mesh):
    groups = mesh.shape["dp"] // 4
    inner = Mesh(mesh.devices.reshape(groups, 2, 2, 2), ("z", "y", "c", "x"))
    data = ("z", "y", "c")
    rows3, rows2 = P(data, "x", None), P(data, "x")
    matrix, row_spec, column_spec = P(None, data, "x"), P(None, data), P(None, "x")
    return jax.shard_map(
        on_device,
        mesh=inner,
        in_specs=(
            rows3,
            rows3,
            rows3,
            rows2,
            P(data, None),
            P(data, None),
            matrix,
            matrix,
            row_spec,
            column_spec,
            row_spec,
            column_spec,
            P(),
            row_spec,
        ),
        out_specs=(
            rows3,
            rows3,
            rows3,
            matrix,
            matrix,
            row_spec,
            matrix,
            matrix,
            row_spec,
            row_spec,
            column_spec,
            row_spec,
            column_spec,
            row_spec,
            row_spec,
        ),
        check_vma=False,
    )
```
